32 devices in a mesh: dp: 4 (over z), fsdp: 8 (over y, x, core).
Axes of the slice: x: 2, y: 2, z: 4, core: 2. Of those that a mesh axis runs over, the one named last changes fastest.
Arguments:
- tokens: bfloat16 [8192, 1024], P(('dp', 'fsdp')), may hold values from -6 to 6
- cotangent: bfloat16 [8192, 1024], P(('dp', 'fsdp')), may hold values from -6 to 6
- teacher: bfloat16 [8192, 1024], P(('dp', 'fsdp')), may hold values from -6 to 6
- valid_mask: int32 [8192], P(('dp', 'fsdp')), may hold values from 0 to 1, as said below
- deal_rows: int32 [8192], P(('dp', 'fsdp')), may hold values from 0 to 8191, as said below
- lengths: int32 [64, 3], P(('dp', 'fsdp')), may hold values from 1 to 96, 128 in all within a row
- w_in: bfloat16 [1024, 4096], P(('dp', 'fsdp')), may hold values from -0.1875 to 0.1875
- w_beta: bfloat16 [1024, 8], P(('dp', 'fsdp')), may hold values from -0.1875 to 0.1875
- conv_kernel: bfloat16 [4, 3072], P(None, ('dp', 'fsdp')), may hold values from -3 to 3
- w_out: bfloat16 [1024, 1024], P(('dp', 'fsdp')), may hold values from -0.1875 to 0.1875
- norm_gain: bfloat16 [1024], P(('dp', 'fsdp')), may hold values from 0.25 to 1.75
- out_gain: bfloat16 [128], replicated, may hold values from 0.25 to 1.75
- ffn_gain: bfloat16 [1024], P(('dp', 'fsdp')), may hold values from 0.25 to 1.75
- w_gu: bfloat16 [1024, 5632], P(('dp', 'fsdp')), may hold values from -0.1875 to 0.1875
- w_down: bfloat16 [2816, 1024], P(('dp', 'fsdp')), may hold values from -0.109375 to 0.109375
Outputs:
- output: bfloat16 [8192, 1024], P(('dp', 'fsdp'))
- input_grad: bfloat16 [8192, 1024], P(('dp', 'fsdp'))
- grad_w_in: float32 [1024, 4096], P(('dp', 'fsdp'))
- grad_w_beta: float32 [1024, 8], P(('dp', 'fsdp'))
- grad_conv_kernel: float32 [4, 3072], P(None, ('dp', 'fsdp'))
- grad_w_out: float32 [1024, 1024], P(('dp', 'fsdp'))
- grad_norm_gain: float32 [1024], P(('dp', 'fsdp'))
- grad_out_gain: float32 [128], replicated
- grad_ffn_gain: float32 [1024], P(('dp', 'fsdp'))
- grad_w_gu: float32 [1024, 5632], P(('dp', 'fsdp'))
- grad_w_down: float32 [2816, 1024], P(('dp', 'fsdp'))
- loss: float32 [], replicated
The draws below stay inside these ranges and needn't reach their ends.
Inputs may be any that keep to these rules, and one draw needn't show every extreme that they name: deal_rows is a permutation of 0 .. 8191. Dealt rows d * 256 to (d+1) * 256 - 1 belong to device d (dp+fsdp order, dp slowest), and each device's arriving rows go exactly 8 to every device. Each row gives the lengths of the 3 sequences that fill one block of 128 dealt rows, in order; the largest of each row is 96. `valid_mask`: the first arriving row of each device is 1.
All inputs are finite; a program needn't handle non-finite values.
Results may differ from the reference program's by a relative error of at most 0.0097.
Values may be sent and summed in bfloat16 or wider, within the bound.
A program may use at most 128 MiB of HBM per device.

```python
import math
import jax
import jax.numpy as jnp
import numpy as np
from jax import lax

D = 1024
HEADS = 8
HEAD_DIM = 128
FF = 2816
CONV = 4
SPAN = 64
MBATCH = 2
NSEQ = 3
ROWS_MB = 128
LONGEST = 96
SHARDS = 32
ROWS_DEV = 256
TOKENS = 8192


def draw_valid_mask(key, part):
    places = jnp.arange(TOKENS, dtype=jnp.int32)
    level = 250 + 500 * (places // ROWS_DEV) // SHARDS
    rolled = jax.random.randint(jax.random.fold_in(key, 5), (TOKENS,), 0, 1000, dtype=jnp.int32)
    return jnp.where((places % ROWS_DEV == 0) | (rolled < level), 1, 0).astype(jnp.int32)


def draw_deal_rows(key, part):
    share = ROWS_DEV // SHARDS
    send_keys = jax.random.split(jax.random.fold_in(key, 11), SHARDS)
    send_order = jax.vmap(lambda item: jax.random.permutation(item, ROWS_DEV))(send_keys).astype(jnp.int32)
    recv_keys = jax.random.split(jax.random.fold_in(key, 23), SHARDS)
    recv_order = jax.vmap(lambda item: jax.random.permutation(item, ROWS_DEV))(recv_keys).astype(jnp.int32)
    target = send_order // share
    within = send_order % share
    sources = jnp.arange(SHARDS, dtype=jnp.int32)[:, None]
    slot_index = sources * share + within
    placed = recv_order[target, slot_index]
    return (target * ROWS_DEV + placed).reshape(TOKENS).astype(jnp.int32)


def levels(stream_key, extent, shards, smallest, largest):
    factor_of, own = 1.0, jax.random.fold_in(stream_key, 6)
    for position, shards_of in shards:
        steps = jnp.exp(jax.random.uniform(jax.random.fold_in(own, position), (shards_of,), jnp.float32, smallest / len(shards), largest / len(shards)))
        factor_of = factor_of * jnp.repeat(steps, extent[position] // shards_of).reshape([-1 if axis == position else 1 for axis in range(len(extent))])
    return factor_of


def profile(count, total, most, lean):
    weights = [(1 << 20) // math.isqrt(standing ** lean) + 1 for standing in range(2, count + 1)]
    surplus, counts = total - most - (count - 1), [1] * (count - 1)
    while surplus > 0:
        free = [i for i in range(count - 1) if counts[i] < most]
        pool, budget = sum([weights[i] for i in free]), surplus
        for i in free:
            more = min(most - counts[i], max(1, budget * weights[i] // pool), surplus)
            counts[i] = counts[i] + more
            surplus = surplus - more
    return np.array([most] + counts)


def uneven_parts(key, amount, total, bound, slope):
    if amount == 2:
        one = jax.random.randint(key, (), max(1, total - bound), min(bound, total - 1) + 1)
        return jnp.stack([one, total - one])
    tallies = jnp.asarray(profile(amount, total, bound, slope), jnp.int32)
    twos = (amount - 1) // 2
    giver, sink = tallies[1:1 + 2 * twos:2], tallies[2:2 + 2 * twos:2]
    slack = jnp.minimum(giver - 1, bound - sink)
    passed = jax.random.randint(jax.random.fold_in(key, 1), (twos,), 0, 1 << 20) % (slack + 1)
    tallies = tallies.at[1:1 + 2 * twos:2].set(giver - passed).at[2:2 + 2 * twos:2].set(sink + passed)
    return tallies[jax.random.permutation(jax.random.fold_in(key, 2), amount)]


def bell_draw(rng, dims, deviation, limit, pieces=(), kind=jnp.bfloat16):
    values = jax.random.normal(rng, dims, jnp.float32) * deviation
    if len(pieces) > 0:
        values = levels(rng, dims, pieces, -0.22, 0.18) * values
    return jnp.clip(values, min=-limit, max=limit).astype(kind)


def setup_inputs(seed: int = 0) -> dict:
    seeds = jax.random.split(jax.random.key(seed), 16)
    tokens = bell_draw(seeds[0], (TOKENS, D), 1.0, 6.0, ((0, 32),))
    cotangent = bell_draw(seeds[1], (TOKENS, D), 1.0, 6.0, ((0, 32),))
    teacher = bell_draw(seeds[2], (TOKENS, D), 1.0, 6.0, ((0, 32),))
    valid_mask = draw_valid_mask(jax.random.fold_in(seeds[15], 71), 0)
    deal_rows = draw_deal_rows(jax.random.fold_in(seeds[15], 71), 0)
    lengths = jax.vmap(lambda own: uneven_parts(own, NSEQ, ROWS_MB, LONGEST, 0))(jax.random.split(seeds[5], (SHARDS * MBATCH))).reshape((SHARDS * MBATCH, NSEQ)).astype(jnp.int32)
    w_in = bell_draw(seeds[6], (D, 4 * D), D ** -0.5, 0.1875, ((0, 32),))
    w_beta = bell_draw(seeds[7], (D, HEADS), D ** -0.5, 0.1875, ((0, 32),))
    conv_kernel = bell_draw(seeds[8], (CONV, 3 * D), CONV ** -0.5, 3.0, ((1, 32),))
    w_out = bell_draw(seeds[9], (D, D), D ** -0.5, 0.1875, ((0, 32),))
    norm_gain = jnp.clip(1.0 + 0.15 * jax.random.normal(seeds[10], (D,), jnp.float32), 0.25, 1.75).astype(jnp.bfloat16)
    out_gain = jnp.clip(1.0 + 0.15 * jax.random.normal(seeds[11], (HEAD_DIM,), jnp.float32), 0.25, 1.75).astype(jnp.bfloat16)
    ffn_gain = jnp.clip(1.0 + 0.15 * jax.random.normal(seeds[12], (D,), jnp.float32), 0.25, 1.75).astype(jnp.bfloat16)
    w_gu = bell_draw(seeds[13], (D, 2 * FF), D ** -0.5, 0.1875, ((0, 32),))
    w_down = bell_draw(seeds[14], (FF, D), FF ** -0.5, 0.109375, ((0, 32),))
    return {"tokens": tokens, "cotangent": cotangent, "teacher": teacher, "valid_mask": valid_mask, "deal_rows": deal_rows, "lengths": lengths, "w_in": w_in, "w_beta": w_beta, "conv_kernel": conv_kernel, "w_out": w_out, "norm_gain": norm_gain, "out_gain": out_gain, "ffn_gain": ffn_gain, "w_gu": w_gu, "w_down": w_down}


highest_precision = lax.Precision.HIGHEST

@jax.custom_vjp
def low(v):
    return lax.optimization_barrier(v.astype(jnp.bfloat16)).astype(jnp.float32)

@jax.custom_vjp
def low_back(v):
    return v

def low_keep(v):
    return (low(v), None)

def low_pass(kept, grad):
    return (grad,)

def back_keep(v):
    return (v, None)

def back_low(kept, grad):
    return (low(grad),)
low.defvjp(low_keep, low_pass)
low_back.defvjp(back_keep, back_low)

def rms_norm(values, gains):
    return values * lax.rsqrt(lax.optimization_barrier(jnp.mean(values * values, axis=-1, keepdims=True)) + 1e-05) * gains

def segment_ids(length_row, row_count):
    ends_at = jnp.cumsum(length_row)
    places = jnp.arange(row_count, dtype=jnp.int32)
    return lax.optimization_barrier(jnp.sum((places[:, None] >= ends_at[None, :]).astype(jnp.int32), axis=1))

def short_conv(projected, kernel, segment):
    row_count = projected.shape[0]
    total = projected * kernel[CONV - 1]
    for offset in range(1, CONV):
        moved = jnp.concatenate([jnp.zeros((offset, projected.shape[1]), jnp.float32), projected[:row_count - offset]], axis=0)
        seg_moved = jnp.concatenate([jnp.full((offset,), -1, jnp.int32), segment[:row_count - offset]])
        same_seq = (seg_moved == segment).astype(jnp.float32)
        total = total + moved * kernel[CONV - 1 - offset] * same_seq[:, None]
    return jax.nn.silu(total)

def delta_rule(queries, keys_in, values, strength, segment):
    row_count, head_count, per_head_width = queries.shape
    span_count = row_count // SPAN

    def blocked(array):
        return jnp.swapaxes(array.reshape(span_count, SPAN, head_count, -1), 1, 2)
    q_all, k_all, v_all = (blocked(queries), blocked(keys_in), blocked(values))
    b_all = jnp.swapaxes(strength.reshape(span_count, SPAN, head_count), 1, 2)
    s_all = segment.reshape(span_count, SPAN)
    p_all = jnp.concatenate([jnp.full((1,), -1, jnp.int32), s_all[:-1, -1]])
    strict_lower = jnp.tril(jnp.ones((SPAN, SPAN), jnp.float32), -1)
    with_diag = jnp.tril(jnp.ones((SPAN, SPAN), jnp.float32))
    identity = jnp.eye(SPAN, dtype=jnp.float32)

    def advance(running_state, sliced):
        query_window, key_window, v_span, b_span, s_span, p_span = sliced
        same_seq = (s_span[:, None] == s_span[None, :]).astype(jnp.float32)
        carried_state = (s_span == p_span).astype(jnp.float32)
        final_sequence = (s_span == s_span[-1]).astype(jnp.float32)
        retain_state = carried_state[-1]
        key_gram = jnp.einsum('hik,hjk->hij', key_window, key_window, precision=highest_precision)
        system = identity + key_gram * same_seq * strict_lower * b_span[:, :, None]
        right_side = jnp.concatenate([v_span, key_window * carried_state[None, :, None]], axis=-1) * b_span[:, :, None]
        solved_system = jax.scipy.linalg.solve_triangular(system, right_side, lower=True, unit_diagonal=True)
        pseudo_target = solved_system[..., :per_head_width] - jnp.einsum('arg,agw->arw', solved_system[..., per_head_width:], running_state, precision=highest_precision)
        scores = jnp.einsum('hik,hjk->hij', query_window, key_window, precision=highest_precision) * same_seq * with_diag
        result_output = jnp.einsum('arg,agw->arw', query_window * carried_state[None, :, None], running_state, precision=highest_precision)
        result_output = result_output + jnp.einsum('hij,hjv->hiv', scores, pseudo_target, precision=highest_precision)
        updated_state = retain_state * running_state + jnp.einsum('cen,cer->cnr', key_window * final_sequence[None, :, None], pseudo_target, precision=highest_precision)
        return (updated_state, result_output)
    initial = jnp.zeros((head_count, per_head_width, per_head_width), jnp.float32)
    final_state, outputs = lax.scan(advance, initial, (q_all, k_all, v_all, b_all, s_all, p_all))
    return jnp.swapaxes(outputs, 1, 2).reshape(row_count, head_count, per_head_width)

def mixer_core(projected, beta_pre, kernel, gains_out, segment):
    row_count = projected.shape[0]
    mixed = short_conv(projected[:, :3 * D], kernel, segment)
    queries = mixed[:, :D].reshape(row_count, HEADS, HEAD_DIM)
    keys_in = mixed[:, D:2 * D].reshape(row_count, HEADS, HEAD_DIM)
    values = mixed[:, 2 * D:].reshape(row_count, HEADS, HEAD_DIM)
    queries = queries * lax.rsqrt(lax.optimization_barrier(jnp.sum(queries * queries, axis=-1, keepdims=True)) + 1e-06) * HEAD_DIM ** (-0.5)
    keys_in = keys_in * lax.rsqrt(lax.optimization_barrier(jnp.sum(keys_in * keys_in, axis=-1, keepdims=True)) + 1e-06)
    strength = jax.nn.sigmoid(beta_pre)
    core = delta_rule(queries, keys_in, values, strength, segment)
    gate_part = projected[:, 3 * D:].reshape(row_count, HEADS, HEAD_DIM)
    normed = rms_norm(core, gains_out) * jax.nn.silu(gate_part)
    return normed.reshape(row_count, D)

def gated_unit(both_parts):
    return jax.nn.silu(both_parts[:, :FF]) * both_parts[:, FF:]

def block_forward(inputs_row, segment, weights):
    w_in, w_beta, conv_kernel, w_out, norm_gain, out_gain, ffn_gain, w_gu, w_down = weights
    normed_in = low(rms_norm(inputs_row, norm_gain))
    projected = low_back(jnp.dot(normed_in, w_in, precision=highest_precision))
    beta_pre = low_back(jnp.dot(normed_in, w_beta, precision=highest_precision))
    mixed_out = low(mixer_core(projected, beta_pre, conv_kernel, out_gain, segment))
    resid = inputs_row + low_back(jnp.dot(mixed_out, w_out, precision=highest_precision))
    normed_ffn = low(rms_norm(resid, ffn_gain))
    both_parts = low_back(jnp.dot(normed_ffn, w_gu, precision=highest_precision))
    hidden = low(gated_unit(both_parts))
    return resid + low_back(jnp.dot(hidden, w_down, precision=highest_precision))

def reference(tokens, cotangent, teacher, valid_mask, deal_rows, lengths, w_in, w_beta, conv_kernel, w_out, norm_gain, out_gain, ffn_gain, w_gu, w_down):
    positions = jnp.arange(TOKENS, dtype=jnp.int32)
    source_of = jnp.zeros((TOKENS,), jnp.int32).at[deal_rows].set(positions)
    inputs_dealt = tokens.astype(jnp.float32)[source_of]
    grads_dealt = cotangent.astype(jnp.float32)[source_of]
    teacher_dealt = teacher.astype(jnp.float32)[source_of]
    mask_dealt = valid_mask.astype(jnp.float32)[source_of]
    counted = jnp.sum(valid_mask.astype(jnp.float32))
    segments = jax.vmap(lambda row: segment_ids(row, ROWS_MB))(lengths)
    block_total = SHARDS * MBATCH
    group = math.gcd(block_total, max(1, 4096 // ROWS_MB))
    step_total = block_total // group
    weights = tuple((item.astype(jnp.float32) for item in (w_in, w_beta, conv_kernel, w_out, norm_gain, out_gain, ffn_gain, w_gu, w_down)))

    def forward(weight_set, inputs_all):
        inputs_g = inputs_all.reshape(step_total, group, ROWS_MB, D)
        segs_g = segments.reshape(step_total, group, ROWS_MB)
        teach_g = teacher_dealt.reshape(step_total, group, ROWS_MB, D)
        mask_g = mask_dealt.reshape(step_total, group, ROWS_MB)

        def one_group(carry, sliced):
            inputs_s, segs_s, teach_s, mask_s = sliced
            outputs_s = jax.vmap(lambda rows_in, seg_in: block_forward(rows_in, seg_in, weight_set))(inputs_s, segs_s)
            errors = jnp.sum(mask_s[..., None] * (outputs_s - teach_s) ** 2)
            return (carry + errors, outputs_s)
        total, outputs_all = lax.scan(jax.checkpoint(one_group), jnp.zeros((), jnp.float32), (inputs_g, segs_g, teach_g, mask_g))
        return (outputs_all.reshape(TOKENS, D), total / (D * counted))
    (outputs_all, loss_value), pull = jax.vjp(forward, weights, inputs_dealt)
    weight_grads, input_grads = pull((grads_dealt, jnp.asarray(TOKENS * D / 2.0, jnp.float32)))
    output = outputs_all[deal_rows].astype(jnp.bfloat16)
    input_grad = input_grads[deal_rows].astype(jnp.bfloat16)
    return (output, input_grad, weight_grads[0], weight_grads[1], weight_grads[2], weight_grads[3], weight_grads[4], weight_grads[5], weight_grads[6], weight_grads[7], weight_grads[8], loss_value)
```

```python
import functools

import jax
import jax.numpy as jnp
from jax import lax
from jax.experimental import pallas as pl
from jax.experimental.pallas import tpu as pltpu
from jax.sharding import PartitionSpec as P

D = 1024
HEADS = 8
HEAD_DIM = 128
FF = 2816
CONV = 4
AXES = ("dp", "fsdp")
F32 = jnp.float32
BF16 = jnp.bfloat16
PAIR = 2


def mm(left, right, lc, rc):
    return lax.dot_general(
        left,
        right,
        (((lc,), (rc,)), ((), ())),
        precision=lax.Precision.HIGHEST,
        preferred_element_type=F32,
    )


def sigmoid(v):
    return 1.0 / (1.0 + jnp.exp(-v))


def iota2(shape, axis):
    return lax.broadcasted_iota(jnp.int32, shape, axis)


def unit_lower_inverses(mats, size):
    row, col = iota2((size, size), 0), iota2((size, size), 1)
    eye = (row == col).astype(F32)
    inverses = None
    width = 1
    while width < size:
        corner = ((row // (2 * width)) == (col // (2 * width))) & (
            (row // width) == (col // width) + 1
        )
        edges = [jnp.where(corner, m, 0.0) for m in mats]
        if inverses is None:
            inverses = [eye - e for e in edges]
        else:
            right = [mm(e, x, 1, 0) for e, x in zip(edges, inverses)]
            inverses = [x - mm(x, r, 1, 0) for x, r in zip(inverses, right)]
        width *= 2
    return inverses


def conv_parts(src, taps, masks):
    rolled = [src]
    total = src * taps[CONV - 1 : CONV, :]
    for s in range(1, CONV):
        moved = pltpu.roll(src, s, 0) * masks[s]
        rolled.append(moved)
        total = total + moved * taps[CONV - 1 - s : CONV - s, :]
    return total, rolled


def l2_norm(c):
    inv = lax.rsqrt(jnp.sum(c * c, axis=-1, keepdims=True) + 1e-06)
    return c * inv, inv


def mixer_fwd_kernel(
    blocks, rows_mb,
    pq, pk, pv, pg, beta, tq, tk, tv, gain, mask, segc, segr,
    on_ref, o_ref, ainv_ref, u_ref, p_ref, l_ref,
):
    step = pl.program_id(0)
    masks = [None] + [mask[:, s : s + 1] for s in range(1, CONV)]
    cs = []
    for src, taps in ((pq, tq), (pk, tk), (pv, tv)):
        pre, _ = conv_parts(src[...], taps[...], masks)
        cs.append(pre * sigmoid(pre))
    cq, ck, cv = cs
    strengths = sigmoid(beta[...])
    lane = iota2(strengths.shape, 1)
    gate = pg[...]
    gate = gate * sigmoid(gate)
    row, col = iota2((rows_mb, rows_mb), 0), iota2((rows_mb, rows_mb), 1)
    systems = [(h, b) for h in range(PAIR) for b in range(blocks)]
    qs, ks, vs, bs, sames, lows = [], [], [], [], [], []
    for h, b in systems:
        rs = slice(b * rows_mb, (b + 1) * rows_mb)
        hs = slice(h * HEAD_DIM, (h + 1) * HEAD_DIM)
        q, _ = l2_norm(cq[rs, hs])
        k, _ = l2_norm(ck[rs, hs])
        qs.append(q * HEAD_DIM ** (-0.5))
        ks.append(k)
        vs.append(cv[rs, hs])
        bs.append(
            jnp.sum(jnp.where(lane == step * PAIR + h, strengths, 0.0), axis=1, keepdims=True)[rs]
        )
        sames.append(segc[rs, :] == segr[:, rs])
    for i in range(len(systems)):
        lows.append(jnp.where(sames[i] & (row > col), mm(ks[i], ks[i], 1, 1), 0.0))
    inverses = unit_lower_inverses([l * b for l, b in zip(lows, bs)], rows_mb)
    us = [mm(a, v * b, 1, 0) for a, v, b in zip(inverses, vs, bs)]
    ps = [
        jnp.where(same & (row >= col), mm(q, k, 1, 1), 0.0)
        for q, k, same in zip(qs, ks, sames)
    ]
    os = [mm(p, u, 1, 0) for p, u in zip(ps, us)]
    for i, (h, b) in enumerate(systems):
        rs = slice(b * rows_mb, (b + 1) * rows_mb)
        hs = slice(h * HEAD_DIM, (h + 1) * HEAD_DIM)
        o = os[i]
        inv = lax.rsqrt(jnp.mean(o * o, axis=-1, keepdims=True) + 1e-05)
        on_ref[rs, hs] = (o * inv * gain[...] * gate[rs, hs]).astype(BF16)
        o_ref[rs, hs] = o
        ainv_ref[h, b] = inverses[i]
        u_ref[h, b] = us[i]
        p_ref[h, b] = ps[i]
        l_ref[h, b] = lows[i]


def mixer_bwd_kernel(
    blocks, rows_mb,
    pq, pk, pv, pg, beta, tq, tk, tv, gain, mask, segc, segr,
    don_ref, o_ref, ainv_ref, u_ref, p_ref, l_ref,
    dq_ref, dk_ref, dv_ref, dg_ref, dbeta_ref, dtq, dtk, dtv, dgain_ref,
):
    step = pl.program_id(0)
    rows = blocks * rows_mb
    masks = [None] + [mask[:, s : s + 1] for s in range(1, CONV)]
    pres, rolls, cs, sig = [], [], [], []
    for src, taps in ((pq, tq), (pk, tk), (pv, tv)):
        pre, rolled = conv_parts(src[...], taps[...], masks)
        s = sigmoid(pre)
        pres.append(pre)
        rolls.append(rolled)
        sig.append(s)
        cs.append(pre * s)
    cq, ck, cv = cs
    strengths = sigmoid(beta[...])
    lane = iota2(strengths.shape, 1)
    row, col = iota2((rows_mb, rows_mb), 0), iota2((rows_mb, rows_mb), 1)
    gates = pg[...]
    gsig = sigmoid(gates)
    gate = gates * gsig
    dgate = gsig * (1.0 + gates * (1.0 - gsig))
    systems = [(h, b) for h in range(PAIR) for b in range(blocks)]
    part = []
    dgain = jnp.zeros((1, HEAD_DIM), F32)
    for h, b in systems:
        rs = slice(b * rows_mb, (b + 1) * rows_mb)
        hs = slice(h * HEAD_DIM, (h + 1) * HEAD_DIM)
        k, ik = l2_norm(ck[rs, hs])
        qn, iq = l2_norm(cq[rs, hs])
        v = cv[rs, hs]
        bb = jnp.sum(jnp.where(lane == step * PAIR + h, strengths, 0.0), axis=1, keepdims=True)[rs]
        same = segc[rs, :] == segr[:, rs]
        o = o_ref[rs, hs]
        don = don_ref[rs, hs]
        inv = lax.rsqrt(jnp.mean(o * o, axis=-1, keepdims=True) + 1e-05)
        no = o * inv
        scaled = don * gain[...]
        dg_ref[rs, hs] = (scaled * no * dgate[rs, hs]).astype(BF16)
        dgain = dgain + jnp.sum(don * no * gate[rs, hs], axis=0, keepdims=True)
        dno = scaled * gate[rs, hs]
        do = inv * (dno - no * jnp.mean(no * dno, axis=-1, keepdims=True))
        part.append([q_ for q_ in (qn, iq, k, ik, v, bb, same, do)])
    dus = [mm(p_ref[h, b], part[i][7], 0, 0) for i, (h, b) in enumerate(systems)]
    dps = [
        jnp.where(part[i][6] & (row >= col), mm(part[i][7], u_ref[h, b], 1, 1), 0.0)
        for i, (h, b) in enumerate(systems)
    ]
    drs = [mm(ainv_ref[h, b], dus[i], 0, 0) for i, (h, b) in enumerate(systems)]
    scale = HEAD_DIM ** (-0.5)
    dqs = [mm(dps[i], part[i][2], 1, 0) * scale for i in range(len(systems))]
    das = [mm(drs[i], u_ref[h, b], 1, 1) for i, (h, b) in enumerate(systems)]
    dks = [mm(dps[i], part[i][0] * scale, 0, 0) for i in range(len(systems))]
    dgs = []
    for i in range(len(systems)):
        g = jnp.where(part[i][6] & (row > col), das[i] * (-part[i][5]), 0.0)
        dgs.append(g + g.T)
    dks = [dks[i] + mm(dgs[i], part[i][2], 1, 0) for i in range(len(systems))]
    dbeta = jnp.zeros(strengths.shape, F32)
    dcs = [[], [], []]
    for i, (h, b) in enumerate(systems):
        qn, iq, k, ik, v, bb, same, do = part[i]
        dv = drs[i] * bb
        db = jnp.sum(drs[i] * v - das[i] * l_ref[h, b], axis=-1, keepdims=True)
        dbp = db * bb * (1.0 - bb)
        pieces = [dbp if b == c else jnp.zeros((rows_mb, 1), F32) for c in range(blocks)]
        column = jnp.concatenate(pieces, axis=0) if blocks > 1 else dbp
        dbeta = dbeta + jnp.where(lane == step * PAIR + h, column, 0.0)
        dcs[0].append(iq * (dqs[i] - qn * jnp.sum(qn * dqs[i], axis=-1, keepdims=True)))
        dcs[1].append(ik * (dks[i] - k * jnp.sum(k * dks[i], axis=-1, keepdims=True)))
        dcs[2].append(dv)
    for j, (out, dtap, taps) in enumerate(((dq_ref, dtq, tq), (dk_ref, dtk, tk), (dv_ref, dtv, tv))):
        whole = jnp.concatenate(
            [
                jnp.concatenate([dcs[j][h * blocks + b] for b in range(blocks)], axis=0)
                for h in range(PAIR)
            ],
            axis=1,
        )
        dpre = whole * (sig[j] * (1.0 + pres[j] * (1.0 - sig[j])))
        tap = taps[...]
        grad = dpre * tap[CONV - 1 : CONV, :]
        dtap[CONV - 1 : CONV, :] = jnp.sum(dpre * rolls[j][0], axis=0, keepdims=True)
        for s in range(1, CONV):
            dtap[CONV - 1 - s : CONV - s, :] = jnp.sum(dpre * rolls[j][s], axis=0, keepdims=True)
            grad = grad + pltpu.roll(dpre * masks[s], rows - s, 0) * tap[CONV - 1 - s : CONV - s, :]
        out[...] = grad.astype(BF16)

    @pl.when(step == 0)
    def _():
        dbeta_ref[...] = jnp.zeros_like(dbeta_ref)
        dgain_ref[...] = jnp.zeros_like(dgain_ref)

    dbeta_ref[...] += dbeta
    dgain_ref[...] += dgain


def mixer_specs(rows, blocks, rows_mb):
    width = PAIR * HEAD_DIM
    per = D // width
    col = lambda k: pl.BlockSpec((rows, width), lambda i, k=k: (0, k * per + i))
    tap = lambda k: pl.BlockSpec((CONV, width), lambda i, k=k: (0, k * per + i))
    full = lambda shape: pl.BlockSpec(shape, lambda i: (0,) * len(shape))
    ins = [col(0), col(1), col(2), col(3), full((rows, HEADS)), tap(0), tap(1), tap(2),
           full((1, HEAD_DIM)), full((rows, 8)), full((rows, 1)), full((1, rows))]
    mat = pl.BlockSpec((PAIR, blocks, rows_mb, rows_mb), lambda i: (i, 0, 0, 0))
    one = pl.BlockSpec((rows, width), lambda i: (0, i))
    otap = pl.BlockSpec((CONV, width), lambda i: (0, i))
    return ins, mat, one, otap, full


def mixer_forward(proj, beta_pre, taps, gain, mask, segc, segr, blocks):
    rows = proj.shape[0]
    rows_mb = rows // blocks
    ins, mat, one, _, _ = mixer_specs(rows, blocks, rows_mb)
    square = jax.ShapeDtypeStruct((HEADS, blocks, rows_mb, rows_mb), F32)
    return pl.pallas_call(
        functools.partial(mixer_fwd_kernel, blocks, rows_mb),
        grid=(HEADS // PAIR,),
        in_specs=ins,
        out_specs=[one, one, mat, mat, mat, mat],
        out_shape=[
            jax.ShapeDtypeStruct((rows, D), BF16),
            jax.ShapeDtypeStruct((rows, D), F32),
            square, square, square, square,
        ],
        compiler_params=pltpu.CompilerParams(vmem_limit_bytes=48 << 20),
        name="mixer_fwd",
    )(proj, proj, proj, proj, beta_pre, taps, taps, taps, gain, mask, segc, segr)


def mixer_backward(proj, beta_pre, taps, gain, mask, segc, segr, don, saved, blocks):
    rows = proj.shape[0]
    rows_mb = rows // blocks
    ins, mat, one, otap, full = mixer_specs(rows, blocks, rows_mb)
    tapshape = jax.ShapeDtypeStruct((CONV, D), F32)
    wide = jax.ShapeDtypeStruct((rows, D), BF16)
    return pl.pallas_call(
        functools.partial(mixer_bwd_kernel, blocks, rows_mb),
        grid=(HEADS // PAIR,),
        in_specs=ins + [one, one, mat, mat, mat, mat],
        out_specs=[one, one, one, one, full((rows, HEADS)), otap, otap, otap, full((1, HEAD_DIM))],
        out_shape=[
            wide, wide, wide, wide,
            jax.ShapeDtypeStruct((rows, HEADS), F32),
            tapshape, tapshape, tapshape,
            jax.ShapeDtypeStruct((1, HEAD_DIM), F32),
        ],
        compiler_params=pltpu.CompilerParams(vmem_limit_bytes=48 << 20),
        name="mixer_bwd",
    )(proj, proj, proj, proj, beta_pre, taps, taps, taps, gain, mask, segc, segr, don, *saved)


def nt(left, right):
    return lax.dot_general(left, right, (((1,), (1,)), ((), ())), preferred_element_type=F32)


def tn(left, right, dtype=F32):
    return lax.dot_general(left, right, (((0,), (0,)), ((), ())), preferred_element_type=dtype)


def nn(left, right):
    return jnp.dot(left, right, preferred_element_type=F32)


def rms(v):
    inv = lax.rsqrt(jnp.mean(v * v, axis=-1, keepdims=True) + 1e-05)
    return v * inv, inv


def rms_back(normed, inv, dn):
    return inv * (dn - normed * jnp.mean(normed * dn, axis=-1, keepdims=True))


def local(
    tokens, cotangent, teacher, valid_mask, deal_rows, lengths, w_in, w_beta, conv_kernel, w_out,
    norm_gain, out_gain, ffn_gain, w_gu, w_down,
):
    shards = lax.axis_size(AXES)
    rows = tokens.shape[0]
    share = rows // shards
    blocks = lengths.shape[0]
    rows_mb = rows // blocks
    small = w_beta.shape[0] * HEADS + CONV * conv_kernel.shape[1] + 2 * norm_gain.shape[0]

    target = deal_rows // rows
    spot = deal_rows % rows
    ahead = (target[None, :] == target[:, None]) & (
        jnp.arange(rows)[None, :] < jnp.arange(rows)[:, None]
    )
    slot = target * share + jnp.sum(ahead.astype(jnp.int32), axis=1)
    sort_t = (slot[:, None] == jnp.arange(rows)[None, :]).astype(BF16)
    sort = (slot[None, :] == jnp.arange(rows)[:, None]).astype(BF16)
    count_own = jnp.sum(valid_mask.astype(F32))
    lane = jnp.arange(128)[None, :]
    notes = jnp.where(
        lane == 0,
        valid_mask.astype(F32)[:, None],
        jnp.where(lane == 1, spot.astype(F32)[:, None], jnp.where(lane == 2, count_own, 0.0)),
    ).astype(BF16)
    packed = jnp.concatenate(
        [conv_kernel.reshape(-1), w_beta.reshape(-1), norm_gain, ffn_gain,
         jnp.zeros((share * 128 - small,), BF16)]
    ).reshape(1, share, 128)
    sorted_rows = nn(sort, jnp.concatenate([tokens, cotangent, teacher, notes], axis=1)).astype(BF16)
    message = jnp.concatenate(
        [sorted_rows.reshape(shards, share, -1), jnp.broadcast_to(packed, (shards, share, 128))],
        axis=2,
    )
    arrived = lax.all_to_all(message, AXES, split_axis=0, concat_axis=0, tiled=True)

    win = lax.all_gather(w_in, AXES, axis=0, tiled=True)
    wout = lax.all_gather(w_out, AXES, axis=0, tiled=True)
    wgu = lax.all_gather(w_gu, AXES, axis=0, tiled=True)
    wdown = lax.all_gather(w_down, AXES, axis=0, tiled=True)

    flat = arrived.reshape(rows, -1)
    info = flat[:, 3 * D : 3 * D + 128].astype(F32)
    place = info[:, 1].astype(jnp.int32)
    counted = jnp.sum(arrived[:, 0, 3 * D + 2].astype(F32))
    extra = arrived[:, :, 3 * D + 128 :].reshape(shards, share * 128)
    a, b, c = CONV * conv_kernel.shape[1], w_beta.shape[0] * HEADS, norm_gain.shape[0]
    taps = extra[:, :a].reshape(shards, CONV, -1).swapaxes(0, 1).reshape(CONV, 3 * D).astype(F32)
    wbeta = extra[:, a : a + b].reshape(D, HEADS)
    gain_one = extra[:, a + b : a + b + c].reshape(D).astype(F32)
    gain_two = extra[:, a + b + c : a + b + 2 * c].reshape(D).astype(F32)
    deal = (place[None, :] == jnp.arange(rows)[:, None]).astype(BF16)
    deal_t = (place[:, None] == jnp.arange(rows)[None, :]).astype(BF16)
    dealt = nn(deal, flat[:, : 3 * D + 128])
    x = dealt[:, :D]
    g = dealt[:, D : 2 * D]
    t = dealt[:, 2 * D : 3 * D]
    m = dealt[:, 3 * D : 3 * D + 1]

    ends = jnp.cumsum(lengths, axis=1)
    within = jnp.arange(rows_mb, dtype=jnp.int32)
    seg = jnp.sum((within[None, :, None] >= ends[:, None, :]).astype(jnp.int32), axis=2)
    seg = (seg + (lengths.shape[1] + 1) * jnp.arange(blocks, dtype=jnp.int32)[:, None]).reshape(rows)
    position = jnp.arange(rows, dtype=jnp.int32)
    mask = jnp.stack(
        [jnp.ones((rows,), F32)]
        + [((position >= s) & (jnp.roll(seg, s) == seg)).astype(F32) for s in range(1, CONV)]
        + [jnp.zeros((rows,), F32)] * (8 - CONV),
        axis=1,
    )
    segc, segr = seg[:, None], seg[None, :]
    gain_out = out_gain.astype(F32)[None, :]

    nx, rx = rms(x)
    a1 = (nx * gain_one).astype(BF16)
    proj = nn(a1, win)
    beta_pre = nn(a1, wbeta)
    on, *saved = mixer_forward(proj, beta_pre, taps, gain_out, mask, segc, segr, blocks)
    resid = x + nn(on, wout)
    nr, rr = rms(resid)
    a2 = (nr * gain_two).astype(BF16)
    gu = nn(a2, wgu)
    gate, up = gu[:, :FF], gu[:, FF:]
    sg = sigmoid(gate)
    hid = (gate * sg * up).astype(BF16)
    y = resid + nn(hid, wdown)
    errors = y - t
    loss_part = jnp.sum(m * errors * errors)
    dy = g + (rows * shards / counted) * m * errors
    df = dy.astype(BF16)
    dhid = nt(df, wdown)
    dgu = jnp.concatenate(
        [dhid * up * (sg * (1.0 + gate * (1.0 - sg))), dhid * (gate * sg)], axis=1
    ).astype(BF16)
    da2 = nt(dgu, wgu)
    d_gain_two = jnp.sum(da2 * nr, axis=0)
    dresid = dy + rms_back(nr, rr, gain_two * da2)
    dz = dresid.astype(BF16)
    don = nt(dz, wout)
    dpq, dpk, dpv, dpg, dbeta, dtq, dtk, dtv, d_gain_out = mixer_backward(
        proj, beta_pre, taps, gain_out, mask, segc, segr, don, saved, blocks
    )
    dproj = jnp.concatenate([dpq, dpk, dpv, dpg], axis=1)
    dbeta = dbeta.astype(BF16)
    da1 = nt(dproj, win) + nt(dbeta, wbeta)
    d_gain_one = jnp.sum(da1 * nx, axis=0)
    dx = dresid + rms_back(nx, rx, gain_one * da1)

    def scatter(v):
        return lax.psum_scatter(v, AXES, scatter_dimension=0, tiled=True).astype(F32)

    g_gu = scatter(tn(a2, dgu).astype(BF16))
    g_down = scatter(tn(hid, df).astype(BF16))
    g_in = scatter(tn(a1, dproj).astype(BF16))
    g_out = scatter(tn(on, dz).astype(BF16))

    d_taps = jnp.concatenate([dtq, dtk, dtv], axis=1)
    d_wbeta = tn(a1, dbeta)
    tail = jnp.concatenate([d_gain_out.reshape(-1), loss_part.reshape(1)])
    extra = jnp.concatenate(
        [
            d_taps.reshape(CONV, shards, -1).swapaxes(0, 1).reshape(shards, a),
            d_wbeta.reshape(shards, b),
            d_gain_one.reshape(shards, c),
            d_gain_two.reshape(shards, c),
            jnp.broadcast_to(tail[None], (shards, tail.shape[0])),
        ],
        axis=1,
    )
    padded = -(-extra.shape[1] // 128) * 128
    extra = jnp.pad(extra, ((0, 0), (0, padded - extra.shape[1])))
    summed = jnp.sum(
        lax.all_to_all(
            extra.reshape(shards, padded // 128, 128), AXES, split_axis=0, concat_axis=0, tiled=True
        ),
        axis=0,
    ).reshape(-1)
    g_taps = summed[:a].reshape(CONV, -1)
    g_beta = summed[a : a + b].reshape(-1, HEADS)
    g_gain_one = summed[a + b : a + b + c]
    g_gain_two = summed[a + b + c : a + b + 2 * c]
    g_gain_out = summed[a + b + 2 * c : a + b + 2 * c + HEAD_DIM]
    loss = summed[a + b + 2 * c + HEAD_DIM] / (D * counted)

    def give_back(v):
        sent = nn(deal_t, v.astype(BF16)).astype(BF16).reshape(shards, share, D)
        got = lax.all_to_all(sent, AXES, split_axis=0, concat_axis=0, tiled=True)
        return nn(sort_t, got.reshape(rows, D)).astype(BF16)

    output = give_back(y)
    input_grad = give_back(dx)
    return (
        output, input_grad, g_in, g_beta, g_taps, g_out, g_gain_one, g_gain_out, g_gain_two, g_gu,
        g_down, loss,
    )


def solution(mesh):
    both = P(AXES, None)
    flat = P(AXES)
    in_specs = (both, both, both, flat, flat, both, both, both, P(None, AXES), both, flat, P(), flat,
                both, both)
    out_specs = (both, both, both, both, P(None, AXES), both, flat, P(), flat, both, both, P())
    return jax.shard_map(local, mesh=mesh, in_specs=in_specs, out_specs=out_specs, check_vma=False)
```

```python
import functools

import jax
import jax.numpy as jnp
from jax import lax
from jax.experimental import pallas as pl
from jax.experimental.pallas import tpu as pltpu
from jax.sharding import PartitionSpec as P

D = 1024
HEADS = 8
HEAD_DIM = 128
FF = 2816
CONV = 4
AXES = ("dp", "fsdp")
F32 = jnp.float32
BF16 = jnp.bfloat16
PAIR = 2
MESH = pl.DeviceIdType.MESH


def mm(left, right, lc, rc):
    return lax.dot_general(
        left,
        right,
        (((lc,), (rc,)), ((), ())),
        precision=lax.Precision.HIGHEST,
        preferred_element_type=F32,
    )


def sigmoid(v):
    return 1.0 / (1.0 + jnp.exp(-v))


def iota2(shape, axis):
    return lax.broadcasted_iota(jnp.int32, shape, axis)


def unit_lower_inverses(mats, size):
    row, col = iota2((size, size), 0), iota2((size, size), 1)
    eye = (row == col).astype(F32)
    inverses = None
    width = 1
    while width < size:
        corner = ((row // (2 * width)) == (col // (2 * width))) & (
            (row // width) == (col // width) + 1
        )
        edges = [jnp.where(corner, m, 0.0) for m in mats]
        if inverses is None:
            inverses = [eye - e for e in edges]
        else:
            right = [mm(e, x, 1, 0) for e, x in zip(edges, inverses)]
            inverses = [x - mm(x, r, 1, 0) for x, r in zip(inverses, right)]
        width *= 2
    return inverses


def conv_parts(src, taps, masks):
    rolled = [src]
    total = src * taps[CONV - 1 : CONV, :]
    for s in range(1, CONV):
        moved = pltpu.roll(src, s, 0) * masks[s]
        rolled.append(moved)
        total = total + moved * taps[CONV - 1 - s : CONV - s, :]
    return total, rolled


def l2_norm(c):
    inv = lax.rsqrt(jnp.sum(c * c, axis=-1, keepdims=True) + 1e-06)
    return c * inv, inv


def mixer_fwd_kernel(
    blocks, rows_mb,
    pq, pk, pv, pg, beta, tq, tk, tv, gain, mask, segc, segr,
    on_ref, o_ref, ainv_ref, u_ref, p_ref, l_ref,
):
    step = pl.program_id(0)
    masks = [None] + [mask[:, s : s + 1] for s in range(1, CONV)]
    cs = []
    for src, taps in ((pq, tq), (pk, tk), (pv, tv)):
        pre, _ = conv_parts(src[...], taps[...], masks)
        cs.append(pre * sigmoid(pre))
    cq, ck, cv = cs
    strengths = sigmoid(beta[...])
    lane = iota2(strengths.shape, 1)
    gate = pg[...]
    gate = gate * sigmoid(gate)
    row, col = iota2((rows_mb, rows_mb), 0), iota2((rows_mb, rows_mb), 1)
    systems = [(h, b) for h in range(PAIR) for b in range(blocks)]
    qs, ks, vs, bs, sames, lows = [], [], [], [], [], []
    for h, b in systems:
        rs = slice(b * rows_mb, (b + 1) * rows_mb)
        hs = slice(h * HEAD_DIM, (h + 1) * HEAD_DIM)
        q, _ = l2_norm(cq[rs, hs])
        k, _ = l2_norm(ck[rs, hs])
        qs.append(q * HEAD_DIM ** (-0.5))
        ks.append(k)
        vs.append(cv[rs, hs])
        bs.append(
            jnp.sum(jnp.where(lane == step * PAIR + h, strengths, 0.0), axis=1, keepdims=True)[rs]
        )
        sames.append(segc[rs, :] == segr[:, rs])
    for i in range(len(systems)):
        lows.append(jnp.where(sames[i] & (row > col), mm(ks[i], ks[i], 1, 1), 0.0))
    inverses = unit_lower_inverses([l * b for l, b in zip(lows, bs)], rows_mb)
    us = [mm(a, v * b, 1, 0) for a, v, b in zip(inverses, vs, bs)]
    ps = [
        jnp.where(same & (row >= col), mm(q, k, 1, 1), 0.0)
        for q, k, same in zip(qs, ks, sames)
    ]
    os = [mm(p, u, 1, 0) for p, u in zip(ps, us)]
    for i, (h, b) in enumerate(systems):
        rs = slice(b * rows_mb, (b + 1) * rows_mb)
        hs = slice(h * HEAD_DIM, (h + 1) * HEAD_DIM)
        o = os[i]
        inv = lax.rsqrt(jnp.mean(o * o, axis=-1, keepdims=True) + 1e-05)
        on_ref[rs, hs] = (o * inv * gain[...] * gate[rs, hs]).astype(BF16)
        o_ref[rs, hs] = o
        ainv_ref[h, b] = inverses[i]
        u_ref[h, b] = us[i]
        p_ref[h, b] = ps[i]
        l_ref[h, b] = lows[i]


def mixer_bwd_kernel(
    blocks, rows_mb,
    pq, pk, pv, pg, beta, tq, tk, tv, gain, mask, segc, segr,
    don_ref, o_ref, ainv_ref, u_ref, p_ref, l_ref,
    dq_ref, dk_ref, dv_ref, dg_ref, dbeta_ref, dtq, dtk, dtv, dgain_ref,
):
    step = pl.program_id(0)
    rows = blocks * rows_mb
    masks = [None] + [mask[:, s : s + 1] for s in range(1, CONV)]
    pres, rolls, cs, sig = [], [], [], []
    for src, taps in ((pq, tq), (pk, tk), (pv, tv)):
        pre, rolled = conv_parts(src[...], taps[...], masks)
        s = sigmoid(pre)
        pres.append(pre)
        rolls.append(rolled)
        sig.append(s)
        cs.append(pre * s)
    cq, ck, cv = cs
    strengths = sigmoid(beta[...])
    lane = iota2(strengths.shape, 1)
    row, col = iota2((rows_mb, rows_mb), 0), iota2((rows_mb, rows_mb), 1)
    gates = pg[...]
    gsig = sigmoid(gates)
    gate = gates * gsig
    dgate = gsig * (1.0 + gates * (1.0 - gsig))
    systems = [(h, b) for h in range(PAIR) for b in range(blocks)]
    part = []
    dgain = jnp.zeros((1, HEAD_DIM), F32)
    for h, b in systems:
        rs = slice(b * rows_mb, (b + 1) * rows_mb)
        hs = slice(h * HEAD_DIM, (h + 1) * HEAD_DIM)
        k, ik = l2_norm(ck[rs, hs])
        qn, iq = l2_norm(cq[rs, hs])
        v = cv[rs, hs]
        bb = jnp.sum(jnp.where(lane == step * PAIR + h, strengths, 0.0), axis=1, keepdims=True)[rs]
        same = segc[rs, :] == segr[:, rs]
        o = o_ref[rs, hs]
        don = don_ref[rs, hs]
        inv = lax.rsqrt(jnp.mean(o * o, axis=-1, keepdims=True) + 1e-05)
        no = o * inv
        scaled = don * gain[...]
        dg_ref[rs, hs] = (scaled * no * dgate[rs, hs]).astype(BF16)
        dgain = dgain + jnp.sum(don * no * gate[rs, hs], axis=0, keepdims=True)
        dno = scaled * gate[rs, hs]
        do = inv * (dno - no * jnp.mean(no * dno, axis=-1, keepdims=True))
        part.append([q_ for q_ in (qn, iq, k, ik, v, bb, same, do)])
    dus = [mm(p_ref[h, b], part[i][7], 0, 0) for i, (h, b) in enumerate(systems)]
    dps = [
        jnp.where(part[i][6] & (row >= col), mm(part[i][7], u_ref[h, b], 1, 1), 0.0)
        for i, (h, b) in enumerate(systems)
    ]
    drs = [mm(ainv_ref[h, b], dus[i], 0, 0) for i, (h, b) in enumerate(systems)]
    scale = HEAD_DIM ** (-0.5)
    dqs = [mm(dps[i], part[i][2], 1, 0) * scale for i in range(len(systems))]
    das = [mm(drs[i], u_ref[h, b], 1, 1) for i, (h, b) in enumerate(systems)]
    dks = [mm(dps[i], part[i][0] * scale, 0, 0) for i in range(len(systems))]
    dgs = []
    for i in range(len(systems)):
        g = jnp.where(part[i][6] & (row > col), das[i] * (-part[i][5]), 0.0)
        dgs.append(g + g.T)
    dks = [dks[i] + mm(dgs[i], part[i][2], 1, 0) for i in range(len(systems))]
    dbeta = jnp.zeros(strengths.shape, F32)
    dcs = [[], [], []]
    for i, (h, b) in enumerate(systems):
        qn, iq, k, ik, v, bb, same, do = part[i]
        dv = drs[i] * bb
        db = jnp.sum(drs[i] * v - das[i] * l_ref[h, b], axis=-1, keepdims=True)
        dbp = db * bb * (1.0 - bb)
        pieces = [dbp if b == c else jnp.zeros((rows_mb, 1), F32) for c in range(blocks)]
        column = jnp.concatenate(pieces, axis=0) if blocks > 1 else dbp
        dbeta = dbeta + jnp.where(lane == step * PAIR + h, column, 0.0)
        dcs[0].append(iq * (dqs[i] - qn * jnp.sum(qn * dqs[i], axis=-1, keepdims=True)))
        dcs[1].append(ik * (dks[i] - k * jnp.sum(k * dks[i], axis=-1, keepdims=True)))
        dcs[2].append(dv)
    for j, (out, dtap, taps) in enumerate(((dq_ref, dtq, tq), (dk_ref, dtk, tk), (dv_ref, dtv, tv))):
        whole = jnp.concatenate(
            [
                jnp.concatenate([dcs[j][h * blocks + b] for b in range(blocks)], axis=0)
                for h in range(PAIR)
            ],
            axis=1,
        )
        dpre = whole * (sig[j] * (1.0 + pres[j] * (1.0 - sig[j])))
        tap = taps[...]
        grad = dpre * tap[CONV - 1 : CONV, :]
        dtap[CONV - 1 : CONV, :] = jnp.sum(dpre * rolls[j][0], axis=0, keepdims=True)
        for s in range(1, CONV):
            dtap[CONV - 1 - s : CONV - s, :] = jnp.sum(dpre * rolls[j][s], axis=0, keepdims=True)
            grad = grad + pltpu.roll(dpre * masks[s], rows - s, 0) * tap[CONV - 1 - s : CONV - s, :]
        out[...] = grad.astype(BF16)

    @pl.when(step == 0)
    def _():
        dbeta_ref[...] = jnp.zeros_like(dbeta_ref)
        dgain_ref[...] = jnp.zeros_like(dgain_ref)

    dbeta_ref[...] += dbeta
    dgain_ref[...] += dgain


def mixer_specs(rows, blocks, rows_mb):
    width = PAIR * HEAD_DIM
    per = D // width
    col = lambda k: pl.BlockSpec((rows, width), lambda i, k=k: (0, k * per + i))
    tap = lambda k: pl.BlockSpec((CONV, width), lambda i, k=k: (0, k * per + i))
    full = lambda shape: pl.BlockSpec(shape, lambda i: (0,) * len(shape))
    ins = [col(0), col(1), col(2), col(3), full((rows, HEADS)), tap(0), tap(1), tap(2),
           full((1, HEAD_DIM)), full((rows, 8)), full((rows, 1)), full((1, rows))]
    mat = pl.BlockSpec((PAIR, blocks, rows_mb, rows_mb), lambda i: (i, 0, 0, 0))
    one = pl.BlockSpec((rows, width), lambda i: (0, i))
    otap = pl.BlockSpec((CONV, width), lambda i: (0, i))
    return ins, mat, one, otap, full


def mixer_forward(proj, beta_pre, taps, gain, mask, segc, segr, blocks):
    rows = proj.shape[0]
    rows_mb = rows // blocks
    ins, mat, one, _, _ = mixer_specs(rows, blocks, rows_mb)
    square = jax.ShapeDtypeStruct((HEADS, blocks, rows_mb, rows_mb), F32)
    return pl.pallas_call(
        functools.partial(mixer_fwd_kernel, blocks, rows_mb),
        grid=(HEADS // PAIR,),
        in_specs=ins,
        out_specs=[one, one, mat, mat, mat, mat],
        out_shape=[
            jax.ShapeDtypeStruct((rows, D), BF16),
            jax.ShapeDtypeStruct((rows, D), F32),
            square, square, square, square,
        ],
        compiler_params=pltpu.CompilerParams(vmem_limit_bytes=48 << 20),
        name="mixer_fwd",
    )(proj, proj, proj, proj, beta_pre, taps, taps, taps, gain, mask, segc, segr)


def mixer_backward(proj, beta_pre, taps, gain, mask, segc, segr, don, saved, blocks):
    rows = proj.shape[0]
    rows_mb = rows // blocks
    ins, mat, one, otap, full = mixer_specs(rows, blocks, rows_mb)
    tapshape = jax.ShapeDtypeStruct((CONV, D), F32)
    wide = jax.ShapeDtypeStruct((rows, D), BF16)
    return pl.pallas_call(
        functools.partial(mixer_bwd_kernel, blocks, rows_mb),
        grid=(HEADS // PAIR,),
        in_specs=ins + [one, one, mat, mat, mat, mat],
        out_specs=[one, one, one, one, full((rows, HEADS)), otap, otap, otap, full((1, HEAD_DIM))],
        out_shape=[
            wide, wide, wide, wide,
            jax.ShapeDtypeStruct((rows, HEADS), F32),
            tapshape, tapshape, tapshape,
            jax.ShapeDtypeStruct((1, HEAD_DIM), F32),
        ],
        compiler_params=pltpu.CompilerParams(vmem_limit_bytes=48 << 20),
        name="mixer_bwd",
    )(proj, proj, proj, proj, beta_pre, taps, taps, taps, gain, mask, segc, segr, don, *saved)


def lin_index():
    return lax.axis_index("dp") * lax.axis_size("fsdp") + lax.axis_index("fsdp")


def mesh_id(index):
    inner = lax.axis_size("fsdp")
    return (lax.div(index, inner), lax.rem(index, inner))


def flip(me, bits, number, always=()):
    result = me
    for bit in always:
        own = lax.rem(lax.div(me, 1 << bit), 2)
        result = result + (1 - 2 * own) * (1 << bit)
    for i, bit in enumerate(reversed(bits)):
        own = lax.rem(lax.div(me, 1 << bit), 2)
        if isinstance(number, int):
            flag = (number >> i) & 1
            if flag == 0:
                continue
        else:
            flag = lax.rem(lax.div(number, 1 << i), 2)
        result = result + flag * (1 - 2 * own) * (1 << bit)
    return result


def routes(shards):
    bits = shards.bit_length() - 1
    rest = list(range(4, bits))
    return [[1, 3, 2] + rest, [2, 1, 3] + rest, [3, 2, 1] + rest]


def colours(width, turn):
    tiles = width // 128
    sizes = [tiles // 3 + (1 if (c - turn) % 3 < tiles % 3 else 0) for c in range(3)]
    cuts, at = [], 0
    for s in sizes:
        cuts.append((at * 128, s * 128))
        at += s
    return cuts


def meet(shards, me):
    barrier = pltpu.get_barrier_semaphore()
    bits = shards.bit_length() - 1
    for bit in range(bits):
        pl.semaphore_signal(
            barrier, inc=1, device_id=mesh_id(flip(me, [], 0, (bit,))), device_id_type=MESH
        )
    pl.semaphore_wait(barrier, bits)


def gather_kernel(shards, count, *refs):
    own, full = refs[:count], refs[count : 2 * count]
    send, recv, pair_send, pair_recv, keep = refs[2 * count :]
    me = lin_index()
    bits = shards.bit_length() - 1
    order = routes(shards)
    cuts = [colours(o.shape[-1], i) for i, o in enumerate(own)]
    core = lax.rem(me, 2)
    kept = [
        pltpu.make_async_copy(own[i], full[i].at[lax.div(me, 2), core], keep.at[i])
        for i in range(count)
    ]
    for copy in kept:
        copy.start()
    meet(shards, me)

    def group(k, i, c):
        at, size = cuts[i][c]
        some = full[i].at[pl.ds(0, 1 << k), 0, :, pl.ds(at, size)]
        partner = flip(me, [], 0, (order[c][bits - 2 - k],))
        return pltpu.make_async_remote_copy(
            src_ref=some, dst_ref=some, send_sem=send.at[k, i, c], recv_sem=recv.at[k, i, c],
            device_id=mesh_id(partner), device_id_type=MESH,
        )

    for k in range(bits - 1):
        for i in range(count):
            for c in range(3):
                if k > 0:
                    group(k - 1, i, c).wait_recv()
                at, size = cuts[i][c]
                partner = flip(me, [], 0, (order[c][bits - 2 - k],))
                have = order[c][bits - 1 - k :]
                for j in range(1 << k):
                    d = flip(me, have, j)
                    there = full[i].at[lax.div(d, 2), core, :, pl.ds(at, size)]
                    pltpu.make_async_remote_copy(
                        src_ref=own[i].at[:, pl.ds(at, size)] if j == 0 else there,
                        dst_ref=there, send_sem=send.at[k, i, c], recv_sem=recv.at[k, i, c],
                        device_id=mesh_id(partner), device_id_type=MESH,
                    ).start()
    pairs = []
    for i in range(count):
        for c in range(3):
            group(bits - 2, i, c).wait_recv()
        kept[i].wait()
        half = full[i].at[:, core]
        pair = pltpu.make_async_remote_copy(
            src_ref=half, dst_ref=half, send_sem=pair_send.at[i], recv_sem=pair_recv.at[i],
            device_id=mesh_id(flip(me, [], 0, (0,))), device_id_type=MESH,
        )
        pair.start()
        pairs.append(pair)
    for k in range(bits - 1):
        for i in range(count):
            for c in range(3):
                group(k, i, c).wait_send()
    for pair in pairs:
        pair.wait()


def gather(weights, shards, collective_id):
    count = len(weights)
    bits = shards.bit_length() - 1
    anywhere = pl.BlockSpec(memory_space=pl.ANY)
    full = pl.pallas_call(
        functools.partial(gather_kernel, shards, count),
        in_specs=[anywhere] * count,
        out_specs=[anywhere] * count,
        out_shape=[jax.ShapeDtypeStruct((shards // 2, 2) + w.shape, w.dtype) for w in weights],
        scratch_shapes=[
            pltpu.SemaphoreType.DMA((bits - 1, count, 3)),
            pltpu.SemaphoreType.DMA((bits - 1, count, 3)),
            pltpu.SemaphoreType.DMA((count,)),
            pltpu.SemaphoreType.DMA((count,)),
            pltpu.SemaphoreType.DMA((count,)),
        ],
        compiler_params=pltpu.CompilerParams(collective_id=collective_id, has_side_effects=True),
        name=f"gather_{collective_id}",
    )(*weights)
    return [f.reshape(-1, f.shape[-1]) for f in full]


def scatter_kernel(shards, count, *refs):
    grads, out = refs[:count], refs[count : 2 * count]
    refs = refs[2 * count :]
    mine, other = refs[:count], refs[count : 2 * count]
    refs = refs[2 * count :]
    bits = shards.bit_length() - 1
    stages = bits - 1
    going = [refs[i * stages : (i + 1) * stages] for i in range(count)]
    refs = refs[count * stages :]
    coming = [refs[i * stages : (i + 1) * stages] for i in range(count)]
    send, recv, pair_send, pair_recv, keep = refs[count * stages :]
    me = lin_index()
    core = lax.rem(me, 2)
    order = routes(shards)
    cuts = [colours(o.shape[-1], i) for i, o in enumerate(out)]
    kept = [
        pltpu.make_async_copy(grads[i].at[:, core], mine[i], keep.at[i]) for i in range(count)
    ]
    for copy in kept:
        copy.start()
    meet(shards, me)
    pairs = []
    for i in range(count):
        pair = pltpu.make_async_remote_copy(
            src_ref=grads[i].at[:, 1 - core], dst_ref=other[i],
            send_sem=pair_send.at[i], recv_sem=pair_recv.at[i],
            device_id=mesh_id(flip(me, [], 0, (0,))), device_id_type=MESH,
        )
        pair.start()
        pairs.append(pair)

    def hop(k, i, c):
        at, size = cuts[i][c]
        cols = pl.ds(at, size)
        return pltpu.make_async_remote_copy(
            src_ref=going[i][k].at[:, :, cols], dst_ref=coming[i][k].at[:, :, cols],
            send_sem=send.at[k, i, c], recv_sem=recv.at[k, i, c],
            device_id=mesh_id(flip(me, [], 0, (order[c][k],))), device_id_type=MESH,
        )

    def total(k, i, c, shard, spot):
        at, size = cuts[i][c]
        cols = pl.ds(at, size)
        q = lax.div(shard, 2)
        value = mine[i][q, :, cols].astype(F32) + other[i][q, :, cols].astype(F32)
        for p in range(k):
            value = value + coming[i][p][spot, :, cols].astype(F32)
        return value

    for k in range(stages):
        for i in range(count):
            if k == 0:
                kept[i].wait()
                pairs[i].wait_recv()
            for c in range(3):
                if k > 0:
                    hop(k - 1, i, c).wait_recv()
                much = 1 << (stages - 1 - k)
                at, size = cuts[i][c]

                def body(j, _, k=k, i=i, c=c, much=much, at=at, size=size):
                    shard = flip(me, order[c][k + 1 :], j, (order[c][k],))
                    going[i][k][j, :, pl.ds(at, size)] = total(k, i, c, shard, much + j).astype(BF16)
                    return 0

                lax.fori_loop(0, much, body, 0)
                hop(k, i, c).start()
    for i in range(count):
        for c in range(3):
            hop(stages - 1, i, c).wait_recv()
            at, size = cuts[i][c]
            out[i][:, pl.ds(at, size)] = total(stages, i, c, me, 0)
    for k in range(stages):
        for i in range(count):
            for c in range(3):
                hop(k, i, c).wait_send()
    for pair in pairs:
        pair.wait_send()


def scatter(grads, shards, collective_id):
    count = len(grads)
    bits = shards.bit_length() - 1
    stages = bits - 1
    shapes = [(g.shape[0] // shards, g.shape[1]) for g in grads]
    steps = [
        pltpu.VMEM((1 << (stages - 1 - k),) + s, BF16) for s in shapes for k in range(stages)
    ]
    halves = [pltpu.VMEM((shards // 2,) + s, BF16) for s in shapes]
    return pl.pallas_call(
        functools.partial(scatter_kernel, shards, count),
        in_specs=[pl.BlockSpec(memory_space=pl.ANY)] * count,
        out_specs=[pl.BlockSpec(memory_space=pltpu.VMEM)] * count,
        out_shape=[jax.ShapeDtypeStruct(s, F32) for s in shapes],
        scratch_shapes=halves + halves + steps + steps + [
            pltpu.SemaphoreType.DMA((stages, count, 3)),
            pltpu.SemaphoreType.DMA((stages, count, 3)),
            pltpu.SemaphoreType.DMA((count,)),
            pltpu.SemaphoreType.DMA((count,)),
            pltpu.SemaphoreType.DMA((count,)),
        ],
        compiler_params=pltpu.CompilerParams(
            collective_id=collective_id, has_side_effects=True, vmem_limit_bytes=60 << 20
        ),
        name=f"scatter_{collective_id}",
    )(*[g.reshape((shards // 2, 2) + s) for g, s in zip(grads, shapes)])


def nt(left, right):
    return lax.dot_general(left, right, (((1,), (1,)), ((), ())), preferred_element_type=F32)


def tn(left, right, dtype=F32):
    return lax.dot_general(left, right, (((0,), (0,)), ((), ())), preferred_element_type=dtype)


def nn(left, right):
    return jnp.dot(left, right, preferred_element_type=F32)


def rms(v):
    inv = lax.rsqrt(jnp.mean(v * v, axis=-1, keepdims=True) + 1e-05)
    return v * inv, inv


def rms_back(normed, inv, dn):
    return inv * (dn - normed * jnp.mean(normed * dn, axis=-1, keepdims=True))


def local(
    tokens, cotangent, teacher, valid_mask, deal_rows, lengths, w_in, w_beta, conv_kernel, w_out,
    norm_gain, out_gain, ffn_gain, w_gu, w_down,
):
    shards = lax.axis_size(AXES)
    rows = tokens.shape[0]
    share = rows // shards
    blocks = lengths.shape[0]
    rows_mb = rows // blocks
    small = w_beta.shape[0] * HEADS + CONV * conv_kernel.shape[1] + 2 * norm_gain.shape[0]

    target = deal_rows // rows
    spot = deal_rows % rows
    ahead = (target[None, :] == target[:, None]) & (
        jnp.arange(rows)[None, :] < jnp.arange(rows)[:, None]
    )
    slot = target * share + jnp.sum(ahead.astype(jnp.int32), axis=1)
    sort_t = (slot[:, None] == jnp.arange(rows)[None, :]).astype(BF16)
    sort = (slot[None, :] == jnp.arange(rows)[:, None]).astype(BF16)
    count_own = jnp.sum(valid_mask.astype(F32))
    lane = jnp.arange(128)[None, :]
    notes = jnp.where(
        lane == 0,
        valid_mask.astype(F32)[:, None],
        jnp.where(lane == 1, spot.astype(F32)[:, None], jnp.where(lane == 2, count_own, 0.0)),
    ).astype(BF16)
    packed = jnp.concatenate(
        [conv_kernel.reshape(-1), w_beta.reshape(-1), norm_gain, ffn_gain,
         jnp.zeros((share * 128 - small,), BF16)]
    ).reshape(1, share, 128)
    sorted_rows = nn(sort, jnp.concatenate([tokens, cotangent, teacher, notes], axis=1)).astype(BF16)
    message = jnp.concatenate(
        [sorted_rows.reshape(shards, share, -1), jnp.broadcast_to(packed, (shards, share, 128))],
        axis=2,
    )
    arrived = lax.all_to_all(message, AXES, split_axis=0, concat_axis=0, tiled=True)

    wout, win, wdown, wgu = gather([w_out, w_in, w_down, w_gu], shards, 0)

    flat = arrived.reshape(rows, -1)
    info = flat[:, 3 * D : 3 * D + 128].astype(F32)
    place = info[:, 1].astype(jnp.int32)
    counted = jnp.sum(arrived[:, 0, 3 * D + 2].astype(F32))
    extra = arrived[:, :, 3 * D + 128 :].reshape(shards, share * 128)
    a, b, c = CONV * conv_kernel.shape[1], w_beta.shape[0] * HEADS, norm_gain.shape[0]
    taps = extra[:, :a].reshape(shards, CONV, -1).swapaxes(0, 1).reshape(CONV, 3 * D).astype(F32)
    wbeta = extra[:, a : a + b].reshape(D, HEADS)
    gain_one = extra[:, a + b : a + b + c].reshape(D).astype(F32)
    gain_two = extra[:, a + b + c : a + b + 2 * c].reshape(D).astype(F32)
    deal = (place[None, :] == jnp.arange(rows)[:, None]).astype(BF16)
    deal_t = (place[:, None] == jnp.arange(rows)[None, :]).astype(BF16)
    dealt = nn(deal, flat[:, : 3 * D + 128])
    x = dealt[:, :D]
    g = dealt[:, D : 2 * D]
    t = dealt[:, 2 * D : 3 * D]
    m = dealt[:, 3 * D : 3 * D + 1]

    ends = jnp.cumsum(lengths, axis=1)
    within = jnp.arange(rows_mb, dtype=jnp.int32)
    seg = jnp.sum((within[None, :, None] >= ends[:, None, :]).astype(jnp.int32), axis=2)
    seg = (seg + (lengths.shape[1] + 1) * jnp.arange(blocks, dtype=jnp.int32)[:, None]).reshape(rows)
    position = jnp.arange(rows, dtype=jnp.int32)
    mask = jnp.stack(
        [jnp.ones((rows,), F32)]
        + [((position >= s) & (jnp.roll(seg, s) == seg)).astype(F32) for s in range(1, CONV)]
        + [jnp.zeros((rows,), F32)] * (8 - CONV),
        axis=1,
    )
    segc, segr = seg[:, None], seg[None, :]
    gain_out = out_gain.astype(F32)[None, :]

    nx, rx = rms(x)
    a1 = (nx * gain_one).astype(BF16)
    proj = nn(a1, win)
    beta_pre = nn(a1, wbeta)
    on, *saved = mixer_forward(proj, beta_pre, taps, gain_out, mask, segc, segr, blocks)
    resid = x + nn(on, wout)
    nr, rr = rms(resid)
    a2 = (nr * gain_two).astype(BF16)
    gu = nn(a2, wgu)
    gate, up = gu[:, :FF], gu[:, FF:]
    sg = sigmoid(gate)
    hid = (gate * sg * up).astype(BF16)
    y = resid + nn(hid, wdown)
    errors = y - t
    loss_part = jnp.sum(m * errors * errors)
    dy = g + (rows * shards / counted) * m * errors
    df = dy.astype(BF16)
    dhid = nt(df, wdown)
    dgu = jnp.concatenate(
        [dhid * up * (sg * (1.0 + gate * (1.0 - sg))), dhid * (gate * sg)], axis=1
    ).astype(BF16)
    da2 = nt(dgu, wgu)
    d_gain_two = jnp.sum(da2 * nr, axis=0)
    dresid = dy + rms_back(nr, rr, gain_two * da2)
    dz = dresid.astype(BF16)
    don = nt(dz, wout)
    dpq, dpk, dpv, dpg, dbeta, dtq, dtk, dtv, d_gain_out = mixer_backward(
        proj, beta_pre, taps, gain_out, mask, segc, segr, don, saved, blocks
    )
    dproj = jnp.concatenate([dpq, dpk, dpv, dpg], axis=1)
    dbeta = dbeta.astype(BF16)
    da1 = nt(dproj, win) + nt(dbeta, wbeta)
    d_gain_one = jnp.sum(da1 * nx, axis=0)
    dx = dresid + rms_back(nx, rx, gain_one * da1)

    g_down, g_gu = scatter([tn(hid, df, BF16), tn(a2, dgu, BF16)], shards, 1)
    g_out, g_in = scatter([tn(on, dz, BF16), tn(a1, dproj, BF16)], shards, 2)

    d_taps = jnp.concatenate([dtq, dtk, dtv], axis=1)
    d_wbeta = tn(a1, dbeta)
    tail = jnp.concatenate([d_gain_out.reshape(-1), loss_part.reshape(1)])
    extra = jnp.concatenate(
        [
            d_taps.reshape(CONV, shards, -1).swapaxes(0, 1).reshape(shards, a),
            d_wbeta.reshape(shards, b),
            d_gain_one.reshape(shards, c),
            d_gain_two.reshape(shards, c),
            jnp.broadcast_to(tail[None], (shards, tail.shape[0])),
        ],
        axis=1,
    )
    padded = -(-extra.shape[1] // 128) * 128
    extra = jnp.pad(extra, ((0, 0), (0, padded - extra.shape[1])))
    summed = jnp.sum(
        lax.all_to_all(
            extra.reshape(shards, padded // 128, 128), AXES, split_axis=0, concat_axis=0, tiled=True
        ),
        axis=0,
    ).reshape(-1)
    g_taps = summed[:a].reshape(CONV, -1)
    g_beta = summed[a : a + b].reshape(-1, HEADS)
    g_gain_one = summed[a + b : a + b + c]
    g_gain_two = summed[a + b + c : a + b + 2 * c]
    g_gain_out = summed[a + b + 2 * c : a + b + 2 * c + HEAD_DIM]
    loss = summed[a + b + 2 * c + HEAD_DIM] / (D * counted)

    def give_back(v):
        sent = nn(deal_t, v.astype(BF16)).astype(BF16).reshape(shards, share, D)
        got = lax.all_to_all(sent, AXES, split_axis=0, concat_axis=0, tiled=True)
        return nn(sort_t, got.reshape(rows, D)).astype(BF16)

    output = give_back(y)
    input_grad = give_back(dx)
    return (
        output, input_grad, g_in, g_beta, g_taps, g_out, g_gain_one, g_gain_out, g_gain_two, g_gu,
        g_down, loss,
    )


def solution(mesh):
    both = P(AXES, None)
    flat = P(AXES)
    in_specs = (both, both, both, flat, flat, both, both, both, P(None, AXES), both, flat, P(), flat,
                both, both)
    out_specs = (both, both, both, both, P(None, AXES), both, flat, P(), flat, both, both, P())
    return jax.shard_map(local, mesh=mesh, in_specs=in_specs, out_specs=out_specs, check_vma=False)
```

```python
import functools

import jax
import jax.numpy as jnp
from jax import lax
from jax.experimental import pallas as pl
from jax.experimental.pallas import tpu as pltpu
from jax.sharding import PartitionSpec as P

D = 1024
HEADS = 8
HEAD_DIM = 128
FF = 2816
CONV = 4
AXES = ("dp", "fsdp")
F32 = jnp.float32
BF16 = jnp.bfloat16
PAIR = 2
MESH = pl.DeviceIdType.MESH


def mm(left, right, lc, rc):
    return lax.dot_general(
        left,
        right,
        (((lc,), (rc,)), ((), ())),
        precision=lax.Precision.HIGHEST,
        preferred_element_type=F32,
    )


def sigmoid(v):
    return 1.0 / (1.0 + jnp.exp(-v))


def iota2(shape, axis):
    return lax.broadcasted_iota(jnp.int32, shape, axis)


def unit_lower_inverses(mats, size):
    row, col = iota2((size, size), 0), iota2((size, size), 1)
    eye = (row == col).astype(F32)
    inverses = None
    width = 1
    while width < size:
        corner = ((row // (2 * width)) == (col // (2 * width))) & (
            (row // width) == (col // width) + 1
        )
        edges = [jnp.where(corner, m, 0.0) for m in mats]
        if inverses is None:
            inverses = [eye - e for e in edges]
        else:
            right = [mm(e, x, 1, 0) for e, x in zip(edges, inverses)]
            inverses = [x - mm(x, r, 1, 0) for x, r in zip(inverses, right)]
        width *= 2
    return inverses


def conv_parts(src, taps, masks):
    rolled = [src]
    total = src * taps[CONV - 1 : CONV, :]
    for s in range(1, CONV):
        moved = pltpu.roll(src, s, 0) * masks[s]
        rolled.append(moved)
        total = total + moved * taps[CONV - 1 - s : CONV - s, :]
    return total, rolled


def l2_norm(c):
    inv = lax.rsqrt(jnp.sum(c * c, axis=-1, keepdims=True) + 1e-06)
    return c * inv, inv


def mixer_fwd_kernel(
    blocks, rows_mb,
    pq, pk, pv, pg, beta, tq, tk, tv, gain, mask, segc, segr,
    on_ref, o_ref, ainv_ref, u_ref, p_ref, l_ref,
):
    step = pl.program_id(0)
    masks = [None] + [mask[:, s : s + 1] for s in range(1, CONV)]
    cs = []
    for src, taps in ((pq, tq), (pk, tk), (pv, tv)):
        pre, _ = conv_parts(src[...], taps[...], masks)
        cs.append(pre * sigmoid(pre))
    cq, ck, cv = cs
    strengths = sigmoid(beta[...])
    lane = iota2(strengths.shape, 1)
    gate = pg[...]
    gate = gate * sigmoid(gate)
    row, col = iota2((rows_mb, rows_mb), 0), iota2((rows_mb, rows_mb), 1)
    systems = [(h, b) for h in range(PAIR) for b in range(blocks)]
    qs, ks, vs, bs, sames, lows = [], [], [], [], [], []
    for h, b in systems:
        rs = slice(b * rows_mb, (b + 1) * rows_mb)
        hs = slice(h * HEAD_DIM, (h + 1) * HEAD_DIM)
        q, _ = l2_norm(cq[rs, hs])
        k, _ = l2_norm(ck[rs, hs])
        qs.append(q * HEAD_DIM ** (-0.5))
        ks.append(k)
        vs.append(cv[rs, hs])
        bs.append(
            jnp.sum(jnp.where(lane == step * PAIR + h, strengths, 0.0), axis=1, keepdims=True)[rs]
        )
        sames.append(segc[rs, :] == segr[:, rs])
    for i in range(len(systems)):
        lows.append(jnp.where(sames[i] & (row > col), mm(ks[i], ks[i], 1, 1), 0.0))
    inverses = unit_lower_inverses([l * b for l, b in zip(lows, bs)], rows_mb)
    us = [mm(a, v * b, 1, 0) for a, v, b in zip(inverses, vs, bs)]
    ps = [
        jnp.where(same & (row >= col), mm(q, k, 1, 1), 0.0)
        for q, k, same in zip(qs, ks, sames)
    ]
    os = [mm(p, u, 1, 0) for p, u in zip(ps, us)]
    for i, (h, b) in enumerate(systems):
        rs = slice(b * rows_mb, (b + 1) * rows_mb)
        hs = slice(h * HEAD_DIM, (h + 1) * HEAD_DIM)
        o = os[i]
        inv = lax.rsqrt(jnp.mean(o * o, axis=-1, keepdims=True) + 1e-05)
        on_ref[rs, hs] = (o * inv * gain[...] * gate[rs, hs]).astype(BF16)
        o_ref[rs, hs] = o
        ainv_ref[h, b] = inverses[i]
        u_ref[h, b] = us[i]
        p_ref[h, b] = ps[i]
        l_ref[h, b] = lows[i]


def mixer_bwd_kernel(
    blocks, rows_mb,
    pq, pk, pv, pg, beta, tq, tk, tv, gain, mask, segc, segr,
    don_ref, o_ref, ainv_ref, u_ref, p_ref, l_ref,
    dq_ref, dk_ref, dv_ref, dg_ref, dbeta_ref, dtq, dtk, dtv, dgain_ref,
):
    step = pl.program_id(0)
    rows = blocks * rows_mb
    masks = [None] + [mask[:, s : s + 1] for s in range(1, CONV)]
    pres, rolls, cs, sig = [], [], [], []
    for src, taps in ((pq, tq), (pk, tk), (pv, tv)):
        pre, rolled = conv_parts(src[...], taps[...], masks)
        s = sigmoid(pre)
        pres.append(pre)
        rolls.append(rolled)
        sig.append(s)
        cs.append(pre * s)
    cq, ck, cv = cs
    strengths = sigmoid(beta[...])
    lane = iota2(strengths.shape, 1)
    row, col = iota2((rows_mb, rows_mb), 0), iota2((rows_mb, rows_mb), 1)
    gates = pg[...]
    gsig = sigmoid(gates)
    gate = gates * gsig
    dgate = gsig * (1.0 + gates * (1.0 - gsig))
    systems = [(h, b) for h in range(PAIR) for b in range(blocks)]
    part = []
    dgain = jnp.zeros((1, HEAD_DIM), F32)
    for h, b in systems:
        rs = slice(b * rows_mb, (b + 1) * rows_mb)
        hs = slice(h * HEAD_DIM, (h + 1) * HEAD_DIM)
        k, ik = l2_norm(ck[rs, hs])
        qn, iq = l2_norm(cq[rs, hs])
        v = cv[rs, hs]
        bb = jnp.sum(jnp.where(lane == step * PAIR + h, strengths, 0.0), axis=1, keepdims=True)[rs]
        same = segc[rs, :] == segr[:, rs]
        o = o_ref[rs, hs]
        don = don_ref[rs, hs]
        inv = lax.rsqrt(jnp.mean(o * o, axis=-1, keepdims=True) + 1e-05)
        no = o * inv
        scaled = don * gain[...]
        dg_ref[rs, hs] = (scaled * no * dgate[rs, hs]).astype(BF16)
        dgain = dgain + jnp.sum(don * no * gate[rs, hs], axis=0, keepdims=True)
        dno = scaled * gate[rs, hs]
        do = inv * (dno - no * jnp.mean(no * dno, axis=-1, keepdims=True))
        part.append([q_ for q_ in (qn, iq, k, ik, v, bb, same, do)])
    dus = [mm(p_ref[h, b], part[i][7], 0, 0) for i, (h, b) in enumerate(systems)]
    dps = [
        jnp.where(part[i][6] & (row >= col), mm(part[i][7], u_ref[h, b], 1, 1), 0.0)
        for i, (h, b) in enumerate(systems)
    ]
    drs = [mm(ainv_ref[h, b], dus[i], 0, 0) for i, (h, b) in enumerate(systems)]
    scale = HEAD_DIM ** (-0.5)
    dqs = [mm(dps[i], part[i][2], 1, 0) * scale for i in range(len(systems))]
    das = [mm(drs[i], u_ref[h, b], 1, 1) for i, (h, b) in enumerate(systems)]
    dks = [mm(dps[i], part[i][0] * scale, 0, 0) for i in range(len(systems))]
    dgs = []
    for i in range(len(systems)):
        g = jnp.where(part[i][6] & (row > col), das[i] * (-part[i][5]), 0.0)
        dgs.append(g + g.T)
    dks = [dks[i] + mm(dgs[i], part[i][2], 1, 0) for i in range(len(systems))]
    dbeta = jnp.zeros(strengths.shape, F32)
    dcs = [[], [], []]
    for i, (h, b) in enumerate(systems):
        qn, iq, k, ik, v, bb, same, do = part[i]
        dv = drs[i] * bb
        db = jnp.sum(drs[i] * v - das[i] * l_ref[h, b], axis=-1, keepdims=True)
        dbp = db * bb * (1.0 - bb)
        pieces = [dbp if b == c else jnp.zeros((rows_mb, 1), F32) for c in range(blocks)]
        column = jnp.concatenate(pieces, axis=0) if blocks > 1 else dbp
        dbeta = dbeta + jnp.where(lane == step * PAIR + h, column, 0.0)
        dcs[0].append(iq * (dqs[i] - qn * jnp.sum(qn * dqs[i], axis=-1, keepdims=True)))
        dcs[1].append(ik * (dks[i] - k * jnp.sum(k * dks[i], axis=-1, keepdims=True)))
        dcs[2].append(dv)
    for j, (out, dtap, taps) in enumerate(((dq_ref, dtq, tq), (dk_ref, dtk, tk), (dv_ref, dtv, tv))):
        whole = jnp.concatenate(
            [
                jnp.concatenate([dcs[j][h * blocks + b] for b in range(blocks)], axis=0)
                for h in range(PAIR)
            ],
            axis=1,
        )
        dpre = whole * (sig[j] * (1.0 + pres[j] * (1.0 - sig[j])))
        tap = taps[...]
        grad = dpre * tap[CONV - 1 : CONV, :]
        dtap[CONV - 1 : CONV, :] = jnp.sum(dpre * rolls[j][0], axis=0, keepdims=True)
        for s in range(1, CONV):
            dtap[CONV - 1 - s : CONV - s, :] = jnp.sum(dpre * rolls[j][s], axis=0, keepdims=True)
            grad = grad + pltpu.roll(dpre * masks[s], rows - s, 0) * tap[CONV - 1 - s : CONV - s, :]
        out[...] = grad.astype(BF16)

    @pl.when(step == 0)
    def _():
        dbeta_ref[...] = jnp.zeros_like(dbeta_ref)
        dgain_ref[...] = jnp.zeros_like(dgain_ref)

    dbeta_ref[...] += dbeta
    dgain_ref[...] += dgain


def mixer_specs(rows, blocks, rows_mb):
    width = PAIR * HEAD_DIM
    per = D // width
    col = lambda k: pl.BlockSpec((rows, width), lambda i, k=k: (0, k * per + i))
    tap = lambda k: pl.BlockSpec((CONV, width), lambda i, k=k: (0, k * per + i))
    full = lambda shape: pl.BlockSpec(shape, lambda i: (0,) * len(shape))
    ins = [col(0), col(1), col(2), col(3), full((rows, HEADS)), tap(0), tap(1), tap(2),
           full((1, HEAD_DIM)), full((rows, 8)), full((rows, 1)), full((1, rows))]
    mat = pl.BlockSpec((PAIR, blocks, rows_mb, rows_mb), lambda i: (i, 0, 0, 0))
    one = pl.BlockSpec((rows, width), lambda i: (0, i))
    otap = pl.BlockSpec((CONV, width), lambda i: (0, i))
    return ins, mat, one, otap, full


def mixer_forward(proj, beta_pre, taps, gain, mask, segc, segr, blocks):
    rows = proj.shape[0]
    rows_mb = rows // blocks
    ins, mat, one, _, _ = mixer_specs(rows, blocks, rows_mb)
    square = jax.ShapeDtypeStruct((HEADS, blocks, rows_mb, rows_mb), F32)
    return pl.pallas_call(
        functools.partial(mixer_fwd_kernel, blocks, rows_mb),
        grid=(HEADS // PAIR,),
        in_specs=ins,
        out_specs=[one, one, mat, mat, mat, mat],
        out_shape=[
            jax.ShapeDtypeStruct((rows, D), BF16),
            jax.ShapeDtypeStruct((rows, D), F32),
            square, square, square, square,
        ],
        compiler_params=pltpu.CompilerParams(vmem_limit_bytes=48 << 20),
        name="mixer_fwd",
    )(proj, proj, proj, proj, beta_pre, taps, taps, taps, gain, mask, segc, segr)


def mixer_backward(proj, beta_pre, taps, gain, mask, segc, segr, don, saved, blocks):
    rows = proj.shape[0]
    rows_mb = rows // blocks
    ins, mat, one, otap, full = mixer_specs(rows, blocks, rows_mb)
    tapshape = jax.ShapeDtypeStruct((CONV, D), F32)
    wide = jax.ShapeDtypeStruct((rows, D), BF16)
    return pl.pallas_call(
        functools.partial(mixer_bwd_kernel, blocks, rows_mb),
        grid=(HEADS // PAIR,),
        in_specs=ins + [one, one, mat, mat, mat, mat],
        out_specs=[one, one, one, one, full((rows, HEADS)), otap, otap, otap, full((1, HEAD_DIM))],
        out_shape=[
            wide, wide, wide, wide,
            jax.ShapeDtypeStruct((rows, HEADS), F32),
            tapshape, tapshape, tapshape,
            jax.ShapeDtypeStruct((1, HEAD_DIM), F32),
        ],
        compiler_params=pltpu.CompilerParams(vmem_limit_bytes=48 << 20),
        name="mixer_bwd",
    )(proj, proj, proj, proj, beta_pre, taps, taps, taps, gain, mask, segc, segr, don, *saved)


def lin_index():
    return lax.axis_index("dp") * lax.axis_size("fsdp") + lax.axis_index("fsdp")


def mesh_id(index):
    inner = lax.axis_size("fsdp")
    return (lax.div(index, inner), lax.rem(index, inner))


def flip(me, bits, number, always=()):
    result = me
    for bit in always:
        own = lax.rem(lax.div(me, 1 << bit), 2)
        result = result + (1 - 2 * own) * (1 << bit)
    for i, bit in enumerate(reversed(bits)):
        own = lax.rem(lax.div(me, 1 << bit), 2)
        if isinstance(number, int):
            flag = (number >> i) & 1
            if flag == 0:
                continue
        else:
            flag = lax.rem(lax.div(number, 1 << i), 2)
        result = result + flag * (1 - 2 * own) * (1 << bit)
    return result


def routes(shards):
    bits = shards.bit_length() - 1
    rest = list(range(4, bits))
    return [[1, 3, 2] + rest, [2, 1, 3] + rest, [3, 2, 1] + rest]


def colours(width, turn):
    tiles = width // 128
    sizes = [tiles // 3 + (1 if (c - turn) % 3 < tiles % 3 else 0) for c in range(3)]
    cuts, at = [], 0
    for s in sizes:
        cuts.append((at * 128, s * 128))
        at += s
    return cuts


def meet(shards, me):
    barrier = pltpu.get_barrier_semaphore()

    def greet(r, _):
        pl.semaphore_signal(
            barrier, inc=1, device_id=mesh_id(lax.rem(me + r, shards)), device_id_type=MESH
        )
        return 0

    lax.fori_loop(1, shards, greet, 0)
    pl.semaphore_wait(barrier, shards - 1)


class Exchange:
    def __init__(self, shards, me, sent, got, send, recv, keep):
        self.shards, self.me, self.sent, self.got = shards, me, sent, got
        self.send, self.recv, self.keep = send, recv, keep

    def own(self):
        return pltpu.make_async_copy(self.sent.at[self.me], self.got.at[self.me], self.keep)

    def start(self):
        self.own().start()

        def one(r, _):
            peer = lax.rem(self.me + r, self.shards)
            pltpu.make_async_remote_copy(
                src_ref=self.sent.at[peer], dst_ref=self.got.at[self.me], send_sem=self.send,
                recv_sem=self.recv, device_id=mesh_id(peer), device_id_type=MESH,
            ).start()
            return 0

        lax.fori_loop(1, self.shards, one, 0)

    def wait(self):
        self.own().wait()
        whole = pl.ds(0, self.shards - 1)
        pltpu.make_async_remote_copy(
            src_ref=self.sent.at[whole], dst_ref=self.got.at[whole], send_sem=self.send,
            recv_sem=self.recv, device_id=mesh_id(self.me), device_id_type=MESH,
        ).wait()


SPLIT = (1, 2, 1, 2)
SPLIT_BACK = (1, 2, 1, 2)


def pieces_of(widths, split):
    result = []
    for i, width in enumerate(widths):
        tiles, at = width // 128, 0
        for j in range(split[i]):
            size = tiles // split[i] + (1 if j < tiles % split[i] else 0)
            result.append((i, at * 128, size * 128))
            at += size
    return result


def gather_kernel(shards, pieces, *refs):
    count = 1 + max(i for i, _, _ in pieces)
    own, sent, full, got = refs[:count], refs[count], refs[count + 1 : 2 * count + 1], refs[2 * count + 1]
    send, recv, pair_send, pair_recv, keep, deal_send, deal_recv, deal_keep = refs[2 * count + 2 :]
    me = lin_index()
    bits = shards.bit_length() - 1
    stages = bits - 1
    order = routes(shards)
    deal = Exchange(shards, me, sent, got, deal_send, deal_recv, deal_keep)
    cuts = [
        [(at + a, s) for a, s in colours(size, n)] for n, (_, at, size) in enumerate(pieces)
    ]
    core = lax.rem(me, 2)
    kept = [
        pltpu.make_async_copy(own[i], full[i].at[lax.div(me, 2), core], keep.at[i])
        for i in range(count)
    ]
    for copy in kept:
        copy.start()
    meet(shards, me)
    deal.start()
    sibling = mesh_id(flip(me, [], 0, (0,)))

    def group(k, n, c):
        at, size = cuts[n][c]
        some = full[pieces[n][0]].at[pl.ds(0, 1 << k), 0, :, pl.ds(at, size)]
        partner = flip(me, [], 0, (order[c][stages - 1 - k],))
        return pltpu.make_async_remote_copy(
            src_ref=some, dst_ref=some, send_sem=send.at[k, n, c], recv_sem=recv.at[k, n, c],
            device_id=mesh_id(partner), device_id_type=MESH,
        )

    def half(n):
        i, at, size = pieces[n]
        some = full[i].at[:, core, :, pl.ds(at, size)]
        return pltpu.make_async_remote_copy(
            src_ref=some, dst_ref=some, send_sem=pair_send.at[n], recv_sem=pair_recv.at[n],
            device_id=sibling, device_id_type=MESH,
        )

    def launch(k, n):
        i = pieces[n][0]
        for c in range(3):
            at, size = cuts[n][c]
            if size == 0:
                continue
            if k > 0:
                group(k - 1, n, c).wait_recv()
            partner = mesh_id(flip(me, [], 0, (order[c][stages - 1 - k],)))
            have = order[c][stages - k :]
            for j in range(1 << k):
                d = flip(me, have, j)
                there = full[i].at[lax.div(d, 2), core, :, pl.ds(at, size)]
                pltpu.make_async_remote_copy(
                    src_ref=own[i].at[:, pl.ds(at, size)] if j == 0 else there,
                    dst_ref=there, send_sem=send.at[k, n, c], recv_sem=recv.at[k, n, c],
                    device_id=partner, device_id_type=MESH,
                ).start()

    def finish(n):
        for c in range(3):
            if cuts[n][c][1]:
                group(stages - 1, n, c).wait_recv()
        if n == 0 or pieces[n - 1][0] != pieces[n][0]:
            kept[pieces[n][0]].wait()
        half(n).start()

    for t in range(len(pieces) + stages):
        for n in range(len(pieces)):
            k = t - n
            if 0 <= k < stages:
                launch(k, n)
            elif k == stages:
                finish(n)
    deal.wait()
    for k in range(stages):
        for n in range(len(pieces)):
            for c in range(3):
                if cuts[n][c][1]:
                    group(k, n, c).wait_send()
    for n in range(len(pieces)):
        half(n).wait()


def gather(weights, message, shards, collective_id):
    count = len(weights)
    bits = shards.bit_length() - 1
    anywhere = pl.BlockSpec(memory_space=pl.ANY)
    pieces = pieces_of([w.shape[1] for w in weights], SPLIT)
    dma = pltpu.SemaphoreType.DMA
    *full, got = pl.pallas_call(
        functools.partial(gather_kernel, shards, pieces),
        in_specs=[anywhere] * (count + 1),
        out_specs=[anywhere] * (count + 1),
        out_shape=[jax.ShapeDtypeStruct((shards // 2, 2) + w.shape, w.dtype) for w in weights]
        + [jax.ShapeDtypeStruct(message.shape, message.dtype)],
        scratch_shapes=[
            dma((bits - 1, len(pieces), 3)), dma((bits - 1, len(pieces), 3)), dma((len(pieces),)),
            dma((len(pieces),)), dma((count,)), dma, dma, dma,
        ],
        compiler_params=pltpu.CompilerParams(collective_id=collective_id, has_side_effects=True),
        name=f"gather_{collective_id}",
    )(*weights, message)
    return [f.reshape(-1, f.shape[-1]) for f in full], got


def scatter_kernel(shards, pieces, *refs):
    count = 1 + max(i for i, _, _ in pieces)
    grads, sent, out, got = refs[:count], refs[count], refs[count + 1 : 2 * count + 1], refs[2 * count + 1]
    refs = refs[2 * count + 2 :]
    mine, other = refs[:count], refs[count : 2 * count]
    refs = refs[2 * count :]
    bits = shards.bit_length() - 1
    stages = bits - 1
    coming = [refs[i * stages : (i + 1) * stages] for i in range(count)]
    send, recv, pair_send, pair_recv, keep, back_send, back_recv, back_keep = refs[count * stages :]
    me = lin_index()
    core = lax.rem(me, 2)
    order = routes(shards)
    back = Exchange(shards, me, sent, got, back_send, back_recv, back_keep)
    cuts = [
        [(at + a, s) for a, s in colours(size, n)] for n, (_, at, size) in enumerate(pieces)
    ]
    kept, pairs = [], []
    for n, (i, at, size) in enumerate(pieces):
        cols = pl.ds(at, size)
        kept.append(
            pltpu.make_async_copy(
                grads[i].at[:, core, :, cols], mine[i].at[:, :, cols], keep.at[n]
            )
        )
        pairs.append(
            pltpu.make_async_remote_copy(
                src_ref=grads[i].at[:, 1 - core, :, cols], dst_ref=other[i].at[:, :, cols],
                send_sem=pair_send.at[n], recv_sem=pair_recv.at[n],
                device_id=mesh_id(flip(me, [], 0, (0,))), device_id_type=MESH,
            )
        )
    for copy in kept:
        copy.start()
    meet(shards, me)
    for pair in pairs:
        pair.start()
    back.start()

    def hop(k, n, c, source, spots):
        i = pieces[n][0]
        at, size = cuts[n][c]
        cols = pl.ds(at, size)
        return pltpu.make_async_remote_copy(
            src_ref=other[i].at[source, :, cols], dst_ref=coming[i][k].at[spots, :, cols],
            send_sem=send.at[k, n, c], recv_sem=recv.at[k, n, c],
            device_id=mesh_id(flip(me, [], 0, (order[c][k],))), device_id_type=MESH,
        )

    def group(k, n, c):
        all_of = pl.ds(0, 1 << (stages - 1 - k))
        return hop(k, n, c, all_of, all_of)

    def total(k, n, c, shard, spot):
        i = pieces[n][0]
        at, size = cuts[n][c]
        cols = pl.ds(at, size)
        q = lax.div(shard, 2)
        value = mine[i][q, :, cols].astype(F32) + other[i][q, :, cols].astype(F32)
        for p in range(k):
            value = value + coming[i][p][spot, :, cols].astype(F32)
        return value

    def launch(k, n):
        if k == 0:
            kept[n].wait()
            pairs[n].wait_recv()
        for c in range(3):
            if k > 0:
                group(k - 1, n, c).wait_recv()
            much = 1 << (stages - 1 - k)
            at, size = cuts[n][c]

            def body(j, _, c=c, at=at, size=size):
                shard = flip(me, order[c][k + 1 :], j, (order[c][k],))
                q = lax.div(shard, 2)
                other[pieces[n][0]][q, :, pl.ds(at, size)] = total(k, n, c, shard, much + j).astype(BF16)
                hop(k, n, c, q, j).start()
                return 0

            lax.fori_loop(0, much, body, 0)

    def finish(n):
        for c in range(3):
            group(stages - 1, n, c).wait_recv()
            at, size = cuts[n][c]
            out[pieces[n][0]][:, pl.ds(at, size)] = total(stages, n, c, me, 0)

    for t in range(len(pieces) + stages):
        for n in range(len(pieces)):
            k = t - n
            if 0 <= k < stages:
                launch(k, n)
            elif k == stages:
                finish(n)
    back.wait()
    for k in range(stages):
        for n in range(len(pieces)):
            for c in range(3):
                group(k, n, c).wait_send()
    for pair in pairs:
        pair.wait_send()


def scatter(grads, message, shards, collective_id):
    count = len(grads)
    bits = shards.bit_length() - 1
    stages = bits - 1
    shapes = [(g.shape[0] // shards, g.shape[1]) for g in grads]
    pieces = pieces_of([g.shape[1] for g in grads], SPLIT_BACK)
    steps = [
        pltpu.VMEM((1 << (stages - 1 - k),) + s, BF16) for s in shapes for k in range(stages)
    ]
    halves = [pltpu.VMEM((shards // 2,) + s, BF16) for s in shapes]
    anywhere = pl.BlockSpec(memory_space=pl.ANY)
    dma = pltpu.SemaphoreType.DMA
    *out, got = pl.pallas_call(
        functools.partial(scatter_kernel, shards, pieces),
        in_specs=[anywhere] * (count + 1),
        out_specs=[pl.BlockSpec(memory_space=pltpu.VMEM)] * count + [anywhere],
        out_shape=[jax.ShapeDtypeStruct(s, F32) for s in shapes]
        + [jax.ShapeDtypeStruct(message.shape, message.dtype)],
        scratch_shapes=halves + halves + steps + [
            dma((stages, len(pieces), 3)), dma((stages, len(pieces), 3)), dma((len(pieces),)),
            dma((len(pieces),)), dma((len(pieces),)), dma, dma, dma,
        ],
        compiler_params=pltpu.CompilerParams(
            collective_id=collective_id, has_side_effects=True, vmem_limit_bytes=60 << 20
        ),
        name=f"scatter_{collective_id}",
    )(*[g.reshape((shards // 2, 2) + s) for g, s in zip(grads, shapes)], message)
    return out, got


def nt(left, right):
    return lax.dot_general(left, right, (((1,), (1,)), ((), ())), preferred_element_type=F32)


def tn(left, right, dtype=F32):
    return lax.dot_general(left, right, (((0,), (0,)), ((), ())), preferred_element_type=dtype)


def nn(left, right):
    return jnp.dot(left, right, preferred_element_type=F32)


def rms(v):
    inv = lax.rsqrt(jnp.mean(v * v, axis=-1, keepdims=True) + 1e-05)
    return v * inv, inv


def rms_back(normed, inv, dn):
    return inv * (dn - normed * jnp.mean(normed * dn, axis=-1, keepdims=True))


def local(
    tokens, cotangent, teacher, valid_mask, deal_rows, lengths, w_in, w_beta, conv_kernel, w_out,
    norm_gain, out_gain, ffn_gain, w_gu, w_down,
):
    shards = lax.axis_size(AXES)
    rows = tokens.shape[0]
    share = rows // shards
    blocks = lengths.shape[0]
    rows_mb = rows // blocks
    small = w_beta.shape[0] * HEADS + CONV * conv_kernel.shape[1] + 2 * norm_gain.shape[0]

    target = deal_rows // rows
    spot = deal_rows % rows
    ahead = (target[None, :] == target[:, None]) & (
        jnp.arange(rows)[None, :] < jnp.arange(rows)[:, None]
    )
    slot = target * share + jnp.sum(ahead.astype(jnp.int32), axis=1)
    sort_t = (slot[:, None] == jnp.arange(rows)[None, :]).astype(BF16)
    sort = (slot[None, :] == jnp.arange(rows)[:, None]).astype(BF16)
    count_own = jnp.sum(valid_mask.astype(F32))
    lane = jnp.arange(128)[None, :]
    notes = jnp.where(
        lane == 0,
        valid_mask.astype(F32)[:, None],
        jnp.where(lane == 1, spot.astype(F32)[:, None], jnp.where(lane == 2, count_own, 0.0)),
    ).astype(BF16)
    packed = jnp.concatenate(
        [conv_kernel.reshape(-1), w_beta.reshape(-1), norm_gain, ffn_gain,
         jnp.zeros((share * 128 - small,), BF16)]
    ).reshape(1, share, 128)
    sorted_rows = nn(sort, jnp.concatenate([tokens, cotangent, teacher, notes], axis=1)).astype(BF16)
    message = jnp.concatenate(
        [sorted_rows.reshape(shards, share, -1), jnp.broadcast_to(packed, (shards, share, 128))],
        axis=2,
    )
    (wout, win, wdown, wgu), arrived = gather([w_out, w_in, w_down, w_gu], message, shards, 0)

    flat = arrived.reshape(rows, -1)
    info = flat[:, 3 * D : 3 * D + 128].astype(F32)
    place = info[:, 1].astype(jnp.int32)
    counted = jnp.sum(arrived[:, 0, 3 * D + 2].astype(F32))
    extra = arrived[:, :, 3 * D + 128 :].reshape(shards, share * 128)
    a, b, c = CONV * conv_kernel.shape[1], w_beta.shape[0] * HEADS, norm_gain.shape[0]
    taps = extra[:, :a].reshape(shards, CONV, -1).swapaxes(0, 1).reshape(CONV, 3 * D).astype(F32)
    wbeta = extra[:, a : a + b].reshape(D, HEADS)
    gain_one = extra[:, a + b : a + b + c].reshape(D).astype(F32)
    gain_two = extra[:, a + b + c : a + b + 2 * c].reshape(D).astype(F32)
    deal = (place[None, :] == jnp.arange(rows)[:, None]).astype(BF16)
    deal_t = (place[:, None] == jnp.arange(rows)[None, :]).astype(BF16)
    dealt = nn(deal, flat[:, : 3 * D + 128])
    x = dealt[:, :D]
    g = dealt[:, D : 2 * D]
    t = dealt[:, 2 * D : 3 * D]
    m = dealt[:, 3 * D : 3 * D + 1]

    ends = jnp.cumsum(lengths, axis=1)
    within = jnp.arange(rows_mb, dtype=jnp.int32)
    seg = jnp.sum((within[None, :, None] >= ends[:, None, :]).astype(jnp.int32), axis=2)
    seg = (seg + (lengths.shape[1] + 1) * jnp.arange(blocks, dtype=jnp.int32)[:, None]).reshape(rows)
    position = jnp.arange(rows, dtype=jnp.int32)
    mask = jnp.stack(
        [jnp.ones((rows,), F32)]
        + [((position >= s) & (jnp.roll(seg, s) == seg)).astype(F32) for s in range(1, CONV)]
        + [jnp.zeros((rows,), F32)] * (8 - CONV),
        axis=1,
    )
    segc, segr = seg[:, None], seg[None, :]
    gain_out = out_gain.astype(F32)[None, :]

    nx, rx = rms(x)
    a1 = (nx * gain_one).astype(BF16)
    proj = nn(a1, win)
    beta_pre = nn(a1, wbeta)
    on, *saved = mixer_forward(proj, beta_pre, taps, gain_out, mask, segc, segr, blocks)
    resid = x + nn(on, wout)
    nr, rr = rms(resid)
    a2 = (nr * gain_two).astype(BF16)
    gu = nn(a2, wgu)
    gate, up = gu[:, :FF], gu[:, FF:]
    sg = sigmoid(gate)
    hid = (gate * sg * up).astype(BF16)
    y = resid + nn(hid, wdown)
    errors = y - t
    loss_part = jnp.sum(m * errors * errors)
    dy = g + (rows * shards / counted) * m * errors
    df = dy.astype(BF16)
    dhid = nt(df, wdown)
    dgu = jnp.concatenate(
        [dhid * up * (sg * (1.0 + gate * (1.0 - sg))), dhid * (gate * sg)], axis=1
    ).astype(BF16)
    da2 = nt(dgu, wgu)
    d_gain_two = jnp.sum(da2 * nr, axis=0)
    dresid = dy + rms_back(nr, rr, gain_two * da2)
    dz = dresid.astype(BF16)
    don = nt(dz, wout)
    dpq, dpk, dpv, dpg, dbeta, dtq, dtk, dtv, d_gain_out = mixer_backward(
        proj, beta_pre, taps, gain_out, mask, segc, segr, don, saved, blocks
    )
    dproj = jnp.concatenate([dpq, dpk, dpv, dpg], axis=1)
    dbeta = dbeta.astype(BF16)
    da1 = nt(dproj, win) + nt(dbeta, wbeta)
    d_gain_one = jnp.sum(da1 * nx, axis=0)
    dx = dresid + rms_back(nx, rx, gain_one * da1)

    back = jnp.concatenate([y.astype(BF16), dx.astype(BF16)], axis=1)
    back = nn(deal_t, back).astype(BF16).reshape(shards, share, 2 * D)
    (g_down, g_gu, g_out, g_in), back = scatter(
        [tn(hid, df, BF16), tn(a2, dgu, BF16), tn(on, dz, BF16), tn(a1, dproj, BF16)], back, shards, 1
    )
    back = nn(sort_t, back.reshape(rows, 2 * D)).astype(BF16)
    output, input_grad = back[:, :D], back[:, D:]

    d_taps = jnp.concatenate([dtq, dtk, dtv], axis=1)
    d_wbeta = tn(a1, dbeta)
    tail = jnp.concatenate([d_gain_out.reshape(-1), loss_part.reshape(1)])
    extra = jnp.concatenate(
        [
            d_taps.reshape(CONV, shards, -1).swapaxes(0, 1).reshape(shards, a),
            d_wbeta.reshape(shards, b),
            d_gain_one.reshape(shards, c),
            d_gain_two.reshape(shards, c),
            jnp.broadcast_to(tail[None], (shards, tail.shape[0])),
        ],
        axis=1,
    )
    padded = -(-extra.shape[1] // 128) * 128
    extra = jnp.pad(extra, ((0, 0), (0, padded - extra.shape[1])))
    summed = jnp.sum(
        lax.all_to_all(
            extra.reshape(shards, padded // 128, 128), AXES, split_axis=0, concat_axis=0, tiled=True
        ),
        axis=0,
    ).reshape(-1)
    g_taps = summed[:a].reshape(CONV, -1)
    g_beta = summed[a : a + b].reshape(-1, HEADS)
    g_gain_one = summed[a + b : a + b + c]
    g_gain_two = summed[a + b + c : a + b + 2 * c]
    g_gain_out = summed[a + b + 2 * c : a + b + 2 * c + HEAD_DIM]
    loss = summed[a + b + 2 * c + HEAD_DIM] / (D * counted)

    return (
        output, input_grad, g_in, g_beta, g_taps, g_out, g_gain_one, g_gain_out, g_gain_two, g_gu,
        g_down, loss,
    )


def solution(mesh):
    both = P(AXES, None)
    flat = P(AXES)
    in_specs = (both, both, both, flat, flat, both, both, both, P(None, AXES), both, flat, P(), flat,
                both, both)
    out_specs = (both, both, both, both, P(None, AXES), both, flat, P(), flat, both, both, P())
    return jax.shard_map(local, mesh=mesh, in_specs=in_specs, out_specs=out_specs, check_vma=False)
```

```python
import functools

import jax
import jax.numpy as jnp
from jax import lax
from jax.experimental import pallas as pl
from jax.experimental.pallas import tpu as pltpu
from jax.sharding import PartitionSpec as P

D = 1024
HEADS = 8
HEAD_DIM = 128
FF = 2816
CONV = 4
AXES = ("dp", "fsdp")
F32 = jnp.float32
BF16 = jnp.bfloat16
PAIR = 2
MESH = pl.DeviceIdType.MESH


def mm(left, right, lc, rc):
    return lax.dot_general(
        left,
        right,
        (((lc,), (rc,)), ((), ())),
        precision=lax.Precision.HIGHEST,
        preferred_element_type=F32,
    )


def sigmoid(v):
    return 1.0 / (1.0 + jnp.exp(-v))


def iota2(shape, axis):
    return lax.broadcasted_iota(jnp.int32, shape, axis)


def unit_lower_inverses(mats, size):
    row, col = iota2((size, size), 0), iota2((size, size), 1)
    eye = (row == col).astype(F32)
    inverses = None
    width = 1
    while width < size:
        corner = ((row // (2 * width)) == (col // (2 * width))) & (
            (row // width) == (col // width) + 1
        )
        edges = [jnp.where(corner, m, 0.0) for m in mats]
        if inverses is None:
            inverses = [eye - e for e in edges]
        else:
            right = [mm(e, x, 1, 0) for e, x in zip(edges, inverses)]
            inverses = [x - mm(x, r, 1, 0) for x, r in zip(inverses, right)]
        width *= 2
    return inverses


def conv_parts(src, taps, masks):
    rolled = [src]
    total = src * taps[CONV - 1 : CONV, :]
    for s in range(1, CONV):
        moved = pltpu.roll(src, s, 0) * masks[s]
        rolled.append(moved)
        total = total + moved * taps[CONV - 1 - s : CONV - s, :]
    return total, rolled


def l2_norm(c):
    inv = lax.rsqrt(jnp.sum(c * c, axis=-1, keepdims=True) + 1e-06)
    return c * inv, inv


def mixer_fwd_kernel(
    blocks, rows_mb,
    pq, pk, pv, pg, beta, tq, tk, tv, gain, mask, segc, segr,
    on_ref, o_ref, ainv_ref, u_ref, p_ref, l_ref,
):
    step = pl.program_id(0)
    masks = [None] + [mask[:, s : s + 1] for s in range(1, CONV)]
    cs = []
    for src, taps in ((pq, tq), (pk, tk), (pv, tv)):
        pre, _ = conv_parts(src[...], taps[...], masks)
        cs.append(pre * sigmoid(pre))
    cq, ck, cv = cs
    strengths = sigmoid(beta[...])
    lane = iota2(strengths.shape, 1)
    gate = pg[...]
    gate = gate * sigmoid(gate)
    row, col = iota2((rows_mb, rows_mb), 0), iota2((rows_mb, rows_mb), 1)
    systems = [(h, b) for h in range(PAIR) for b in range(blocks)]
    qs, ks, vs, bs, sames, lows = [], [], [], [], [], []
    for h, b in systems:
        rs = slice(b * rows_mb, (b + 1) * rows_mb)
        hs = slice(h * HEAD_DIM, (h + 1) * HEAD_DIM)
        q, _ = l2_norm(cq[rs, hs])
        k, _ = l2_norm(ck[rs, hs])
        qs.append(q * HEAD_DIM ** (-0.5))
        ks.append(k)
        vs.append(cv[rs, hs])
        bs.append(
            jnp.sum(jnp.where(lane == step * PAIR + h, strengths, 0.0), axis=1, keepdims=True)[rs]
        )
        sames.append(segc[rs, :] == segr[:, rs])
    for i in range(len(systems)):
        lows.append(jnp.where(sames[i] & (row > col), mm(ks[i], ks[i], 1, 1), 0.0))
    inverses = unit_lower_inverses([l * b for l, b in zip(lows, bs)], rows_mb)
    us = [mm(a, v * b, 1, 0) for a, v, b in zip(inverses, vs, bs)]
    ps = [
        jnp.where(same & (row >= col), mm(q, k, 1, 1), 0.0)
        for q, k, same in zip(qs, ks, sames)
    ]
    os = [mm(p, u, 1, 0) for p, u in zip(ps, us)]
    for i, (h, b) in enumerate(systems):
        rs = slice(b * rows_mb, (b + 1) * rows_mb)
        hs = slice(h * HEAD_DIM, (h + 1) * HEAD_DIM)
        o = os[i]
        inv = lax.rsqrt(jnp.mean(o * o, axis=-1, keepdims=True) + 1e-05)
        on_ref[rs, hs] = (o * inv * gain[...] * gate[rs, hs]).astype(BF16)
        o_ref[rs, hs] = o
        ainv_ref[h, b] = inverses[i]
        u_ref[h, b] = us[i]
        p_ref[h, b] = ps[i]
        l_ref[h, b] = lows[i]


def mixer_bwd_kernel(
    blocks, rows_mb, step,
    pq, pk, pv, pg, beta, tq, tk, tv, gain, mask, segc, segr,
    don_ref, o_ref, ainv_ref, u_ref, p_ref, l_ref,
    dq_ref, dk_ref, dv_ref, dg_ref, dbeta_ref, dtq, dtk, dtv, dgain_ref,
):
    rows = blocks * rows_mb
    masks = [None] + [mask[:, s : s + 1] for s in range(1, CONV)]
    pres, rolls, cs, sig = [], [], [], []
    for src, taps in ((pq, tq), (pk, tk), (pv, tv)):
        pre, rolled = conv_parts(src[...], taps[...], masks)
        s = sigmoid(pre)
        pres.append(pre)
        rolls.append(rolled)
        sig.append(s)
        cs.append(pre * s)
    cq, ck, cv = cs
    strengths = sigmoid(beta[...])
    lane = iota2(strengths.shape, 1)
    row, col = iota2((rows_mb, rows_mb), 0), iota2((rows_mb, rows_mb), 1)
    gates = pg[...]
    gsig = sigmoid(gates)
    gate = gates * gsig
    dgate = gsig * (1.0 + gates * (1.0 - gsig))
    systems = [(h, b) for h in range(PAIR) for b in range(blocks)]
    part = []
    dgain = jnp.zeros((1, HEAD_DIM), F32)
    for h, b in systems:
        rs = slice(b * rows_mb, (b + 1) * rows_mb)
        hs = slice(h * HEAD_DIM, (h + 1) * HEAD_DIM)
        k, ik = l2_norm(ck[rs, hs])
        qn, iq = l2_norm(cq[rs, hs])
        v = cv[rs, hs]
        bb = jnp.sum(jnp.where(lane == step * PAIR + h, strengths, 0.0), axis=1, keepdims=True)[rs]
        same = segc[rs, :] == segr[:, rs]
        o = o_ref[rs, hs]
        don = don_ref[rs, hs]
        inv = lax.rsqrt(jnp.mean(o * o, axis=-1, keepdims=True) + 1e-05)
        no = o * inv
        scaled = don * gain[...]
        dg_ref[rs, hs] = (scaled * no * dgate[rs, hs]).astype(BF16)
        dgain = dgain + jnp.sum(don * no * gate[rs, hs], axis=0, keepdims=True)
        dno = scaled * gate[rs, hs]
        do = inv * (dno - no * jnp.mean(no * dno, axis=-1, keepdims=True))
        part.append([q_ for q_ in (qn, iq, k, ik, v, bb, same, do)])
    dus = [mm(p_ref[h, b], part[i][7], 0, 0) for i, (h, b) in enumerate(systems)]
    dps = [
        jnp.where(part[i][6] & (row >= col), mm(part[i][7], u_ref[h, b], 1, 1), 0.0)
        for i, (h, b) in enumerate(systems)
    ]
    drs = [mm(ainv_ref[h, b], dus[i], 0, 0) for i, (h, b) in enumerate(systems)]
    scale = HEAD_DIM ** (-0.5)
    dqs = [mm(dps[i], part[i][2], 1, 0) * scale for i in range(len(systems))]
    das = [mm(drs[i], u_ref[h, b], 1, 1) for i, (h, b) in enumerate(systems)]
    dks = [mm(dps[i], part[i][0] * scale, 0, 0) for i in range(len(systems))]
    dgs = []
    for i in range(len(systems)):
        g = jnp.where(part[i][6] & (row > col), das[i] * (-part[i][5]), 0.0)
        dgs.append(g + g.T)
    dks = [dks[i] + mm(dgs[i], part[i][2], 1, 0) for i in range(len(systems))]
    dbeta = jnp.zeros(strengths.shape, F32)
    dcs = [[], [], []]
    for i, (h, b) in enumerate(systems):
        qn, iq, k, ik, v, bb, same, do = part[i]
        dv = drs[i] * bb
        db = jnp.sum(drs[i] * v - das[i] * l_ref[h, b], axis=-1, keepdims=True)
        dbp = db * bb * (1.0 - bb)
        pieces = [dbp if b == c else jnp.zeros((rows_mb, 1), F32) for c in range(blocks)]
        column = jnp.concatenate(pieces, axis=0) if blocks > 1 else dbp
        dbeta = dbeta + jnp.where(lane == step * PAIR + h, column, 0.0)
        dcs[0].append(iq * (dqs[i] - qn * jnp.sum(qn * dqs[i], axis=-1, keepdims=True)))
        dcs[1].append(ik * (dks[i] - k * jnp.sum(k * dks[i], axis=-1, keepdims=True)))
        dcs[2].append(dv)
    for j, (out, dtap, taps) in enumerate(((dq_ref, dtq, tq), (dk_ref, dtk, tk), (dv_ref, dtv, tv))):
        whole = jnp.concatenate(
            [
                jnp.concatenate([dcs[j][h * blocks + b] for b in range(blocks)], axis=0)
                for h in range(PAIR)
            ],
            axis=1,
        )
        dpre = whole * (sig[j] * (1.0 + pres[j] * (1.0 - sig[j])))
        tap = taps[...]
        grad = dpre * tap[CONV - 1 : CONV, :]
        dtap[CONV - 1 : CONV, :] = jnp.sum(dpre * rolls[j][0], axis=0, keepdims=True)
        for s in range(1, CONV):
            dtap[CONV - 1 - s : CONV - s, :] = jnp.sum(dpre * rolls[j][s], axis=0, keepdims=True)
            grad = grad + pltpu.roll(dpre * masks[s], rows - s, 0) * tap[CONV - 1 - s : CONV - s, :]
        out[...] = grad.astype(BF16)

    @pl.when(step == 0)
    def _():
        dbeta_ref[...] = jnp.zeros_like(dbeta_ref)
        dgain_ref[...] = jnp.zeros_like(dgain_ref)

    dbeta_ref[...] += dbeta
    dgain_ref[...] += dgain


def mixer_specs(rows, blocks, rows_mb):
    width = PAIR * HEAD_DIM
    per = D // width
    col = lambda k: pl.BlockSpec((rows, width), lambda i, k=k: (0, k * per + i))
    tap = lambda k: pl.BlockSpec((CONV, width), lambda i, k=k: (0, k * per + i))
    full = lambda shape: pl.BlockSpec(shape, lambda i: (0,) * len(shape))
    ins = [col(0), col(1), col(2), col(3), full((rows, HEADS)), tap(0), tap(1), tap(2),
           full((1, HEAD_DIM)), full((rows, 8)), full((rows, 1)), full((1, rows))]
    mat = pl.BlockSpec((PAIR, blocks, rows_mb, rows_mb), lambda i: (i, 0, 0, 0))
    one = pl.BlockSpec((rows, width), lambda i: (0, i))
    otap = pl.BlockSpec((CONV, width), lambda i: (0, i))
    return ins, mat, one, otap, full


def lin_index():
    return lax.axis_index("dp") * lax.axis_size("fsdp") + lax.axis_index("fsdp")


def mesh_id(index):
    inner = lax.axis_size("fsdp")
    return (lax.div(index, inner), lax.rem(index, inner))


def flip(me, bits, number, always=()):
    result = me
    for bit in always:
        own = lax.rem(lax.div(me, 1 << bit), 2)
        result = result + (1 - 2 * own) * (1 << bit)
    for i, bit in enumerate(reversed(bits)):
        own = lax.rem(lax.div(me, 1 << bit), 2)
        if isinstance(number, int):
            flag = (number >> i) & 1
            if flag == 0:
                continue
        else:
            flag = lax.rem(lax.div(number, 1 << i), 2)
        result = result + flag * (1 - 2 * own) * (1 << bit)
    return result


def routes(shards):
    bits = shards.bit_length() - 1
    rest = list(range(4, bits))
    return [[1, 3, 2] + rest, [2, 1, 3] + rest, [3, 2, 1] + rest]


def colours(width, turn):
    tiles = width // 128
    sizes = [tiles // 3 + (1 if (c - turn) % 3 < tiles % 3 else 0) for c in range(3)]
    cuts, at = [], 0
    for s in sizes:
        cuts.append((at * 128, s * 128))
        at += s
    return cuts


def meet(shards, me, everyone):
    barrier = pltpu.get_barrier_semaphore()
    if everyone:

        def greet(r, _):
            pl.semaphore_signal(
                barrier, inc=1, device_id=mesh_id(lax.rem(me + r, shards)), device_id_type=MESH
            )
            return 0

        lax.fori_loop(1, shards, greet, 0)
        pl.semaphore_wait(barrier, shards - 1)
    else:
        bits = shards.bit_length() - 1
        for bit in range(bits):
            pl.semaphore_signal(
                barrier, inc=1, device_id=mesh_id(flip(me, [], 0, (bit,))), device_id_type=MESH
            )
        pl.semaphore_wait(barrier, bits)


class Exchange:
    def __init__(self, shards, me, sent, got, send, recv, keep):
        self.shards, self.me, self.sent, self.got = shards, me, sent, got
        self.send, self.recv, self.keep = send, recv, keep

    def own(self):
        return pltpu.make_async_copy(self.sent.at[self.me], self.got.at[self.me], self.keep)

    def start(self):
        self.own().start()

        def one(r, _):
            peer = lax.rem(self.me + r, self.shards)
            pltpu.make_async_remote_copy(
                src_ref=self.sent.at[peer], dst_ref=self.got.at[self.me], send_sem=self.send,
                recv_sem=self.recv, device_id=mesh_id(peer), device_id_type=MESH,
            ).start()
            return 0

        lax.fori_loop(1, self.shards, one, 0)

    def wait(self):
        self.own().wait()
        whole = pl.ds(0, self.shards - 1)
        pltpu.make_async_remote_copy(
            src_ref=self.sent.at[whole], dst_ref=self.got.at[whole], send_sem=self.send,
            recv_sem=self.recv, device_id=mesh_id(self.me), device_id_type=MESH,
        ).wait()


DEAL_AT = 0
CHUNK = 256


def pieces_of(widths, split):
    result = []
    for i, width in enumerate(widths):
        tiles, at = width // 128, 0
        for j in range(split[i]):
            size = tiles // split[i] + (1 if j < tiles % split[i] else 0)
            result.append((i, at * 128, size * 128))
            at += size
    return result


class Gather:
    def __init__(self, shards, me, pieces, own, full, sems):
        self.me, self.pieces, self.own, self.full = me, pieces, own, full
        self.send, self.recv, self.pair_send, self.pair_recv, self.keep = sems
        self.stages = shards.bit_length() - 2
        self.order = routes(shards)
        self.core = lax.rem(me, 2)
        self.cuts = [
            [(at + a, s) for a, s in colours(size, n)] for n, (_, at, size) in enumerate(pieces)
        ]
        self.last = len(pieces) + self.stages - 1

    @staticmethod
    def semaphores(shards, pieces):
        dma, stages = pltpu.SemaphoreType.DMA, shards.bit_length() - 2
        number = len(pieces)
        return [dma((stages, number, 3)), dma((stages, number, 3)), dma((number,)), dma((number,)),
                dma((number,))]

    def kept(self, i):
        return pltpu.make_async_copy(
            self.own[i], self.full[i].at[lax.div(self.me, 2), self.core], self.keep.at[i]
        )

    def begin(self):
        for i in range(len(self.own)):
            self.kept(i).start()

    def partner(self, k, c):
        return mesh_id(flip(self.me, [], 0, (self.order[c][self.stages - 1 - k],)))

    def group(self, k, n, c):
        at, size = self.cuts[n][c]
        some = self.full[self.pieces[n][0]].at[pl.ds(0, 1 << k), 0, :, pl.ds(at, size)]
        return pltpu.make_async_remote_copy(
            src_ref=some, dst_ref=some, send_sem=self.send.at[k, n, c],
            recv_sem=self.recv.at[k, n, c], device_id=self.partner(k, c), device_id_type=MESH,
        )

    def half(self, n):
        i, at, size = self.pieces[n]
        some = self.full[i].at[:, self.core, :, pl.ds(at, size)]
        return pltpu.make_async_remote_copy(
            src_ref=some, dst_ref=some, send_sem=self.pair_send.at[n],
            recv_sem=self.pair_recv.at[n], device_id=mesh_id(flip(self.me, [], 0, (0,))),
            device_id_type=MESH,
        )

    def launch(self, k, n):
        i = self.pieces[n][0]
        for c in range(3):
            at, size = self.cuts[n][c]
            if k > 0:
                self.group(k - 1, n, c).wait_recv()
            have = self.order[c][self.stages - k :]
            for j in range(1 << k):
                d = flip(self.me, have, j)
                there = self.full[i].at[lax.div(d, 2), self.core, :, pl.ds(at, size)]
                pltpu.make_async_remote_copy(
                    src_ref=self.own[i].at[:, pl.ds(at, size)] if j == 0 else there,
                    dst_ref=there, send_sem=self.send.at[k, n, c], recv_sem=self.recv.at[k, n, c],
                    device_id=self.partner(k, c), device_id_type=MESH,
                ).start()

    def finish(self, n):
        for c in range(3):
            self.group(self.stages - 1, n, c).wait_recv()
        if n == 0 or self.pieces[n - 1][0] != self.pieces[n][0]:
            self.kept(self.pieces[n][0]).wait()
        self.half(n).start()

    def step(self, t):
        for n in range(len(self.pieces)):
            k = t - n
            if 0 <= k < self.stages:
                self.launch(k, n)
            elif k == self.stages:
                self.finish(n)

    def end(self):
        for k in range(self.stages):
            for n in range(len(self.pieces)):
                for c in range(3):
                    self.group(k, n, c).wait_send()
        for n in range(len(self.pieces)):
            self.half(n).wait()


def first_kernel(shards, pieces, *refs):
    count = 1 + max(i for i, _, _ in pieces)
    own, sent, full, got = refs[:count], refs[count], refs[count + 1 : 2 * count + 1], refs[2 * count + 1]
    sems = refs[2 * count + 2 :]
    me = lin_index()
    deal = Exchange(shards, me, sent, got, *sems[5:])
    weights = Gather(shards, me, pieces, own, full, sems[:5])
    weights.begin()
    meet(shards, me, True)
    deal.start()
    for t in range(weights.last + 1):
        weights.step(t)
    deal.wait()
    weights.end()


def spread(weight, shards):
    return jax.ShapeDtypeStruct((shards // 2, 2) + weight.shape, weight.dtype)


def first(weights, split, message, shards, collective_id):
    count = len(weights)
    anywhere = pl.BlockSpec(memory_space=pl.ANY)
    pieces = pieces_of([w.shape[1] for w in weights], split)
    dma = pltpu.SemaphoreType.DMA
    *full, got = pl.pallas_call(
        functools.partial(first_kernel, shards, pieces),
        in_specs=[anywhere] * (count + 1),
        out_specs=[anywhere] * (count + 1),
        out_shape=[spread(w, shards) for w in weights]
        + [jax.ShapeDtypeStruct(message.shape, message.dtype)],
        scratch_shapes=Gather.semaphores(shards, pieces) + [dma, dma, dma],
        compiler_params=pltpu.CompilerParams(collective_id=collective_id, has_side_effects=True),
        name="gather_first",
    )(*weights, message)
    return [f.reshape(-1, f.shape[-1]) for f in full], got


def forward_kernel(
    shards, pieces, blocks, rows_mb,
    own_down, own_gu, sent, a1, wq, wk, wv, wg, wout, wbeta, x, gain_two, tq, tk, tv, gain, mask,
    segc, segr,
    full_down, full_gu, got, pq, pk, pv, pg, beta, on, o, ainv, u, p, l, resid, a2,
    *sems,
):
    step = pl.program_id(0)
    steps = HEADS // PAIR
    me = lin_index()
    weights = Gather(shards, me, pieces, (own_down, own_gu), (full_down, full_gu), sems[:5])
    deal = Exchange(shards, me, sent, got, *sems[5:])

    @pl.when(step == 0)
    def _():
        weights.begin()
        meet(shards, me, True)
        weights.step(0)
        resid[...] = x[...]

    normed = a1[...]
    beta[...] = jnp.dot(normed, wbeta[...], preferred_element_type=F32)
    for out, w in ((pq, wq), (pk, wk), (pv, wv), (pg, wg)):
        out[...] = jnp.dot(normed, w[...], preferred_element_type=F32)
    mixer_fwd_kernel(
        blocks, rows_mb, pq, pk, pv, pg, beta, tq, tk, tv, gain, mask, segc, segr, on, o, ainv, u,
        p, l,
    )
    resid[...] += jnp.dot(on[...], wout[...], preferred_element_type=F32)
    for s in range(steps):

        @pl.when(step == s)
        def _(s=s):
            weights.step(s + 1)
            if s == DEAL_AT:
                deal.start()
            if s == steps - 1:
                r = resid[...]
                a2[...] = (rms(r)[0] * gain_two[...]).astype(BF16)
                for t in range(steps + 1, weights.last + 1):
                    weights.step(t)
                deal.wait()
                weights.end()


def forward(
    w_down, w_gu, message, split, a1, win, wout, wbeta, x, gain_two, taps, gain, mask, segc, segr, blocks,
    shards, collective_id,
):
    rows = x.shape[0]
    rows_mb = rows // blocks
    width = PAIR * HEAD_DIM
    pieces = pieces_of([w_down.shape[1], w_gu.shape[1]], split)
    anywhere = pl.BlockSpec(memory_space=pl.ANY)
    ins, mat, one, _, full = mixer_specs(rows, blocks, rows_mb)
    per = D // width
    wcol = lambda k: pl.BlockSpec((D, width), lambda i, k=k: (0, k * per + i))
    square = jax.ShapeDtypeStruct((HEADS, blocks, rows_mb, rows_mb), F32)
    wide = jax.ShapeDtypeStruct((rows, D), F32)
    dma = pltpu.SemaphoreType.DMA
    full_down, full_gu, got, *rest = pl.pallas_call(
        functools.partial(forward_kernel, shards, pieces, blocks, rows_mb),
        grid=(HEADS // PAIR,),
        in_specs=[
            anywhere, anywhere, anywhere, full((rows, D)), wcol(0), wcol(1), wcol(2), wcol(3),
            pl.BlockSpec((width, D), lambda i: (i, 0)), full((D, HEADS)), full((rows, D)),
            full((1, D)), *ins[5:],
        ],
        out_specs=[anywhere, anywhere, anywhere, one, one, one, one, full((rows, HEADS)), one, one, mat, mat,
                   mat, mat, full((rows, D)), full((rows, D))],
        out_shape=[
            spread(w_down, shards), spread(w_gu, shards),
            jax.ShapeDtypeStruct(message.shape, message.dtype), wide, wide, wide, wide,
            jax.ShapeDtypeStruct((rows, HEADS), F32), jax.ShapeDtypeStruct((rows, D), BF16), wide,
            square, square, square, square, wide, jax.ShapeDtypeStruct((rows, D), BF16),
        ],
        scratch_shapes=Gather.semaphores(shards, pieces) + [dma, dma, dma],
        compiler_params=pltpu.CompilerParams(
            collective_id=collective_id, has_side_effects=True, vmem_limit_bytes=48 << 20
        ),
        name="mixer_forward",
    )(w_down, w_gu, message, a1, win, win, win, win, wout, wbeta, x, gain_two, taps, taps, taps, gain, mask,
      segc, segr)
    return full_down.reshape(FF, D), full_gu.reshape(D, 2 * FF), got, rest


class Scatter:
    def __init__(self, shards, me, pieces, whole, mine, other, coming, sems, kept):
        self.me, self.pieces, self.whole, self.mine = me, pieces, whole, mine
        self.other, self.coming, self.kept_of = other, coming, kept
        self.send, self.recv, self.pair_send, self.pair_recv = sems
        self.stages = shards.bit_length() - 2
        self.order = routes(shards)
        self.core = lax.rem(me, 2)
        self.cuts = [
            [(at + a, s) for a, s in colours(size, n)] for n, (_, at, size) in enumerate(pieces)
        ]

    @staticmethod
    def semaphores(shards, number):
        dma, stages = pltpu.SemaphoreType.DMA, shards.bit_length() - 2
        return [dma((stages, number, 3)), dma((stages, number, 3)), dma((number,)), dma((number,))]

    @staticmethod
    def buffers(shards, shapes):
        stages = shards.bit_length() - 2
        return [pltpu.VMEM((shards // 2,) + s, BF16) for s in shapes] + [
            pltpu.VMEM((1 << (stages - 1 - k),) + s, BF16) for s in shapes for k in range(stages)
        ]

    @staticmethod
    def split(shards, count, refs):
        stages = shards.bit_length() - 2
        other, refs = refs[:count], refs[count:]
        return other, [refs[i * stages : (i + 1) * stages] for i in range(count)]

    def pair(self, n):
        i, at, size = self.pieces[n]
        return pltpu.make_async_remote_copy(
            src_ref=self.whole(n, 1 - self.core), dst_ref=self.other[i].at[:, :, pl.ds(at, size)],
            send_sem=self.pair_send.at[n], recv_sem=self.pair_recv.at[n],
            device_id=mesh_id(flip(self.me, [], 0, (0,))), device_id_type=MESH,
        )

    def hop(self, k, n, c, source, spots):
        i = self.pieces[n][0]
        at, size = self.cuts[n][c]
        cols = pl.ds(at, size)
        return pltpu.make_async_remote_copy(
            src_ref=self.other[i].at[source, :, cols],
            dst_ref=self.coming[i][k].at[spots, :, cols],
            send_sem=self.send.at[k, n, c], recv_sem=self.recv.at[k, n, c],
            device_id=mesh_id(flip(self.me, [], 0, (self.order[c][k],))), device_id_type=MESH,
        )

    def group(self, k, n, c):
        all_of = pl.ds(0, 1 << (self.stages - 1 - k))
        return self.hop(k, n, c, all_of, all_of)

    def total(self, k, n, c, shard, spot):
        i = self.pieces[n][0]
        at, size = self.cuts[n][c]
        cols = pl.ds(at, size)
        q = lax.div(shard, 2)
        value = self.mine(i, q, cols).astype(F32) + self.other[i][q, :, cols].astype(F32)
        for p in range(k):
            value = value + self.coming[i][p][spot, :, cols].astype(F32)
        return value

    def launch(self, k, n):
        if k == 0:
            kept = self.kept_of(n)
            if kept is not None:
                kept.wait()
            self.pair(n).wait_recv()
        for c in range(3):
            if k > 0:
                self.group(k - 1, n, c).wait_recv()
            much = 1 << (self.stages - 1 - k)
            at, size = self.cuts[n][c]

            def body(j, _, c=c, at=at, size=size):
                shard = flip(self.me, self.order[c][k + 1 :], j, (self.order[c][k],))
                q = lax.div(shard, 2)
                self.other[self.pieces[n][0]][q, :, pl.ds(at, size)] = self.total(
                    k, n, c, shard, much + j
                ).astype(BF16)
                self.hop(k, n, c, q, j).start()
                return 0

            lax.fori_loop(0, much, body, 0)

    def finish(self, n, write):
        for c in range(3):
            self.group(self.stages - 1, n, c).wait_recv()
            at, size = self.cuts[n][c]
            write(self.pieces[n][0], at, size, self.total(self.stages, n, c, self.me, 0))

    def end(self, n):
        for k in range(self.stages):
            for c in range(3):
                self.group(k, n, c).wait_send()
        self.pair(n).wait_send()


def backward_kernel(shards, blocks, rows_mb, pieces, *refs):
    (d_down, df, a2, gate, up, wga, wup, wdn, dy, resid, gain_two, wout, wq, wk, wv, wg, a1, on, x,
     gain_one, wbeta, *mixer), refs = refs[:38], refs[38:]
    (g_down, g_gu, dwq, dwk, dwv, dwg, dw_out, d_wbeta, dx, d_two, d_one, dtq, dtk, dtv,
     d_gain), refs = refs[:15], refs[15:]
    (mine_down, d_gu, acc, dresid, dz, don, dpq, dpk, dpv, dpg, dbeta, keep), refs = refs[:12], refs[12:]
    sems, buffers = refs[:4], refs[4:]
    step = pl.program_id(0)
    chunks = FF // CHUNK
    pairs = HEADS // PAIR
    me = lin_index()
    core = lax.rem(me, 2)
    other, coming = Scatter.split(shards, 2, buffers)
    r_gu = d_gu.shape[2]

    def whole(n, parity):
        i, at, size = pieces[n]
        if i == 0:
            return d_down.at[:, parity, :, pl.ds(at, size)]
        return d_gu.at[:, parity, :, pl.ds(at, size)]

    def mine(i, q, cols):
        return mine_down[q, :, cols] if i == 0 else d_gu[q, core, :, cols]

    def kept(n):
        if n > 0:
            return None
        return pltpu.make_async_copy(d_down.at[:, core], mine_down, keep)

    net = Scatter(shards, me, pieces, whole, mine, other, coming, sems, kept)

    def write(i, at, size, value):
        if i == 0:
            g_down[:, pl.ds(at, size)] = value
            return
        for tile in range(at // 128, (at + size) // 128):
            chunk, inner = tile * 128 // (2 * CHUNK), tile * 128 % (2 * CHUNK)
            start = chunk * CHUNK + inner if inner < CHUNK else FF + chunk * CHUNK + inner - CHUNK
            g_gu[:, start : start + 128] = value[:, tile * 128 - at : tile * 128 - at + 128]

    @pl.when(step == 0)
    def _():
        kept(0).start()
        meet(shards, me, False)
        net.pair(0).start()
        acc[...] = jnp.zeros_like(acc)

    @pl.when(step < chunks)
    def _():
        dhid = nt(df[...], wdn[...])
        g = gate[...]
        s = sigmoid(g)
        d_gate = (dhid * up[...] * (s * (1.0 + g * (1.0 - s)))).astype(BF16)
        d_up = (dhid * (g * s)).astype(BF16)
        acc[...] += nt(d_gate, wga[...]) + nt(d_up, wup[...])
        for at, part in ((0, d_gate), (CHUNK, d_up)):
            grad = tn(a2[...], part).reshape(shards // 2, 2, r_gu, CHUNK).astype(BF16)
            start = pl.multiple_of(step * (2 * CHUNK) + at, CHUNK)
            d_gu[:, :, :, pl.ds(start, CHUNK)] = grad

    @pl.when(step == chunks - 1)
    def _():
        nr, rr = rms(resid[...])
        da2 = acc[...]
        d_two[...] = jnp.sum(da2 * nr, axis=0, keepdims=True)
        dresid[...] = dy[...] + rms_back(nr, rr, gain_two[...] * da2)
        acc[...] = jnp.zeros_like(acc)
        dz[...] = dresid[...].astype(BF16)

    @pl.when(step >= chunks)
    def _():
        don[...] = nt(dz[...], wout[...])
        mixer_bwd_kernel(
            blocks, rows_mb, step - chunks, *mixer[:12], don, *mixer[12:], dpq, dpk, dpv, dpg, dbeta, dtq,
            dtk, dtv, d_gain,
        )
        for dp, w, out in ((dpq, wq, dwq), (dpk, wk, dwk), (dpv, wv, dwv), (dpg, wg, dwg)):
            acc[...] += nt(dp[...], w[...])
            out[...] = tn(a1[...], dp[...]).astype(BF16)
        dw_out[...] = tn(on[...], dz[...]).astype(BF16)

    @pl.when(step == chunks + pairs - 1)
    def _():
        d_beta = dbeta[...].astype(BF16)
        grad = acc[...] + nt(d_beta, wbeta[...])
        d_wbeta[...] = tn(a1[...], d_beta)
        nx, rx = rms(x[...])
        d_one[...] = jnp.sum(grad * nx, axis=0, keepdims=True)
        dx[...] = (dresid[...] + rms_back(nx, rx, gain_one[...] * grad)).astype(BF16)

    ready = {pieces[n][1] // (2 * CHUNK) + pieces[n][2] // (2 * CHUNK) - 1: n for n in (1, 2)}
    plan = {}
    for s, n in ready.items():
        plan.setdefault(s, []).append((net.pair, n))
    tail = range(chunks - 1, chunks + pairs)
    plan.setdefault(3, []).append((net.launch, 0, 0))
    for place, s in enumerate(tail):
        for n in range(3):
            k = place + 1 - n
            if (k, n) != (0, 0) and 0 <= k < net.stages:
                plan.setdefault(s, []).append((net.launch, k, n))
            elif k == net.stages:
                plan.setdefault(s, []).append((net.finish, n, write))
    last = tail[-1]
    for place in range(len(tail), net.stages + 3):
        for n in range(3):
            k = place + 1 - n
            if 0 <= k < net.stages:
                plan[last].append((net.launch, k, n))
            elif k == net.stages:
                plan[last].append((net.finish, n, write))
    for s, actions in plan.items():

        @pl.when(step == s)
        def _(actions=actions, s=s):
            for act, *args in actions:
                result = act(*args)
                if act == net.pair:
                    result.start()
            if s == last:
                for n in range(3):
                    net.end(n)


def backward(
    d_down, df, a2, gu, wgu, wdown, dy, resid, gain_two, wout, win, a1, on, x, gain_one, wbeta, proj,
    beta_pre, taps, gain, mask, segc, segr, saved, blocks, shards, collective_id,
):
    rows = x.shape[0]
    rows_mb = rows // blocks
    width = PAIR * HEAD_DIM
    chunks, pairs = FF // CHUNK, HEADS // PAIR
    anywhere = pl.BlockSpec(memory_space=pl.ANY)
    full = lambda shape: pl.BlockSpec(shape, lambda s: (0,) * len(shape))
    early = lambda s: jnp.minimum(s, chunks - 1)
    late = lambda s: jnp.maximum(s - chunks, 0)
    lane_e = lambda r, w, off=0: pl.BlockSpec((r, w), lambda s: (0, off + early(s)))
    lane_l = lambda r, w, off=0: pl.BlockSpec((r, w), lambda s: (0, off + late(s)))
    wide_l = lambda off=0: pl.BlockSpec(
        (D, width), lambda s: (0, off + late(s)), pipeline_mode=pl.Buffered(1)
    )
    row_l = lambda r, w: pl.BlockSpec((r, w), lambda s: (late(s), 0))
    mat = pl.BlockSpec(
        (PAIR, blocks, rows_mb, rows_mb), lambda s: (late(s), 0, 0, 0), pipeline_mode=pl.Buffered(1)
    )
    part_l = pl.BlockSpec(
        (rows, width), lambda s: (0, late(s)), pipeline_mode=pl.Buffered(1)
    )
    per = D // width
    tap = lambda k: lane_l(CONV, width, k * per)
    r_down, r_gu = FF // shards, D // shards
    a, b = chunks // 2 * 2 * CHUNK, 2 * FF
    pieces = [(0, 0, D), (1, 0, a), (1, a, b - a)]
    f32 = lambda *shape: jax.ShapeDtypeStruct(shape, F32)
    bf = lambda *shape: jax.ShapeDtypeStruct(shape, BF16)
    square = bf(D, D)
    vm = pltpu.VMEM
    return pl.pallas_call(
        functools.partial(backward_kernel, shards, blocks, rows_mb, pieces),
        grid=(chunks + pairs,),
        in_specs=[
            anywhere, full((rows, D)), full((rows, D)), lane_e(rows, CHUNK),
            lane_e(rows, CHUNK, chunks), lane_e(D, CHUNK), lane_e(D, CHUNK, chunks),
            pl.BlockSpec((CHUNK, D), lambda s: (early(s), 0)), full((rows, D)), full((rows, D)),
            full((1, D)), row_l(width, D), wide_l(), wide_l(per), wide_l(2 * per),
            wide_l(3 * per), full((rows, D)),
            lane_l(rows, width), full((rows, D)), full((1, D)), full((D, HEADS)),
            part_l, part_l, part_l, part_l, full((rows, HEADS)), tap(0), tap(1), tap(2), full((1, HEAD_DIM)), full((rows, 8)),
            full((rows, 1)), full((1, rows)), lane_l(rows, width), mat, mat, mat, mat,
        ],
        out_specs=[
            full((r_down, D)), full((r_gu, 2 * FF)), wide_l(), wide_l(), wide_l(), wide_l(),
            row_l(width, D), full((D, HEADS)), full((rows, D)),
            full((1, D)), full((1, D)), lane_l(CONV, width), lane_l(CONV, width),
            lane_l(CONV, width), full((1, HEAD_DIM)),
        ],
        out_shape=[
            f32(r_down, D), f32(r_gu, 2 * FF), square, square, square, square, square,
            f32(D, HEADS), bf(rows, D), f32(1, D), f32(1, D), f32(CONV, D), f32(CONV, D),
            f32(CONV, D), f32(1, HEAD_DIM),
        ],
        scratch_shapes=[
            vm((shards // 2, r_down, D), BF16), vm((shards // 2, 2, r_gu, 2 * FF), BF16),
            vm((rows, D), F32), vm((rows, D), F32), vm((rows, D), BF16), vm((rows, width), F32),
            vm((rows, width), BF16), vm((rows, width), BF16), vm((rows, width), BF16),
            vm((rows, width), BF16), vm((rows, HEADS), F32),
            pltpu.SemaphoreType.DMA,
        ] + Scatter.semaphores(shards, 3) + Scatter.buffers(shards, [(r_down, D), (r_gu, 2 * FF)]),
        compiler_params=pltpu.CompilerParams(
            collective_id=collective_id, has_side_effects=True, vmem_limit_bytes=60 << 20
        ),
        name="backward",
    )(d_down.reshape(shards // 2, 2, r_down, D), df, a2, gu, gu, wgu, wgu, wdown, dy, resid, gain_two,
      wout, win, win, win, win, a1, on, x, gain_one, wbeta, *proj, beta_pre, taps, taps, taps, gain,
      mask, segc, segr, *saved)


def scatter_kernel(shards, count, *refs):
    grads, sent, out, got = refs[:count], refs[count], refs[count + 1 : 2 * count + 1], refs[2 * count + 1]
    refs = refs[2 * count + 2 :]
    mine, refs = refs[:count], refs[count:]
    sems, (keep, *back_sems), buffers = refs[:4], refs[4:8], refs[8:]
    me = lin_index()
    core = lax.rem(me, 2)
    back = Exchange(shards, me, sent, got, *back_sems)
    other, coming = Scatter.split(shards, count, buffers)
    pieces = [(i, 0, g.shape[-1]) for i, g in enumerate(grads)]

    def kept(n):
        return pltpu.make_async_copy(grads[n].at[:, core], mine[n], keep.at[n])

    net = Scatter(
        shards, me, pieces, lambda n, parity: grads[n].at[:, parity],
        lambda i, q, cols: mine[i][q, :, cols], other, coming, sems, kept,
    )

    def write(i, at, size, value):
        out[i][:, pl.ds(at, size)] = value

    for n in range(count):
        kept(n).start()
    meet(shards, me, True)
    for n in range(count):
        net.pair(n).start()
    back.start()
    for t in range(count + net.stages):
        for n in range(count):
            k = t - n
            if 0 <= k < net.stages:
                net.launch(k, n)
            elif k == net.stages:
                net.finish(n, write)
    back.wait()
    for n in range(count):
        net.end(n)


def scatter(grads, message, shards, collective_id):
    count = len(grads)
    shapes = [(g.shape[0] // shards, g.shape[1]) for g in grads]
    anywhere = pl.BlockSpec(memory_space=pl.ANY)
    dma = pltpu.SemaphoreType.DMA
    *out, got = pl.pallas_call(
        functools.partial(scatter_kernel, shards, count),
        in_specs=[anywhere] * (count + 1),
        out_specs=[pl.BlockSpec(memory_space=pltpu.VMEM)] * count + [anywhere],
        out_shape=[jax.ShapeDtypeStruct(s, F32) for s in shapes]
        + [jax.ShapeDtypeStruct(message.shape, message.dtype)],
        scratch_shapes=[pltpu.VMEM((shards // 2,) + s, BF16) for s in shapes]
        + Scatter.semaphores(shards, count) + [dma((count,)), dma, dma, dma]
        + Scatter.buffers(shards, shapes),
        compiler_params=pltpu.CompilerParams(
            collective_id=collective_id, has_side_effects=True, vmem_limit_bytes=60 << 20
        ),
        name="scatter_last",
    )(*[g.reshape((shards // 2, 2) + s) for g, s in zip(grads, shapes)], message)
    return out, got


def nt(left, right):
    return lax.dot_general(left, right, (((1,), (1,)), ((), ())), preferred_element_type=F32)


def tn(left, right, dtype=F32):
    return lax.dot_general(left, right, (((0,), (0,)), ((), ())), preferred_element_type=dtype)


def nn(left, right):
    return jnp.dot(left, right, preferred_element_type=F32)


def rms(v):
    inv = lax.rsqrt(jnp.mean(v * v, axis=-1, keepdims=True) + 1e-05)
    return v * inv, inv


def rms_back(normed, inv, dn):
    return inv * (dn - normed * jnp.mean(normed * dn, axis=-1, keepdims=True))


def local(
    tokens, cotangent, teacher, valid_mask, deal_rows, lengths, w_in, w_beta, conv_kernel, w_out,
    norm_gain, out_gain, ffn_gain, w_gu, w_down,
):
    shards = lax.axis_size(AXES)
    rows = tokens.shape[0]
    share = rows // shards
    blocks = lengths.shape[0]
    rows_mb = rows // blocks
    small = w_beta.shape[0] * HEADS + CONV * conv_kernel.shape[1] + 2 * norm_gain.shape[0]

    target = deal_rows // rows
    spot = deal_rows % rows
    ahead = (target[None, :] == target[:, None]) & (
        jnp.arange(rows)[None, :] < jnp.arange(rows)[:, None]
    )
    slot = target * share + jnp.sum(ahead.astype(jnp.int32), axis=1)
    sort_t = (slot[:, None] == jnp.arange(rows)[None, :]).astype(BF16)
    sort = (slot[None, :] == jnp.arange(rows)[:, None]).astype(BF16)
    count_own = jnp.sum(valid_mask.astype(F32))
    lane = jnp.arange(128)[None, :]
    notes = jnp.where(
        lane == 0,
        valid_mask.astype(F32)[:, None],
        jnp.where(lane == 1, spot.astype(F32)[:, None], jnp.where(lane == 2, count_own, 0.0)),
    ).astype(BF16)
    packed = jnp.concatenate(
        [conv_kernel.reshape(-1), w_beta.reshape(-1), norm_gain, ffn_gain,
         jnp.zeros((share * 128 - small,), BF16)]
    ).reshape(1, share, 128)
    sorted_rows = nn(sort, jnp.concatenate([tokens, notes], axis=1)).astype(BF16)
    message = jnp.concatenate(
        [sorted_rows.reshape(shards, share, -1), jnp.broadcast_to(packed, (shards, share, 128))],
        axis=2,
    )
    later = nn(sort, jnp.concatenate([cotangent, teacher], axis=1)).astype(BF16)
    later = later.reshape(shards, share, 2 * D)
    (win, wout), arrived = first([w_in, w_out], (2, 1), message, shards, 0)

    flat = arrived.reshape(rows, -1)
    info = flat[:, D : D + 128].astype(F32)
    place = info[:, 1].astype(jnp.int32)
    counted = jnp.sum(arrived[:, 0, D + 2].astype(F32))
    extra = arrived[:, :, D + 128 :].reshape(shards, share * 128)
    a, b, c = CONV * conv_kernel.shape[1], w_beta.shape[0] * HEADS, norm_gain.shape[0]
    taps = extra[:, :a].reshape(shards, CONV, -1).swapaxes(0, 1).reshape(CONV, 3 * D).astype(F32)
    wbeta = extra[:, a : a + b].reshape(D, HEADS)
    gain_one = extra[:, a + b : a + b + c].reshape(D).astype(F32)
    gain_two = extra[:, a + b + c : a + b + 2 * c].reshape(D).astype(F32)
    deal = (place[None, :] == jnp.arange(rows)[:, None]).astype(BF16)
    deal_t = (place[:, None] == jnp.arange(rows)[None, :]).astype(BF16)
    dealt = nn(deal, flat[:, : D + 128])
    x = dealt[:, :D]
    m = dealt[:, D : D + 1]

    ends = jnp.cumsum(lengths, axis=1)
    within = jnp.arange(rows_mb, dtype=jnp.int32)
    seg = jnp.sum((within[None, :, None] >= ends[:, None, :]).astype(jnp.int32), axis=2)
    seg = (seg + (lengths.shape[1] + 1) * jnp.arange(blocks, dtype=jnp.int32)[:, None]).reshape(rows)
    position = jnp.arange(rows, dtype=jnp.int32)
    mask = jnp.stack(
        [jnp.ones((rows,), F32)]
        + [((position >= s) & (jnp.roll(seg, s) == seg)).astype(F32) for s in range(1, CONV)]
        + [jnp.zeros((rows,), F32)] * (8 - CONV),
        axis=1,
    )
    segc, segr = seg[:, None], seg[None, :]
    gain_out = out_gain.astype(F32)[None, :]

    nx, rx = rms(x)
    a1 = (nx * gain_one).astype(BF16)
    wdown, wgu, later, (*proj, beta_pre, on, o, ainv, u, p, l, resid, a2) = forward(
        w_down, w_gu, later, (1, 2), a1, win, wout, wbeta, x, gain_two[None, :], taps, gain_out, mask, segc,
        segr, blocks, shards, 2,
    )
    saved = (o, ainv, u, p, l)
    later = nn(deal, later.reshape(rows, 2 * D))
    g, t = later[:, :D], later[:, D:]
    gu = nn(a2, wgu)
    gate, up = gu[:, :FF], gu[:, FF:]
    hid = (gate * sigmoid(gate) * up).astype(BF16)
    y = resid + nn(hid, wdown)
    errors = y - t
    loss_part = jnp.sum(m * errors * errors)
    dy = g + (rows * shards / counted) * m * errors
    df = dy.astype(BF16)
    (g_down, g_gu, dwq, dwk, dwv, dwg, dw_out, d_wbeta, dx, d_gain_two, d_gain_one, dtq, dtk, dtv,
     d_gain_out) = backward(
        tn(hid, df, BF16), df, a2, gu, wgu, wdown, dy, resid, gain_two[None, :], wout, win, a1, on, x,
        gain_one[None, :], wbeta, proj, beta_pre, taps, gain_out, mask, segc, segr, saved, blocks, shards,
        1,
    )
    back = jnp.concatenate([y.astype(BF16), dx], axis=1)
    back = nn(deal_t, back).astype(BF16).reshape(shards, share, 2 * D)
    (g_out, *g_in), back = scatter([dw_out, dwq, dwk, dwv, dwg], back, shards, 3)
    g_in = jnp.concatenate(g_in, axis=1)
    back = nn(sort_t, back.reshape(rows, 2 * D)).astype(BF16)
    output, input_grad = back[:, :D], back[:, D:]

    d_taps = jnp.concatenate([dtq, dtk, dtv], axis=1)
    tail = jnp.concatenate([d_gain_out.reshape(-1), loss_part.reshape(1)])
    extra = jnp.concatenate(
        [
            d_taps.reshape(CONV, shards, -1).swapaxes(0, 1).reshape(shards, a),
            d_wbeta.reshape(shards, b),
            d_gain_one.reshape(shards, c),
            d_gain_two.reshape(shards, c),
            jnp.broadcast_to(tail[None], (shards, tail.shape[0])),
        ],
        axis=1,
    )
    padded = -(-extra.shape[1] // 128) * 128
    extra = jnp.pad(extra, ((0, 0), (0, padded - extra.shape[1])))
    summed = jnp.sum(
        lax.all_to_all(
            extra.reshape(shards, padded // 128, 128), AXES, split_axis=0, concat_axis=0, tiled=True
        ),
        axis=0,
    ).reshape(-1)
    g_taps = summed[:a].reshape(CONV, -1)
    g_beta = summed[a : a + b].reshape(-1, HEADS)
    g_gain_one = summed[a + b : a + b + c]
    g_gain_two = summed[a + b + c : a + b + 2 * c]
    g_gain_out = summed[a + b + 2 * c : a + b + 2 * c + HEAD_DIM]
    loss = summed[a + b + 2 * c + HEAD_DIM] / (D * counted)

    return (
        output, input_grad, g_in, g_beta, g_taps, g_out, g_gain_one, g_gain_out, g_gain_two, g_gu,
        g_down, loss,
    )


def solution(mesh):
    both = P(AXES, None)
    flat = P(AXES)
    in_specs = (both, both, both, flat, flat, both, both, both, P(None, AXES), both, flat, P(), flat,
                both, both)
    out_specs = (both, both, both, both, P(None, AXES), both, flat, P(), flat, both, both, P())
    return jax.shard_map(local, mesh=mesh, in_specs=in_specs, out_specs=out_specs, check_vma=False)
```

```python
import functools

import jax
import jax.numpy as jnp
from jax import lax
from jax.experimental import pallas as pl
from jax.experimental.pallas import tpu as pltpu
from jax.sharding import PartitionSpec as P

D = 1024
HEADS = 8
HEAD_DIM = 128
FF = 2816
CONV = 4
AXES = ("dp", "fsdp")
F32 = jnp.float32
BF16 = jnp.bfloat16
PAIR = 2
MESH = pl.DeviceIdType.MESH


def mm(left, right, lc, rc):
    return lax.dot_general(
        left,
        right,
        (((lc,), (rc,)), ((), ())),
        precision=lax.Precision.HIGHEST,
        preferred_element_type=F32,
    )


def sigmoid(v):
    return 1.0 / (1.0 + jnp.exp(-v))


def iota2(shape, axis):
    return lax.broadcasted_iota(jnp.int32, shape, axis)


def unit_lower_inverses(mats, size):
    row, col = iota2((size, size), 0), iota2((size, size), 1)
    eye = (row == col).astype(F32)
    inverses = None
    width = 1
    while width < size:
        corner = ((row // (2 * width)) == (col // (2 * width))) & (
            (row // width) == (col // width) + 1
        )
        edges = [jnp.where(corner, m, 0.0) for m in mats]
        if inverses is None:
            inverses = [eye - e for e in edges]
        else:
            right = [mm(e, x, 1, 0) for e, x in zip(edges, inverses)]
            inverses = [x - mm(x, r, 1, 0) for x, r in zip(inverses, right)]
        width *= 2
    return inverses


def conv_parts(src, taps, masks):
    rolled = [src]
    total = src * taps[CONV - 1 : CONV, :]
    for s in range(1, CONV):
        moved = pltpu.roll(src, s, 0) * masks[s]
        rolled.append(moved)
        total = total + moved * taps[CONV - 1 - s : CONV - s, :]
    return total, rolled


def l2_norm(c):
    inv = lax.rsqrt(jnp.sum(c * c, axis=-1, keepdims=True) + 1e-06)
    return c * inv, inv


def mixer_fwd_kernel(
    blocks, rows_mb,
    pq, pk, pv, pg, beta, tq, tk, tv, gain, mask, segc, segr,
    on_ref, o_ref, ainv_ref, u_ref, p_ref, l_ref,
):
    step = pl.program_id(0)
    masks = [None] + [mask[:, s : s + 1] for s in range(1, CONV)]
    cs = []
    for src, taps in ((pq, tq), (pk, tk), (pv, tv)):
        pre, _ = conv_parts(src[...], taps[...], masks)
        cs.append(pre * sigmoid(pre))
    cq, ck, cv = cs
    strengths = sigmoid(beta[...])
    lane = iota2(strengths.shape, 1)
    gate = pg[...]
    gate = gate * sigmoid(gate)
    row, col = iota2((rows_mb, rows_mb), 0), iota2((rows_mb, rows_mb), 1)
    systems = [(h, b) for h in range(PAIR) for b in range(blocks)]
    qs, ks, vs, bs, sames, lows = [], [], [], [], [], []
    for h, b in systems:
        rs = slice(b * rows_mb, (b + 1) * rows_mb)
        hs = slice(h * HEAD_DIM, (h + 1) * HEAD_DIM)
        q, _ = l2_norm(cq[rs, hs])
        k, _ = l2_norm(ck[rs, hs])
        qs.append(q * HEAD_DIM ** (-0.5))
        ks.append(k)
        vs.append(cv[rs, hs])
        bs.append(
            jnp.sum(jnp.where(lane == step * PAIR + h, strengths, 0.0), axis=1, keepdims=True)[rs]
        )
        sames.append(segc[rs, :] == segr[:, rs])
    for i in range(len(systems)):
        lows.append(jnp.where(sames[i] & (row > col), mm(ks[i], ks[i], 1, 1), 0.0))
    inverses = unit_lower_inverses([l * b for l, b in zip(lows, bs)], rows_mb)
    us = [mm(a, v * b, 1, 0) for a, v, b in zip(inverses, vs, bs)]
    ps = [
        jnp.where(same & (row >= col), mm(q, k, 1, 1), 0.0)
        for q, k, same in zip(qs, ks, sames)
    ]
    os = [mm(p, u, 1, 0) for p, u in zip(ps, us)]
    for i, (h, b) in enumerate(systems):
        rs = slice(b * rows_mb, (b + 1) * rows_mb)
        hs = slice(h * HEAD_DIM, (h + 1) * HEAD_DIM)
        o = os[i]
        inv = lax.rsqrt(jnp.mean(o * o, axis=-1, keepdims=True) + 1e-05)
        on_ref[rs, hs] = (o * inv * gain[...] * gate[rs, hs]).astype(BF16)
        o_ref[rs, hs] = o
        ainv_ref[h, b] = inverses[i]
        u_ref[h, b] = us[i]
        p_ref[h, b] = ps[i]
        l_ref[h, b] = lows[i]


def mixer_bwd_kernel(
    blocks, rows_mb, step,
    pq, pk, pv, pg, beta, tq, tk, tv, gain, mask, segc, segr,
    don_ref, o_ref, ainv_ref, u_ref, p_ref, l_ref,
    dq_ref, dk_ref, dv_ref, dg_ref, dbeta_ref, dtq, dtk, dtv, dgain_ref,
):
    rows = blocks * rows_mb
    masks = [None] + [mask[:, s : s + 1] for s in range(1, CONV)]
    pres, rolls, cs, sig = [], [], [], []
    for src, taps in ((pq, tq), (pk, tk), (pv, tv)):
        pre, rolled = conv_parts(src[...], taps[...], masks)
        s = sigmoid(pre)
        pres.append(pre)
        rolls.append(rolled)
        sig.append(s)
        cs.append(pre * s)
    cq, ck, cv = cs
    strengths = sigmoid(beta[...])
    lane = iota2(strengths.shape, 1)
    row, col = iota2((rows_mb, rows_mb), 0), iota2((rows_mb, rows_mb), 1)
    gates = pg[...]
    gsig = sigmoid(gates)
    gate = gates * gsig
    dgate = gsig * (1.0 + gates * (1.0 - gsig))
    systems = [(h, b) for h in range(PAIR) for b in range(blocks)]
    part = []
    dgain = jnp.zeros((1, HEAD_DIM), F32)
    for h, b in systems:
        rs = slice(b * rows_mb, (b + 1) * rows_mb)
        hs = slice(h * HEAD_DIM, (h + 1) * HEAD_DIM)
        k, ik = l2_norm(ck[rs, hs])
        qn, iq = l2_norm(cq[rs, hs])
        v = cv[rs, hs]
        bb = jnp.sum(jnp.where(lane == step * PAIR + h, strengths, 0.0), axis=1, keepdims=True)[rs]
        same = segc[rs, :] == segr[:, rs]
        o = o_ref[rs, hs]
        don = don_ref[rs, hs]
        inv = lax.rsqrt(jnp.mean(o * o, axis=-1, keepdims=True) + 1e-05)
        no = o * inv
        scaled = don * gain[...]
        dg_ref[rs, hs] = (scaled * no * dgate[rs, hs]).astype(BF16)
        dgain = dgain + jnp.sum(don * no * gate[rs, hs], axis=0, keepdims=True)
        dno = scaled * gate[rs, hs]
        do = inv * (dno - no * jnp.mean(no * dno, axis=-1, keepdims=True))
        part.append([q_ for q_ in (qn, iq, k, ik, v, bb, same, do)])
    dus = [mm(p_ref[h, b], part[i][7], 0, 0) for i, (h, b) in enumerate(systems)]
    dps = [
        jnp.where(part[i][6] & (row >= col), mm(part[i][7], u_ref[h, b], 1, 1), 0.0)
        for i, (h, b) in enumerate(systems)
    ]
    drs = [mm(ainv_ref[h, b], dus[i], 0, 0) for i, (h, b) in enumerate(systems)]
    scale = HEAD_DIM ** (-0.5)
    dqs = [mm(dps[i], part[i][2], 1, 0) * scale for i in range(len(systems))]
    das = [mm(drs[i], u_ref[h, b], 1, 1) for i, (h, b) in enumerate(systems)]
    dks = [mm(dps[i], part[i][0] * scale, 0, 0) for i in range(len(systems))]
    dgs = []
    for i in range(len(systems)):
        g = jnp.where(part[i][6] & (row > col), das[i] * (-part[i][5]), 0.0)
        dgs.append(g + g.T)
    dks = [dks[i] + mm(dgs[i], part[i][2], 1, 0) for i in range(len(systems))]
    dbeta = jnp.zeros(strengths.shape, F32)
    dcs = [[], [], []]
    for i, (h, b) in enumerate(systems):
        qn, iq, k, ik, v, bb, same, do = part[i]
        dv = drs[i] * bb
        db = jnp.sum(drs[i] * v - das[i] * l_ref[h, b], axis=-1, keepdims=True)
        dbp = db * bb * (1.0 - bb)
        pieces = [dbp if b == c else jnp.zeros((rows_mb, 1), F32) for c in range(blocks)]
        column = jnp.concatenate(pieces, axis=0) if blocks > 1 else dbp
        dbeta = dbeta + jnp.where(lane == step * PAIR + h, column, 0.0)
        dcs[0].append(iq * (dqs[i] - qn * jnp.sum(qn * dqs[i], axis=-1, keepdims=True)))
        dcs[1].append(ik * (dks[i] - k * jnp.sum(k * dks[i], axis=-1, keepdims=True)))
        dcs[2].append(dv)
    for j, (out, dtap, taps) in enumerate(((dq_ref, dtq, tq), (dk_ref, dtk, tk), (dv_ref, dtv, tv))):
        whole = jnp.concatenate(
            [
                jnp.concatenate([dcs[j][h * blocks + b] for b in range(blocks)], axis=0)
                for h in range(PAIR)
            ],
            axis=1,
        )
        dpre = whole * (sig[j] * (1.0 + pres[j] * (1.0 - sig[j])))
        tap = taps[...]
        grad = dpre * tap[CONV - 1 : CONV, :]
        dtap[CONV - 1 : CONV, :] = jnp.sum(dpre * rolls[j][0], axis=0, keepdims=True)
        for s in range(1, CONV):
            dtap[CONV - 1 - s : CONV - s, :] = jnp.sum(dpre * rolls[j][s], axis=0, keepdims=True)
            grad = grad + pltpu.roll(dpre * masks[s], rows - s, 0) * tap[CONV - 1 - s : CONV - s, :]
        out[...] = grad.astype(BF16)

    @pl.when(step == 0)
    def _():
        dbeta_ref[...] = jnp.zeros_like(dbeta_ref)
        dgain_ref[...] = jnp.zeros_like(dgain_ref)

    dbeta_ref[...] += dbeta
    dgain_ref[...] += dgain


def mixer_specs(rows, blocks, rows_mb):
    width = PAIR * HEAD_DIM
    per = D // width
    col = lambda k: pl.BlockSpec((rows, width), lambda i, k=k: (0, k * per + i))
    tap = lambda k: pl.BlockSpec((CONV, width), lambda i, k=k: (0, k * per + i))
    full = lambda shape: pl.BlockSpec(shape, lambda i: (0,) * len(shape))
    ins = [col(0), col(1), col(2), col(3), full((rows, HEADS)), tap(0), tap(1), tap(2),
           full((1, HEAD_DIM)), full((rows, 8)), full((rows, 1)), full((1, rows))]
    mat = pl.BlockSpec((PAIR, blocks, rows_mb, rows_mb), lambda i: (i, 0, 0, 0))
    one = pl.BlockSpec((rows, width), lambda i: (0, i))
    otap = pl.BlockSpec((CONV, width), lambda i: (0, i))
    return ins, mat, one, otap, full


def lin_index():
    return lax.axis_index("dp") * lax.axis_size("fsdp") + lax.axis_index("fsdp")


def mesh_id(index):
    inner = lax.axis_size("fsdp")
    return (lax.div(index, inner), lax.rem(index, inner))


class Here:
    def __init__(self, shards):
        self.shards, self.me = shards, lin_index()
        self.bits = shards.bit_length() - 1
        own = [lax.rem(lax.div(self.me, 1 << b), 2) for b in range(self.bits)]
        self.core = own[0]
        self.change = [(1 - 2 * o) * (1 << b) for b, o in enumerate(own)]
        self.partner = [mesh_id(self.me + c) for c in self.change]

    def flip(self, bits, number, always=()):
        result = self.me
        for bit in always:
            result = result + self.change[bit]
        for i, bit in enumerate(reversed(bits)):
            if isinstance(number, int):
                if (number >> i) & 1:
                    result = result + self.change[bit]
            else:
                result = result + lax.rem(lax.div(number, 1 << i), 2) * self.change[bit]
        return result


def routes(shards):
    bits = shards.bit_length() - 1
    rest = list(range(4, bits))
    return [[1, 2, 3] + rest, [2, 3, 1] + rest, [3, 1, 2] + rest]


def colours(width, turn):
    tiles = width // 128
    one, three = round(tiles * 0.36), round(tiles * 0.28)
    sizes = (one, tiles - one - three, three)
    return [(sum(sizes[:c]) * 128, sizes[c] * 128) for c in range(3)]


def meet(here, everyone):
    barrier = pltpu.get_barrier_semaphore()
    if everyone:

        def greet(r, _):
            peer = lax.rem(here.me + r, here.shards)
            pl.semaphore_signal(barrier, inc=1, device_id=mesh_id(peer), device_id_type=MESH)
            return 0

        lax.fori_loop(1, here.shards, greet, 0)
        pl.semaphore_wait(barrier, here.shards - 1)
    else:
        for partner in here.partner:
            pl.semaphore_signal(barrier, inc=1, device_id=partner, device_id_type=MESH)
        pl.semaphore_wait(barrier, here.bits)


def spread_order(shards):
    bits = shards.bit_length() - 1
    turned = [sum(((i >> b) & 1) << (bits - 1 - b) for b in range(bits)) for i in range(shards)]
    return turned[1:]


class Exchange:
    def __init__(self, here, sent, got, send, recv, keep, same=False):
        self.here, self.shards, self.me, self.got = here, here.shards, here.me, got
        self.block = (lambda d: sent) if same else (lambda d: sent.at[d])
        self.send, self.recv, self.keep = send, recv, keep

    def own(self):
        return pltpu.make_async_copy(self.block(self.me), self.got.at[self.me], self.keep)

    def start(self):
        self.own().start()

        def one(r, _):
            peer = lax.rem(self.me + r, self.shards)
            pltpu.make_async_remote_copy(
                src_ref=self.block(peer), dst_ref=self.got.at[self.me], send_sem=self.send,
                recv_sem=self.recv, device_id=mesh_id(peer), device_id_type=MESH,
            ).start()
            return 0

        lax.fori_loop(1, self.shards, one, 0)

    def start_part(self, part, parts):
        others = self.shards - 1
        if part == 0:
            self.own().start()
        for r in range(others * part // parts, others * (part + 1) // parts):
            peer = lax.rem(self.me + spread_order(self.shards)[r], self.shards)
            pltpu.make_async_remote_copy(
                src_ref=self.block(peer), dst_ref=self.got.at[self.me], send_sem=self.send,
                recv_sem=self.recv, device_id=mesh_id(peer), device_id_type=MESH,
            ).start()

    def wait(self):
        self.own().wait()
        whole = pl.ds(0, self.shards - 1)
        pltpu.make_async_remote_copy(
            src_ref=self.got.at[whole], dst_ref=self.got.at[whole], send_sem=self.send,
            recv_sem=self.recv, device_id=self.here.partner[0], device_id_type=MESH,
        ).wait()


DEAL_AT = 0
CHUNK = 256
X_STEPS = 5
GT_FROM = 6


def pieces_of(widths, split):
    result = []
    for i, width in enumerate(widths):
        tiles, at = width // 128, 0
        for j in range(split[i]):
            size = tiles // split[i] + (1 if j < tiles % split[i] else 0)
            result.append((i, at * 128, size * 128))
            at += size
    return result


class Gather:
    def __init__(self, here, pieces, own, full, sems):
        self.here, self.pieces, self.own, self.full = here, pieces, own, full
        self.send, self.recv, self.pair_send, self.pair_recv, self.keep = sems
        self.stages = here.bits - 1
        self.order = routes(here.shards)
        self.core = here.core
        self.cuts = [
            [(at + a, s) for a, s in colours(size, n)] for n, (_, at, size) in enumerate(pieces)
        ]
        self.last = len(pieces) + self.stages - 1

    @staticmethod
    def semaphores(shards, pieces):
        dma, stages = pltpu.SemaphoreType.DMA, shards.bit_length() - 2
        number = len(pieces)
        return [dma((stages, number, 3)), dma((stages, number, 3)), dma((number,)), dma((number,)),
                dma((number,))]

    def kept(self, i):
        return pltpu.make_async_copy(
            self.own[i], self.full[i].at[lax.div(self.here.me, 2), self.core], self.keep.at[i]
        )

    def begin(self):
        for i in range(len(self.own)):
            self.kept(i).start()

    def partner(self, k, c):
        return self.here.partner[self.order[c][self.stages - 1 - k]]

    def group(self, k, n, c):
        at, size = self.cuts[n][c]
        some = self.full[self.pieces[n][0]].at[pl.ds(0, 1 << k), 0, :, pl.ds(at, size)]
        return pltpu.make_async_remote_copy(
            src_ref=some, dst_ref=some, send_sem=self.send.at[k, n, c],
            recv_sem=self.recv.at[k, n, c], device_id=self.partner(k, c), device_id_type=MESH,
        )

    def half(self, n):
        i, at, size = self.pieces[n]
        some = self.full[i].at[:, self.core, :, pl.ds(at, size)]
        return pltpu.make_async_remote_copy(
            src_ref=some, dst_ref=some, send_sem=self.pair_send.at[n],
            recv_sem=self.pair_recv.at[n], device_id=self.here.partner[0],
            device_id_type=MESH,
        )

    def launch(self, k, n):
        i = self.pieces[n][0]
        for c in range(3):
            at, size = self.cuts[n][c]
            if k > 0:
                self.group(k - 1, n, c).wait_recv()
            have = self.order[c][self.stages - k :]
            for j in range(1 << k):
                d = self.here.flip(have, j)
                there = self.full[i].at[lax.div(d, 2), self.core, :, pl.ds(at, size)]
                pltpu.make_async_remote_copy(
                    src_ref=self.own[i].at[:, pl.ds(at, size)] if j == 0 else there,
                    dst_ref=there, send_sem=self.send.at[k, n, c], recv_sem=self.recv.at[k, n, c],
                    device_id=self.partner(k, c), device_id_type=MESH,
                ).start()

    def finish(self, n):
        for c in range(3):
            self.group(self.stages - 1, n, c).wait_recv()
        if n == 0 or self.pieces[n - 1][0] != self.pieces[n][0]:
            self.kept(self.pieces[n][0]).wait()
        self.half(n).start()

    def slots(self, first, last):
        return sum(
            0 <= t - n <= self.stages for t in range(first, last) for n in range(len(self.pieces))
        )

    def step(self, t, between=None):
        for n in range(len(self.pieces)):
            k = t - n
            if 0 <= k < self.stages:
                self.launch(k, n)
            elif k == self.stages:
                self.finish(n)
            if between is not None and 0 <= k <= self.stages:
                between()

    def end(self, arrived=0):
        for k in range(self.stages):
            for n in range(len(self.pieces)):
                for c in range(3):
                    self.group(k, n, c).wait_send()
        for n in range(len(self.pieces)):
            self.half(n).wait_send()
            if n >= arrived:
                self.half(n).wait_recv()


def first_kernel(shards, pieces, *refs):
    count = 1 + max(i for i, _, _ in pieces)
    own, sent, full, got = refs[:count], refs[count], refs[count + 1 : 2 * count + 1], refs[2 * count + 1]
    sems = refs[2 * count + 2 :]
    here = Here(shards)
    deal = Exchange(here, sent, got, *sems[5:])
    weights = Gather(here, pieces, own, full, sems[:5])
    weights.begin()
    meet(here, True)
    deal.start()
    for t in range(weights.last + 1):
        weights.step(t)
    deal.wait()
    weights.end()


def spread(weight, shards):
    return jax.ShapeDtypeStruct((shards // 2, 2) + weight.shape, weight.dtype)


def first(weights, split, message, shards, collective_id):
    count = len(weights)
    anywhere = pl.BlockSpec(memory_space=pl.ANY)
    pieces = pieces_of([w.shape[1] for w in weights], split)
    dma = pltpu.SemaphoreType.DMA
    *full, got = pl.pallas_call(
        functools.partial(first_kernel, shards, pieces),
        in_specs=[anywhere] * (count + 1),
        out_specs=[anywhere] * (count + 1),
        out_shape=[spread(w, shards) for w in weights]
        + [jax.ShapeDtypeStruct(message.shape, message.dtype)],
        scratch_shapes=Gather.semaphores(shards, pieces) + [dma, dma, dma],
        compiler_params=pltpu.CompilerParams(collective_id=collective_id, has_side_effects=True),
        name="gather_first",
    )(*weights, message)
    return [f.reshape(-1, f.shape[-1]) for f in full], got


def forward_kernel(
    shards, pieces, blocks, rows_mb,
    own_down, own_gu, sent, a1, wq, wk, wv, wg, wout, wbeta, x, gain_two, tq, tk, tv, gain, mask,
    segc, segr,
    full_down, full_gu, got, pq, pk, pv, pg, beta, on, o, ainv, u, p, l, resid, a2,
    *sems,
):
    step = pl.program_id(0)
    steps = HEADS // PAIR
    here = Here(shards)
    weights = Gather(here, pieces, (own_down, own_gu), (full_down, full_gu), sems[:5])
    deal = Exchange(here, sent, got, *sems[5:])

    @pl.when(step == 0)
    def _():
        weights.begin()
        meet(here, True)
        weights.step(0)
        resid[...] = x[...]

    normed = a1[...]
    beta[...] = jnp.dot(normed, wbeta[...], preferred_element_type=F32)
    for out, w in ((pq, wq), (pk, wk), (pv, wv), (pg, wg)):
        out[...] = jnp.dot(normed, w[...], preferred_element_type=F32)
    mixer_fwd_kernel(
        blocks, rows_mb, pq, pk, pv, pg, beta, tq, tk, tv, gain, mask, segc, segr, on, o, ainv, u,
        p, l,
    )
    resid[...] += jnp.dot(on[...], wout[...], preferred_element_type=F32)
    for s in range(steps):

        @pl.when(step == s)
        def _(s=s):
            weights.step(s + 1)
            if s == DEAL_AT:
                deal.start()
            if s == steps - 1:
                r = resid[...]
                a2[...] = (rms(r)[0] * gain_two[...]).astype(BF16)
                for t in range(steps + 1, weights.last + 1):
                    weights.step(t)
                deal.wait()
                weights.end()


def forward(
    w_down, w_gu, message, split, a1, win, wout, wbeta, x, gain_two, taps, gain, mask, segc, segr, blocks,
    shards, collective_id,
):
    rows = x.shape[0]
    rows_mb = rows // blocks
    width = PAIR * HEAD_DIM
    pieces = pieces_of([w_down.shape[1], w_gu.shape[1]], split)
    anywhere = pl.BlockSpec(memory_space=pl.ANY)
    ins, mat, one, _, full = mixer_specs(rows, blocks, rows_mb)
    per = D // width
    wcol = lambda k: pl.BlockSpec((D, width), lambda i, k=k: (0, k * per + i))
    square = jax.ShapeDtypeStruct((HEADS, blocks, rows_mb, rows_mb), F32)
    wide = jax.ShapeDtypeStruct((rows, D), F32)
    dma = pltpu.SemaphoreType.DMA
    full_down, full_gu, got, *rest = pl.pallas_call(
        functools.partial(forward_kernel, shards, pieces, blocks, rows_mb),
        grid=(HEADS // PAIR,),
        in_specs=[
            anywhere, anywhere, anywhere, full((rows, D)), wcol(0), wcol(1), wcol(2), wcol(3),
            pl.BlockSpec((width, D), lambda i: (i, 0)), full((D, HEADS)), full((rows, D)),
            full((1, D)), *ins[5:],
        ],
        out_specs=[anywhere, anywhere, anywhere, one, one, one, one, full((rows, HEADS)), one, one, mat, mat,
                   mat, mat, full((rows, D)), full((rows, D))],
        out_shape=[
            spread(w_down, shards), spread(w_gu, shards),
            jax.ShapeDtypeStruct(message.shape, message.dtype), wide, wide, wide, wide,
            jax.ShapeDtypeStruct((rows, HEADS), F32), jax.ShapeDtypeStruct((rows, D), BF16), wide,
            square, square, square, square, wide, jax.ShapeDtypeStruct((rows, D), BF16),
        ],
        scratch_shapes=Gather.semaphores(shards, pieces) + [dma, dma, dma],
        compiler_params=pltpu.CompilerParams(
            collective_id=collective_id, has_side_effects=True, vmem_limit_bytes=48 << 20
        ),
        name="mixer_forward",
    )(w_down, w_gu, message, a1, win, win, win, win, wout, wbeta, x, gain_two, taps, taps, taps, gain, mask,
      segc, segr)
    return full_down.reshape(FF, D), full_gu.reshape(D, 2 * FF), got, rest


class Scatter:
    def __init__(self, here, pieces, whole, mine, other, coming, sems, kept):
        self.here, self.pieces, self.whole, self.mine = here, pieces, whole, mine
        self.other, self.coming, self.kept_of = other, coming, kept
        self.send, self.recv, self.pair_send, self.pair_recv = sems
        self.stages = here.bits - 1
        self.order = routes(here.shards)
        self.core = here.core
        self.cuts = [
            [(at + a, s) for a, s in colours(size, n)] for n, (_, at, size) in enumerate(pieces)
        ]

    @staticmethod
    def semaphores(shards, number):
        dma, stages = pltpu.SemaphoreType.DMA, shards.bit_length() - 2
        return [dma((stages, number, 3)), dma((stages, number, 3)), dma((number,)), dma((number,))]

    @staticmethod
    def buffers(shards, shapes):
        stages = shards.bit_length() - 2
        return [pltpu.VMEM((shards // 2,) + s, BF16) for s in shapes] + [
            pltpu.VMEM((1 << (stages - 1 - k),) + s, BF16) for s in shapes for k in range(stages)
        ]

    @staticmethod
    def split(shards, count, refs):
        stages = shards.bit_length() - 2
        other, refs = refs[:count], refs[count:]
        return other, [refs[i * stages : (i + 1) * stages] for i in range(count)]

    def pair(self, n):
        i, at, size = self.pieces[n]
        return pltpu.make_async_remote_copy(
            src_ref=self.whole(n, 1 - self.core), dst_ref=self.other[i].at[:, :, pl.ds(at, size)],
            send_sem=self.pair_send.at[n], recv_sem=self.pair_recv.at[n],
            device_id=self.here.partner[0], device_id_type=MESH,
        )

    def hop(self, k, n, c, source, spots):
        i = self.pieces[n][0]
        at, size = self.cuts[n][c]
        cols = pl.ds(at, size)
        return pltpu.make_async_remote_copy(
            src_ref=self.other[i].at[source, :, cols],
            dst_ref=self.coming[i][k].at[spots, :, cols],
            send_sem=self.send.at[k, n, c], recv_sem=self.recv.at[k, n, c],
            device_id=self.here.partner[self.order[c][k]], device_id_type=MESH,
        )

    def group(self, k, n, c):
        all_of = pl.ds(0, 1 << (self.stages - 1 - k))
        return self.hop(k, n, c, all_of, all_of)

    def total(self, k, n, c, shard, spot):
        i = self.pieces[n][0]
        at, size = self.cuts[n][c]
        cols = pl.ds(at, size)
        q = lax.div(shard, 2)
        value = self.mine(i, q, cols).astype(F32) + self.other[i][q, :, cols].astype(F32)
        for p in range(k):
            value = value + self.coming[i][p][spot, :, cols].astype(F32)
        return value

    def launch(self, k, n):
        if k == 0:
            kept = self.kept_of(n)
            if kept is not None:
                kept.wait()
            self.pair(n).wait_recv()
        for c in range(3):
            if k > 0:
                self.group(k - 1, n, c).wait_recv()
            much = 1 << (self.stages - 1 - k)
            at, size = self.cuts[n][c]

            def body(j, _, c=c, at=at, size=size):
                shard = self.here.flip(self.order[c][k + 1 :], j, (self.order[c][k],))
                q = lax.div(shard, 2)
                self.other[self.pieces[n][0]][q, :, pl.ds(at, size)] = self.total(
                    k, n, c, shard, much + j
                ).astype(BF16)
                self.hop(k, n, c, q, j).start()
                return 0

            lax.fori_loop(0, much, body, 0)

    def finish(self, n, write):
        for c in range(3):
            self.group(self.stages - 1, n, c).wait_recv()
            at, size = self.cuts[n][c]
            write(self.pieces[n][0], at, size, self.total(self.stages, n, c, self.here.me, 0))

    def end(self, n):
        for k in range(self.stages):
            for c in range(3):
                self.group(k, n, c).wait_send()
        self.pair(n).wait_send()


def front_kernel(shards, blocks, rows_mb, split, *refs):
    (own_in, own_out, own_down, own_gu, small, tokens, later_rows, deal_row, valid_row, lengths, gain), refs = refs[:11], refs[11:]
    (full_in, full_out, full_down, full_gu, pq, pk, pv, pg, beta, on, o, ainv, u, p, l, resid, a2, x, info, gt, taps,
     gain_one, gain_two, wbeta, segc, segr, mask, a1), refs = refs[:28], refs[28:]
    (sent, got, sent_gt, got_gt, got_small, wbuf, wout, deal, w_sem, out_sem), refs = refs[:10], refs[10:]
    sems, deal_sems, later_sems, small_sems = refs[:5], refs[5:8], refs[8:11], refs[11:14]
    step = pl.program_id(0)
    steps = HEADS // PAIR
    width = PAIR * HEAD_DIM
    rows = blocks * rows_mb
    share = rows // shards
    here = Here(shards)
    pieces = pieces_of([4 * D, D, D, 2 * FF], split)
    weights = Gather(here, pieces, (own_in, own_out, own_down, own_gu), (full_in, full_out, full_down, full_gu), sems)
    first_send = Exchange(here, sent, got, *deal_sems)
    second_send = Exchange(here, sent_gt, got_gt, *later_sems)
    small_send = Exchange(here, small, got_small, *small_sems, same=True)
    of_in = split[0]
    hidden_from = len(pieces) + weights.stages - steps
    deal_to, later_from = X_STEPS, GT_FROM

    def trickle(exchange, first, last):
        parts, done = weights.slots(first, last), [0]

        def at(t):
            if not first <= t < last:
                return None
            done[0] = weights.slots(first, t)

            def one():
                exchange.start_part(done[0], parts)
                done[0] += 1

            return one

        return at

    deal_some = trickle(first_send, 1, deal_to)
    later_some = trickle(second_send, later_from, weights.last + 1)

    def between(t):
        acts = [f for f in (deal_some(t), later_some(t)) if f is not None]
        return (lambda: [f() for f in acts]) if acts else None

    def fetch(s, g):
        return pltpu.make_async_copy(
            full_in.at[:, :, :, pl.ds(g * D + s * width, width)], wbuf.at[s % 2, g], w_sem.at[s % 2, g]
        )

    def fetch_out():
        return pltpu.make_async_copy(full_out, wout, out_sem)

    @pl.when(step == 0)
    def _():
        weights.begin()
        meet(here, True)
        weights.step(0)
        small_send.start()
        row, col = iota2((rows, rows), 0), iota2((rows, rows), 1)
        column = lambda v: jnp.sum(jnp.where(row == col, v, 0.0), axis=1, keepdims=True)
        dealt = deal_row[...].astype(F32)
        target = jnp.floor((dealt + 0.5) * (1.0 / rows))
        valid = valid_row[...].astype(F32)
        target_c = column(target)
        rank = jnp.sum(jnp.where((target == target_c) & (col < row), 1.0, 0.0), axis=1, keepdims=True)
        slot = target_c * share + rank
        sort_t = (slot == col.astype(F32)).astype(BF16)
        lane = iota2((rows, 128), 1)
        notes = jnp.where(
            lane == 0, column(valid),
            jnp.where(lane == 1, column(dealt - target * rows), jnp.where(lane == 2, jnp.sum(valid), 0.0)),
        ).astype(BF16)
        sent[:, :, :D] = tn(sort_t, tokens[...]).reshape(shards, share, D).astype(BF16)
        sent[:, :, D:] = tn(sort_t, notes).reshape(shards, share, 128).astype(BF16)
        weights.step(1, between(1))
        half = later_rows.shape[1] // 2
        for at in (0, half):
            sent_gt[:, :, at : at + half] = (
                tn(sort_t, later_rows[:, at : at + half]).reshape(shards, share, half).astype(BF16)
            )
        weights.step(2, between(2))
        at_row, at_col = iota2((rows, 1), 0), iota2((1, rows), 1)
        seg_c, seg_r = jnp.zeros((rows, 1), F32), jnp.zeros((1, rows), F32)
        lens = lengths[...].astype(F32)
        for b in range(blocks):
            end = jnp.zeros((1, 1), F32) + b * rows_mb
            for i in range(lengths.shape[1]):
                seg_c = seg_c + jnp.where(at_row >= b * rows_mb, 1.0, 0.0) * (i == 0)
                seg_r = seg_r + jnp.where(at_col >= b * rows_mb, 1.0, 0.0) * (i == 0)
                end = end + lens[b : b + 1, i : i + 1]
                if i < lengths.shape[1] - 1:
                    seg_c = seg_c + jnp.where(at_row.astype(F32) >= end, 1.0, 0.0)
                    seg_r = seg_r + jnp.where(at_col.astype(F32) >= end, 1.0, 0.0)
        segc[...] = seg_c.astype(jnp.int32)
        segr[...] = seg_r.astype(jnp.int32)
        lane8 = iota2((rows, 8), 1)
        wide = jnp.broadcast_to(seg_c, (rows, 128))
        marks = jnp.where(lane8 == 0, 1.0, 0.0)
        for s in range(1, CONV):
            before = pltpu.roll(wide, s, 0)[:, :1]
            same = jnp.where((before == seg_c) & (at_row >= s), 1.0, 0.0)
            marks = marks + jnp.where(lane8 == s, same, 0.0)
        mask[...] = marks
        small_send.wait()
        own_taps, own_gain = 3 * D // shards, D // shards
        per = 128 // own_gain
        a, c = iota2((per * 128, per * own_taps), 0), iota2((per * 128, per * own_taps), 1)
        pick_taps = ((a // 128 == c // own_taps) & (a % 128 == c % own_taps)).astype(BF16)
        a, c = iota2((per * 128, 128), 0), iota2((per * 128, 128), 1)
        pick_gain = ((a // 128 == c // own_gain) & (a % 128 == c % own_gain)).astype(BF16)
        for g in range(shards // per):
            left = jnp.concatenate([got_small[g * per + i, :, :128].astype(F32) for i in range(per)], axis=1).astype(BF16)
            right = jnp.concatenate([got_small[g * per + i, :, 128:].astype(F32) for i in range(per)], axis=1).astype(BF16)
            tap = nn(left, pick_taps)
            taps[:, g * per * own_taps : (g + 1) * per * own_taps] = tap[:CONV]
            gains = nn(left, pick_gain)
            gain_one[:, g * 128 : (g + 1) * 128] = gains[4:5]
            gain_two[:, g * 128 : (g + 1) * 128] = gains[5:6]
            wbeta[:, g * 128 : (g + 1) * 128] = nn(right, pick_gain).astype(BF16)
        for t in range(3, hidden_from):
            weights.step(t, between(t))
        first_send.wait()
        flat = got[...].astype(F32).reshape(rows, D + 128)
        notes = flat[:, D:]
        info[...] = notes
        deal[...] = (notes[:, 1:2] == col.astype(F32)).astype(BF16)
        x_now = tn(deal[...], flat[:, :D].astype(BF16))
        x[...] = x_now
        a1[...] = (rms(x_now)[0] * gain_one[...]).astype(BF16)
        beta[...] = nt(a1[...], wbeta[...])
        for n in range(of_in):
            weights.half(n).wait_recv()
        for g in range(4):
            fetch(0, g).start()

    for s in range(steps):

        @pl.when(step == s)
        def _(s=s):
            for g in range(4):
                fetch(s, g).wait()
            if s + 1 < steps:
                for g in range(4):
                    fetch(s + 1, g).start()

    slot_now = lax.rem(step, 2)
    for g, out in enumerate((pq, pk, pv, pg)):
        out[...] = nn(a1[...], wbuf[slot_now, g].reshape(D, width))
    here_cols = pl.ds(pl.multiple_of(step * width, width), width)
    taps_of = lambda j: taps.at[:, pl.ds(pl.multiple_of(j * D + step * width, width), width)]
    mixer_fwd_kernel(
        blocks, rows_mb, pq, pk, pv, pg, beta, taps_of(0), taps_of(1), taps_of(2), gain, mask, segc, segr,
        on.at[:, here_cols], o, ainv, u, p, l,
    )
    for s in range(steps):

        @pl.when(step == s)
        def _(s=s):
            weights.step(hidden_from + s, between(hidden_from + s))
            if s == steps - 1:
                for n in range(of_in, of_in + split[1]):
                    weights.half(n).wait_recv()
                fetch_out().start()
                second_send.wait()
                gt[...] = tn(deal[...], got_gt[...].astype(F32).reshape(rows, gt.shape[1]).astype(BF16))
                fetch_out().wait()
                r = x[...] + nn(on[...], wout[...].reshape(D, D))
                resid[...] = r
                a2[...] = (rms(r)[0] * gain_two[...]).astype(BF16)
                weights.end(of_in + split[1])


def front(weights, small, tokens, later_rows, deal_rows, valid_mask, lengths, gain, shards, collective_id):
    rows, blocks = tokens.shape[0], lengths.shape[0]
    rows_mb, share = rows // blocks, rows // shards
    width = PAIR * HEAD_DIM
    split = (2, 1, 1, 2)
    pieces = pieces_of([w.shape[1] for w in weights], split)
    anywhere = pl.BlockSpec(memory_space=pl.ANY)
    _, mat, one, _, full = mixer_specs(rows, blocks, rows_mb)
    f32 = lambda *shape: jax.ShapeDtypeStruct(shape, F32)
    bf = lambda *shape: jax.ShapeDtypeStruct(shape, BF16)
    square = f32(HEADS, blocks, rows_mb, rows_mb)
    wide = f32(rows, D)
    vm, dma = pltpu.VMEM, pltpu.SemaphoreType.DMA
    outs = [
        (spread(w, shards), anywhere) for w in weights
    ] + [(wide, one)] * 4 + [
        (f32(rows, HEADS), full((rows, HEADS))), (bf(rows, D), full((rows, D))), (wide, one),
        (square, mat), (square, mat), (square, mat), (square, mat), (wide, full((rows, D))),
        (bf(rows, D), full((rows, D))), (wide, full((rows, D))), (f32(rows, 128), full((rows, 128))),
        (f32(rows, 2 * D), full((rows, 2 * D))), (f32(CONV, 3 * D), full((CONV, 3 * D))),
        (f32(1, D), full((1, D))), (f32(1, D), full((1, D))), (bf(8, D), full((8, D))),
        (jax.ShapeDtypeStruct((rows, 1), jnp.int32), full((rows, 1))),
        (jax.ShapeDtypeStruct((1, rows), jnp.int32), full((1, rows))), (f32(rows, 8), full((rows, 8))),
        (bf(rows, D), full((rows, D))),
    ]
    return pl.pallas_call(
        functools.partial(front_kernel, shards, blocks, rows_mb, split),
        grid=(HEADS // PAIR,),
        in_specs=[anywhere] * 4 + [
            full(small.shape), full((rows, D)), full((rows, 2 * D)), full((1, rows)), full((1, rows)),
            full(lengths.shape), full((1, HEAD_DIM)),
        ],
        out_specs=[s for _, s in outs],
        out_shape=[s for s, _ in outs],
        scratch_shapes=[
            vm((shards, share, D + 128), BF16), vm((shards, share, D + 128), BF16),
            vm((shards, share, 2 * D), BF16), vm((shards, share, 2 * D), BF16),
            vm((shards,) + small.shape, BF16),
            vm((2, 4, shards // 2, 2, D // shards, width), BF16),
            vm((shards // 2, 2, D // shards, D), BF16), vm((rows, rows), BF16), dma((2, 4)), dma,
        ] + Gather.semaphores(shards, pieces) + [dma] * 9,
        compiler_params=pltpu.CompilerParams(
            collective_id=collective_id, has_side_effects=True, vmem_limit_bytes=58 << 20
        ),
        name="front",
    )(*weights, small, tokens, later_rows, deal_rows[None, :], valid_mask[None, :], lengths, gain)


def backward_kernel(shards, blocks, rows_mb, pieces, *refs):
    (d_down, df, a2, gate, up, wga, wup, wdn, dy, resid, gain_two, wout, wq, wk, wv, wg, a1, on, x,
     gain_one, wbeta, *mixer), refs = refs[:38], refs[38:]
    (g_down, g_gu, dwq, dwk, dwv, dwg, dw_out, d_wbeta, dx, d_two, d_one, dtq, dtk, dtv,
     d_gain), refs = refs[:15], refs[15:]
    (mine_down, d_gu, acc, dresid, dz, don, dpq, dpk, dpv, dpg, dbeta, keep), refs = refs[:12], refs[12:]
    sems, buffers = refs[:4], refs[4:]
    step = pl.program_id(0)
    chunks = FF // CHUNK
    pairs = HEADS // PAIR
    here = Here(shards)
    core = here.core
    other, coming = Scatter.split(shards, 2, buffers)
    r_gu = d_gu.shape[2]

    def whole(n, parity):
        i, at, size = pieces[n]
        if i == 0:
            return d_down.at[:, parity, :, pl.ds(at, size)]
        return d_gu.at[:, parity, :, pl.ds(at, size)]

    def mine(i, q, cols):
        return mine_down[q, :, cols] if i == 0 else d_gu[q, core, :, cols]

    def kept(n):
        if n > 0:
            return None
        return pltpu.make_async_copy(d_down.at[:, core], mine_down, keep)

    net = Scatter(here, pieces, whole, mine, other, coming, sems, kept)

    def write(i, at, size, value):
        if i == 0:
            g_down[:, pl.ds(at, size)] = value
            return
        for tile in range(at // 128, (at + size) // 128):
            chunk, inner = tile * 128 // (2 * CHUNK), tile * 128 % (2 * CHUNK)
            start = chunk * CHUNK + inner if inner < CHUNK else FF + chunk * CHUNK + inner - CHUNK
            g_gu[:, start : start + 128] = value[:, tile * 128 - at : tile * 128 - at + 128]

    @pl.when(step == 0)
    def _():
        kept(0).start()
        meet(here, False)
        net.pair(0).start()
        acc[...] = jnp.zeros_like(acc)

    @pl.when(step < chunks)
    def _():
        dhid = nt(df[...], wdn[...])
        g = gate[...]
        s = sigmoid(g)
        d_gate = (dhid * up[...] * (s * (1.0 + g * (1.0 - s)))).astype(BF16)
        d_up = (dhid * (g * s)).astype(BF16)
        acc[...] += nt(d_gate, wga[...]) + nt(d_up, wup[...])
        for at, part in ((0, d_gate), (CHUNK, d_up)):
            grad = tn(a2[...], part).reshape(shards // 2, 2, r_gu, CHUNK).astype(BF16)
            start = pl.multiple_of(step * (2 * CHUNK) + at, CHUNK)
            d_gu[:, :, :, pl.ds(start, CHUNK)] = grad

    @pl.when(step == chunks - 1)
    def _():
        nr, rr = rms(resid[...])
        da2 = acc[...]
        d_two[...] = jnp.sum(da2 * nr, axis=0, keepdims=True)
        dresid[...] = dy[...] + rms_back(nr, rr, gain_two[...] * da2)
        acc[...] = jnp.zeros_like(acc)
        dz[...] = dresid[...].astype(BF16)

    @pl.when(step >= chunks)
    def _():
        don[...] = nt(dz[...], wout[...])
        mixer_bwd_kernel(
            blocks, rows_mb, step - chunks, *mixer[:12], don, *mixer[12:], dpq, dpk, dpv, dpg, dbeta, dtq,
            dtk, dtv, d_gain,
        )
        for dp, w, out in ((dpq, wq, dwq), (dpk, wk, dwk), (dpv, wv, dwv), (dpg, wg, dwg)):
            acc[...] += nt(dp[...], w[...])
            out[...] = tn(a1[...], dp[...]).astype(BF16)
        dw_out[...] = tn(on[...], dz[...]).astype(BF16)

    @pl.when(step == chunks + pairs - 1)
    def _():
        d_beta = dbeta[...].astype(BF16)
        grad = acc[...] + nt(d_beta, wbeta[...])
        d_wbeta[...] = tn(a1[...], d_beta)
        nx, rx = rms(x[...])
        d_one[...] = jnp.sum(grad * nx, axis=0, keepdims=True)
        dx[...] = (dresid[...] + rms_back(nx, rx, gain_one[...] * grad)).astype(BF16)

    ready = {pieces[n][1] // (2 * CHUNK) + pieces[n][2] // (2 * CHUNK) - 1: n for n in (1, 2)}
    plan = {}
    for s, n in ready.items():
        plan.setdefault(s, []).append((net.pair, n))
    tail = range(chunks - 1, chunks + pairs)
    plan.setdefault(3, []).append((net.launch, 0, 0))
    for place, s in enumerate(tail):
        for n in range(3):
            k = place + 1 - n
            if (k, n) != (0, 0) and 0 <= k < net.stages:
                plan.setdefault(s, []).append((net.launch, k, n))
            elif k == net.stages:
                plan.setdefault(s, []).append((net.finish, n, write))
    last = tail[-1]
    for place in range(len(tail), net.stages + 3):
        for n in range(3):
            k = place + 1 - n
            if 0 <= k < net.stages:
                plan[last].append((net.launch, k, n))
            elif k == net.stages:
                plan[last].append((net.finish, n, write))
    for s, actions in plan.items():

        @pl.when(step == s)
        def _(actions=actions, s=s):
            for act, *args in actions:
                result = act(*args)
                if act == net.pair:
                    result.start()
            if s == last:
                for n in range(3):
                    net.end(n)


def backward(
    d_down, df, a2, gu, wgu, wdown, dy, resid, gain_two, wout, win, a1, on, x, gain_one, wbeta, proj,
    beta_pre, taps, gain, mask, segc, segr, saved, blocks, shards, collective_id,
):
    rows = x.shape[0]
    rows_mb = rows // blocks
    width = PAIR * HEAD_DIM
    chunks, pairs = FF // CHUNK, HEADS // PAIR
    anywhere = pl.BlockSpec(memory_space=pl.ANY)
    full = lambda shape: pl.BlockSpec(shape, lambda s: (0,) * len(shape))
    early = lambda s: jnp.minimum(s, chunks - 1)
    late = lambda s: jnp.maximum(s - chunks, 0)
    lane_e = lambda r, w, off=0: pl.BlockSpec((r, w), lambda s: (0, off + early(s)))
    lane_l = lambda r, w, off=0: pl.BlockSpec((r, w), lambda s: (0, off + late(s)))
    wide_l = lambda off=0: pl.BlockSpec(
        (D, width), lambda s: (0, off + late(s)), pipeline_mode=pl.Buffered(1)
    )
    row_l = lambda r, w: pl.BlockSpec((r, w), lambda s: (late(s), 0))
    mat = pl.BlockSpec(
        (PAIR, blocks, rows_mb, rows_mb), lambda s: (late(s), 0, 0, 0), pipeline_mode=pl.Buffered(1)
    )
    part_l = pl.BlockSpec(
        (rows, width), lambda s: (0, late(s)), pipeline_mode=pl.Buffered(1)
    )
    per = D // width
    tap = lambda k: lane_l(CONV, width, k * per)
    r_down, r_gu = FF // shards, D // shards
    a, b = chunks // 2 * 2 * CHUNK, 2 * FF
    pieces = [(0, 0, D), (1, 0, a), (1, a, b - a)]
    f32 = lambda *shape: jax.ShapeDtypeStruct(shape, F32)
    bf = lambda *shape: jax.ShapeDtypeStruct(shape, BF16)
    square = bf(D, D)
    vm = pltpu.VMEM
    return pl.pallas_call(
        functools.partial(backward_kernel, shards, blocks, rows_mb, pieces),
        grid=(chunks + pairs,),
        in_specs=[
            anywhere, full((rows, D)), full((rows, D)), lane_e(rows, CHUNK),
            lane_e(rows, CHUNK, chunks), lane_e(D, CHUNK), lane_e(D, CHUNK, chunks),
            pl.BlockSpec((CHUNK, D), lambda s: (early(s), 0)), full((rows, D)), full((rows, D)),
            full((1, D)), row_l(width, D), wide_l(), wide_l(per), wide_l(2 * per),
            wide_l(3 * per), full((rows, D)),
            lane_l(rows, width), full((rows, D)), full((1, D)), full((D, HEADS)),
            part_l, part_l, part_l, part_l, full((rows, HEADS)), tap(0), tap(1), tap(2), full((1, HEAD_DIM)), full((rows, 8)),
            full((rows, 1)), full((1, rows)), lane_l(rows, width), mat, mat, mat, mat,
        ],
        out_specs=[
            full((r_down, D)), full((r_gu, 2 * FF)), wide_l(), wide_l(), wide_l(), wide_l(),
            row_l(width, D), full((D, HEADS)), full((rows, D)),
            full((1, D)), full((1, D)), lane_l(CONV, width), lane_l(CONV, width),
            lane_l(CONV, width), full((1, HEAD_DIM)),
        ],
        out_shape=[
            f32(r_down, D), f32(r_gu, 2 * FF), square, square, square, square, square,
            f32(D, HEADS), bf(rows, D), f32(1, D), f32(1, D), f32(CONV, D), f32(CONV, D),
            f32(CONV, D), f32(1, HEAD_DIM),
        ],
        scratch_shapes=[
            vm((shards // 2, r_down, D), BF16), vm((shards // 2, 2, r_gu, 2 * FF), BF16),
            vm((rows, D), F32), vm((rows, D), F32), vm((rows, D), BF16), vm((rows, width), F32),
            vm((rows, width), BF16), vm((rows, width), BF16), vm((rows, width), BF16),
            vm((rows, width), BF16), vm((rows, HEADS), F32),
            pltpu.SemaphoreType.DMA,
        ] + Scatter.semaphores(shards, 3) + Scatter.buffers(shards, [(r_down, D), (r_gu, 2 * FF)]),
        compiler_params=pltpu.CompilerParams(
            collective_id=collective_id, has_side_effects=True, vmem_limit_bytes=60 << 20
        ),
        name="backward",
    )(d_down.reshape(shards // 2, 2, r_down, D), df, a2, gu, gu, wgu, wgu, wdown, dy, resid, gain_two,
      wout, win, win, win, win, a1, on, x, gain_one, wbeta, *proj, beta_pre, taps, taps, taps, gain,
      mask, segc, segr, *saved)


def scatter_kernel(shards, count, *refs):
    grads, sent, out, got = refs[:count], refs[count], refs[count + 1 : 2 * count + 1], refs[2 * count + 1]
    refs = refs[2 * count + 2 :]
    mine, refs = refs[:count], refs[count:]
    sems, (keep, *back_sems), buffers = refs[:4], refs[4:8], refs[8:]
    here = Here(shards)
    core = here.core
    back = Exchange(here, sent, got, *back_sems)
    other, coming = Scatter.split(shards, count, buffers)
    pieces = [(i, 0, g.shape[-1]) for i, g in enumerate(grads)]

    def kept(n):
        return pltpu.make_async_copy(grads[n].at[:, core], mine[n], keep.at[n])

    net = Scatter(
        here, pieces, lambda n, parity: grads[n].at[:, parity],
        lambda i, q, cols: mine[i][q, :, cols], other, coming, sems, kept,
    )

    def write(i, at, size, value):
        out[i][:, pl.ds(at, size)] = value

    for n in range(count):
        kept(n).start()
    meet(here, True)
    for n in range(count):
        net.pair(n).start()
    back.start()
    for t in range(count + net.stages):
        for n in range(count):
            k = t - n
            if 0 <= k < net.stages:
                net.launch(k, n)
            elif k == net.stages:
                net.finish(n, write)
    back.wait()
    for n in range(count):
        net.end(n)


def scatter(grads, message, shards, collective_id):
    count = len(grads)
    shapes = [(g.shape[0] // shards, g.shape[1]) for g in grads]
    anywhere = pl.BlockSpec(memory_space=pl.ANY)
    dma = pltpu.SemaphoreType.DMA
    *out, got = pl.pallas_call(
        functools.partial(scatter_kernel, shards, count),
        in_specs=[anywhere] * (count + 1),
        out_specs=[pl.BlockSpec(memory_space=pltpu.VMEM)] * count + [anywhere],
        out_shape=[jax.ShapeDtypeStruct(s, F32) for s in shapes]
        + [jax.ShapeDtypeStruct(message.shape, message.dtype)],
        scratch_shapes=[pltpu.VMEM((shards // 2,) + s, BF16) for s in shapes]
        + Scatter.semaphores(shards, count) + [dma((count,)), dma, dma, dma]
        + Scatter.buffers(shards, shapes),
        compiler_params=pltpu.CompilerParams(
            collective_id=collective_id, has_side_effects=True, vmem_limit_bytes=60 << 20
        ),
        name="scatter_last",
    )(*[g.reshape((shards // 2, 2) + s) for g, s in zip(grads, shapes)], message)
    return out, got


def nt(left, right):
    return lax.dot_general(left, right, (((1,), (1,)), ((), ())), preferred_element_type=F32)


def tn(left, right, dtype=F32):
    return lax.dot_general(left, right, (((0,), (0,)), ((), ())), preferred_element_type=dtype)


def nn(left, right):
    return jnp.dot(left, right, preferred_element_type=F32)


def rms(v):
    inv = lax.rsqrt(jnp.mean(v * v, axis=-1, keepdims=True) + 1e-05)
    return v * inv, inv


def rms_back(normed, inv, dn):
    return inv * (dn - normed * jnp.mean(normed * dn, axis=-1, keepdims=True))


def local(
    tokens, cotangent, teacher, valid_mask, deal_rows, lengths, w_in, w_beta, conv_kernel, w_out,
    norm_gain, out_gain, ffn_gain, w_gu, w_down,
):
    shards = lax.axis_size(AXES)
    rows = tokens.shape[0]
    share = rows // shards
    blocks = lengths.shape[0]
    rows_mb = rows // blocks
    a, b, c = CONV * conv_kernel.shape[1], w_beta.shape[0] * HEADS, norm_gain.shape[0]
    small = w_beta.shape[0] * HEADS + CONV * conv_kernel.shape[1] + 2 * norm_gain.shape[0]

    if share % 8 == 0 and (D // shards) % 16 == 0:
        half = jnp.pad(
            jnp.concatenate([conv_kernel, jnp.pad(jnp.stack([norm_gain, ffn_gain]), ((0, 0), (0, conv_kernel.shape[1] - norm_gain.shape[0])))]),
            ((0, 2), (0, 128 - conv_kernel.shape[1])),
        )
        small_block = jnp.concatenate(
            [half, jnp.pad(w_beta.T, ((0, 0), (0, 128 - w_beta.shape[0])))], axis=1
        )
        gain_out = out_gain.astype(F32)[None, :]
        (win, wout, wdown, wgu, *proj, beta_pre, on, o, ainv, u, p, l, resid, a2, x, info, later, taps,
         gain_one, gain_two, wbeta, segc, segr, mask, a1) = front(
            [w_in, w_out, w_down, w_gu], small_block, tokens, jnp.concatenate([cotangent, teacher], axis=1),
            deal_rows, valid_mask, lengths, gain_out, shards, 0,
        )
        win, wout, wdown, wgu = (w.reshape(-1, w.shape[-1]) for w in (win, wout, wdown, wgu))
        saved = (o, ainv, u, p, l)
        place = info[:, 1].astype(jnp.int32)
        counted = jnp.sum(info[::share, 2])
        g, t = later[:, :D], later[:, D:]
        target = deal_rows // rows
        ahead = (target[None, :] == target[:, None]) & (
            jnp.arange(rows)[None, :] < jnp.arange(rows)[:, None]
        )
        slot = target * share + jnp.sum(ahead.astype(jnp.int32), axis=1)
        sort_t = (slot[:, None] == jnp.arange(rows)[None, :]).astype(BF16)
        deal_t = (place[:, None] == jnp.arange(rows)[None, :]).astype(BF16)
        deal = (place[None, :] == jnp.arange(rows)[:, None]).astype(BF16)
        m = jnp.sum(deal.astype(F32) * info[:, 0][None, :], axis=1, keepdims=True)
        gain_one, gain_two = gain_one[0], gain_two[0]
        wbeta = wbeta.T
    else:
        target = deal_rows // rows
        spot = deal_rows % rows
        ahead = (target[None, :] == target[:, None]) & (
            jnp.arange(rows)[None, :] < jnp.arange(rows)[:, None]
        )
        slot = target * share + jnp.sum(ahead.astype(jnp.int32), axis=1)
        sort_t = (slot[:, None] == jnp.arange(rows)[None, :]).astype(BF16)
        sort = (slot[None, :] == jnp.arange(rows)[:, None]).astype(BF16)
        count_own = jnp.sum(valid_mask.astype(F32))
        lane = jnp.arange(128)[None, :]
        notes = jnp.where(
            lane == 0,
            valid_mask.astype(F32)[:, None],
            jnp.where(lane == 1, spot.astype(F32)[:, None], jnp.where(lane == 2, count_own, 0.0)),
        ).astype(BF16)
        packed = jnp.concatenate(
            [conv_kernel.reshape(-1), w_beta.reshape(-1), norm_gain, ffn_gain,
             jnp.zeros((share * 128 - small,), BF16)]
        ).reshape(1, share, 128)
        sorted_rows = nn(sort, jnp.concatenate([tokens, notes], axis=1)).astype(BF16)
        message = jnp.concatenate(
            [sorted_rows.reshape(shards, share, -1), jnp.broadcast_to(packed, (shards, share, 128))],
            axis=2,
        )
        later = nn(sort, jnp.concatenate([cotangent, teacher], axis=1)).astype(BF16)
        later = later.reshape(shards, share, 2 * D)
        (win, wout), arrived = first([w_in, w_out], (2, 1), message, shards, 0)

        flat = arrived.reshape(rows, -1)
        info = flat[:, D : D + 128].astype(F32)
        place = info[:, 1].astype(jnp.int32)
        counted = jnp.sum(arrived[:, 0, D + 2].astype(F32))
        extra = arrived[:, :, D + 128 :].reshape(shards, share * 128)
        taps = extra[:, :a].reshape(shards, CONV, -1).swapaxes(0, 1).reshape(CONV, 3 * D).astype(F32)
        wbeta = extra[:, a : a + b].reshape(D, HEADS)
        gain_one = extra[:, a + b : a + b + c].reshape(D).astype(F32)
        gain_two = extra[:, a + b + c : a + b + 2 * c].reshape(D).astype(F32)
        deal = (place[None, :] == jnp.arange(rows)[:, None]).astype(BF16)
        deal_t = (place[:, None] == jnp.arange(rows)[None, :]).astype(BF16)
        dealt = nn(deal, flat[:, : D + 128])
        x = dealt[:, :D]
        m = dealt[:, D : D + 1]

        ends = jnp.cumsum(lengths, axis=1)
        within = jnp.arange(rows_mb, dtype=jnp.int32)
        seg = jnp.sum((within[None, :, None] >= ends[:, None, :]).astype(jnp.int32), axis=2)
        seg = (seg + (lengths.shape[1] + 1) * jnp.arange(blocks, dtype=jnp.int32)[:, None]).reshape(rows)
        position = jnp.arange(rows, dtype=jnp.int32)
        mask = jnp.stack(
            [jnp.ones((rows,), F32)]
            + [((position >= s) & (jnp.roll(seg, s) == seg)).astype(F32) for s in range(1, CONV)]
            + [jnp.zeros((rows,), F32)] * (8 - CONV),
            axis=1,
        )
        segc, segr = seg[:, None], seg[None, :]
        gain_out = out_gain.astype(F32)[None, :]

        nx, rx = rms(x)
        a1 = (nx * gain_one).astype(BF16)
        wdown, wgu, later, (*proj, beta_pre, on, o, ainv, u, p, l, resid, a2) = forward(
            w_down, w_gu, later, (1, 2), a1, win, wout, wbeta, x, gain_two[None, :], taps, gain_out, mask, segc,
            segr, blocks, shards, 2,
        )
        saved = (o, ainv, u, p, l)
        later = nn(deal, later.reshape(rows, 2 * D))
        g, t = later[:, :D], later[:, D:]
    gu = nn(a2, wgu)
    gate, up = gu[:, :FF], gu[:, FF:]
    hid = (gate * sigmoid(gate) * up).astype(BF16)
    y = resid + nn(hid, wdown)
    errors = y - t
    loss_part = jnp.sum(m * errors * errors)
    dy = g + (rows * shards / counted) * m * errors
    df = dy.astype(BF16)
    (g_down, g_gu, dwq, dwk, dwv, dwg, dw_out, d_wbeta, dx, d_gain_two, d_gain_one, dtq, dtk, dtv,
     d_gain_out) = backward(
        tn(hid, df, BF16), df, a2, gu, wgu, wdown, dy, resid, gain_two[None, :], wout, win, a1, on, x,
        gain_one[None, :], wbeta, proj, beta_pre, taps, gain_out, mask, segc, segr, saved, blocks, shards,
        1,
    )
    back = jnp.concatenate([y.astype(BF16), dx], axis=1)
    back = nn(deal_t, back).astype(BF16).reshape(shards, share, 2 * D)
    (g_out, *g_in), back = scatter([dw_out, dwq, dwk, dwv, dwg], back, shards, 3)
    g_in = jnp.concatenate(g_in, axis=1)
    back = nn(sort_t, back.reshape(rows, 2 * D)).astype(BF16)
    output, input_grad = back[:, :D], back[:, D:]

    d_taps = jnp.concatenate([dtq, dtk, dtv], axis=1)
    tail = jnp.concatenate([d_gain_out.reshape(-1), loss_part.reshape(1)])
    extra = jnp.concatenate(
        [
            d_taps.reshape(CONV, shards, -1).swapaxes(0, 1).reshape(shards, a),
            d_wbeta.reshape(shards, b),
            d_gain_one.reshape(shards, c),
            d_gain_two.reshape(shards, c),
            jnp.broadcast_to(tail[None], (shards, tail.shape[0])),
        ],
        axis=1,
    )
    padded = -(-extra.shape[1] // 128) * 128
    extra = jnp.pad(extra, ((0, 0), (0, padded - extra.shape[1])))
    summed = jnp.sum(
        lax.all_to_all(
            extra.reshape(shards, padded // 128, 128), AXES, split_axis=0, concat_axis=0, tiled=True
        ),
        axis=0,
    ).reshape(-1)
    g_taps = summed[:a].reshape(CONV, -1)
    g_beta = summed[a : a + b].reshape(-1, HEADS)
    g_gain_one = summed[a + b : a + b + c]
    g_gain_two = summed[a + b + c : a + b + 2 * c]
    g_gain_out = summed[a + b + 2 * c : a + b + 2 * c + HEAD_DIM]
    loss = summed[a + b + 2 * c + HEAD_DIM] / (D * counted)

    return (
        output, input_grad, g_in, g_beta, g_taps, g_out, g_gain_one, g_gain_out, g_gain_two, g_gu,
        g_down, loss,
    )


def solution(mesh):
    both = P(AXES, None)
    flat = P(AXES)
    in_specs = (both, both, both, flat, flat, both, both, both, P(None, AXES), both, flat, P(), flat,
                both, both)
    out_specs = (both, both, both, both, P(None, AXES), both, flat, P(), flat, both, both, P())
    return jax.shard_map(local, mesh=mesh, in_specs=in_specs, out_specs=out_specs, check_vma=False)
```

```python
import functools

import jax
import jax.numpy as jnp
from jax import lax
from jax.experimental import pallas as pl
from jax.experimental.pallas import tpu as pltpu
from jax.sharding import PartitionSpec as P

D = 1024
HEADS = 8
HEAD_DIM = 128
FF = 2816
CONV = 4
AXES = ("dp", "fsdp")
F32 = jnp.float32
BF16 = jnp.bfloat16
PAIR = 2
MESH = pl.DeviceIdType.MESH


def mm(left, right, lc, rc):
    return lax.dot_general(
        left,
        right,
        (((lc,), (rc,)), ((), ())),
        precision=lax.Precision.HIGHEST,
        preferred_element_type=F32,
    )


def sigmoid(v):
    return 1.0 / (1.0 + jnp.exp(-v))


def iota2(shape, axis):
    return lax.broadcasted_iota(jnp.int32, shape, axis)


def unit_lower_inverses(mats, size):
    row, col = iota2((size, size), 0), iota2((size, size), 1)
    eye = (row == col).astype(F32)
    inverses = None
    width = 1
    while width < size:
        corner = ((row // (2 * width)) == (col // (2 * width))) & (
            (row // width) == (col // width) + 1
        )
        edges = [jnp.where(corner, m, 0.0) for m in mats]
        if inverses is None:
            inverses = [eye - e for e in edges]
        else:
            right = [mm(e, x, 1, 0) for e, x in zip(edges, inverses)]
            inverses = [x - mm(x, r, 1, 0) for x, r in zip(inverses, right)]
        width *= 2
    return inverses


def conv_parts(src, taps, masks):
    rolled = [src]
    total = src * taps[CONV - 1 : CONV, :]
    for s in range(1, CONV):
        moved = pltpu.roll(src, s, 0) * masks[s]
        rolled.append(moved)
        total = total + moved * taps[CONV - 1 - s : CONV - s, :]
    return total, rolled


def l2_norm(c):
    inv = lax.rsqrt(jnp.sum(c * c, axis=-1, keepdims=True) + 1e-06)
    return c * inv, inv


def mixer_fwd_kernel(
    blocks, rows_mb,
    pq, pk, pv, pg, beta, tq, tk, tv, gain, mask, segc, segr,
    on_ref, o_ref, ainv_ref, u_ref, p_ref, l_ref,
):
    step = pl.program_id(0)
    masks = [None] + [mask[:, s : s + 1] for s in range(1, CONV)]
    cs = []
    for src, taps in ((pq, tq), (pk, tk), (pv, tv)):
        pre, _ = conv_parts(src[...], taps[...], masks)
        cs.append(pre * sigmoid(pre))
    cq, ck, cv = cs
    strengths = sigmoid(beta[...])
    lane = iota2(strengths.shape, 1)
    gate = pg[...]
    gate = gate * sigmoid(gate)
    row, col = iota2((rows_mb, rows_mb), 0), iota2((rows_mb, rows_mb), 1)
    systems = [(h, b) for h in range(PAIR) for b in range(blocks)]
    qs, ks, vs, bs, sames, lows = [], [], [], [], [], []
    for h, b in systems:
        rs = slice(b * rows_mb, (b + 1) * rows_mb)
        hs = slice(h * HEAD_DIM, (h + 1) * HEAD_DIM)
        q, _ = l2_norm(cq[rs, hs])
        k, _ = l2_norm(ck[rs, hs])
        qs.append(q * HEAD_DIM ** (-0.5))
        ks.append(k)
        vs.append(cv[rs, hs])
        bs.append(
            jnp.sum(jnp.where(lane == step * PAIR + h, strengths, 0.0), axis=1, keepdims=True)[rs]
        )
        sames.append(segc[rs, :] == segr[:, rs])
    for i in range(len(systems)):
        lows.append(jnp.where(sames[i] & (row > col), mm(ks[i], ks[i], 1, 1), 0.0))
    inverses = unit_lower_inverses([l * b for l, b in zip(lows, bs)], rows_mb)
    us = [mm(a, v * b, 1, 0) for a, v, b in zip(inverses, vs, bs)]
    ps = [
        jnp.where(same & (row >= col), mm(q, k, 1, 1), 0.0)
        for q, k, same in zip(qs, ks, sames)
    ]
    os = [mm(p, u, 1, 0) for p, u in zip(ps, us)]
    for i, (h, b) in enumerate(systems):
        rs = slice(b * rows_mb, (b + 1) * rows_mb)
        hs = slice(h * HEAD_DIM, (h + 1) * HEAD_DIM)
        o = os[i]
        inv = lax.rsqrt(jnp.mean(o * o, axis=-1, keepdims=True) + 1e-05)
        on_ref[rs, hs] = (o * inv * gain[...] * gate[rs, hs]).astype(BF16)
        o_ref[rs, hs] = o
        ainv_ref[h, b] = inverses[i]
        u_ref[h, b] = us[i]
        p_ref[h, b] = ps[i]
        l_ref[h, b] = lows[i]


def mixer_bwd_kernel(
    blocks, rows_mb, pair, step,
    pq, pk, pv, pg, beta, tq, tk, tv, gain, mask, segc, segr,
    don_ref, o_ref, ainv_ref, u_ref, p_ref, l_ref,
    dq_ref, dk_ref, dv_ref, dg_ref, dbeta_ref, dtq, dtk, dtv, dgain_ref,
):
    rows = blocks * rows_mb
    masks = [None] + [mask[:, s : s + 1] for s in range(1, CONV)]
    pres, rolls, cs, sig = [], [], [], []
    for src, taps in ((pq, tq), (pk, tk), (pv, tv)):
        pre, rolled = conv_parts(src[...], taps[...], masks)
        s = sigmoid(pre)
        pres.append(pre)
        rolls.append(rolled)
        sig.append(s)
        cs.append(pre * s)
    cq, ck, cv = cs
    strengths = sigmoid(beta[...])
    lane = iota2(strengths.shape, 1)
    row, col = iota2((rows_mb, rows_mb), 0), iota2((rows_mb, rows_mb), 1)
    gates = pg[...]
    gsig = sigmoid(gates)
    gate = gates * gsig
    dgate = gsig * (1.0 + gates * (1.0 - gsig))
    systems = [(h, b) for h in range(pair) for b in range(blocks)]
    part = []
    dgain = jnp.zeros((1, HEAD_DIM), F32)
    for h, b in systems:
        rs = slice(b * rows_mb, (b + 1) * rows_mb)
        hs = slice(h * HEAD_DIM, (h + 1) * HEAD_DIM)
        k, ik = l2_norm(ck[rs, hs])
        qn, iq = l2_norm(cq[rs, hs])
        v = cv[rs, hs]
        bb = jnp.sum(jnp.where(lane == step * pair + h, strengths, 0.0), axis=1, keepdims=True)[rs]
        same = segc[rs, :] == segr[:, rs]
        o = o_ref[rs, hs]
        don = don_ref[rs, hs]
        inv = lax.rsqrt(jnp.mean(o * o, axis=-1, keepdims=True) + 1e-05)
        no = o * inv
        scaled = don * gain[...]
        dg_ref[rs, hs] = (scaled * no * dgate[rs, hs]).astype(BF16)
        dgain = dgain + jnp.sum(don * no * gate[rs, hs], axis=0, keepdims=True)
        dno = scaled * gate[rs, hs]
        do = inv * (dno - no * jnp.mean(no * dno, axis=-1, keepdims=True))
        part.append([q_ for q_ in (qn, iq, k, ik, v, bb, same, do)])
    dus = [mm(p_ref[h, b], part[i][7], 0, 0) for i, (h, b) in enumerate(systems)]
    dps = [
        jnp.where(part[i][6] & (row >= col), mm(part[i][7], u_ref[h, b], 1, 1), 0.0)
        for i, (h, b) in enumerate(systems)
    ]
    drs = [mm(ainv_ref[h, b], dus[i], 0, 0) for i, (h, b) in enumerate(systems)]
    scale = HEAD_DIM ** (-0.5)
    dqs = [mm(dps[i], part[i][2], 1, 0) * scale for i in range(len(systems))]
    das = [mm(drs[i], u_ref[h, b], 1, 1) for i, (h, b) in enumerate(systems)]
    dks = [mm(dps[i], part[i][0] * scale, 0, 0) for i in range(len(systems))]
    dgs = []
    for i in range(len(systems)):
        g = jnp.where(part[i][6] & (row > col), das[i] * (-part[i][5]), 0.0)
        dgs.append(g + g.T)
    dks = [dks[i] + mm(dgs[i], part[i][2], 1, 0) for i in range(len(systems))]
    dbeta = jnp.zeros(strengths.shape, F32)
    dcs = [[], [], []]
    for i, (h, b) in enumerate(systems):
        qn, iq, k, ik, v, bb, same, do = part[i]
        dv = drs[i] * bb
        db = jnp.sum(drs[i] * v - das[i] * l_ref[h, b], axis=-1, keepdims=True)
        dbp = db * bb * (1.0 - bb)
        pieces = [dbp if b == c else jnp.zeros((rows_mb, 1), F32) for c in range(blocks)]
        column = jnp.concatenate(pieces, axis=0) if blocks > 1 else dbp
        dbeta = dbeta + jnp.where(lane == step * pair + h, column, 0.0)
        dcs[0].append(iq * (dqs[i] - qn * jnp.sum(qn * dqs[i], axis=-1, keepdims=True)))
        dcs[1].append(ik * (dks[i] - k * jnp.sum(k * dks[i], axis=-1, keepdims=True)))
        dcs[2].append(dv)
    for j, (out, dtap, taps) in enumerate(((dq_ref, dtq, tq), (dk_ref, dtk, tk), (dv_ref, dtv, tv))):
        whole = jnp.concatenate(
            [
                jnp.concatenate([dcs[j][h * blocks + b] for b in range(blocks)], axis=0)
                for h in range(pair)
            ],
            axis=1,
        )
        dpre = whole * (sig[j] * (1.0 + pres[j] * (1.0 - sig[j])))
        tap = taps[...]
        grad = dpre * tap[CONV - 1 : CONV, :]
        dtap[CONV - 1 : CONV, :] = jnp.sum(dpre * rolls[j][0], axis=0, keepdims=True)
        for s in range(1, CONV):
            dtap[CONV - 1 - s : CONV - s, :] = jnp.sum(dpre * rolls[j][s], axis=0, keepdims=True)
            grad = grad + pltpu.roll(dpre * masks[s], rows - s, 0) * tap[CONV - 1 - s : CONV - s, :]
        out[...] = grad.astype(BF16)

    @pl.when(step == 0)
    def _():
        dbeta_ref[...] = jnp.zeros_like(dbeta_ref)
        dgain_ref[...] = jnp.zeros_like(dgain_ref)

    dbeta_ref[...] += dbeta
    dgain_ref[...] += dgain


def mixer_specs(rows, blocks, rows_mb):
    width = PAIR * HEAD_DIM
    per = D // width
    col = lambda k: pl.BlockSpec((rows, width), lambda i, k=k: (0, k * per + i))
    tap = lambda k: pl.BlockSpec((CONV, width), lambda i, k=k: (0, k * per + i))
    full = lambda shape: pl.BlockSpec(shape, lambda i: (0,) * len(shape))
    ins = [col(0), col(1), col(2), col(3), full((rows, HEADS)), tap(0), tap(1), tap(2),
           full((1, HEAD_DIM)), full((rows, 8)), full((rows, 1)), full((1, rows))]
    mat = pl.BlockSpec((PAIR, blocks, rows_mb, rows_mb), lambda i: (i, 0, 0, 0))
    one = pl.BlockSpec((rows, width), lambda i: (0, i))
    otap = pl.BlockSpec((CONV, width), lambda i: (0, i))
    return ins, mat, one, otap, full


def lin_index():
    return lax.axis_index("dp") * lax.axis_size("fsdp") + lax.axis_index("fsdp")


def mesh_id(index):
    inner = lax.axis_size("fsdp")
    return (lax.div(index, inner), lax.rem(index, inner))


class Here:
    def __init__(self, shards):
        self.shards, self.me = shards, lin_index()
        self.bits = shards.bit_length() - 1
        own = [lax.rem(lax.div(self.me, 1 << b), 2) for b in range(self.bits)]
        self.core = own[0]
        self.change = [(1 - 2 * o) * (1 << b) for b, o in enumerate(own)]
        self.partner = [mesh_id(self.me + c) for c in self.change]

    def flip(self, bits, number, always=()):
        result = self.me
        for bit in always:
            result = result + self.change[bit]
        for i, bit in enumerate(reversed(bits)):
            if isinstance(number, int):
                if (number >> i) & 1:
                    result = result + self.change[bit]
            else:
                result = result + lax.rem(lax.div(number, 1 << i), 2) * self.change[bit]
        return result


def routes(shards):
    bits = shards.bit_length() - 1
    rest = list(range(4, bits))
    return [[1, 2, 3] + rest, [2, 3, 1] + rest, [3, 1, 2] + rest]


def colours(width, turn):
    tiles = width // 128
    one, three = round(tiles * 0.36), round(tiles * 0.28)
    sizes = (one, tiles - one - three, three)
    return [(sum(sizes[:c]) * 128, sizes[c] * 128) for c in range(3)]


def meet(here, everyone):
    barrier = pltpu.get_barrier_semaphore()
    if everyone:

        def greet(r, _):
            peer = lax.rem(here.me + r, here.shards)
            pl.semaphore_signal(barrier, inc=1, device_id=mesh_id(peer), device_id_type=MESH)
            return 0

        lax.fori_loop(1, here.shards, greet, 0)
        pl.semaphore_wait(barrier, here.shards - 1)
    else:
        for partner in here.partner:
            pl.semaphore_signal(barrier, inc=1, device_id=partner, device_id_type=MESH)
        pl.semaphore_wait(barrier, here.bits)


def spread_order(shards):
    bits = shards.bit_length() - 1
    turned = [sum(((i >> b) & 1) << (bits - 1 - b) for b in range(bits)) for i in range(shards)]
    return turned[1:]


class Exchange:
    def __init__(self, here, sent, got, send, recv, keep, same=False):
        self.here, self.shards, self.me, self.got = here, here.shards, here.me, got
        self.block = (lambda d: sent) if same else (lambda d: sent.at[d])
        self.send, self.recv, self.keep = send, recv, keep

    def own(self):
        return pltpu.make_async_copy(self.block(self.me), self.got.at[self.me], self.keep)

    def start(self):
        self.own().start()

        def one(r, _):
            peer = lax.rem(self.me + r, self.shards)
            pltpu.make_async_remote_copy(
                src_ref=self.block(peer), dst_ref=self.got.at[self.me], send_sem=self.send,
                recv_sem=self.recv, device_id=mesh_id(peer), device_id_type=MESH,
            ).start()
            return 0

        lax.fori_loop(1, self.shards, one, 0)

    def start_part(self, part, parts):
        others = self.shards - 1
        if part == 0:
            self.own().start()
        for r in range(others * part // parts, others * (part + 1) // parts):
            peer = lax.rem(self.me + spread_order(self.shards)[r], self.shards)
            pltpu.make_async_remote_copy(
                src_ref=self.block(peer), dst_ref=self.got.at[self.me], send_sem=self.send,
                recv_sem=self.recv, device_id=mesh_id(peer), device_id_type=MESH,
            ).start()

    def wait(self):
        self.own().wait()
        whole = pl.ds(0, self.shards - 1)
        pltpu.make_async_remote_copy(
            src_ref=self.got.at[whole], dst_ref=self.got.at[whole], send_sem=self.send,
            recv_sem=self.recv, device_id=self.here.partner[0], device_id_type=MESH,
        ).wait()


DEAL_AT = 0
CHUNK = 256
X_STEPS = 5
GT_FROM = 6
SLICE = 256
MIXER_BUFFERS = 2
DX_PARTS = 6


def pieces_of(widths, split):
    result = []
    for i, width in enumerate(widths):
        tiles, at = width // 128, 0
        for j in range(split[i]):
            size = tiles // split[i] + (1 if j < tiles % split[i] else 0)
            result.append((i, at * 128, size * 128))
            at += size
    return result


class Gather:
    def __init__(self, here, pieces, own, full, sems):
        self.here, self.pieces, self.own, self.full = here, pieces, own, full
        self.send, self.recv, self.pair_send, self.pair_recv, self.keep = sems
        self.stages = here.bits - 1
        self.order = routes(here.shards)
        self.core = here.core
        self.cuts = [
            [(at + a, s) for a, s in colours(size, n)] for n, (_, at, size) in enumerate(pieces)
        ]
        self.last = len(pieces) + self.stages - 1

    @staticmethod
    def semaphores(shards, pieces):
        dma, stages = pltpu.SemaphoreType.DMA, shards.bit_length() - 2
        number = len(pieces)
        return [dma((stages, number, 3)), dma((stages, number, 3)), dma((number,)), dma((number,)),
                dma((number,))]

    def kept(self, i):
        return pltpu.make_async_copy(
            self.own[i], self.full[i].at[lax.div(self.here.me, 2), self.core], self.keep.at[i]
        )

    def begin(self):
        for i in range(len(self.own)):
            self.kept(i).start()

    def partner(self, k, c):
        return self.here.partner[self.order[c][self.stages - 1 - k]]

    def group(self, k, n, c):
        at, size = self.cuts[n][c]
        some = self.full[self.pieces[n][0]].at[pl.ds(0, 1 << k), 0, :, pl.ds(at, size)]
        return pltpu.make_async_remote_copy(
            src_ref=some, dst_ref=some, send_sem=self.send.at[k, n, c],
            recv_sem=self.recv.at[k, n, c], device_id=self.partner(k, c), device_id_type=MESH,
        )

    def half(self, n):
        i, at, size = self.pieces[n]
        some = self.full[i].at[:, self.core, :, pl.ds(at, size)]
        return pltpu.make_async_remote_copy(
            src_ref=some, dst_ref=some, send_sem=self.pair_send.at[n],
            recv_sem=self.pair_recv.at[n], device_id=self.here.partner[0],
            device_id_type=MESH,
        )

    def launch(self, k, n):
        i = self.pieces[n][0]
        for c in range(3):
            at, size = self.cuts[n][c]
            if k > 0:
                self.group(k - 1, n, c).wait_recv()
            have = self.order[c][self.stages - k :]
            for j in range(1 << k):
                d = self.here.flip(have, j)
                there = self.full[i].at[lax.div(d, 2), self.core, :, pl.ds(at, size)]
                pltpu.make_async_remote_copy(
                    src_ref=self.own[i].at[:, pl.ds(at, size)] if j == 0 else there,
                    dst_ref=there, send_sem=self.send.at[k, n, c], recv_sem=self.recv.at[k, n, c],
                    device_id=self.partner(k, c), device_id_type=MESH,
                ).start()

    def finish(self, n):
        for c in range(3):
            self.group(self.stages - 1, n, c).wait_recv()
        if n == 0 or self.pieces[n - 1][0] != self.pieces[n][0]:
            self.kept(self.pieces[n][0]).wait()
        self.half(n).start()

    def slots(self, first, last):
        return sum(
            0 <= t - n <= self.stages for t in range(first, last) for n in range(len(self.pieces))
        )

    def step(self, t, between=None):
        for n in range(len(self.pieces)):
            k = t - n
            if 0 <= k < self.stages:
                self.launch(k, n)
            elif k == self.stages:
                self.finish(n)
            if between is not None and 0 <= k <= self.stages:
                between()

    def end(self, arrived=0):
        for k in range(self.stages):
            for n in range(len(self.pieces)):
                for c in range(3):
                    self.group(k, n, c).wait_send()
        for n in range(len(self.pieces)):
            self.half(n).wait_send()
            if n >= arrived:
                self.half(n).wait_recv()


def first_kernel(shards, pieces, *refs):
    count = 1 + max(i for i, _, _ in pieces)
    own, sent, full, got = refs[:count], refs[count], refs[count + 1 : 2 * count + 1], refs[2 * count + 1]
    sems = refs[2 * count + 2 :]
    here = Here(shards)
    deal = Exchange(here, sent, got, *sems[5:])
    weights = Gather(here, pieces, own, full, sems[:5])
    weights.begin()
    meet(here, True)
    deal.start()
    for t in range(weights.last + 1):
        weights.step(t)
    deal.wait()
    weights.end()


def spread(weight, shards):
    return jax.ShapeDtypeStruct((shards // 2, 2) + weight.shape, weight.dtype)


def first(weights, split, message, shards, collective_id):
    count = len(weights)
    anywhere = pl.BlockSpec(memory_space=pl.ANY)
    pieces = pieces_of([w.shape[1] for w in weights], split)
    dma = pltpu.SemaphoreType.DMA
    *full, got = pl.pallas_call(
        functools.partial(first_kernel, shards, pieces),
        in_specs=[anywhere] * (count + 1),
        out_specs=[anywhere] * (count + 1),
        out_shape=[spread(w, shards) for w in weights]
        + [jax.ShapeDtypeStruct(message.shape, message.dtype)],
        scratch_shapes=Gather.semaphores(shards, pieces) + [dma, dma, dma],
        compiler_params=pltpu.CompilerParams(collective_id=collective_id, has_side_effects=True),
        name="gather_first",
    )(*weights, message)
    return [f.reshape(-1, f.shape[-1]) for f in full], got


def forward_kernel(
    shards, pieces, blocks, rows_mb,
    own_down, own_gu, sent, a1, wq, wk, wv, wg, wout, wbeta, x, gain_two, tq, tk, tv, gain, mask,
    segc, segr,
    full_down, full_gu, got, pq, pk, pv, pg, beta, on, o, ainv, u, p, l, resid, a2,
    *sems,
):
    step = pl.program_id(0)
    steps = HEADS // PAIR
    here = Here(shards)
    weights = Gather(here, pieces, (own_down, own_gu), (full_down, full_gu), sems[:5])
    deal = Exchange(here, sent, got, *sems[5:])

    @pl.when(step == 0)
    def _():
        weights.begin()
        meet(here, True)
        weights.step(0)
        resid[...] = x[...]

    normed = a1[...]
    beta[...] = jnp.dot(normed, wbeta[...], preferred_element_type=F32)
    for out, w in ((pq, wq), (pk, wk), (pv, wv), (pg, wg)):
        out[...] = jnp.dot(normed, w[...], preferred_element_type=F32)
    mixer_fwd_kernel(
        blocks, rows_mb, pq, pk, pv, pg, beta, tq, tk, tv, gain, mask, segc, segr, on, o, ainv, u,
        p, l,
    )
    resid[...] += jnp.dot(on[...], wout[...], preferred_element_type=F32)
    for s in range(steps):

        @pl.when(step == s)
        def _(s=s):
            weights.step(s + 1)
            if s == DEAL_AT:
                deal.start()
            if s == steps - 1:
                r = resid[...]
                a2[...] = (rms(r)[0] * gain_two[...]).astype(BF16)
                for t in range(steps + 1, weights.last + 1):
                    weights.step(t)
                deal.wait()
                weights.end()


def forward(
    w_down, w_gu, message, split, a1, win, wout, wbeta, x, gain_two, taps, gain, mask, segc, segr, blocks,
    shards, collective_id,
):
    rows = x.shape[0]
    rows_mb = rows // blocks
    width = PAIR * HEAD_DIM
    pieces = pieces_of([w_down.shape[1], w_gu.shape[1]], split)
    anywhere = pl.BlockSpec(memory_space=pl.ANY)
    ins, mat, one, _, full = mixer_specs(rows, blocks, rows_mb)
    per = D // width
    wcol = lambda k: pl.BlockSpec((D, width), lambda i, k=k: (0, k * per + i))
    square = jax.ShapeDtypeStruct((HEADS, blocks, rows_mb, rows_mb), F32)
    wide = jax.ShapeDtypeStruct((rows, D), F32)
    dma = pltpu.SemaphoreType.DMA
    full_down, full_gu, got, *rest = pl.pallas_call(
        functools.partial(forward_kernel, shards, pieces, blocks, rows_mb),
        grid=(HEADS // PAIR,),
        in_specs=[
            anywhere, anywhere, anywhere, full((rows, D)), wcol(0), wcol(1), wcol(2), wcol(3),
            pl.BlockSpec((width, D), lambda i: (i, 0)), full((D, HEADS)), full((rows, D)),
            full((1, D)), *ins[5:],
        ],
        out_specs=[anywhere, anywhere, anywhere, one, one, one, one, full((rows, HEADS)), one, one, mat, mat,
                   mat, mat, full((rows, D)), full((rows, D))],
        out_shape=[
            spread(w_down, shards), spread(w_gu, shards),
            jax.ShapeDtypeStruct(message.shape, message.dtype), wide, wide, wide, wide,
            jax.ShapeDtypeStruct((rows, HEADS), F32), jax.ShapeDtypeStruct((rows, D), BF16), wide,
            square, square, square, square, wide, jax.ShapeDtypeStruct((rows, D), BF16),
        ],
        scratch_shapes=Gather.semaphores(shards, pieces) + [dma, dma, dma],
        compiler_params=pltpu.CompilerParams(
            collective_id=collective_id, has_side_effects=True, vmem_limit_bytes=48 << 20
        ),
        name="mixer_forward",
    )(w_down, w_gu, message, a1, win, win, win, win, wout, wbeta, x, gain_two, taps, taps, taps, gain, mask,
      segc, segr)
    return full_down.reshape(FF, D), full_gu.reshape(D, 2 * FF), got, rest


class Scatter:
    def __init__(self, here, pieces, whole, mine, other, coming, sems, kept):
        self.here, self.pieces, self.whole, self.mine = here, pieces, whole, mine
        self.other, self.coming, self.kept_of = other, coming, kept
        self.send, self.recv, self.pair_send, self.pair_recv = sems
        self.stages = here.bits - 1
        self.order = routes(here.shards)
        self.core = here.core
        self.cuts = [
            [(at + a, s) for a, s in colours(size, n)] for n, (_, at, size) in enumerate(pieces)
        ]

    @staticmethod
    def semaphores(shards, number):
        dma, stages = pltpu.SemaphoreType.DMA, shards.bit_length() - 2
        return [dma((stages, number, 3)), dma((stages, number, 3)), dma((number,)), dma((number,))]

    @staticmethod
    def buffers(shards, shapes):
        stages = shards.bit_length() - 2
        return [pltpu.VMEM((shards // 2,) + s, BF16) for s in shapes] + [
            pltpu.VMEM((1 << (stages - 1 - k),) + s, BF16) for s in shapes for k in range(stages)
        ]

    @staticmethod
    def split(shards, count, refs):
        stages = shards.bit_length() - 2
        other, refs = refs[:count], refs[count:]
        return other, [refs[i * stages : (i + 1) * stages] for i in range(count)]

    def pair(self, n):
        i, at, size = self.pieces[n]
        return pltpu.make_async_remote_copy(
            src_ref=self.whole(n, 1 - self.core), dst_ref=self.other[i].at[:, :, pl.ds(at, size)],
            send_sem=self.pair_send.at[n], recv_sem=self.pair_recv.at[n],
            device_id=self.here.partner[0], device_id_type=MESH,
        )

    def hop(self, k, n, c, source, spots):
        i = self.pieces[n][0]
        at, size = self.cuts[n][c]
        cols = pl.ds(at, size)
        return pltpu.make_async_remote_copy(
            src_ref=self.other[i].at[source, :, cols],
            dst_ref=self.coming[i][k].at[spots, :, cols],
            send_sem=self.send.at[k, n, c], recv_sem=self.recv.at[k, n, c],
            device_id=self.here.partner[self.order[c][k]], device_id_type=MESH,
        )

    def group(self, k, n, c):
        all_of = pl.ds(0, 1 << (self.stages - 1 - k))
        return self.hop(k, n, c, all_of, all_of)

    def total(self, k, n, c, shard, spot):
        i = self.pieces[n][0]
        at, size = self.cuts[n][c]
        cols = pl.ds(at, size)
        q = lax.div(shard, 2)
        value = self.mine(i, q, cols).astype(F32) + self.other[i][q, :, cols].astype(F32)
        for p in range(k):
            value = value + self.coming[i][p][spot, :, cols].astype(F32)
        return value

    def launch(self, k, n):
        if k == 0:
            kept = self.kept_of(n)
            if kept is not None:
                kept.wait()
            self.pair(n).wait_recv()
        for c in range(3):
            if k > 0:
                self.group(k - 1, n, c).wait_recv()
            much = 1 << (self.stages - 1 - k)
            at, size = self.cuts[n][c]

            def body(j, _, c=c, at=at, size=size):
                shard = self.here.flip(self.order[c][k + 1 :], j, (self.order[c][k],))
                q = lax.div(shard, 2)
                self.other[self.pieces[n][0]][q, :, pl.ds(at, size)] = self.total(
                    k, n, c, shard, much + j
                ).astype(BF16)
                self.hop(k, n, c, q, j).start()
                return 0

            lax.fori_loop(0, much, body, 0)

    def finish(self, n, write):
        for c in range(3):
            self.group(self.stages - 1, n, c).wait_recv()
            at, size = self.cuts[n][c]
            write(self.pieces[n][0], at, size, self.total(self.stages, n, c, self.here.me, 0))

    def end(self, n, paired=True):
        for k in range(self.stages):
            for c in range(3):
                self.group(k, n, c).wait_send()
        if paired:
            self.pair(n).wait_send()


def front_kernel(shards, blocks, rows_mb, split, *refs):
    (own_in, own_out, own_down, own_gu, small, tokens, later_rows, deal_row, valid_row, lengths, gain), refs = refs[:11], refs[11:]
    (full_in, full_out, full_down, full_gu, pq, pk, pv, pg, beta, on, o, ainv, u, p, l, resid, a2, x, info, gt, taps,
     gain_one, gain_two, wbeta, segc, segr, mask, a1, a1_t, a2_t), refs = refs[:30], refs[30:]
    (sent, got, sent_gt, got_gt, got_small, wbuf, wout, deal, w_sem, out_sem), refs = refs[:10], refs[10:]
    sems, deal_sems, later_sems, small_sems = refs[:5], refs[5:8], refs[8:11], refs[11:14]
    step = pl.program_id(0)
    steps = HEADS // PAIR
    width = PAIR * HEAD_DIM
    rows = blocks * rows_mb
    share = rows // shards
    here = Here(shards)
    pieces = pieces_of([4 * D, D, D, 2 * FF], split)
    weights = Gather(here, pieces, (own_in, own_out, own_down, own_gu), (full_in, full_out, full_down, full_gu), sems)
    first_send = Exchange(here, sent, got, *deal_sems)
    second_send = Exchange(here, sent_gt, got_gt, *later_sems)
    small_send = Exchange(here, small, got_small, *small_sems, same=True)
    of_in = split[0]
    hidden_from = len(pieces) + weights.stages - steps
    deal_to, later_from = X_STEPS, GT_FROM

    def trickle(exchange, first, last):
        parts, done = weights.slots(first, last), [0]

        def at(t):
            if not first <= t < last:
                return None
            done[0] = weights.slots(first, t)

            def one():
                exchange.start_part(done[0], parts)
                done[0] += 1

            return one

        return at

    deal_some = trickle(first_send, 1, deal_to)
    later_some = trickle(second_send, later_from, weights.last + 1)

    def between(t):
        acts = [f for f in (deal_some(t), later_some(t)) if f is not None]
        return (lambda: [f() for f in acts]) if acts else None

    def fetch(s, g):
        return pltpu.make_async_copy(
            full_in.at[:, :, :, pl.ds(g * D + s * width, width)], wbuf.at[s % 2, g], w_sem.at[s % 2, g]
        )

    def fetch_out():
        return pltpu.make_async_copy(full_out, wout, out_sem)

    @pl.when(step == 0)
    def _():
        weights.begin()
        meet(here, True)
        weights.step(0)
        small_send.start()
        row, col = iota2((rows, rows), 0), iota2((rows, rows), 1)
        column = lambda v: jnp.sum(jnp.where(row == col, v, 0.0), axis=1, keepdims=True)
        dealt = deal_row[...].astype(F32)
        target = jnp.floor((dealt + 0.5) * (1.0 / rows))
        valid = valid_row[...].astype(F32)
        target_c = column(target)
        rank = jnp.sum(jnp.where((target == target_c) & (col < row), 1.0, 0.0), axis=1, keepdims=True)
        slot = target_c * share + rank
        sort_t = (slot == col.astype(F32)).astype(BF16)
        lane = iota2((rows, 128), 1)
        notes = jnp.where(
            lane == 0, column(valid),
            jnp.where(lane == 1, column(dealt - target * rows), jnp.where(lane == 2, jnp.sum(valid), 0.0)),
        ).astype(BF16)
        sent[:, :, :D] = tn(sort_t, tokens[...]).reshape(shards, share, D).astype(BF16)
        sent[:, :, D:] = tn(sort_t, notes).reshape(shards, share, 128).astype(BF16)
        weights.step(1, between(1))
        half = later_rows.shape[1] // 2
        for at in (0, half):
            sent_gt[:, :, at : at + half] = (
                tn(sort_t, later_rows[:, at : at + half]).reshape(shards, share, half).astype(BF16)
            )
        weights.step(2, between(2))
        at_row, at_col = iota2((rows, 1), 0), iota2((1, rows), 1)
        seg_c, seg_r = jnp.zeros((rows, 1), F32), jnp.zeros((1, rows), F32)
        lens = lengths[...].astype(F32)
        for b in range(blocks):
            end = jnp.zeros((1, 1), F32) + b * rows_mb
            for i in range(lengths.shape[1]):
                seg_c = seg_c + jnp.where(at_row >= b * rows_mb, 1.0, 0.0) * (i == 0)
                seg_r = seg_r + jnp.where(at_col >= b * rows_mb, 1.0, 0.0) * (i == 0)
                end = end + lens[b : b + 1, i : i + 1]
                if i < lengths.shape[1] - 1:
                    seg_c = seg_c + jnp.where(at_row.astype(F32) >= end, 1.0, 0.0)
                    seg_r = seg_r + jnp.where(at_col.astype(F32) >= end, 1.0, 0.0)
        segc[...] = seg_c.astype(jnp.int32)
        segr[...] = seg_r.astype(jnp.int32)
        lane8 = iota2((rows, 8), 1)
        wide = jnp.broadcast_to(seg_c, (rows, 128))
        marks = jnp.where(lane8 == 0, 1.0, 0.0)
        for s in range(1, CONV):
            before = pltpu.roll(wide, s, 0)[:, :1]
            same = jnp.where((before == seg_c) & (at_row >= s), 1.0, 0.0)
            marks = marks + jnp.where(lane8 == s, same, 0.0)
        mask[...] = marks
        small_send.wait()
        own_taps, own_gain = 3 * D // shards, D // shards
        per = 128 // own_gain
        a, c = iota2((per * 128, per * own_taps), 0), iota2((per * 128, per * own_taps), 1)
        pick_taps = ((a // 128 == c // own_taps) & (a % 128 == c % own_taps)).astype(BF16)
        a, c = iota2((per * 128, 128), 0), iota2((per * 128, 128), 1)
        pick_gain = ((a // 128 == c // own_gain) & (a % 128 == c % own_gain)).astype(BF16)
        for g in range(shards // per):
            left = jnp.concatenate([got_small[g * per + i, :, :128].astype(F32) for i in range(per)], axis=1).astype(BF16)
            right = jnp.concatenate([got_small[g * per + i, :, 128:].astype(F32) for i in range(per)], axis=1).astype(BF16)
            tap = nn(left, pick_taps)
            taps[:, g * per * own_taps : (g + 1) * per * own_taps] = tap[:CONV]
            gains = nn(left, pick_gain)
            gain_one[:, g * 128 : (g + 1) * 128] = gains[4:5]
            gain_two[:, g * 128 : (g + 1) * 128] = gains[5:6]
            wbeta[:, g * 128 : (g + 1) * 128] = nn(right, pick_gain).astype(BF16)
        for t in range(3, hidden_from):
            weights.step(t, between(t))
        first_send.wait()
        flat = got[...].astype(F32).reshape(rows, D + 128)
        notes = flat[:, D:]
        info[...] = notes
        deal[...] = (notes[:, 1:2] == col.astype(F32)).astype(BF16)
        x_now = tn(deal[...], flat[:, :D].astype(BF16))
        x[...] = x_now
        a1[...] = (rms(x_now)[0] * gain_one[...]).astype(BF16)
        beta[...] = nt(a1[...], wbeta[...])
        a1_t[...] = a1[...].T
        for n in range(of_in):
            weights.half(n).wait_recv()
        for g in range(4):
            fetch(0, g).start()

    for s in range(steps):

        @pl.when(step == s)
        def _(s=s):
            for g in range(4):
                fetch(s, g).wait()
            if s + 1 < steps:
                for g in range(4):
                    fetch(s + 1, g).start()

    slot_now = lax.rem(step, 2)
    for g, out in enumerate((pq, pk, pv, pg)):
        out[...] = nn(a1[...], wbuf[slot_now, g].reshape(D, width))
    here_cols = pl.ds(pl.multiple_of(step * width, width), width)
    taps_of = lambda j: taps.at[:, pl.ds(pl.multiple_of(j * D + step * width, width), width)]
    mixer_fwd_kernel(
        blocks, rows_mb, pq, pk, pv, pg, beta, taps_of(0), taps_of(1), taps_of(2), gain, mask, segc, segr,
        on.at[:, here_cols], o, ainv, u, p, l,
    )
    for s in range(steps):

        @pl.when(step == s)
        def _(s=s):
            weights.step(hidden_from + s, between(hidden_from + s))
            if s == steps - 1:
                for n in range(of_in, of_in + split[1]):
                    weights.half(n).wait_recv()
                fetch_out().start()
                second_send.wait()
                gt[...] = tn(deal[...], got_gt[...].astype(F32).reshape(rows, gt.shape[1]).astype(BF16))
                fetch_out().wait()
                r = x[...] + nn(on[...], wout[...].reshape(D, D))
                resid[...] = r
                a2[...] = (rms(r)[0] * gain_two[...]).astype(BF16)
                a2_t[...] = a2[...].T
                weights.end(of_in + split[1])


def front(weights, small, tokens, later_rows, deal_rows, valid_mask, lengths, gain, shards, collective_id):
    rows, blocks = tokens.shape[0], lengths.shape[0]
    rows_mb, share = rows // blocks, rows // shards
    width = PAIR * HEAD_DIM
    split = (2, 1, 1, 2)
    pieces = pieces_of([w.shape[1] for w in weights], split)
    anywhere = pl.BlockSpec(memory_space=pl.ANY)
    _, mat, one, _, full = mixer_specs(rows, blocks, rows_mb)
    f32 = lambda *shape: jax.ShapeDtypeStruct(shape, F32)
    bf = lambda *shape: jax.ShapeDtypeStruct(shape, BF16)
    square = f32(HEADS, blocks, rows_mb, rows_mb)
    wide = f32(rows, D)
    vm, dma = pltpu.VMEM, pltpu.SemaphoreType.DMA
    outs = [
        (spread(w, shards), anywhere) for w in weights
    ] + [(wide, one)] * 4 + [
        (f32(rows, HEADS), full((rows, HEADS))), (bf(rows, D), full((rows, D))), (wide, one),
        (square, mat), (square, mat), (square, mat), (square, mat), (wide, full((rows, D))),
        (bf(rows, D), full((rows, D))), (wide, full((rows, D))), (f32(rows, 128), full((rows, 128))),
        (f32(rows, 2 * D), full((rows, 2 * D))), (f32(CONV, 3 * D), full((CONV, 3 * D))),
        (f32(1, D), full((1, D))), (f32(1, D), full((1, D))), (bf(8, D), full((8, D))),
        (jax.ShapeDtypeStruct((rows, 1), jnp.int32), full((rows, 1))),
        (jax.ShapeDtypeStruct((1, rows), jnp.int32), full((1, rows))), (f32(rows, 8), full((rows, 8))),
        (bf(rows, D), full((rows, D))), (bf(D, rows), full((D, rows))), (bf(D, rows), full((D, rows))),
    ]
    return pl.pallas_call(
        functools.partial(front_kernel, shards, blocks, rows_mb, split),
        grid=(HEADS // PAIR,),
        in_specs=[anywhere] * 4 + [
            full(small.shape), full((rows, D)), full((rows, 2 * D)), full((1, rows)), full((1, rows)),
            full(lengths.shape), full((1, HEAD_DIM)),
        ],
        out_specs=[s for _, s in outs],
        out_shape=[s for s, _ in outs],
        scratch_shapes=[
            vm((shards, share, D + 128), BF16), vm((shards, share, D + 128), BF16),
            vm((shards, share, 2 * D), BF16), vm((shards, share, 2 * D), BF16),
            vm((shards,) + small.shape, BF16),
            vm((2, 4, shards // 2, 2, D // shards, width), BF16),
            vm((shards // 2, 2, D // shards, D), BF16), vm((rows, rows), BF16), dma((2, 4)), dma,
        ] + Gather.semaphores(shards, pieces) + [dma] * 9,
        compiler_params=pltpu.CompilerParams(
            collective_id=collective_id, has_side_effects=True, vmem_limit_bytes=58 << 20
        ),
        name="front",
    )(*weights, small, tokens, later_rows, deal_rows[None, :], valid_mask[None, :], lengths, gain)


def backward_kernel(shards, blocks, rows_mb, pieces, *refs):
    (d_down, df, a2, gate, up, wga, wup, wdn, dy, resid, gain_two, wout, wq, wk, wv, wg, a1, on, x,
     gain_one, wbeta, *mixer), refs = refs[:38], refs[38:]
    (g_down, g_gu, dwq, dwk, dwv, dwg, dw_out, d_wbeta, dx, d_two, d_one, dtq, dtk, dtv,
     d_gain), refs = refs[:15], refs[15:]
    (mine_down, d_gu, acc, dresid, dz, don, dpq, dpk, dpv, dpg, dbeta, keep), refs = refs[:12], refs[12:]
    sems, buffers = refs[:4], refs[4:]
    step = pl.program_id(0)
    chunks = FF // CHUNK
    pairs = HEADS // PAIR
    here = Here(shards)
    core = here.core
    other, coming = Scatter.split(shards, 2, buffers)
    r_gu = d_gu.shape[2]

    def whole(n, parity):
        i, at, size = pieces[n]
        if i == 0:
            return d_down.at[:, parity, :, pl.ds(at, size)]
        return d_gu.at[:, parity, :, pl.ds(at, size)]

    def mine(i, q, cols):
        return mine_down[q, :, cols] if i == 0 else d_gu[q, core, :, cols]

    def kept(n):
        if n > 0:
            return None
        return pltpu.make_async_copy(d_down.at[:, core], mine_down, keep)

    net = Scatter(here, pieces, whole, mine, other, coming, sems, kept)

    def write(i, at, size, value):
        if i == 0:
            g_down[:, pl.ds(at, size)] = value
            return
        for tile in range(at // 128, (at + size) // 128):
            chunk, inner = tile * 128 // (2 * CHUNK), tile * 128 % (2 * CHUNK)
            start = chunk * CHUNK + inner if inner < CHUNK else FF + chunk * CHUNK + inner - CHUNK
            g_gu[:, start : start + 128] = value[:, tile * 128 - at : tile * 128 - at + 128]

    @pl.when(step == 0)
    def _():
        kept(0).start()
        meet(here, False)
        net.pair(0).start()
        acc[...] = jnp.zeros_like(acc)

    @pl.when(step < chunks)
    def _():
        dhid = nt(df[...], wdn[...])
        g = gate[...]
        s = sigmoid(g)
        d_gate = (dhid * up[...] * (s * (1.0 + g * (1.0 - s)))).astype(BF16)
        d_up = (dhid * (g * s)).astype(BF16)
        acc[...] += nt(d_gate, wga[...]) + nt(d_up, wup[...])
        for at, part in ((0, d_gate), (CHUNK, d_up)):
            grad = tn(a2[...], part).reshape(shards // 2, 2, r_gu, CHUNK).astype(BF16)
            start = pl.multiple_of(step * (2 * CHUNK) + at, CHUNK)
            d_gu[:, :, :, pl.ds(start, CHUNK)] = grad

    @pl.when(step == chunks - 1)
    def _():
        nr, rr = rms(resid[...])
        da2 = acc[...]
        d_two[...] = jnp.sum(da2 * nr, axis=0, keepdims=True)
        dresid[...] = dy[...] + rms_back(nr, rr, gain_two[...] * da2)
        acc[...] = jnp.zeros_like(acc)
        dz[...] = dresid[...].astype(BF16)

    @pl.when(step >= chunks)
    def _():
        don[...] = nt(dz[...], wout[...])
        mixer_bwd_kernel(
            blocks, rows_mb, PAIR, step - chunks, *mixer[:12], don, *mixer[12:], dpq, dpk, dpv, dpg, dbeta, dtq,
            dtk, dtv, d_gain,
        )
        for dp, w, out in ((dpq, wq, dwq), (dpk, wk, dwk), (dpv, wv, dwv), (dpg, wg, dwg)):
            acc[...] += nt(dp[...], w[...])
            out[...] = tn(a1[...], dp[...]).astype(BF16)
        dw_out[...] = tn(on[...], dz[...]).astype(BF16)

    @pl.when(step == chunks + pairs - 1)
    def _():
        d_beta = dbeta[...].astype(BF16)
        grad = acc[...] + nt(d_beta, wbeta[...])
        d_wbeta[...] = tn(a1[...], d_beta)
        nx, rx = rms(x[...])
        d_one[...] = jnp.sum(grad * nx, axis=0, keepdims=True)
        dx[...] = (dresid[...] + rms_back(nx, rx, gain_one[...] * grad)).astype(BF16)

    ready = {pieces[n][1] // (2 * CHUNK) + pieces[n][2] // (2 * CHUNK) - 1: n for n in (1, 2)}
    plan = {}
    for s, n in ready.items():
        plan.setdefault(s, []).append((net.pair, n))
    tail = range(chunks - 1, chunks + pairs)
    plan.setdefault(3, []).append((net.launch, 0, 0))
    for place, s in enumerate(tail):
        for n in range(3):
            k = place + 1 - n
            if (k, n) != (0, 0) and 0 <= k < net.stages:
                plan.setdefault(s, []).append((net.launch, k, n))
            elif k == net.stages:
                plan.setdefault(s, []).append((net.finish, n, write))
    last = tail[-1]
    for place in range(len(tail), net.stages + 3):
        for n in range(3):
            k = place + 1 - n
            if 0 <= k < net.stages:
                plan[last].append((net.launch, k, n))
            elif k == net.stages:
                plan[last].append((net.finish, n, write))
    for s, actions in plan.items():

        @pl.when(step == s)
        def _(actions=actions, s=s):
            for act, *args in actions:
                result = act(*args)
                if act == net.pair:
                    result.start()
            if s == last:
                for n in range(3):
                    net.end(n)


def backward(
    d_down, df, a2, gu, wgu, wdown, dy, resid, gain_two, wout, win, a1, on, x, gain_one, wbeta, proj,
    beta_pre, taps, gain, mask, segc, segr, saved, blocks, shards, collective_id,
):
    rows = x.shape[0]
    rows_mb = rows // blocks
    width = PAIR * HEAD_DIM
    chunks, pairs = FF // CHUNK, HEADS // PAIR
    anywhere = pl.BlockSpec(memory_space=pl.ANY)
    full = lambda shape: pl.BlockSpec(shape, lambda s: (0,) * len(shape))
    early = lambda s: jnp.minimum(s, chunks - 1)
    late = lambda s: jnp.maximum(s - chunks, 0)
    lane_e = lambda r, w, off=0: pl.BlockSpec((r, w), lambda s: (0, off + early(s)))
    lane_l = lambda r, w, off=0: pl.BlockSpec((r, w), lambda s: (0, off + late(s)))
    wide_l = lambda off=0: pl.BlockSpec(
        (D, width), lambda s: (0, off + late(s)), pipeline_mode=pl.Buffered(1)
    )
    row_l = lambda r, w: pl.BlockSpec((r, w), lambda s: (late(s), 0))
    mat = pl.BlockSpec(
        (PAIR, blocks, rows_mb, rows_mb), lambda s: (late(s), 0, 0, 0), pipeline_mode=pl.Buffered(1)
    )
    part_l = pl.BlockSpec(
        (rows, width), lambda s: (0, late(s)), pipeline_mode=pl.Buffered(1)
    )
    per = D // width
    tap = lambda k: lane_l(CONV, width, k * per)
    r_down, r_gu = FF // shards, D // shards
    a, b = chunks // 2 * 2 * CHUNK, 2 * FF
    pieces = [(0, 0, D), (1, 0, a), (1, a, b - a)]
    f32 = lambda *shape: jax.ShapeDtypeStruct(shape, F32)
    bf = lambda *shape: jax.ShapeDtypeStruct(shape, BF16)
    square = bf(D, D)
    vm = pltpu.VMEM
    return pl.pallas_call(
        functools.partial(backward_kernel, shards, blocks, rows_mb, pieces),
        grid=(chunks + pairs,),
        in_specs=[
            anywhere, full((rows, D)), full((rows, D)), lane_e(rows, CHUNK),
            lane_e(rows, CHUNK, chunks), lane_e(D, CHUNK), lane_e(D, CHUNK, chunks),
            pl.BlockSpec((CHUNK, D), lambda s: (early(s), 0)), full((rows, D)), full((rows, D)),
            full((1, D)), row_l(width, D), wide_l(), wide_l(per), wide_l(2 * per),
            wide_l(3 * per), full((rows, D)),
            lane_l(rows, width), full((rows, D)), full((1, D)), full((D, HEADS)),
            part_l, part_l, part_l, part_l, full((rows, HEADS)), tap(0), tap(1), tap(2), full((1, HEAD_DIM)), full((rows, 8)),
            full((rows, 1)), full((1, rows)), lane_l(rows, width), mat, mat, mat, mat,
        ],
        out_specs=[
            full((r_down, D)), full((r_gu, 2 * FF)), wide_l(), wide_l(), wide_l(), wide_l(),
            row_l(width, D), full((D, HEADS)), full((rows, D)),
            full((1, D)), full((1, D)), lane_l(CONV, width), lane_l(CONV, width),
            lane_l(CONV, width), full((1, HEAD_DIM)),
        ],
        out_shape=[
            f32(r_down, D), f32(r_gu, 2 * FF), square, square, square, square, square,
            f32(D, HEADS), bf(rows, D), f32(1, D), f32(1, D), f32(CONV, D), f32(CONV, D),
            f32(CONV, D), f32(1, HEAD_DIM),
        ],
        scratch_shapes=[
            vm((shards // 2, r_down, D), BF16), vm((shards // 2, 2, r_gu, 2 * FF), BF16),
            vm((rows, D), F32), vm((rows, D), F32), vm((rows, D), BF16), vm((rows, width), F32),
            vm((rows, width), BF16), vm((rows, width), BF16), vm((rows, width), BF16),
            vm((rows, width), BF16), vm((rows, HEADS), F32),
            pltpu.SemaphoreType.DMA,
        ] + Scatter.semaphores(shards, 3) + Scatter.buffers(shards, [(r_down, D), (r_gu, 2 * FF)]),
        compiler_params=pltpu.CompilerParams(
            collective_id=collective_id, has_side_effects=True, vmem_limit_bytes=60 << 20
        ),
        name="backward",
    )(d_down.reshape(shards // 2, 2, r_down, D), df, a2, gu, gu, wgu, wgu, wdown, dy, resid, gain_two,
      wout, win, win, win, win, a1, on, x, gain_one, wbeta, *proj, beta_pre, taps, taps, taps, gain,
      mask, segc, segr, *saved)


def link_plan(half_way, done, last, heads):
    return [
        [3, 8, 10, 12], [half_way + 2, done, done + 2], [done + 1, done + 3], [done + heads // 2 + 2], [last],
        [last],
    ]


def rear_kernel(shards, blocks, rows_mb, pieces, *refs):
    (d_down, sent_y, dy, resid, x, a2_t, a1_t, df, gate, up, wga, wup, wdn, gain_two, gain_one, wout, wq, wk, wv, wg,
     on, wbeta, deal, loss, *mixer), refs = refs[:41], refs[41:]
    (g_down, g_gu, g_in, g_out, got_y, got_dx, small_sum), refs = refs[:7], refs[7:]
    (mine_down, mine_gu, mine_in, mine_out, stage_gu, stage_in, stage_out, acc, dresid, held, dz, don, dpq, dpk, dpv,
     dpg, turned, dbeta, dtaps, d_gain, d_two, sent_dx, small, small_got, keep, load, gu_sem, in_sem, out_sem), refs = refs[:29], refs[29:]
    y_sems, dx_sems, small_sems, sems, buffers = refs[:3], refs[3:6], refs[6:9], refs[9:13], refs[13:]
    step = pl.program_id(0)
    chunks, heads = FF // SLICE, HEADS
    rows = blocks * rows_mb
    share, r_gu = rows // shards, D // shards
    here = Here(shards)
    core = here.core
    other, coming = Scatter.split(shards, 4, buffers)
    mines = (mine_down, mine_gu, mine_in, mine_out)
    pair_recv = sems[3]

    def whole(n, parity):
        i, at, size = pieces[n]
        if i == 0:
            return d_down.at[:, parity, :, pl.ds(at, size)]
        return other[i].at[:, :, pl.ds(at, size)]

    def kept(n):
        if n > 0:
            return None
        return pltpu.make_async_copy(d_down.at[:, core], mine_down, keep)

    net = Scatter(
        here, pieces, whole, lambda i, q, cols: mines[i][q, :, cols], other, coming, sems, kept
    )
    give_y = Exchange(here, sent_y, got_y, *y_sems)
    give_dx = Exchange(here, sent_dx, got_dx, *dx_sems)
    give_small = Exchange(here, small, small_got, *small_sems)

    def cross(stage, slot, there, send, n):
        return pltpu.make_async_remote_copy(
            src_ref=stage.at[slot], dst_ref=there, send_sem=send.at[slot], recv_sem=pair_recv.at[n],
            device_id=here.partner[0], device_id_type=MESH,
        )

    def cross_gu(j):
        cols = pl.ds(pl.multiple_of(j * (2 * SLICE), 2 * SLICE), 2 * SLICE)
        return cross(stage_gu, lax.rem(j, 2), other[1].at[:, :, cols], gu_sem, 1 + lax.div(j + chunks % 2, (chunks + 1) // 2))

    def cross_in(s):
        width = 4 * HEAD_DIM
        cols = pl.ds(pl.multiple_of(s * width, width), width)
        return cross(stage_in, lax.rem(s, 2), other[2].at[:, :, cols], in_sem, 3 + lax.div(s, heads // 2))

    def cross_out(s):
        much = shards // 2 // heads
        return cross(stage_out, lax.rem(s, 2), other[3].at[pl.ds(s * much, much)], out_sem, 5)

    def by_core(value):
        first, second = value[:, 0], value[:, 1]
        return (
            jnp.where(core == 0, first, second).astype(BF16), jnp.where(core == 0, second, first).astype(BF16)
        )

    def write(i, at, size, value):
        if i == 0:
            g_down[:, pl.ds(at, size)] = value
        elif i == 3:
            g_out[:, pl.ds(at, size)] = value
        else:
            for tile in range(at // 128, (at + size) // 128):
                if i == 1:
                    chunk, inner = divmod(tile * 128, 2 * SLICE)
                    start = chunk * SLICE + inner + (FF - SLICE if inner >= SLICE else 0)
                else:
                    start = tile % 4 * D + tile // 4 * HEAD_DIM
                target = g_gu if i == 1 else g_in
                target[:, start : start + 128] = value[:, tile * 128 - at : tile * 128 - at + 128]

    load_dy = pltpu.make_async_copy(dy, dresid, load.at[0])
    load_resid = pltpu.make_async_copy(resid, held, load.at[1])
    load_x = pltpu.make_async_copy(x, held, load.at[1])
    load_a2 = pltpu.make_async_copy(a2_t, turned, load.at[2])
    load_a1 = pltpu.make_async_copy(a1_t, turned, load.at[2])

    @pl.when(step == 0)
    def _():
        kept(0).start()
        load_dy.start()
        load_resid.start()
        meet(here, True)
        net.pair(0).start()
        give_y.start()
        acc[...] = jnp.zeros_like(acc)
        load_a2.start()
        load_a2.wait()

    @pl.when(step < chunks)
    def _():
        dhid = nt(df[...], wdn[...])
        g = gate[...]
        s = sigmoid(g)
        d_gate = (dhid * up[...] * (s * (1.0 + g * (1.0 - s)))).astype(BF16)
        d_up = (dhid * (g * s)).astype(BF16)
        acc[...] += nt(d_gate, wga[...]) + nt(d_up, wup[...])

        @pl.when(step >= 2)
        def _():
            cross_gu(step - 2).wait_send()

        slot = lax.rem(step, 2)
        part = jnp.concatenate([d_gate, d_up], axis=1)
        near, far = by_core(nn(turned[...], part).reshape(shards // 2, 2, r_gu, 2 * SLICE))
        mine_gu[:, :, pl.ds(pl.multiple_of(step * (2 * SLICE), 2 * SLICE), 2 * SLICE)] = near
        stage_gu[slot] = far
        cross_gu(step).start()

    @pl.when(step == chunks - 1)
    def _():
        load_dy.wait()
        load_resid.wait()
        nr, rr = rms(held[...])
        da2 = acc[...]
        d_two[...] = jnp.sum(da2 * nr, axis=0, keepdims=True)
        dresid[...] = dresid[...] + rms_back(nr, rr, gain_two[...] * da2)
        dz[...] = dresid[...].astype(BF16)
        acc[...] = jnp.zeros_like(acc)
        load_a1.start()
        load_x.start()
        load_a1.wait()

    @pl.when(step >= chunks)
    def _():
        head = step - chunks
        don[...] = nt(dz[...], wout[...])
        taps_of = lambda j: dtaps.at[:, pl.ds(pl.multiple_of(j * D + head * HEAD_DIM, HEAD_DIM), HEAD_DIM)]
        mixer_bwd_kernel(
            blocks, rows_mb, 1, head, *mixer[:12], don, *mixer[12:], dpq, dpk, dpv, dpg, dbeta, taps_of(0),
            taps_of(1), taps_of(2), d_gain,
        )

        @pl.when(head >= 2)
        def _():
            cross_in(head - 2).wait_send()
            cross_out(head - 2).wait_send()

        slot = lax.rem(head, 2)
        acc[...] += nt(dpq[...], wq[...]) + nt(dpk[...], wk[...]) + nt(dpv[...], wv[...]) + nt(dpg[...], wg[...])
        width = 4 * HEAD_DIM
        part = jnp.concatenate([dpq[...], dpk[...], dpv[...], dpg[...]], axis=1)
        near, far = by_core(nn(turned[...], part).reshape(shards // 2, 2, r_gu, width))
        mine_in[:, :, pl.ds(pl.multiple_of(head * width, width), width)] = near
        stage_in[slot] = far
        cross_in(head).start()
        much = shards // 2 // heads
        near, far = by_core(tn(on[...], dz[...]).reshape(much, 2, r_gu, D))
        mine_out[pl.ds(head * much, much)] = near
        stage_out[slot] = far
        cross_out(head).start()

    def last_rows():
        d_beta = dbeta[...].astype(BF16)
        grad = acc[...] + nn(d_beta, wbeta[...])
        d_wbeta = lax.dot_general(
            d_beta, turned[...], (((0,), (1,)), ((), ())), preferred_element_type=F32
        )
        load_x.wait()
        nx, rx = rms(held[...])
        d_one = jnp.sum(grad * nx, axis=0, keepdims=True)
        dx = (dresid[...] + rms_back(nx, rx, gain_one[...] * grad)).astype(BF16)
        sent_dx[...] = nn(deal[...], dx).reshape(shards, share, D).astype(BF16)
        own_taps, own_gain = 3 * D // shards, D // shards
        per = 128 // own_gain
        a, c = iota2((per * own_taps, per * 128), 1), iota2((per * own_taps, per * 128), 0)
        put_taps = ((a // 128 == c // own_taps) & (a % 128 == c % own_taps)).astype(F32)
        a, c = iota2((128, per * 128), 1), iota2((128, per * 128), 0)
        put_gain = ((a // 128 == c // own_gain) & (a % 128 == c % own_gain)).astype(F32)
        lane = iota2((1, 128), 1)
        row8 = iota2((8, 128), 0)
        shared = jnp.where(row8 == 6, d_gain[...], jnp.where((row8 == 7) & (lane == 0), loss[...], 0.0))
        for g in range(shards // per):
            top = jnp.concatenate(
                [dtaps[:, g * per * own_taps : (g + 1) * per * own_taps],
                 jnp.zeros((8 - CONV, per * own_taps), F32)], axis=0
            )
            cols = slice(g * 128, (g + 1) * 128)
            gains = jnp.where(row8 == 4, d_one[:, cols], jnp.where(row8 == 5, d_two[:, cols], 0.0))
            upper = mm(top, put_taps, 1, 0) + mm(gains, put_gain, 1, 0)
            lower = mm(d_wbeta[:, cols], put_gain, 1, 0)
            for i in range(per):
                small[g * per + i, 0:8, :] = upper[:, i * 128 : (i + 1) * 128] + shared
                small[g * per + i, 8:16, :] = lower[:, i * 128 : (i + 1) * 128]

    last = chunks + heads - 1
    half_way, done = chunks // 2 - 1, chunks - 1
    starts = link_plan(half_way, done, last, heads)
    timed = []
    for n in range(len(pieces)):
        for k in range(net.stages + 1):
            at = starts[n][k] if k < len(starts[n]) else starts[n][-1] + 2 * (k - len(starts[n]) + 1)
            timed.append((at, k != net.stages, n, k))
    timed.sort()

    def act(n, k):
        if k < net.stages:
            net.launch(k, n)
        else:
            net.finish(n, write)

    for s in sorted({t[0] for t in timed if t[0] < last}):

        @pl.when(step == s)
        def _(s=s):
            for at, _, n, k in timed:
                if at == s:
                    act(n, k)

    @pl.when(step == last)
    def _():
        for at, _, n, k in timed:
            if at == last:
                act(n, k)
        last_rows()
        give_small.start()
        tail = [(n, k) for at, _, n, k in timed if at > last]
        for i, (n, k) in enumerate(tail):
            act(n, k)
            if i < DX_PARTS:
                give_dx.start_part(i, DX_PARTS)
        give_small.wait()
        small_sum[...] = jnp.sum(small_got[...], axis=0)
        give_y.wait()
        give_dx.wait()
        for j in (chunks - 2, chunks - 1):
            cross_gu(j).wait_send()
        for s in (heads - 2, heads - 1):
            cross_in(s).wait_send()
            cross_out(s).wait_send()
        for n in range(len(pieces)):
            net.end(n, paired=n == 0)


def rear(
    d_down, sent_y, dy, resid, x, a2_t, a1_t, df, gu, wgu, wdown, gain_two, gain_one, wout, win, on, wbeta, deal, loss,
    proj, beta_pre, taps, gain, mask, segc, segr, saved, blocks, shards, collective_id,
):
    rows = x.shape[0]
    rows_mb, share = rows // blocks, rows // shards
    chunks = FF // SLICE
    anywhere = pl.BlockSpec(memory_space=pl.ANY)
    once = pl.Buffered(MIXER_BUFFERS)
    full = lambda shape: pl.BlockSpec(shape, lambda s: (0,) * len(shape))
    early = lambda s: jnp.minimum(s, chunks - 1)
    late = lambda s: jnp.maximum(s - chunks, 0)
    lane_e = lambda r, w, off=0: pl.BlockSpec((r, w), lambda s: (0, off + early(s)))
    lane_l = lambda r, w, off=0: pl.BlockSpec((r, w), lambda s: (0, off + late(s)), pipeline_mode=once)
    mat = pl.BlockSpec((1, blocks, rows_mb, rows_mb), lambda s: (late(s), 0, 0, 0), pipeline_mode=pl.Buffered(1))
    tap = lambda k: pl.BlockSpec((CONV, HEAD_DIM), lambda s: (0, k * HEADS + late(s)))
    r_down, r = FF // shards, D // shards
    a, b = chunks // 2 * 2 * SLICE, 4 * D // 2
    pieces = [(0, 0, D), (1, 0, a), (1, a, 2 * FF - a), (2, 0, b), (2, b, b), (3, 0, D)]
    shapes = [(r_down, D), (r, 2 * FF), (r, 4 * D), (r, D)]
    f32 = lambda *shape: jax.ShapeDtypeStruct(shape, F32)
    bf = lambda *shape: jax.ShapeDtypeStruct(shape, BF16)
    vm, dma = pltpu.VMEM, pltpu.SemaphoreType.DMA
    hd = HEAD_DIM
    half = shards // 2
    return pl.pallas_call(
        functools.partial(rear_kernel, shards, blocks, rows_mb, pieces),
        grid=(chunks + HEADS,),
        in_specs=[
            anywhere, anywhere, anywhere, anywhere, anywhere, anywhere, anywhere, full((rows, D)),
            lane_e(rows, SLICE), lane_e(rows, SLICE, chunks), lane_e(D, SLICE), lane_e(D, SLICE, chunks),
            pl.BlockSpec((SLICE, D), lambda s: (early(s), 0)), full((1, D)), full((1, D)),
            pl.BlockSpec((hd, D), lambda s: (late(s), 0), pipeline_mode=pl.Buffered(1)), lane_l(D, hd), lane_l(D, hd, HEADS),
            lane_l(D, hd, 2 * HEADS), lane_l(D, hd, 3 * HEADS), lane_l(rows, hd),
            full((HEADS, D)), full((rows, rows)), full((1, 1)),
            lane_l(rows, hd), lane_l(rows, hd), lane_l(rows, hd), lane_l(rows, hd), full((rows, HEADS)), tap(0),
            tap(1), tap(2), full((1, hd)), full((rows, 8)), full((rows, 1)), full((1, rows)), lane_l(rows, hd),
            mat, mat, mat, mat,
        ],
        out_specs=[full(s) for s in shapes] + [anywhere, anywhere, full((16, 128))],
        out_shape=[f32(*s) for s in shapes] + [bf(shards, share, D), bf(shards, share, D), f32(16, 128)],
        scratch_shapes=[vm((half,) + s, BF16) for s in shapes] + [
            vm((2, half, r, 2 * SLICE), BF16), vm((2, half, r, 4 * hd), BF16), vm((2, half // HEADS, r, D), BF16),
            vm((rows, D), F32), vm((rows, D), F32), vm((rows, D), F32), vm((rows, D), BF16), vm((rows, hd), F32),
            vm((rows, hd), BF16), vm((rows, hd), BF16), vm((rows, hd), BF16), vm((rows, hd), BF16),
            vm((D, rows), BF16), vm((rows, HEADS), F32), vm((CONV, 3 * D), F32), vm((1, hd), F32), vm((1, D), F32),
            vm((shards, share, D), BF16), vm((shards, 16, 128), F32), vm((shards, 16, 128), F32),
            dma, dma((3,)), dma((2,)), dma((2,)), dma((2,)),
        ] + [dma] * 9 + Scatter.semaphores(shards, len(pieces)) + Scatter.buffers(shards, shapes),
        compiler_params=pltpu.CompilerParams(
            collective_id=collective_id, has_side_effects=True, vmem_limit_bytes=62 << 20
        ),
        name="rear",
    )(d_down.reshape(half, 2, r_down, D), sent_y, dy, resid, x, a2_t, a1_t, df, gu, gu, wgu, wgu, wdown, gain_two, gain_one,
      wout, win, win, win, win, on, wbeta, deal, loss, *proj, beta_pre, taps, taps, taps, gain, mask, segc, segr,
      *saved)


def scatter_kernel(shards, count, *refs):
    grads, sent, out, got = refs[:count], refs[count], refs[count + 1 : 2 * count + 1], refs[2 * count + 1]
    refs = refs[2 * count + 2 :]
    mine, refs = refs[:count], refs[count:]
    sems, (keep, *back_sems), buffers = refs[:4], refs[4:8], refs[8:]
    here = Here(shards)
    core = here.core
    back = Exchange(here, sent, got, *back_sems)
    other, coming = Scatter.split(shards, count, buffers)
    pieces = [(i, 0, g.shape[-1]) for i, g in enumerate(grads)]

    def kept(n):
        return pltpu.make_async_copy(grads[n].at[:, core], mine[n], keep.at[n])

    net = Scatter(
        here, pieces, lambda n, parity: grads[n].at[:, parity],
        lambda i, q, cols: mine[i][q, :, cols], other, coming, sems, kept,
    )

    def write(i, at, size, value):
        out[i][:, pl.ds(at, size)] = value

    for n in range(count):
        kept(n).start()
    meet(here, True)
    for n in range(count):
        net.pair(n).start()
    back.start()
    for t in range(count + net.stages):
        for n in range(count):
            k = t - n
            if 0 <= k < net.stages:
                net.launch(k, n)
            elif k == net.stages:
                net.finish(n, write)
    back.wait()
    for n in range(count):
        net.end(n)


def scatter(grads, message, shards, collective_id):
    count = len(grads)
    shapes = [(g.shape[0] // shards, g.shape[1]) for g in grads]
    anywhere = pl.BlockSpec(memory_space=pl.ANY)
    dma = pltpu.SemaphoreType.DMA
    *out, got = pl.pallas_call(
        functools.partial(scatter_kernel, shards, count),
        in_specs=[anywhere] * (count + 1),
        out_specs=[pl.BlockSpec(memory_space=pltpu.VMEM)] * count + [anywhere],
        out_shape=[jax.ShapeDtypeStruct(s, F32) for s in shapes]
        + [jax.ShapeDtypeStruct(message.shape, message.dtype)],
        scratch_shapes=[pltpu.VMEM((shards // 2,) + s, BF16) for s in shapes]
        + Scatter.semaphores(shards, count) + [dma((count,)), dma, dma, dma]
        + Scatter.buffers(shards, shapes),
        compiler_params=pltpu.CompilerParams(
            collective_id=collective_id, has_side_effects=True, vmem_limit_bytes=60 << 20
        ),
        name="scatter_last",
    )(*[g.reshape((shards // 2, 2) + s) for g, s in zip(grads, shapes)], message)
    return out, got


def nt(left, right):
    return lax.dot_general(left, right, (((1,), (1,)), ((), ())), preferred_element_type=F32)


def tn(left, right, dtype=F32):
    return lax.dot_general(left, right, (((0,), (0,)), ((), ())), preferred_element_type=dtype)


def nn(left, right):
    return jnp.dot(left, right, preferred_element_type=F32)


def rms(v):
    inv = lax.rsqrt(jnp.mean(v * v, axis=-1, keepdims=True) + 1e-05)
    return v * inv, inv


def rms_back(normed, inv, dn):
    return inv * (dn - normed * jnp.mean(normed * dn, axis=-1, keepdims=True))


def local(
    tokens, cotangent, teacher, valid_mask, deal_rows, lengths, w_in, w_beta, conv_kernel, w_out,
    norm_gain, out_gain, ffn_gain, w_gu, w_down,
):
    shards = lax.axis_size(AXES)
    rows = tokens.shape[0]
    share = rows // shards
    blocks = lengths.shape[0]
    rows_mb = rows // blocks
    a, b, c = CONV * conv_kernel.shape[1], w_beta.shape[0] * HEADS, norm_gain.shape[0]
    small = w_beta.shape[0] * HEADS + CONV * conv_kernel.shape[1] + 2 * norm_gain.shape[0]

    if share % 8 == 0 and (D // shards) % 16 == 0:
        half = jnp.pad(
            jnp.concatenate([conv_kernel, jnp.pad(jnp.stack([norm_gain, ffn_gain]), ((0, 0), (0, conv_kernel.shape[1] - norm_gain.shape[0])))]),
            ((0, 2), (0, 128 - conv_kernel.shape[1])),
        )
        small_block = jnp.concatenate(
            [half, jnp.pad(w_beta.T, ((0, 0), (0, 128 - w_beta.shape[0])))], axis=1
        )
        gain_out = out_gain.astype(F32)[None, :]
        (win, wout, wdown, wgu, *proj, beta_pre, on, o, ainv, u, p, l, resid, a2, x, info, later, taps,
         gain_one, gain_two, wbeta, segc, segr, mask, a1, a1_t, a2_t) = front(
            [w_in, w_out, w_down, w_gu], small_block, tokens, jnp.concatenate([cotangent, teacher], axis=1),
            deal_rows, valid_mask, lengths, gain_out, shards, 0,
        )
        win, wout, wdown, wgu = (w.reshape(-1, w.shape[-1]) for w in (win, wout, wdown, wgu))
        saved = (o, ainv, u, p, l)
        place = info[:, 1].astype(jnp.int32)
        counted = jnp.sum(info[::share, 2])
        g, t = later[:, :D], later[:, D:]
        target = deal_rows // rows
        ahead = (target[None, :] == target[:, None]) & (
            jnp.arange(rows)[None, :] < jnp.arange(rows)[:, None]
        )
        slot = target * share + jnp.sum(ahead.astype(jnp.int32), axis=1)
        sort_t = (slot[:, None] == jnp.arange(rows)[None, :]).astype(BF16)
        deal_t = (place[:, None] == jnp.arange(rows)[None, :]).astype(BF16)
        deal = (place[None, :] == jnp.arange(rows)[:, None]).astype(BF16)
        m = jnp.sum(deal.astype(F32) * info[:, 0][None, :], axis=1, keepdims=True)
        gain_one, gain_two = gain_one[0], gain_two[0]
    else:
        target = deal_rows // rows
        spot = deal_rows % rows
        ahead = (target[None, :] == target[:, None]) & (
            jnp.arange(rows)[None, :] < jnp.arange(rows)[:, None]
        )
        slot = target * share + jnp.sum(ahead.astype(jnp.int32), axis=1)
        sort_t = (slot[:, None] == jnp.arange(rows)[None, :]).astype(BF16)
        sort = (slot[None, :] == jnp.arange(rows)[:, None]).astype(BF16)
        count_own = jnp.sum(valid_mask.astype(F32))
        lane = jnp.arange(128)[None, :]
        notes = jnp.where(
            lane == 0,
            valid_mask.astype(F32)[:, None],
            jnp.where(lane == 1, spot.astype(F32)[:, None], jnp.where(lane == 2, count_own, 0.0)),
        ).astype(BF16)
        packed = jnp.concatenate(
            [conv_kernel.reshape(-1), w_beta.reshape(-1), norm_gain, ffn_gain,
             jnp.zeros((share * 128 - small,), BF16)]
        ).reshape(1, share, 128)
        sorted_rows = nn(sort, jnp.concatenate([tokens, notes], axis=1)).astype(BF16)
        message = jnp.concatenate(
            [sorted_rows.reshape(shards, share, -1), jnp.broadcast_to(packed, (shards, share, 128))],
            axis=2,
        )
        later = nn(sort, jnp.concatenate([cotangent, teacher], axis=1)).astype(BF16)
        later = later.reshape(shards, share, 2 * D)
        (win, wout), arrived = first([w_in, w_out], (2, 1), message, shards, 0)

        flat = arrived.reshape(rows, -1)
        info = flat[:, D : D + 128].astype(F32)
        place = info[:, 1].astype(jnp.int32)
        counted = jnp.sum(arrived[:, 0, D + 2].astype(F32))
        extra = arrived[:, :, D + 128 :].reshape(shards, share * 128)
        taps = extra[:, :a].reshape(shards, CONV, -1).swapaxes(0, 1).reshape(CONV, 3 * D).astype(F32)
        wbeta = extra[:, a : a + b].reshape(D, HEADS)
        gain_one = extra[:, a + b : a + b + c].reshape(D).astype(F32)
        gain_two = extra[:, a + b + c : a + b + 2 * c].reshape(D).astype(F32)
        deal = (place[None, :] == jnp.arange(rows)[:, None]).astype(BF16)
        deal_t = (place[:, None] == jnp.arange(rows)[None, :]).astype(BF16)
        dealt = nn(deal, flat[:, : D + 128])
        x = dealt[:, :D]
        m = dealt[:, D : D + 1]

        ends = jnp.cumsum(lengths, axis=1)
        within = jnp.arange(rows_mb, dtype=jnp.int32)
        seg = jnp.sum((within[None, :, None] >= ends[:, None, :]).astype(jnp.int32), axis=2)
        seg = (seg + (lengths.shape[1] + 1) * jnp.arange(blocks, dtype=jnp.int32)[:, None]).reshape(rows)
        position = jnp.arange(rows, dtype=jnp.int32)
        mask = jnp.stack(
            [jnp.ones((rows,), F32)]
            + [((position >= s) & (jnp.roll(seg, s) == seg)).astype(F32) for s in range(1, CONV)]
            + [jnp.zeros((rows,), F32)] * (8 - CONV),
            axis=1,
        )
        segc, segr = seg[:, None], seg[None, :]
        gain_out = out_gain.astype(F32)[None, :]

        nx, rx = rms(x)
        a1 = (nx * gain_one).astype(BF16)
        wdown, wgu, later, (*proj, beta_pre, on, o, ainv, u, p, l, resid, a2) = forward(
            w_down, w_gu, later, (1, 2), a1, win, wout, wbeta, x, gain_two[None, :], taps, gain_out, mask, segc,
            segr, blocks, shards, 2,
        )
        saved = (o, ainv, u, p, l)
        later = nn(deal, later.reshape(rows, 2 * D))
        g, t = later[:, :D], later[:, D:]
    gu = nn(a2, wgu)
    gate, up = gu[:, :FF], gu[:, FF:]
    hid = (gate * sigmoid(gate) * up).astype(BF16)
    y = resid + nn(hid, wdown)
    errors = y - t
    loss_part = jnp.sum(m * errors * errors)
    dy = g + (rows * shards / counted) * m * errors
    df = dy.astype(BF16)
    if share % 8 == 0 and (D // shards) % 16 == 0:
        sent_y = nn(deal_t, y.astype(BF16)).astype(BF16).reshape(shards, share, D)
        g_down, g_gu, g_in, g_out, got_y, got_dx, summed = rear(
            tn(hid, df, BF16), sent_y, dy, resid, x, a2_t, a1_t, df, gu, wgu, wdown, gain_two[None, :], gain_one[None, :],
            wout, win, on, wbeta, deal_t, loss_part.reshape(1, 1), proj, beta_pre, taps, gain_out, mask, segc,
            segr, saved, blocks, shards, 1,
        )
        output = nn(sort_t, got_y.reshape(rows, D)).astype(BF16)
        input_grad = nn(sort_t, got_dx.reshape(rows, D)).astype(BF16)
        own = D // shards
        g_taps = summed[:CONV, : 3 * own]
        g_gain_one, g_gain_two = summed[4, :own], summed[5, :own]
        g_gain_out, loss = summed[6], summed[7, 0] / (D * counted)
        g_beta = summed[8:, :own].T
    else:
        (g_down, g_gu, dwq, dwk, dwv, dwg, dw_out, d_wbeta, dx, d_gain_two, d_gain_one, dtq, dtk, dtv,
         d_gain_out) = backward(
            tn(hid, df, BF16), df, a2, gu, wgu, wdown, dy, resid, gain_two[None, :], wout, win, a1, on, x,
            gain_one[None, :], wbeta, proj, beta_pre, taps, gain_out, mask, segc, segr, saved, blocks, shards,
            1,
        )
        back = jnp.concatenate([y.astype(BF16), dx], axis=1)
        back = nn(deal_t, back).astype(BF16).reshape(shards, share, 2 * D)
        (g_out, *g_in), back = scatter([dw_out, dwq, dwk, dwv, dwg], back, shards, 3)
        g_in = jnp.concatenate(g_in, axis=1)
        back = nn(sort_t, back.reshape(rows, 2 * D)).astype(BF16)
        output, input_grad = back[:, :D], back[:, D:]

        d_taps = jnp.concatenate([dtq, dtk, dtv], axis=1)
        tail = jnp.concatenate([d_gain_out.reshape(-1), loss_part.reshape(1)])
        extra = jnp.concatenate(
            [
                d_taps.reshape(CONV, shards, -1).swapaxes(0, 1).reshape(shards, a),
                d_wbeta.reshape(shards, b),
                d_gain_one.reshape(shards, c),
                d_gain_two.reshape(shards, c),
                jnp.broadcast_to(tail[None], (shards, tail.shape[0])),
            ],
            axis=1,
        )
        padded = -(-extra.shape[1] // 128) * 128
        extra = jnp.pad(extra, ((0, 0), (0, padded - extra.shape[1])))
        summed = jnp.sum(
            lax.all_to_all(
                extra.reshape(shards, padded // 128, 128), AXES, split_axis=0, concat_axis=0, tiled=True
            ),
            axis=0,
        ).reshape(-1)
        g_taps = summed[:a].reshape(CONV, -1)
        g_beta = summed[a : a + b].reshape(-1, HEADS)
        g_gain_one = summed[a + b : a + b + c]
        g_gain_two = summed[a + b + c : a + b + 2 * c]
        g_gain_out = summed[a + b + 2 * c : a + b + 2 * c + HEAD_DIM]
        loss = summed[a + b + 2 * c + HEAD_DIM] / (D * counted)

    return (
        output, input_grad, g_in, g_beta, g_taps, g_out, g_gain_one, g_gain_out, g_gain_two, g_gu,
        g_down, loss,
    )


def solution(mesh):
    both = P(AXES, None)
    flat = P(AXES)
    in_specs = (both, both, both, flat, flat, both, both, both, P(None, AXES), both, flat, P(), flat,
                both, both)
    out_specs = (both, both, both, both, P(None, AXES), both, flat, P(), flat, both, both, P())
    return jax.shard_map(local, mesh=mesh, in_specs=in_specs, out_specs=out_specs, check_vma=False)
```

```python
import functools

import jax
import jax.numpy as jnp
from jax import lax
from jax.experimental import pallas as pl
from jax.experimental.pallas import tpu as pltpu
from jax.sharding import PartitionSpec as P

D = 1024
HEADS = 8
HEAD_DIM = 128
FF = 2816
CONV = 4
AXES = ("dp", "fsdp")
F32 = jnp.float32
BF16 = jnp.bfloat16
PAIR = 2
MESH = pl.DeviceIdType.MESH


def mm(left, right, lc, rc):
    return lax.dot_general(
        left,
        right,
        (((lc,), (rc,)), ((), ())),
        precision=lax.Precision.HIGHEST,
        preferred_element_type=F32,
    )


def sigmoid(v):
    return 1.0 / (1.0 + jnp.exp(-v))


def iota2(shape, axis):
    return lax.broadcasted_iota(jnp.int32, shape, axis)


def unit_lower_inverses(mats, size):
    row, col = iota2((size, size), 0), iota2((size, size), 1)
    eye = (row == col).astype(F32)
    inverses = None
    width = 1
    while width < size:
        corner = ((row // (2 * width)) == (col // (2 * width))) & (
            (row // width) == (col // width) + 1
        )
        edges = [jnp.where(corner, m, 0.0) for m in mats]
        if inverses is None:
            inverses = [eye - e for e in edges]
        else:
            right = [mm(e, x, 1, 0) for e, x in zip(edges, inverses)]
            inverses = [x - mm(x, r, 1, 0) for x, r in zip(inverses, right)]
        width *= 2
    return inverses


def conv_parts(src, taps, masks):
    rolled = [src]
    total = src * taps[CONV - 1 : CONV, :]
    for s in range(1, CONV):
        moved = pltpu.roll(src, s, 0) * masks[s]
        rolled.append(moved)
        total = total + moved * taps[CONV - 1 - s : CONV - s, :]
    return total, rolled


def l2_norm(c):
    inv = lax.rsqrt(jnp.sum(c * c, axis=-1, keepdims=True) + 1e-06)
    return c * inv, inv


def mixer_fwd_kernel(
    blocks, rows_mb,
    pq, pk, pv, pg, beta, tq, tk, tv, gain, mask, segc, segr,
    on_ref, o_ref, ainv_ref, u_ref, p_ref, l_ref,
):
    step = pl.program_id(0)
    masks = [None] + [mask[:, s : s + 1] for s in range(1, CONV)]
    cs = []
    for src, taps in ((pq, tq), (pk, tk), (pv, tv)):
        pre, _ = conv_parts(src[...], taps[...], masks)
        cs.append(pre * sigmoid(pre))
    cq, ck, cv = cs
    strengths = sigmoid(beta[...])
    lane = iota2(strengths.shape, 1)
    gate = pg[...]
    gate = gate * sigmoid(gate)
    row, col = iota2((rows_mb, rows_mb), 0), iota2((rows_mb, rows_mb), 1)
    systems = [(h, b) for h in range(PAIR) for b in range(blocks)]
    qs, ks, vs, bs, sames, lows = [], [], [], [], [], []
    for h, b in systems:
        rs = slice(b * rows_mb, (b + 1) * rows_mb)
        hs = slice(h * HEAD_DIM, (h + 1) * HEAD_DIM)
        q, _ = l2_norm(cq[rs, hs])
        k, _ = l2_norm(ck[rs, hs])
        qs.append(q * HEAD_DIM ** (-0.5))
        ks.append(k)
        vs.append(cv[rs, hs])
        bs.append(
            jnp.sum(jnp.where(lane == step * PAIR + h, strengths, 0.0), axis=1, keepdims=True)[rs]
        )
        sames.append(segc[rs, :] == segr[:, rs])
    for i in range(len(systems)):
        lows.append(jnp.where(sames[i] & (row > col), mm(ks[i], ks[i], 1, 1), 0.0))
    inverses = unit_lower_inverses([l * b for l, b in zip(lows, bs)], rows_mb)
    us = [mm(a, v * b, 1, 0) for a, v, b in zip(inverses, vs, bs)]
    ps = [
        jnp.where(same & (row >= col), mm(q, k, 1, 1), 0.0)
        for q, k, same in zip(qs, ks, sames)
    ]
    os = [mm(p, u, 1, 0) for p, u in zip(ps, us)]
    for i, (h, b) in enumerate(systems):
        rs = slice(b * rows_mb, (b + 1) * rows_mb)
        hs = slice(h * HEAD_DIM, (h + 1) * HEAD_DIM)
        o = os[i]
        inv = lax.rsqrt(jnp.mean(o * o, axis=-1, keepdims=True) + 1e-05)
        on_ref[rs, hs] = (o * inv * gain[...] * gate[rs, hs]).astype(BF16)
        o_ref[rs, hs] = o
        ainv_ref[h, b] = inverses[i]
        u_ref[h, b] = us[i]
        p_ref[h, b] = ps[i]
        l_ref[h, b] = lows[i]


def mixer_bwd_kernel(
    blocks, rows_mb, pair, step,
    pq, pk, pv, pg, beta, tq, tk, tv, gain, mask, segc, segr,
    don_ref, o_ref, ainv_ref, u_ref, p_ref, l_ref,
    dq_ref, dk_ref, dv_ref, dg_ref, dbeta_ref, dtq, dtk, dtv, dgain_ref,
):
    rows = blocks * rows_mb
    masks = [None] + [mask[:, s : s + 1] for s in range(1, CONV)]
    pres, rolls, cs, sig = [], [], [], []
    for src, taps in ((pq, tq), (pk, tk), (pv, tv)):
        pre, rolled = conv_parts(src[...], taps[...], masks)
        s = sigmoid(pre)
        pres.append(pre)
        rolls.append(rolled)
        sig.append(s)
        cs.append(pre * s)
    cq, ck, cv = cs
    strengths = sigmoid(beta[...])
    lane = iota2(strengths.shape, 1)
    row, col = iota2((rows_mb, rows_mb), 0), iota2((rows_mb, rows_mb), 1)
    gates = pg[...]
    gsig = sigmoid(gates)
    gate = gates * gsig
    dgate = gsig * (1.0 + gates * (1.0 - gsig))
    systems = [(h, b) for h in range(pair) for b in range(blocks)]
    part = []
    dgain = jnp.zeros((1, HEAD_DIM), F32)
    for h, b in systems:
        rs = slice(b * rows_mb, (b + 1) * rows_mb)
        hs = slice(h * HEAD_DIM, (h + 1) * HEAD_DIM)
        k, ik = l2_norm(ck[rs, hs])
        qn, iq = l2_norm(cq[rs, hs])
        v = cv[rs, hs]
        bb = jnp.sum(jnp.where(lane == step * pair + h, strengths, 0.0), axis=1, keepdims=True)[rs]
        same = segc[rs, :] == segr[:, rs]
        o = o_ref[rs, hs]
        don = don_ref[rs, hs]
        inv = lax.rsqrt(jnp.mean(o * o, axis=-1, keepdims=True) + 1e-05)
        no = o * inv
        scaled = don * gain[...]
        dg_ref[rs, hs] = (scaled * no * dgate[rs, hs]).astype(BF16)
        dgain = dgain + jnp.sum(don * no * gate[rs, hs], axis=0, keepdims=True)
        dno = scaled * gate[rs, hs]
        do = inv * (dno - no * jnp.mean(no * dno, axis=-1, keepdims=True))
        part.append([q_ for q_ in (qn, iq, k, ik, v, bb, same, do)])
    dus = [mm(p_ref[h, b], part[i][7], 0, 0) for i, (h, b) in enumerate(systems)]
    dps = [
        jnp.where(part[i][6] & (row >= col), mm(part[i][7], u_ref[h, b], 1, 1), 0.0)
        for i, (h, b) in enumerate(systems)
    ]
    drs = [mm(ainv_ref[h, b], dus[i], 0, 0) for i, (h, b) in enumerate(systems)]
    scale = HEAD_DIM ** (-0.5)
    dqs = [mm(dps[i], part[i][2], 1, 0) * scale for i in range(len(systems))]
    das = [mm(drs[i], u_ref[h, b], 1, 1) for i, (h, b) in enumerate(systems)]
    dks = [mm(dps[i], part[i][0] * scale, 0, 0) for i in range(len(systems))]
    dgs = []
    for i in range(len(systems)):
        g = jnp.where(part[i][6] & (row > col), das[i] * (-part[i][5]), 0.0)
        dgs.append(g + g.T)
    dks = [dks[i] + mm(dgs[i], part[i][2], 1, 0) for i in range(len(systems))]
    dbeta = jnp.zeros(strengths.shape, F32)
    dcs = [[], [], []]
    for i, (h, b) in enumerate(systems):
        qn, iq, k, ik, v, bb, same, do = part[i]
        dv = drs[i] * bb
        db = jnp.sum(drs[i] * v - das[i] * l_ref[h, b], axis=-1, keepdims=True)
        dbp = db * bb * (1.0 - bb)
        pieces = [dbp if b == c else jnp.zeros((rows_mb, 1), F32) for c in range(blocks)]
        column = jnp.concatenate(pieces, axis=0) if blocks > 1 else dbp
        dbeta = dbeta + jnp.where(lane == step * pair + h, column, 0.0)
        dcs[0].append(iq * (dqs[i] - qn * jnp.sum(qn * dqs[i], axis=-1, keepdims=True)))
        dcs[1].append(ik * (dks[i] - k * jnp.sum(k * dks[i], axis=-1, keepdims=True)))
        dcs[2].append(dv)
    for j, (out, dtap, taps) in enumerate(((dq_ref, dtq, tq), (dk_ref, dtk, tk), (dv_ref, dtv, tv))):
        whole = jnp.concatenate(
            [
                jnp.concatenate([dcs[j][h * blocks + b] for b in range(blocks)], axis=0)
                for h in range(pair)
            ],
            axis=1,
        )
        dpre = whole * (sig[j] * (1.0 + pres[j] * (1.0 - sig[j])))
        tap = taps[...]
        grad = dpre * tap[CONV - 1 : CONV, :]
        dtap[CONV - 1 : CONV, :] = jnp.sum(dpre * rolls[j][0], axis=0, keepdims=True)
        for s in range(1, CONV):
            dtap[CONV - 1 - s : CONV - s, :] = jnp.sum(dpre * rolls[j][s], axis=0, keepdims=True)
            grad = grad + pltpu.roll(dpre * masks[s], rows - s, 0) * tap[CONV - 1 - s : CONV - s, :]
        out[...] = grad.astype(BF16)

    @pl.when(step == 0)
    def _():
        dbeta_ref[...] = jnp.zeros_like(dbeta_ref)
        dgain_ref[...] = jnp.zeros_like(dgain_ref)

    dbeta_ref[...] += dbeta
    dgain_ref[...] += dgain


def mixer_specs(rows, blocks, rows_mb):
    width = PAIR * HEAD_DIM
    per = D // width
    col = lambda k: pl.BlockSpec((rows, width), lambda i, k=k: (0, k * per + i))
    tap = lambda k: pl.BlockSpec((CONV, width), lambda i, k=k: (0, k * per + i))
    full = lambda shape: pl.BlockSpec(shape, lambda i: (0,) * len(shape))
    ins = [col(0), col(1), col(2), col(3), full((rows, HEADS)), tap(0), tap(1), tap(2),
           full((1, HEAD_DIM)), full((rows, 8)), full((rows, 1)), full((1, rows))]
    mat = pl.BlockSpec((PAIR, blocks, rows_mb, rows_mb), lambda i: (i, 0, 0, 0))
    one = pl.BlockSpec((rows, width), lambda i: (0, i))
    otap = pl.BlockSpec((CONV, width), lambda i: (0, i))
    return ins, mat, one, otap, full


def lin_index():
    return lax.axis_index("dp") * lax.axis_size("fsdp") + lax.axis_index("fsdp")


def mesh_id(index):
    inner = lax.axis_size("fsdp")
    return (lax.div(index, inner), lax.rem(index, inner))


class Here:
    def __init__(self, shards):
        self.shards, self.me = shards, lin_index()
        self.bits = shards.bit_length() - 1
        own = [lax.rem(lax.div(self.me, 1 << b), 2) for b in range(self.bits)]
        self.core = own[0]
        self.change = [(1 - 2 * o) * (1 << b) for b, o in enumerate(own)]
        self.partner = [mesh_id(self.me + c) for c in self.change]

    def flip(self, bits, number, always=()):
        result = self.me
        for bit in always:
            result = result + self.change[bit]
        for i, bit in enumerate(reversed(bits)):
            if isinstance(number, int):
                if (number >> i) & 1:
                    result = result + self.change[bit]
            else:
                result = result + lax.rem(lax.div(number, 1 << i), 2) * self.change[bit]
        return result


def routes(shards):
    bits = shards.bit_length() - 1
    rest = list(range(4, bits))
    return [[1, 2, 3] + rest, [2, 3, 1] + rest, [3, 1, 2] + rest]


def colours(width, turn):
    tiles = width // 128
    one, three = round(tiles * 0.36), round(tiles * 0.28)
    sizes = (one, tiles - one - three, three)
    return [(sum(sizes[:c]) * 128, sizes[c] * 128) for c in range(3)]


def meet(here, everyone):
    barrier = pltpu.get_barrier_semaphore()
    if everyone:

        def greet(r, _):
            peer = lax.rem(here.me + r, here.shards)
            pl.semaphore_signal(barrier, inc=1, device_id=mesh_id(peer), device_id_type=MESH)
            return 0

        lax.fori_loop(1, here.shards, greet, 0)
        pl.semaphore_wait(barrier, here.shards - 1)
    else:
        for partner in here.partner:
            pl.semaphore_signal(barrier, inc=1, device_id=partner, device_id_type=MESH)
        pl.semaphore_wait(barrier, here.bits)


def spread_order(shards):
    bits = shards.bit_length() - 1
    turned = [sum(((i >> b) & 1) << (bits - 1 - b) for b in range(bits)) for i in range(shards)]
    return turned[1:]


class Exchange:
    def __init__(self, here, sent, got, send, recv, keep, same=False):
        self.here, self.shards, self.me, self.got = here, here.shards, here.me, got
        self.block = (lambda d: sent) if same else (lambda d: sent.at[d])
        self.send, self.recv, self.keep = send, recv, keep

    def own(self):
        return pltpu.make_async_copy(self.block(self.me), self.got.at[self.me], self.keep)

    def start(self):
        self.own().start()

        def one(r, _):
            peer = lax.rem(self.me + r, self.shards)
            pltpu.make_async_remote_copy(
                src_ref=self.block(peer), dst_ref=self.got.at[self.me], send_sem=self.send,
                recv_sem=self.recv, device_id=mesh_id(peer), device_id_type=MESH,
            ).start()
            return 0

        lax.fori_loop(1, self.shards, one, 0)

    def start_part(self, part, parts):
        others = self.shards - 1
        if part == 0:
            self.own().start()
        for r in range(others * part // parts, others * (part + 1) // parts):
            peer = lax.rem(self.me + spread_order(self.shards)[r], self.shards)
            pltpu.make_async_remote_copy(
                src_ref=self.block(peer), dst_ref=self.got.at[self.me], send_sem=self.send,
                recv_sem=self.recv, device_id=mesh_id(peer), device_id_type=MESH,
            ).start()

    def wait(self):
        self.own().wait()
        whole = pl.ds(0, self.shards - 1)
        pltpu.make_async_remote_copy(
            src_ref=self.got.at[whole], dst_ref=self.got.at[whole], send_sem=self.send,
            recv_sem=self.recv, device_id=self.here.partner[0], device_id_type=MESH,
        ).wait()


DEAL_AT = 0
CHUNK = 256
X_STEPS = 5
GT_FROM = 6
SLICE = 256
MIXER_BUFFERS = 2
DX_PARTS = 6


def pieces_of(widths, split):
    result = []
    for i, width in enumerate(widths):
        tiles, at = width // 128, 0
        for j in range(split[i]):
            size = tiles // split[i] + (1 if j < tiles % split[i] else 0)
            result.append((i, at * 128, size * 128))
            at += size
    return result


class Gather:
    def __init__(self, here, pieces, own, full, sems):
        self.here, self.pieces, self.own, self.full = here, pieces, own, full
        self.send, self.recv, self.pair_send, self.pair_recv, self.keep = sems
        self.stages = here.bits - 1
        self.order = routes(here.shards)
        self.core = here.core
        self.cuts = [
            [(at + a, s) for a, s in colours(size, n)] for n, (_, at, size) in enumerate(pieces)
        ]
        self.last = len(pieces) + self.stages - 1

    @staticmethod
    def semaphores(shards, pieces):
        dma, stages = pltpu.SemaphoreType.DMA, shards.bit_length() - 2
        number = len(pieces)
        return [dma((stages, number, 3)), dma((stages, number, 3)), dma((number,)), dma((number,)),
                dma((number,))]

    def kept(self, i):
        return pltpu.make_async_copy(
            self.own[i], self.full[i].at[lax.div(self.here.me, 2), self.core], self.keep.at[i]
        )

    def begin(self):
        for i in range(len(self.own)):
            self.kept(i).start()

    def partner(self, k, c):
        return self.here.partner[self.order[c][self.stages - 1 - k]]

    def group(self, k, n, c):
        at, size = self.cuts[n][c]
        some = self.full[self.pieces[n][0]].at[pl.ds(0, 1 << k), 0, :, pl.ds(at, size)]
        return pltpu.make_async_remote_copy(
            src_ref=some, dst_ref=some, send_sem=self.send.at[k, n, c],
            recv_sem=self.recv.at[k, n, c], device_id=self.partner(k, c), device_id_type=MESH,
        )

    def half(self, n):
        i, at, size = self.pieces[n]
        some = self.full[i].at[:, self.core, :, pl.ds(at, size)]
        return pltpu.make_async_remote_copy(
            src_ref=some, dst_ref=some, send_sem=self.pair_send.at[n],
            recv_sem=self.pair_recv.at[n], device_id=self.here.partner[0],
            device_id_type=MESH,
        )

    def launch(self, k, n):
        i = self.pieces[n][0]
        for c in range(3):
            at, size = self.cuts[n][c]
            if k > 0:
                self.group(k - 1, n, c).wait_recv()
            have = self.order[c][self.stages - k :]
            for j in range(1 << k):
                d = self.here.flip(have, j)
                there = self.full[i].at[lax.div(d, 2), self.core, :, pl.ds(at, size)]
                pltpu.make_async_remote_copy(
                    src_ref=self.own[i].at[:, pl.ds(at, size)] if j == 0 else there,
                    dst_ref=there, send_sem=self.send.at[k, n, c], recv_sem=self.recv.at[k, n, c],
                    device_id=self.partner(k, c), device_id_type=MESH,
                ).start()

    def finish(self, n):
        for c in range(3):
            self.group(self.stages - 1, n, c).wait_recv()
        if n == 0 or self.pieces[n - 1][0] != self.pieces[n][0]:
            self.kept(self.pieces[n][0]).wait()
        self.half(n).start()

    def slots(self, first, last):
        return sum(
            0 <= t - n <= self.stages for t in range(first, last) for n in range(len(self.pieces))
        )

    def step(self, t, between=None):
        for n in range(len(self.pieces)):
            k = t - n
            if 0 <= k < self.stages:
                self.launch(k, n)
            elif k == self.stages:
                self.finish(n)
            if between is not None and 0 <= k <= self.stages:
                between()

    def end(self, arrived=0):
        for k in range(self.stages):
            for n in range(len(self.pieces)):
                for c in range(3):
                    self.group(k, n, c).wait_send()
        for n in range(len(self.pieces)):
            self.half(n).wait_send()
            if n >= arrived:
                self.half(n).wait_recv()


def first_kernel(shards, pieces, *refs):
    count = 1 + max(i for i, _, _ in pieces)
    own, sent, full, got = refs[:count], refs[count], refs[count + 1 : 2 * count + 1], refs[2 * count + 1]
    sems = refs[2 * count + 2 :]
    here = Here(shards)
    deal = Exchange(here, sent, got, *sems[5:])
    weights = Gather(here, pieces, own, full, sems[:5])
    weights.begin()
    meet(here, True)
    deal.start()
    for t in range(weights.last + 1):
        weights.step(t)
    deal.wait()
    weights.end()


def spread(weight, shards):
    return jax.ShapeDtypeStruct((shards // 2, 2) + weight.shape, weight.dtype)


def first(weights, split, message, shards, collective_id):
    count = len(weights)
    anywhere = pl.BlockSpec(memory_space=pl.ANY)
    pieces = pieces_of([w.shape[1] for w in weights], split)
    dma = pltpu.SemaphoreType.DMA
    *full, got = pl.pallas_call(
        functools.partial(first_kernel, shards, pieces),
        in_specs=[anywhere] * (count + 1),
        out_specs=[anywhere] * (count + 1),
        out_shape=[spread(w, shards) for w in weights]
        + [jax.ShapeDtypeStruct(message.shape, message.dtype)],
        scratch_shapes=Gather.semaphores(shards, pieces) + [dma, dma, dma],
        compiler_params=pltpu.CompilerParams(collective_id=collective_id, has_side_effects=True),
        name="gather_first",
    )(*weights, message)
    return [f.reshape(-1, f.shape[-1]) for f in full], got


def forward_kernel(
    shards, pieces, blocks, rows_mb,
    own_down, own_gu, sent, a1, wq, wk, wv, wg, wout, wbeta, x, gain_two, tq, tk, tv, gain, mask,
    segc, segr,
    full_down, full_gu, got, pq, pk, pv, pg, beta, on, o, ainv, u, p, l, resid, a2,
    *sems,
):
    step = pl.program_id(0)
    steps = HEADS // PAIR
    here = Here(shards)
    weights = Gather(here, pieces, (own_down, own_gu), (full_down, full_gu), sems[:5])
    deal = Exchange(here, sent, got, *sems[5:])

    @pl.when(step == 0)
    def _():
        weights.begin()
        meet(here, True)
        weights.step(0)
        resid[...] = x[...]

    normed = a1[...]
    beta[...] = jnp.dot(normed, wbeta[...], preferred_element_type=F32)
    for out, w in ((pq, wq), (pk, wk), (pv, wv), (pg, wg)):
        out[...] = jnp.dot(normed, w[...], preferred_element_type=F32)
    mixer_fwd_kernel(
        blocks, rows_mb, pq, pk, pv, pg, beta, tq, tk, tv, gain, mask, segc, segr, on, o, ainv, u,
        p, l,
    )
    resid[...] += jnp.dot(on[...], wout[...], preferred_element_type=F32)
    for s in range(steps):

        @pl.when(step == s)
        def _(s=s):
            weights.step(s + 1)
            if s == DEAL_AT:
                deal.start()
            if s == steps - 1:
                r = resid[...]
                a2[...] = (rms(r)[0] * gain_two[...]).astype(BF16)
                for t in range(steps + 1, weights.last + 1):
                    weights.step(t)
                deal.wait()
                weights.end()


def forward(
    w_down, w_gu, message, split, a1, win, wout, wbeta, x, gain_two, taps, gain, mask, segc, segr, blocks,
    shards, collective_id,
):
    rows = x.shape[0]
    rows_mb = rows // blocks
    width = PAIR * HEAD_DIM
    pieces = pieces_of([w_down.shape[1], w_gu.shape[1]], split)
    anywhere = pl.BlockSpec(memory_space=pl.ANY)
    ins, mat, one, _, full = mixer_specs(rows, blocks, rows_mb)
    per = D // width
    wcol = lambda k: pl.BlockSpec((D, width), lambda i, k=k: (0, k * per + i))
    square = jax.ShapeDtypeStruct((HEADS, blocks, rows_mb, rows_mb), F32)
    wide = jax.ShapeDtypeStruct((rows, D), F32)
    dma = pltpu.SemaphoreType.DMA
    full_down, full_gu, got, *rest = pl.pallas_call(
        functools.partial(forward_kernel, shards, pieces, blocks, rows_mb),
        grid=(HEADS // PAIR,),
        in_specs=[
            anywhere, anywhere, anywhere, full((rows, D)), wcol(0), wcol(1), wcol(2), wcol(3),
            pl.BlockSpec((width, D), lambda i: (i, 0)), full((D, HEADS)), full((rows, D)),
            full((1, D)), *ins[5:],
        ],
        out_specs=[anywhere, anywhere, anywhere, one, one, one, one, full((rows, HEADS)), one, one, mat, mat,
                   mat, mat, full((rows, D)), full((rows, D))],
        out_shape=[
            spread(w_down, shards), spread(w_gu, shards),
            jax.ShapeDtypeStruct(message.shape, message.dtype), wide, wide, wide, wide,
            jax.ShapeDtypeStruct((rows, HEADS), F32), jax.ShapeDtypeStruct((rows, D), BF16), wide,
            square, square, square, square, wide, jax.ShapeDtypeStruct((rows, D), BF16),
        ],
        scratch_shapes=Gather.semaphores(shards, pieces) + [dma, dma, dma],
        compiler_params=pltpu.CompilerParams(
            collective_id=collective_id, has_side_effects=True, vmem_limit_bytes=48 << 20
        ),
        name="mixer_forward",
    )(w_down, w_gu, message, a1, win, win, win, win, wout, wbeta, x, gain_two, taps, taps, taps, gain, mask,
      segc, segr)
    return full_down.reshape(FF, D), full_gu.reshape(D, 2 * FF), got, rest


class Scatter:
    def __init__(self, here, pieces, whole, mine, other, coming, sems, kept):
        self.here, self.pieces, self.whole, self.mine = here, pieces, whole, mine
        self.other, self.coming, self.kept_of = other, coming, kept
        self.send, self.recv, self.pair_send, self.pair_recv = sems
        self.stages = here.bits - 1
        self.order = routes(here.shards)
        self.core = here.core
        self.cuts = [
            [(at + a, s) for a, s in colours(size, n)] for n, (_, at, size) in enumerate(pieces)
        ]

    @staticmethod
    def semaphores(shards, number):
        dma, stages = pltpu.SemaphoreType.DMA, shards.bit_length() - 2
        return [dma((stages, number, 3)), dma((stages, number, 3)), dma((number,)), dma((number,))]

    @staticmethod
    def buffers(shards, shapes):
        stages = shards.bit_length() - 2
        return [pltpu.VMEM((shards // 2,) + s, BF16) for s in shapes] + [
            pltpu.VMEM((1 << (stages - 1 - k),) + s, BF16) for s in shapes for k in range(stages)
        ]

    @staticmethod
    def split(shards, count, refs):
        stages = shards.bit_length() - 2
        other, refs = refs[:count], refs[count:]
        return other, [refs[i * stages : (i + 1) * stages] for i in range(count)]

    def pair(self, n):
        i, at, size = self.pieces[n]
        return pltpu.make_async_remote_copy(
            src_ref=self.whole(n, 1 - self.core), dst_ref=self.other[i].at[:, :, pl.ds(at, size)],
            send_sem=self.pair_send.at[n], recv_sem=self.pair_recv.at[n],
            device_id=self.here.partner[0], device_id_type=MESH,
        )

    def hop(self, k, n, c, source, spots):
        i = self.pieces[n][0]
        at, size = self.cuts[n][c]
        cols = pl.ds(at, size)
        return pltpu.make_async_remote_copy(
            src_ref=self.other[i].at[source, :, cols],
            dst_ref=self.coming[i][k].at[spots, :, cols],
            send_sem=self.send.at[k, n, c], recv_sem=self.recv.at[k, n, c],
            device_id=self.here.partner[self.order[c][k]], device_id_type=MESH,
        )

    def group(self, k, n, c):
        all_of = pl.ds(0, 1 << (self.stages - 1 - k))
        return self.hop(k, n, c, all_of, all_of)

    def total(self, k, n, c, shard, spot):
        i = self.pieces[n][0]
        at, size = self.cuts[n][c]
        cols = pl.ds(at, size)
        q = lax.div(shard, 2)
        value = self.mine(i, q, cols).astype(F32) + self.other[i][q, :, cols].astype(F32)
        for p in range(k):
            value = value + self.coming[i][p][spot, :, cols].astype(F32)
        return value

    def launch(self, k, n):
        if k == 0:
            kept = self.kept_of(n)
            if kept is not None:
                kept.wait()
            self.pair(n).wait_recv()
        for c in range(3):
            if k > 0:
                self.group(k - 1, n, c).wait_recv()
            much = 1 << (self.stages - 1 - k)
            at, size = self.cuts[n][c]

            def body(j, _, c=c, at=at, size=size):
                shard = self.here.flip(self.order[c][k + 1 :], j, (self.order[c][k],))
                q = lax.div(shard, 2)
                self.other[self.pieces[n][0]][q, :, pl.ds(at, size)] = self.total(
                    k, n, c, shard, much + j
                ).astype(BF16)
                self.hop(k, n, c, q, j).start()
                return 0

            lax.fori_loop(0, much, body, 0)

    def finish(self, n, write):
        for c in range(3):
            self.group(self.stages - 1, n, c).wait_recv()
            at, size = self.cuts[n][c]
            write(self.pieces[n][0], at, size, self.total(self.stages, n, c, self.here.me, 0))

    def end(self, n, paired=True):
        for k in range(self.stages):
            for c in range(3):
                self.group(k, n, c).wait_send()
        if paired:
            self.pair(n).wait_send()


def front_kernel(shards, blocks, rows_mb, split, *refs):
    (own_in, own_out, own_down, own_gu, small, tokens, cotangent, teacher, deal_row, valid_row, lengths, gain), refs = refs[:12], refs[12:]
    (full_in, full_out, full_down, full_gu, pq, pk, pv, pg, beta, on, o, ainv, u, p, l, resid, a2, x, m, counted, deal, sort_t, gt, taps,
     gain_one, gain_two, wbeta, segc, segr, mask, a1, a1_t, a2_t), refs = refs[:33], refs[33:]
    (sent, got, sent_gt, got_gt, got_small, wbuf, wout, w_sem, out_sem), refs = refs[:9], refs[9:]
    sems, deal_sems, later_sems, small_sems = refs[:5], refs[5:8], refs[8:11], refs[11:14]
    step = pl.program_id(0)
    steps = HEADS // PAIR
    width = PAIR * HEAD_DIM
    rows = blocks * rows_mb
    share = rows // shards
    here = Here(shards)
    pieces = pieces_of([4 * D, D, D, 2 * FF], split)
    weights = Gather(here, pieces, (own_in, own_out, own_down, own_gu), (full_in, full_out, full_down, full_gu), sems)
    first_send = Exchange(here, sent, got, *deal_sems)
    second_send = Exchange(here, sent_gt, got_gt, *later_sems)
    small_send = Exchange(here, small, got_small, *small_sems, same=True)
    of_in = split[0]
    hidden_from = len(pieces) + weights.stages - steps
    deal_to, later_from = X_STEPS, GT_FROM

    def trickle(exchange, first, last):
        parts, done = weights.slots(first, last), [0]

        def at(t):
            if not first <= t < last:
                return None
            done[0] = weights.slots(first, t)

            def one():
                exchange.start_part(done[0], parts)
                done[0] += 1

            return one

        return at

    deal_some = trickle(first_send, 1, deal_to)
    later_some = trickle(second_send, later_from, weights.last + 1)

    def between(t):
        acts = [f for f in (deal_some(t), later_some(t)) if f is not None]
        return (lambda: [f() for f in acts]) if acts else None

    def fetch(s, g):
        return pltpu.make_async_copy(
            full_in.at[:, :, :, pl.ds(g * D + s * width, width)], wbuf.at[s % 2, g], w_sem.at[s % 2, g]
        )

    def fetch_out():
        return pltpu.make_async_copy(full_out, wout, out_sem)

    @pl.when(step == 0)
    def _():
        weights.begin()
        meet(here, True)
        weights.step(0)
        small_send.start()
        row, col = iota2((rows, rows), 0), iota2((rows, rows), 1)
        column = lambda v: jnp.sum(jnp.where(row == col, v, 0.0), axis=1, keepdims=True)
        dealt = deal_row[...].astype(F32)
        target = jnp.floor((dealt + 0.5) * (1.0 / rows))
        valid = valid_row[...].astype(F32)
        target_c = column(target)
        rank = jnp.sum(jnp.where((target == target_c) & (col < row), 1.0, 0.0), axis=1, keepdims=True)
        slot = target_c * share + rank
        sort_t[...] = (slot == col.astype(F32)).astype(BF16)
        lane = iota2((rows, 128), 1)
        notes = jnp.where(
            lane == 0, column(valid),
            jnp.where(lane == 1, column(dealt - target * rows), jnp.where(lane == 2, jnp.sum(valid), 0.0)),
        ).astype(BF16)
        sent[:, :, :D] = tn(sort_t[...], tokens[...]).reshape(shards, share, D).astype(BF16)
        sent[:, :, D:] = tn(sort_t[...], notes).reshape(shards, share, 128).astype(BF16)
        weights.step(1, between(1))
        for at, part in ((0, cotangent), (D, teacher)):
            sent_gt[:, :, at : at + D] = tn(sort_t[...], part[...]).reshape(shards, share, D).astype(BF16)
        weights.step(2, between(2))
        at_row, at_col = iota2((rows, 1), 0), iota2((1, rows), 1)
        seg_c, seg_r = jnp.zeros((rows, 1), F32), jnp.zeros((1, rows), F32)
        lens = lengths[...].astype(F32)
        for b in range(blocks):
            end = jnp.zeros((1, 1), F32) + b * rows_mb
            for i in range(lengths.shape[1]):
                seg_c = seg_c + jnp.where(at_row >= b * rows_mb, 1.0, 0.0) * (i == 0)
                seg_r = seg_r + jnp.where(at_col >= b * rows_mb, 1.0, 0.0) * (i == 0)
                end = end + lens[b : b + 1, i : i + 1]
                if i < lengths.shape[1] - 1:
                    seg_c = seg_c + jnp.where(at_row.astype(F32) >= end, 1.0, 0.0)
                    seg_r = seg_r + jnp.where(at_col.astype(F32) >= end, 1.0, 0.0)
        segc[...] = seg_c.astype(jnp.int32)
        segr[...] = seg_r.astype(jnp.int32)
        lane8 = iota2((rows, 8), 1)
        wide = jnp.broadcast_to(seg_c, (rows, 128))
        marks = jnp.where(lane8 == 0, 1.0, 0.0)
        for s in range(1, CONV):
            before = pltpu.roll(wide, s, 0)[:, :1]
            same = jnp.where((before == seg_c) & (at_row >= s), 1.0, 0.0)
            marks = marks + jnp.where(lane8 == s, same, 0.0)
        mask[...] = marks
        small_send.wait()
        own_taps, own_gain = 3 * D // shards, D // shards
        per = 128 // own_gain
        a, c = iota2((per * 128, per * own_taps), 0), iota2((per * 128, per * own_taps), 1)
        pick_taps = ((a // 128 == c // own_taps) & (a % 128 == c % own_taps)).astype(BF16)
        a, c = iota2((per * 128, 128), 0), iota2((per * 128, 128), 1)
        pick_gain = ((a // 128 == c // own_gain) & (a % 128 == c % own_gain)).astype(BF16)
        for g in range(shards // per):
            left = jnp.concatenate([got_small[g * per + i, :, :128].astype(F32) for i in range(per)], axis=1).astype(BF16)
            right = jnp.concatenate([got_small[g * per + i, :, 128:].astype(F32) for i in range(per)], axis=1).astype(BF16)
            tap = nn(left, pick_taps)
            taps[:, g * per * own_taps : (g + 1) * per * own_taps] = tap[:CONV]
            gains = nn(left, pick_gain)
            gain_one[:, g * 128 : (g + 1) * 128] = gains[4:5]
            gain_two[:, g * 128 : (g + 1) * 128] = gains[5:6]
            wbeta[:, g * 128 : (g + 1) * 128] = nn(right, pick_gain).astype(BF16)
        for t in range(3, hidden_from):
            weights.step(t, between(t))
        first_send.wait()
        flat = got[...].astype(F32).reshape(rows, D + 128)
        notes = flat[:, D:]
        deal[...] = (notes[:, 1:2] == col.astype(F32)).astype(BF16)
        m[...] = tn(deal[...], notes.astype(BF16))[:, :1]
        firsts = jnp.where(lax.rem(iota2((rows, 1), 0), share) == 0, notes[:, 2:3], 0.0)
        counted[...] = jnp.sum(firsts, axis=0, keepdims=True)
        x_now = tn(deal[...], flat[:, :D].astype(BF16))
        x[...] = x_now
        a1[...] = (rms(x_now)[0] * gain_one[...]).astype(BF16)
        beta[...] = nt(a1[...], wbeta[...])
        a1_t[...] = a1[...].T
        for n in range(of_in):
            weights.half(n).wait_recv()
        for g in range(4):
            fetch(0, g).start()

    for s in range(steps):

        @pl.when(step == s)
        def _(s=s):
            for g in range(4):
                fetch(s, g).wait()
            if s + 1 < steps:
                for g in range(4):
                    fetch(s + 1, g).start()

    slot_now = lax.rem(step, 2)
    for g, out in enumerate((pq, pk, pv, pg)):
        out[...] = nn(a1[...], wbuf[slot_now, g].reshape(D, width))
    here_cols = pl.ds(pl.multiple_of(step * width, width), width)
    taps_of = lambda j: taps.at[:, pl.ds(pl.multiple_of(j * D + step * width, width), width)]
    mixer_fwd_kernel(
        blocks, rows_mb, pq, pk, pv, pg, beta, taps_of(0), taps_of(1), taps_of(2), gain, mask, segc, segr,
        on.at[:, here_cols], o, ainv, u, p, l,
    )
    for s in range(steps):

        @pl.when(step == s)
        def _(s=s):
            weights.step(hidden_from + s, between(hidden_from + s))
            if s == steps - 1:
                for n in range(of_in, of_in + split[1]):
                    weights.half(n).wait_recv()
                fetch_out().start()
                second_send.wait()
                gt[...] = tn(deal[...], got_gt[...].astype(F32).reshape(rows, gt.shape[1]).astype(BF16))
                fetch_out().wait()
                r = x[...] + nn(on[...], wout[...].reshape(D, D))
                resid[...] = r
                a2[...] = (rms(r)[0] * gain_two[...]).astype(BF16)
                a2_t[...] = a2[...].T
                weights.end(of_in + split[1])


def front(weights, small, tokens, cotangent, teacher, deal_rows, valid_mask, lengths, gain, shards, collective_id):
    rows, blocks = tokens.shape[0], lengths.shape[0]
    rows_mb, share = rows // blocks, rows // shards
    width = PAIR * HEAD_DIM
    split = (2, 1, 1, 2)
    pieces = pieces_of([w.shape[1] for w in weights], split)
    anywhere = pl.BlockSpec(memory_space=pl.ANY)
    _, mat, one, _, full = mixer_specs(rows, blocks, rows_mb)
    f32 = lambda *shape: jax.ShapeDtypeStruct(shape, F32)
    bf = lambda *shape: jax.ShapeDtypeStruct(shape, BF16)
    square = f32(HEADS, blocks, rows_mb, rows_mb)
    wide = f32(rows, D)
    vm, dma = pltpu.VMEM, pltpu.SemaphoreType.DMA
    outs = [
        (spread(w, shards), anywhere) for w in weights
    ] + [(wide, one)] * 4 + [
        (f32(rows, HEADS), full((rows, HEADS))), (bf(rows, D), full((rows, D))), (wide, one),
        (square, mat), (square, mat), (square, mat), (square, mat), (wide, full((rows, D))),
        (bf(rows, D), full((rows, D))), (wide, full((rows, D))), (f32(rows, 1), full((rows, 1))),
        (f32(1, 1), full((1, 1))), (bf(rows, rows), full((rows, rows))), (bf(rows, rows), full((rows, rows))),
        (f32(rows, 2 * D), full((rows, 2 * D))), (f32(CONV, 3 * D), full((CONV, 3 * D))),
        (f32(1, D), full((1, D))), (f32(1, D), full((1, D))), (bf(8, D), full((8, D))),
        (jax.ShapeDtypeStruct((rows, 1), jnp.int32), full((rows, 1))),
        (jax.ShapeDtypeStruct((1, rows), jnp.int32), full((1, rows))), (f32(rows, 8), full((rows, 8))),
        (bf(rows, D), full((rows, D))), (bf(D, rows), full((D, rows))), (bf(D, rows), full((D, rows))),
    ]
    return pl.pallas_call(
        functools.partial(front_kernel, shards, blocks, rows_mb, split),
        grid=(HEADS // PAIR,),
        in_specs=[anywhere] * 4 + [
            full(small.shape), full((rows, D)), full((rows, D)), full((rows, D)), full((1, rows)), full((1, rows)),
            full(lengths.shape), full((1, HEAD_DIM)),
        ],
        out_specs=[s for _, s in outs],
        out_shape=[s for s, _ in outs],
        scratch_shapes=[
            vm((shards, share, D + 128), BF16), vm((shards, share, D + 128), BF16),
            vm((shards, share, 2 * D), BF16), vm((shards, share, 2 * D), BF16),
            vm((shards,) + small.shape, BF16),
            vm((2, 4, shards // 2, 2, D // shards, width), BF16),
            vm((shards // 2, 2, D // shards, D), BF16), dma((2, 4)), dma,
        ] + Gather.semaphores(shards, pieces) + [dma] * 9,
        compiler_params=pltpu.CompilerParams(
            collective_id=collective_id, has_side_effects=True, vmem_limit_bytes=58 << 20
        ),
        name="front",
    )(*weights, small, tokens, cotangent, teacher, deal_rows[None, :], valid_mask[None, :], lengths, gain)


def backward_kernel(shards, blocks, rows_mb, pieces, *refs):
    (d_down, df, a2, gate, up, wga, wup, wdn, dy, resid, gain_two, wout, wq, wk, wv, wg, a1, on, x,
     gain_one, wbeta, *mixer), refs = refs[:38], refs[38:]
    (g_down, g_gu, dwq, dwk, dwv, dwg, dw_out, d_wbeta, dx, d_two, d_one, dtq, dtk, dtv,
     d_gain), refs = refs[:15], refs[15:]
    (mine_down, d_gu, acc, dresid, dz, don, dpq, dpk, dpv, dpg, dbeta, keep), refs = refs[:12], refs[12:]
    sems, buffers = refs[:4], refs[4:]
    step = pl.program_id(0)
    chunks = FF // CHUNK
    pairs = HEADS // PAIR
    here = Here(shards)
    core = here.core
    other, coming = Scatter.split(shards, 2, buffers)
    r_gu = d_gu.shape[2]

    def whole(n, parity):
        i, at, size = pieces[n]
        if i == 0:
            return d_down.at[:, parity, :, pl.ds(at, size)]
        return d_gu.at[:, parity, :, pl.ds(at, size)]

    def mine(i, q, cols):
        return mine_down[q, :, cols] if i == 0 else d_gu[q, core, :, cols]

    def kept(n):
        if n > 0:
            return None
        return pltpu.make_async_copy(d_down.at[:, core], mine_down, keep)

    net = Scatter(here, pieces, whole, mine, other, coming, sems, kept)

    def write(i, at, size, value):
        if i == 0:
            g_down[:, pl.ds(at, size)] = value
            return
        for tile in range(at // 128, (at + size) // 128):
            chunk, inner = tile * 128 // (2 * CHUNK), tile * 128 % (2 * CHUNK)
            start = chunk * CHUNK + inner if inner < CHUNK else FF + chunk * CHUNK + inner - CHUNK
            g_gu[:, start : start + 128] = value[:, tile * 128 - at : tile * 128 - at + 128]

    @pl.when(step == 0)
    def _():
        kept(0).start()
        meet(here, False)
        net.pair(0).start()
        acc[...] = jnp.zeros_like(acc)

    @pl.when(step < chunks)
    def _():
        dhid = nt(df[...], wdn[...])
        g = gate[...]
        s = sigmoid(g)
        d_gate = (dhid * up[...] * (s * (1.0 + g * (1.0 - s)))).astype(BF16)
        d_up = (dhid * (g * s)).astype(BF16)
        acc[...] += nt(d_gate, wga[...]) + nt(d_up, wup[...])
        for at, part in ((0, d_gate), (CHUNK, d_up)):
            grad = tn(a2[...], part).reshape(shards // 2, 2, r_gu, CHUNK).astype(BF16)
            start = pl.multiple_of(step * (2 * CHUNK) + at, CHUNK)
            d_gu[:, :, :, pl.ds(start, CHUNK)] = grad

    @pl.when(step == chunks - 1)
    def _():
        nr, rr = rms(resid[...])
        da2 = acc[...]
        d_two[...] = jnp.sum(da2 * nr, axis=0, keepdims=True)
        dresid[...] = dy[...] + rms_back(nr, rr, gain_two[...] * da2)
        acc[...] = jnp.zeros_like(acc)
        dz[...] = dresid[...].astype(BF16)

    @pl.when(step >= chunks)
    def _():
        don[...] = nt(dz[...], wout[...])
        mixer_bwd_kernel(
            blocks, rows_mb, PAIR, step - chunks, *mixer[:12], don, *mixer[12:], dpq, dpk, dpv, dpg, dbeta, dtq,
            dtk, dtv, d_gain,
        )
        for dp, w, out in ((dpq, wq, dwq), (dpk, wk, dwk), (dpv, wv, dwv), (dpg, wg, dwg)):
            acc[...] += nt(dp[...], w[...])
            out[...] = tn(a1[...], dp[...]).astype(BF16)
        dw_out[...] = tn(on[...], dz[...]).astype(BF16)

    @pl.when(step == chunks + pairs - 1)
    def _():
        d_beta = dbeta[...].astype(BF16)
        grad = acc[...] + nt(d_beta, wbeta[...])
        d_wbeta[...] = tn(a1[...], d_beta)
        nx, rx = rms(x[...])
        d_one[...] = jnp.sum(grad * nx, axis=0, keepdims=True)
        dx[...] = (dresid[...] + rms_back(nx, rx, gain_one[...] * grad)).astype(BF16)

    ready = {pieces[n][1] // (2 * CHUNK) + pieces[n][2] // (2 * CHUNK) - 1: n for n in (1, 2)}
    plan = {}
    for s, n in ready.items():
        plan.setdefault(s, []).append((net.pair, n))
    tail = range(chunks - 1, chunks + pairs)
    plan.setdefault(3, []).append((net.launch, 0, 0))
    for place, s in enumerate(tail):
        for n in range(3):
            k = place + 1 - n
            if (k, n) != (0, 0) and 0 <= k < net.stages:
                plan.setdefault(s, []).append((net.launch, k, n))
            elif k == net.stages:
                plan.setdefault(s, []).append((net.finish, n, write))
    last = tail[-1]
    for place in range(len(tail), net.stages + 3):
        for n in range(3):
            k = place + 1 - n
            if 0 <= k < net.stages:
                plan[last].append((net.launch, k, n))
            elif k == net.stages:
                plan[last].append((net.finish, n, write))
    for s, actions in plan.items():

        @pl.when(step == s)
        def _(actions=actions, s=s):
            for act, *args in actions:
                result = act(*args)
                if act == net.pair:
                    result.start()
            if s == last:
                for n in range(3):
                    net.end(n)


def backward(
    d_down, df, a2, gu, wgu, wdown, dy, resid, gain_two, wout, win, a1, on, x, gain_one, wbeta, proj,
    beta_pre, taps, gain, mask, segc, segr, saved, blocks, shards, collective_id,
):
    rows = x.shape[0]
    rows_mb = rows // blocks
    width = PAIR * HEAD_DIM
    chunks, pairs = FF // CHUNK, HEADS // PAIR
    anywhere = pl.BlockSpec(memory_space=pl.ANY)
    full = lambda shape: pl.BlockSpec(shape, lambda s: (0,) * len(shape))
    early = lambda s: jnp.minimum(s, chunks - 1)
    late = lambda s: jnp.maximum(s - chunks, 0)
    lane_e = lambda r, w, off=0: pl.BlockSpec((r, w), lambda s: (0, off + early(s)))
    lane_l = lambda r, w, off=0: pl.BlockSpec((r, w), lambda s: (0, off + late(s)))
    wide_l = lambda off=0: pl.BlockSpec(
        (D, width), lambda s: (0, off + late(s)), pipeline_mode=pl.Buffered(1)
    )
    row_l = lambda r, w: pl.BlockSpec((r, w), lambda s: (late(s), 0))
    mat = pl.BlockSpec(
        (PAIR, blocks, rows_mb, rows_mb), lambda s: (late(s), 0, 0, 0), pipeline_mode=pl.Buffered(1)
    )
    part_l = pl.BlockSpec(
        (rows, width), lambda s: (0, late(s)), pipeline_mode=pl.Buffered(1)
    )
    per = D // width
    tap = lambda k: lane_l(CONV, width, k * per)
    r_down, r_gu = FF // shards, D // shards
    a, b = chunks // 2 * 2 * CHUNK, 2 * FF
    pieces = [(0, 0, D), (1, 0, a), (1, a, b - a)]
    f32 = lambda *shape: jax.ShapeDtypeStruct(shape, F32)
    bf = lambda *shape: jax.ShapeDtypeStruct(shape, BF16)
    square = bf(D, D)
    vm = pltpu.VMEM
    return pl.pallas_call(
        functools.partial(backward_kernel, shards, blocks, rows_mb, pieces),
        grid=(chunks + pairs,),
        in_specs=[
            anywhere, full((rows, D)), full((rows, D)), lane_e(rows, CHUNK),
            lane_e(rows, CHUNK, chunks), lane_e(D, CHUNK), lane_e(D, CHUNK, chunks),
            pl.BlockSpec((CHUNK, D), lambda s: (early(s), 0)), full((rows, D)), full((rows, D)),
            full((1, D)), row_l(width, D), wide_l(), wide_l(per), wide_l(2 * per),
            wide_l(3 * per), full((rows, D)),
            lane_l(rows, width), full((rows, D)), full((1, D)), full((D, HEADS)),
            part_l, part_l, part_l, part_l, full((rows, HEADS)), tap(0), tap(1), tap(2), full((1, HEAD_DIM)), full((rows, 8)),
            full((rows, 1)), full((1, rows)), lane_l(rows, width), mat, mat, mat, mat,
        ],
        out_specs=[
            full((r_down, D)), full((r_gu, 2 * FF)), wide_l(), wide_l(), wide_l(), wide_l(),
            row_l(width, D), full((D, HEADS)), full((rows, D)),
            full((1, D)), full((1, D)), lane_l(CONV, width), lane_l(CONV, width),
            lane_l(CONV, width), full((1, HEAD_DIM)),
        ],
        out_shape=[
            f32(r_down, D), f32(r_gu, 2 * FF), square, square, square, square, square,
            f32(D, HEADS), bf(rows, D), f32(1, D), f32(1, D), f32(CONV, D), f32(CONV, D),
            f32(CONV, D), f32(1, HEAD_DIM),
        ],
        scratch_shapes=[
            vm((shards // 2, r_down, D), BF16), vm((shards // 2, 2, r_gu, 2 * FF), BF16),
            vm((rows, D), F32), vm((rows, D), F32), vm((rows, D), BF16), vm((rows, width), F32),
            vm((rows, width), BF16), vm((rows, width), BF16), vm((rows, width), BF16),
            vm((rows, width), BF16), vm((rows, HEADS), F32),
            pltpu.SemaphoreType.DMA,
        ] + Scatter.semaphores(shards, 3) + Scatter.buffers(shards, [(r_down, D), (r_gu, 2 * FF)]),
        compiler_params=pltpu.CompilerParams(
            collective_id=collective_id, has_side_effects=True, vmem_limit_bytes=60 << 20
        ),
        name="backward",
    )(d_down.reshape(shards // 2, 2, r_down, D), df, a2, gu, gu, wgu, wgu, wdown, dy, resid, gain_two,
      wout, win, win, win, win, a1, on, x, gain_one, wbeta, *proj, beta_pre, taps, taps, taps, gain,
      mask, segc, segr, *saved)


def link_plan(half_way, done, last, heads):
    return [
        [4, 9, 11, 12], [half_way + 3, done + 1, done + 2], [done + 1, done + 3], [done + 6], [last], [last],
        [done + 5],
    ]


def rear_kernel(shards, blocks, rows_mb, pieces, *refs):
    (d_down, sent_y, dy, resid, x, a2_t, a1_t, df, gate, up, wga, wup, wdn, gain_two, gain_one, wout, wq, wk, wv, wg,
     on, wbeta, deal, loss, *mixer), refs = refs[:41], refs[41:]
    (g_down, g_gu, g_in, g_out, got_y, got_dx, small_sum), refs = refs[:7], refs[7:]
    (mine_down, mine_gu, mine_in, mine_out, stage_gu, stage_in, stage_out, acc, dresid, held, dz, don, dpq, dpk, dpv,
     dpg, turned, dbeta, dtaps, d_gain, d_two, sent_dx, small, small_got, keep, load, gu_sem, in_sem, out_sem), refs = refs[:29], refs[29:]
    y_sems, dx_sems, small_sems, sems, buffers = refs[:3], refs[3:6], refs[6:9], refs[9:13], refs[13:]
    step = pl.program_id(0)
    chunks, heads = FF // SLICE, HEADS
    rows = blocks * rows_mb
    share, r_gu = rows // shards, D // shards
    here = Here(shards)
    core = here.core
    other, coming = Scatter.split(shards, 4, buffers)
    mines = (mine_down, mine_gu, mine_in, mine_out)
    pair_recv = sems[3]

    def whole(n, parity):
        i, at, size = pieces[n]
        if i == 0:
            return d_down.at[:, parity, :, pl.ds(at, size)]
        return other[i].at[:, :, pl.ds(at, size)]

    def kept(n):
        if n > 0:
            return None
        return pltpu.make_async_copy(d_down.at[:, core], mine_down, keep)

    net = Scatter(
        here, pieces, whole, lambda i, q, cols: mines[i][q, :, cols], other, coming, sems, kept
    )
    give_y = Exchange(here, sent_y, got_y, *y_sems)
    give_dx = Exchange(here, sent_dx, got_dx, *dx_sems)
    give_small = Exchange(here, small, small_got, *small_sems)

    def cross(stage, slot, there, send, n):
        return pltpu.make_async_remote_copy(
            src_ref=stage.at[slot], dst_ref=there, send_sem=send.at[slot], recv_sem=pair_recv.at[n],
            device_id=here.partner[0], device_id_type=MESH,
        )

    def cross_gu(j):
        cols = pl.ds(pl.multiple_of(j * (2 * SLICE), 2 * SLICE), 2 * SLICE)
        return cross(stage_gu, lax.rem(j, 2), other[1].at[:, :, cols], gu_sem, 1 + lax.div(j + chunks % 2, (chunks + 1) // 2))

    def cross_in(s):
        width = 4 * HEAD_DIM
        cols = pl.ds(pl.multiple_of(s * width, width), width)
        return cross(stage_in, lax.rem(s, 2), other[2].at[:, :, cols], in_sem, 3 + lax.div(s, heads // 2) + lax.div(s, 3 * heads // 4))

    def cross_out(s):
        much = shards // 2 // heads
        return cross(stage_out, s % 2, other[3].at[pl.ds(s * much, much)], out_sem, 6)

    def by_core(value):
        first, second = value[:, 0], value[:, 1]
        return (
            jnp.where(core == 0, first, second).astype(BF16), jnp.where(core == 0, second, first).astype(BF16)
        )

    def write(i, at, size, value):
        if i == 0:
            g_down[:, pl.ds(at, size)] = value
        elif i == 3:
            g_out[:, pl.ds(at, size)] = value
        else:
            for tile in range(at // 128, (at + size) // 128):
                if i == 1:
                    chunk, inner = divmod(tile * 128, 2 * SLICE)
                    start = chunk * SLICE + inner + (FF - SLICE if inner >= SLICE else 0)
                else:
                    start = tile % 4 * D + tile // 4 * HEAD_DIM
                target = g_gu if i == 1 else g_in
                target[:, start : start + 128] = value[:, tile * 128 - at : tile * 128 - at + 128]

    load_dy = pltpu.make_async_copy(dy, dresid, load.at[0])
    load_resid = pltpu.make_async_copy(resid, held, load.at[1])
    load_x = pltpu.make_async_copy(x, held, load.at[1])
    load_a2 = pltpu.make_async_copy(a2_t, turned, load.at[2])
    load_a1 = pltpu.make_async_copy(a1_t, turned, load.at[2])

    @pl.when(step == 0)
    def _():
        kept(0).start()
        load_dy.start()
        load_resid.start()
        meet(here, True)
        net.pair(0).start()
        give_y.start()
        acc[...] = jnp.zeros_like(acc)
        load_a2.start()
        load_a2.wait()

    @pl.when(step < chunks)
    def _():
        dhid = nt(df[...], wdn[...])
        g = gate[...]
        s = sigmoid(g)
        d_gate = (dhid * up[...] * (s * (1.0 + g * (1.0 - s)))).astype(BF16)
        d_up = (dhid * (g * s)).astype(BF16)
        acc[...] += nt(d_gate, wga[...]) + nt(d_up, wup[...])

        @pl.when(step >= 2)
        def _():
            cross_gu(step - 2).wait_send()

        slot = lax.rem(step, 2)
        part = jnp.concatenate([d_gate, d_up], axis=1)
        near, far = by_core(nn(turned[...], part).reshape(shards // 2, 2, r_gu, 2 * SLICE))
        mine_gu[:, :, pl.ds(pl.multiple_of(step * (2 * SLICE), 2 * SLICE), 2 * SLICE)] = near
        stage_gu[slot] = far
        cross_gu(step).start()

    @pl.when(step == chunks - 1)
    def _():
        load_dy.wait()
        load_resid.wait()
        nr, rr = rms(held[...])
        da2 = acc[...]
        d_two[...] = jnp.sum(da2 * nr, axis=0, keepdims=True)
        dresid[...] = dresid[...] + rms_back(nr, rr, gain_two[...] * da2)
        dz[...] = dresid[...].astype(BF16)
        acc[...] = jnp.zeros_like(acc)
        load_a1.start()
        load_x.start()
        load_a1.wait()

    @pl.when(step >= chunks)
    def _():
        head = step - chunks
        don[...] = nt(dz[...], wout[...])
        taps_of = lambda j: dtaps.at[:, pl.ds(pl.multiple_of(j * D + head * HEAD_DIM, HEAD_DIM), HEAD_DIM)]
        mixer_bwd_kernel(
            blocks, rows_mb, 1, head, *mixer[:12], don, *mixer[12:], dpq, dpk, dpv, dpg, dbeta, taps_of(0),
            taps_of(1), taps_of(2), d_gain,
        )

        @pl.when(head >= 2)
        def _():
            cross_in(head - 2).wait_send()

        slot = lax.rem(head, 2)
        acc[...] += nt(dpq[...], wq[...]) + nt(dpk[...], wk[...]) + nt(dpv[...], wv[...]) + nt(dpg[...], wg[...])
        width = 4 * HEAD_DIM
        part = jnp.concatenate([dpq[...], dpk[...], dpv[...], dpg[...]], axis=1)
        near, far = by_core(nn(turned[...], part).reshape(shards // 2, 2, r_gu, width))
        mine_in[:, :, pl.ds(pl.multiple_of(head * width, width), width)] = near
        stage_in[slot] = far
        cross_in(head).start()

    @pl.when(step == chunks)
    def _():
        much = shards // 2 // heads
        for s in range(heads):
            if s >= 2:
                cross_out(s - 2).wait_send()
            part = tn(on[:, s * HEAD_DIM : (s + 1) * HEAD_DIM], dz[...])
            near, far = by_core(part.reshape(much, 2, r_gu, D))
            mine_out[s * much : (s + 1) * much] = near
            stage_out[s % 2] = far
            cross_out(s).start()
        for s in (heads - 2, heads - 1):
            cross_out(s).wait_send()

    def last_rows():
        d_beta = dbeta[...].astype(BF16)
        grad = acc[...] + nn(d_beta, wbeta[...])
        d_wbeta = lax.dot_general(
            d_beta, turned[...], (((0,), (1,)), ((), ())), preferred_element_type=F32
        )
        load_x.wait()
        nx, rx = rms(held[...])
        d_one = jnp.sum(grad * nx, axis=0, keepdims=True)
        dx = (dresid[...] + rms_back(nx, rx, gain_one[...] * grad)).astype(BF16)
        sent_dx[...] = nn(deal[...], dx).reshape(shards, share, D).astype(BF16)
        own_taps, own_gain = 3 * D // shards, D // shards
        per = 128 // own_gain
        a, c = iota2((per * own_taps, per * 128), 1), iota2((per * own_taps, per * 128), 0)
        put_taps = ((a // 128 == c // own_taps) & (a % 128 == c % own_taps)).astype(F32)
        a, c = iota2((128, per * 128), 1), iota2((128, per * 128), 0)
        put_gain = ((a // 128 == c // own_gain) & (a % 128 == c % own_gain)).astype(F32)
        lane = iota2((1, 128), 1)
        row8 = iota2((8, 128), 0)
        shared = jnp.where(row8 == 6, d_gain[...], jnp.where((row8 == 7) & (lane == 0), loss[...], 0.0))
        for g in range(shards // per):
            top = jnp.concatenate(
                [dtaps[:, g * per * own_taps : (g + 1) * per * own_taps],
                 jnp.zeros((8 - CONV, per * own_taps), F32)], axis=0
            )
            cols = slice(g * 128, (g + 1) * 128)
            gains = jnp.where(row8 == 4, d_one[:, cols], jnp.where(row8 == 5, d_two[:, cols], 0.0))
            upper = mm(top, put_taps, 1, 0) + mm(gains, put_gain, 1, 0)
            lower = mm(d_wbeta[:, cols], put_gain, 1, 0)
            for i in range(per):
                small[g * per + i, 0:8, :] = upper[:, i * 128 : (i + 1) * 128] + shared
                small[g * per + i, 8:16, :] = lower[:, i * 128 : (i + 1) * 128]

    last = chunks + heads - 1
    half_way, done = chunks // 2 - 1, chunks - 1
    starts = link_plan(half_way, done, last, heads)
    timed = []
    for n in range(len(pieces)):
        for k in range(net.stages + 1):
            at = starts[n][k] if k < len(starts[n]) else starts[n][-1] + 2 * (k - len(starts[n]) + 1)
            timed.append((at, k != net.stages, n, k))
    timed.sort()

    def act(n, k):
        if k < net.stages:
            net.launch(k, n)
        else:
            net.finish(n, write)

    for s in sorted({t[0] for t in timed if t[0] < last}):

        @pl.when(step == s)
        def _(s=s):
            for at, _, n, k in timed:
                if at == s:
                    act(n, k)

    @pl.when(step == last)
    def _():
        for at, _, n, k in timed:
            if at == last:
                act(n, k)
        last_rows()
        give_small.start()
        tail = [(n, k) for at, _, n, k in timed if at > last]
        for i, (n, k) in enumerate(tail):
            act(n, k)
            if i < DX_PARTS:
                give_dx.start_part(i, DX_PARTS)
        give_small.wait()
        small_sum[...] = jnp.sum(small_got[...], axis=0)
        give_y.wait()
        give_dx.wait()
        for j in (chunks - 2, chunks - 1):
            cross_gu(j).wait_send()
        for s in (heads - 2, heads - 1):
            cross_in(s).wait_send()
        for n in range(len(pieces)):
            net.end(n, paired=n == 0)


def rear(
    d_down, sent_y, dy, resid, x, a2_t, a1_t, df, gu, wgu, wdown, gain_two, gain_one, wout, win, on, wbeta, deal, loss,
    proj, beta_pre, taps, gain, mask, segc, segr, saved, blocks, shards, collective_id,
):
    rows = x.shape[0]
    rows_mb, share = rows // blocks, rows // shards
    chunks = FF // SLICE
    anywhere = pl.BlockSpec(memory_space=pl.ANY)
    once = pl.Buffered(MIXER_BUFFERS)
    full = lambda shape: pl.BlockSpec(shape, lambda s: (0,) * len(shape))
    early = lambda s: jnp.minimum(s, chunks - 1)
    late = lambda s: jnp.maximum(s - chunks, 0)
    lane_e = lambda r, w, off=0: pl.BlockSpec((r, w), lambda s: (0, off + early(s)))
    lane_l = lambda r, w, off=0: pl.BlockSpec((r, w), lambda s: (0, off + late(s)), pipeline_mode=once)
    mat = pl.BlockSpec((1, blocks, rows_mb, rows_mb), lambda s: (late(s), 0, 0, 0), pipeline_mode=pl.Buffered(1))
    tap = lambda k: pl.BlockSpec((CONV, HEAD_DIM), lambda s: (0, k * HEADS + late(s)))
    r_down, r = FF // shards, D // shards
    a, b = chunks // 2 * 2 * SLICE, 4 * D // 2
    c = b // 2
    pieces = [(0, 0, D), (1, 0, a), (1, a, 2 * FF - a), (2, 0, b), (2, b, c), (2, b + c, c), (3, 0, D)]
    shapes = [(r_down, D), (r, 2 * FF), (r, 4 * D), (r, D)]
    f32 = lambda *shape: jax.ShapeDtypeStruct(shape, F32)
    bf = lambda *shape: jax.ShapeDtypeStruct(shape, BF16)
    vm, dma = pltpu.VMEM, pltpu.SemaphoreType.DMA
    hd = HEAD_DIM
    half = shards // 2
    return pl.pallas_call(
        functools.partial(rear_kernel, shards, blocks, rows_mb, pieces),
        grid=(chunks + HEADS,),
        in_specs=[
            anywhere, anywhere, anywhere, anywhere, anywhere, anywhere, anywhere, full((rows, D)),
            lane_e(rows, SLICE), lane_e(rows, SLICE, chunks), lane_e(D, SLICE), lane_e(D, SLICE, chunks),
            pl.BlockSpec((SLICE, D), lambda s: (early(s), 0)), full((1, D)), full((1, D)),
            pl.BlockSpec((hd, D), lambda s: (late(s), 0), pipeline_mode=pl.Buffered(1)), lane_l(D, hd), lane_l(D, hd, HEADS),
            lane_l(D, hd, 2 * HEADS), lane_l(D, hd, 3 * HEADS), full((rows, D)),
            full((HEADS, D)), full((rows, rows)), full((1, 1)),
            lane_l(rows, hd), lane_l(rows, hd), lane_l(rows, hd), lane_l(rows, hd), full((rows, HEADS)), tap(0),
            tap(1), tap(2), full((1, hd)), full((rows, 8)), full((rows, 1)), full((1, rows)), lane_l(rows, hd),
            mat, mat, mat, mat,
        ],
        out_specs=[full(s) for s in shapes] + [anywhere, anywhere, full((16, 128))],
        out_shape=[f32(*s) for s in shapes] + [bf(shards, share, D), bf(shards, share, D), f32(16, 128)],
        scratch_shapes=[vm((half,) + s, BF16) for s in shapes] + [
            vm((2, half, r, 2 * SLICE), BF16), vm((2, half, r, 4 * hd), BF16), vm((2, half // HEADS, r, D), BF16),
            vm((rows, D), F32), vm((rows, D), F32), vm((rows, D), F32), vm((rows, D), BF16), vm((rows, hd), F32),
            vm((rows, hd), BF16), vm((rows, hd), BF16), vm((rows, hd), BF16), vm((rows, hd), BF16),
            vm((D, rows), BF16), vm((rows, HEADS), F32), vm((CONV, 3 * D), F32), vm((1, hd), F32), vm((1, D), F32),
            vm((shards, share, D), BF16), vm((shards, 16, 128), F32), vm((shards, 16, 128), F32),
            dma, dma((3,)), dma((2,)), dma((2,)), dma((2,)),
        ] + [dma] * 9 + Scatter.semaphores(shards, len(pieces)) + Scatter.buffers(shards, shapes),
        compiler_params=pltpu.CompilerParams(
            collective_id=collective_id, has_side_effects=True, vmem_limit_bytes=62 << 20
        ),
        name="rear",
    )(d_down.reshape(half, 2, r_down, D), sent_y, dy, resid, x, a2_t, a1_t, df, gu, gu, wgu, wgu, wdown, gain_two, gain_one,
      wout, win, win, win, win, on, wbeta, deal, loss, *proj, beta_pre, taps, taps, taps, gain, mask, segc, segr,
      *saved)


def settle_kernel(
    got_y, got_dx, sort_t, summed, counted, g_down, g_gu, g_in, g_out,
    output, input_grad, o_in, o_beta, o_taps, o_out, o_one, o_gain, o_two, o_gu, o_down, loss,
):
    shards, share, _ = got_y.shape
    own = o_one.shape[1]
    for got, out in ((got_y, output), (got_dx, input_grad)):
        out[...] = nn(sort_t[...], got[...].astype(F32).reshape(shards * share, D).astype(BF16)).astype(BF16)
    o_in[...], o_out[...], o_gu[...], o_down[...] = g_in[...], g_out[...], g_gu[...], g_down[...]
    total = summed[...]
    o_taps[...] = total[:CONV, : 3 * own]
    o_one[...], o_two[...], o_gain[...] = total[4:5, :own], total[5:6, :own], total[6:7]
    loss[...] = total[7:8, :1] / (D * counted[...])
    o_beta[...] = total[8:].T[:own]


def settle(got_y, got_dx, sort_t, summed, counted, g_down, g_gu, g_in, g_out):
    rows = sort_t.shape[0]
    own = g_in.shape[0]
    f32 = lambda *shape: jax.ShapeDtypeStruct(shape, F32)
    row = jax.ShapeDtypeStruct((rows, D), BF16)
    return pl.pallas_call(
        settle_kernel,
        out_shape=[row, row, f32(*g_in.shape), f32(own, HEADS), f32(CONV, 3 * own), f32(*g_out.shape), f32(1, own),
                   f32(1, HEAD_DIM), f32(1, own), f32(*g_gu.shape), f32(*g_down.shape), f32(1, 1)],
        name="settle",
    )(got_y, got_dx, sort_t, summed, counted, g_down, g_gu, g_in, g_out)


def scatter_kernel(shards, count, *refs):
    grads, sent, out, got = refs[:count], refs[count], refs[count + 1 : 2 * count + 1], refs[2 * count + 1]
    refs = refs[2 * count + 2 :]
    mine, refs = refs[:count], refs[count:]
    sems, (keep, *back_sems), buffers = refs[:4], refs[4:8], refs[8:]
    here = Here(shards)
    core = here.core
    back = Exchange(here, sent, got, *back_sems)
    other, coming = Scatter.split(shards, count, buffers)
    pieces = [(i, 0, g.shape[-1]) for i, g in enumerate(grads)]

    def kept(n):
        return pltpu.make_async_copy(grads[n].at[:, core], mine[n], keep.at[n])

    net = Scatter(
        here, pieces, lambda n, parity: grads[n].at[:, parity],
        lambda i, q, cols: mine[i][q, :, cols], other, coming, sems, kept,
    )

    def write(i, at, size, value):
        out[i][:, pl.ds(at, size)] = value

    for n in range(count):
        kept(n).start()
    meet(here, True)
    for n in range(count):
        net.pair(n).start()
    back.start()
    for t in range(count + net.stages):
        for n in range(count):
            k = t - n
            if 0 <= k < net.stages:
                net.launch(k, n)
            elif k == net.stages:
                net.finish(n, write)
    back.wait()
    for n in range(count):
        net.end(n)


def scatter(grads, message, shards, collective_id):
    count = len(grads)
    shapes = [(g.shape[0] // shards, g.shape[1]) for g in grads]
    anywhere = pl.BlockSpec(memory_space=pl.ANY)
    dma = pltpu.SemaphoreType.DMA
    *out, got = pl.pallas_call(
        functools.partial(scatter_kernel, shards, count),
        in_specs=[anywhere] * (count + 1),
        out_specs=[pl.BlockSpec(memory_space=pltpu.VMEM)] * count + [anywhere],
        out_shape=[jax.ShapeDtypeStruct(s, F32) for s in shapes]
        + [jax.ShapeDtypeStruct(message.shape, message.dtype)],
        scratch_shapes=[pltpu.VMEM((shards // 2,) + s, BF16) for s in shapes]
        + Scatter.semaphores(shards, count) + [dma((count,)), dma, dma, dma]
        + Scatter.buffers(shards, shapes),
        compiler_params=pltpu.CompilerParams(
            collective_id=collective_id, has_side_effects=True, vmem_limit_bytes=60 << 20
        ),
        name="scatter_last",
    )(*[g.reshape((shards // 2, 2) + s) for g, s in zip(grads, shapes)], message)
    return out, got


def nt(left, right):
    return lax.dot_general(left, right, (((1,), (1,)), ((), ())), preferred_element_type=F32)


def tn(left, right, dtype=F32):
    return lax.dot_general(left, right, (((0,), (0,)), ((), ())), preferred_element_type=dtype)


def nn(left, right):
    return jnp.dot(left, right, preferred_element_type=F32)


def rms(v):
    inv = lax.rsqrt(jnp.mean(v * v, axis=-1, keepdims=True) + 1e-05)
    return v * inv, inv


def rms_back(normed, inv, dn):
    return inv * (dn - normed * jnp.mean(normed * dn, axis=-1, keepdims=True))


def local(
    tokens, cotangent, teacher, valid_mask, deal_rows, lengths, w_in, w_beta, conv_kernel, w_out,
    norm_gain, out_gain, ffn_gain, w_gu, w_down,
):
    shards = lax.axis_size(AXES)
    rows = tokens.shape[0]
    share = rows // shards
    blocks = lengths.shape[0]
    rows_mb = rows // blocks
    a, b, c = CONV * conv_kernel.shape[1], w_beta.shape[0] * HEADS, norm_gain.shape[0]
    small = w_beta.shape[0] * HEADS + CONV * conv_kernel.shape[1] + 2 * norm_gain.shape[0]

    if share % 8 == 0 and (D // shards) % 16 == 0:
        half = jnp.pad(
            jnp.concatenate([conv_kernel, jnp.pad(jnp.stack([norm_gain, ffn_gain]), ((0, 0), (0, conv_kernel.shape[1] - norm_gain.shape[0])))]),
            ((0, 2), (0, 128 - conv_kernel.shape[1])),
        )
        small_block = jnp.concatenate(
            [half, jnp.pad(w_beta.T, ((0, 0), (0, 128 - w_beta.shape[0])))], axis=1
        )
        gain_out = out_gain.astype(F32)[None, :]
        (win, wout, wdown, wgu, *proj, beta_pre, on, o, ainv, u, p, l, resid, a2, x, m, counted, deal_t, sort_t, later,
         taps, gain_one, gain_two, wbeta, segc, segr, mask, a1, a1_t, a2_t) = front(
            [w_in, w_out, w_down, w_gu], small_block, tokens, cotangent, teacher, deal_rows, valid_mask, lengths,
            gain_out, shards, 0,
        )
        win, wout, wdown, wgu = (w.reshape(-1, w.shape[-1]) for w in (win, wout, wdown, wgu))
        saved = (o, ainv, u, p, l)
        counted = counted[0, 0]
        g, t = later[:, :D], later[:, D:]
        gain_one, gain_two = gain_one[0], gain_two[0]
    else:
        target = deal_rows // rows
        spot = deal_rows % rows
        ahead = (target[None, :] == target[:, None]) & (
            jnp.arange(rows)[None, :] < jnp.arange(rows)[:, None]
        )
        slot = target * share + jnp.sum(ahead.astype(jnp.int32), axis=1)
        sort_t = (slot[:, None] == jnp.arange(rows)[None, :]).astype(BF16)
        sort = (slot[None, :] == jnp.arange(rows)[:, None]).astype(BF16)
        count_own = jnp.sum(valid_mask.astype(F32))
        lane = jnp.arange(128)[None, :]
        notes = jnp.where(
            lane == 0,
            valid_mask.astype(F32)[:, None],
            jnp.where(lane == 1, spot.astype(F32)[:, None], jnp.where(lane == 2, count_own, 0.0)),
        ).astype(BF16)
        packed = jnp.concatenate(
            [conv_kernel.reshape(-1), w_beta.reshape(-1), norm_gain, ffn_gain,
             jnp.zeros((share * 128 - small,), BF16)]
        ).reshape(1, share, 128)
        sorted_rows = nn(sort, jnp.concatenate([tokens, notes], axis=1)).astype(BF16)
        message = jnp.concatenate(
            [sorted_rows.reshape(shards, share, -1), jnp.broadcast_to(packed, (shards, share, 128))],
            axis=2,
        )
        later = nn(sort, jnp.concatenate([cotangent, teacher], axis=1)).astype(BF16)
        later = later.reshape(shards, share, 2 * D)
        (win, wout), arrived = first([w_in, w_out], (2, 1), message, shards, 0)

        flat = arrived.reshape(rows, -1)
        info = flat[:, D : D + 128].astype(F32)
        place = info[:, 1].astype(jnp.int32)
        counted = jnp.sum(arrived[:, 0, D + 2].astype(F32))
        extra = arrived[:, :, D + 128 :].reshape(shards, share * 128)
        taps = extra[:, :a].reshape(shards, CONV, -1).swapaxes(0, 1).reshape(CONV, 3 * D).astype(F32)
        wbeta = extra[:, a : a + b].reshape(D, HEADS)
        gain_one = extra[:, a + b : a + b + c].reshape(D).astype(F32)
        gain_two = extra[:, a + b + c : a + b + 2 * c].reshape(D).astype(F32)
        deal = (place[None, :] == jnp.arange(rows)[:, None]).astype(BF16)
        deal_t = (place[:, None] == jnp.arange(rows)[None, :]).astype(BF16)
        dealt = nn(deal, flat[:, : D + 128])
        x = dealt[:, :D]
        m = dealt[:, D : D + 1]

        ends = jnp.cumsum(lengths, axis=1)
        within = jnp.arange(rows_mb, dtype=jnp.int32)
        seg = jnp.sum((within[None, :, None] >= ends[:, None, :]).astype(jnp.int32), axis=2)
        seg = (seg + (lengths.shape[1] + 1) * jnp.arange(blocks, dtype=jnp.int32)[:, None]).reshape(rows)
        position = jnp.arange(rows, dtype=jnp.int32)
        mask = jnp.stack(
            [jnp.ones((rows,), F32)]
            + [((position >= s) & (jnp.roll(seg, s) == seg)).astype(F32) for s in range(1, CONV)]
            + [jnp.zeros((rows,), F32)] * (8 - CONV),
            axis=1,
        )
        segc, segr = seg[:, None], seg[None, :]
        gain_out = out_gain.astype(F32)[None, :]

        nx, rx = rms(x)
        a1 = (nx * gain_one).astype(BF16)
        wdown, wgu, later, (*proj, beta_pre, on, o, ainv, u, p, l, resid, a2) = forward(
            w_down, w_gu, later, (1, 2), a1, win, wout, wbeta, x, gain_two[None, :], taps, gain_out, mask, segc,
            segr, blocks, shards, 2,
        )
        saved = (o, ainv, u, p, l)
        later = nn(deal, later.reshape(rows, 2 * D))
        g, t = later[:, :D], later[:, D:]
    gu = nn(a2, wgu)
    gate, up = gu[:, :FF], gu[:, FF:]
    hid = (gate * sigmoid(gate) * up).astype(BF16)
    y = resid + nn(hid, wdown)
    errors = y - t
    loss_part = jnp.sum(m * errors * errors)
    dy = g + (rows * shards / counted) * m * errors
    df = dy.astype(BF16)
    if share % 8 == 0 and (D // shards) % 16 == 0:
        sent_y = nn(deal_t, y.astype(BF16)).astype(BF16).reshape(shards, share, D)
        g_down, g_gu, g_in, g_out, got_y, got_dx, summed = rear(
            tn(hid, df, BF16), sent_y, dy, resid, x, a2_t, a1_t, df, gu, wgu, wdown, gain_two[None, :], gain_one[None, :],
            wout, win, on, wbeta, deal_t, loss_part.reshape(1, 1), proj, beta_pre, taps, gain_out, mask, segc,
            segr, saved, blocks, shards, 1,
        )
        (output, input_grad, g_in, g_beta, g_taps, g_out, g_gain_one, g_gain_out, g_gain_two, g_gu, g_down,
         loss) = settle(got_y, got_dx, sort_t, summed, counted.reshape(1, 1), g_down, g_gu, g_in, g_out)
        g_gain_one, g_gain_out, g_gain_two = g_gain_one[0], g_gain_out[0], g_gain_two[0]
        loss = loss[0, 0]
    else:
        (g_down, g_gu, dwq, dwk, dwv, dwg, dw_out, d_wbeta, dx, d_gain_two, d_gain_one, dtq, dtk, dtv,
         d_gain_out) = backward(
            tn(hid, df, BF16), df, a2, gu, wgu, wdown, dy, resid, gain_two[None, :], wout, win, a1, on, x,
            gain_one[None, :], wbeta, proj, beta_pre, taps, gain_out, mask, segc, segr, saved, blocks, shards,
            1,
        )
        back = jnp.concatenate([y.astype(BF16), dx], axis=1)
        back = nn(deal_t, back).astype(BF16).reshape(shards, share, 2 * D)
        (g_out, *g_in), back = scatter([dw_out, dwq, dwk, dwv, dwg], back, shards, 3)
        g_in = jnp.concatenate(g_in, axis=1)
        back = nn(sort_t, back.reshape(rows, 2 * D)).astype(BF16)
        output, input_grad = back[:, :D], back[:, D:]

        d_taps = jnp.concatenate([dtq, dtk, dtv], axis=1)
        tail = jnp.concatenate([d_gain_out.reshape(-1), loss_part.reshape(1)])
        extra = jnp.concatenate(
            [
                d_taps.reshape(CONV, shards, -1).swapaxes(0, 1).reshape(shards, a),
                d_wbeta.reshape(shards, b),
                d_gain_one.reshape(shards, c),
                d_gain_two.reshape(shards, c),
                jnp.broadcast_to(tail[None], (shards, tail.shape[0])),
            ],
            axis=1,
        )
        padded = -(-extra.shape[1] // 128) * 128
        extra = jnp.pad(extra, ((0, 0), (0, padded - extra.shape[1])))
        summed = jnp.sum(
            lax.all_to_all(
                extra.reshape(shards, padded // 128, 128), AXES, split_axis=0, concat_axis=0, tiled=True
            ),
            axis=0,
        ).reshape(-1)
        g_taps = summed[:a].reshape(CONV, -1)
        g_beta = summed[a : a + b].reshape(-1, HEADS)
        g_gain_one = summed[a + b : a + b + c]
        g_gain_two = summed[a + b + c : a + b + 2 * c]
        g_gain_out = summed[a + b + 2 * c : a + b + 2 * c + HEAD_DIM]
        loss = summed[a + b + 2 * c + HEAD_DIM] / (D * counted)

    return (
        output, input_grad, g_in, g_beta, g_taps, g_out, g_gain_one, g_gain_out, g_gain_two, g_gu,
        g_down, loss,
    )


def solution(mesh):
    both = P(AXES, None)
    flat = P(AXES)
    in_specs = (both, both, both, flat, flat, both, both, both, P(None, AXES), both, flat, P(), flat,
                both, both)
    out_specs = (both, both, both, both, P(None, AXES), both, flat, P(), flat, both, both, P())
    return jax.shard_map(local, mesh=mesh, in_specs=in_specs, out_specs=out_specs, check_vma=False)
```

```python
import functools

import jax
import jax.numpy as jnp
from jax import lax
from jax.experimental import pallas as pl
from jax.experimental.pallas import tpu as pltpu
from jax.sharding import PartitionSpec as P

D = 1024
HEADS = 8
HEAD_DIM = 128
FF = 2816
CONV = 4
AXES = ("dp", "fsdp")
F32 = jnp.float32
BF16 = jnp.bfloat16
PAIR = 2
MESH = pl.DeviceIdType.MESH


def mm(left, right, lc, rc):
    return lax.dot_general(
        left,
        right,
        (((lc,), (rc,)), ((), ())),
        precision=lax.Precision.HIGHEST,
        preferred_element_type=F32,
    )


def sigmoid(v):
    return 1.0 / (1.0 + jnp.exp(-v))


def iota2(shape, axis):
    return lax.broadcasted_iota(jnp.int32, shape, axis)


def unit_lower_inverses(mats, size):
    row, col = iota2((size, size), 0), iota2((size, size), 1)
    eye = (row == col).astype(F32)
    inverses = None
    width = 1
    while width < size:
        corner = ((row // (2 * width)) == (col // (2 * width))) & (
            (row // width) == (col // width) + 1
        )
        edges = [jnp.where(corner, m, 0.0) for m in mats]
        if inverses is None:
            inverses = [eye - e for e in edges]
        else:
            right = [mm(e, x, 1, 0) for e, x in zip(edges, inverses)]
            inverses = [x - mm(x, r, 1, 0) for x, r in zip(inverses, right)]
        width *= 2
    return inverses


def conv_parts(src, taps, masks):
    rolled = [src]
    total = src * taps[CONV - 1 : CONV, :]
    for s in range(1, CONV):
        moved = pltpu.roll(src, s, 0) * masks[s]
        rolled.append(moved)
        total = total + moved * taps[CONV - 1 - s : CONV - s, :]
    return total, rolled


def l2_norm(c):
    inv = lax.rsqrt(jnp.sum(c * c, axis=-1, keepdims=True) + 1e-06)
    return c * inv, inv


def mixer_fwd_kernel(
    blocks, rows_mb,
    pq, pk, pv, pg, beta, tq, tk, tv, gain, mask, segc, segr,
    on_ref, o_ref, ainv_ref, u_ref, p_ref, l_ref,
):
    step = pl.program_id(0)
    masks = [None] + [mask[:, s : s + 1] for s in range(1, CONV)]
    cs = []
    for src, taps in ((pq, tq), (pk, tk), (pv, tv)):
        pre, _ = conv_parts(src[...], taps[...], masks)
        cs.append(pre * sigmoid(pre))
    cq, ck, cv = cs
    strengths = sigmoid(beta[...])
    lane = iota2(strengths.shape, 1)
    gate = pg[...]
    gate = gate * sigmoid(gate)
    row, col = iota2((rows_mb, rows_mb), 0), iota2((rows_mb, rows_mb), 1)
    systems = [(h, b) for h in range(PAIR) for b in range(blocks)]
    qs, ks, vs, bs, sames, lows = [], [], [], [], [], []
    for h, b in systems:
        rs = slice(b * rows_mb, (b + 1) * rows_mb)
        hs = slice(h * HEAD_DIM, (h + 1) * HEAD_DIM)
        q, _ = l2_norm(cq[rs, hs])
        k, _ = l2_norm(ck[rs, hs])
        qs.append(q * HEAD_DIM ** (-0.5))
        ks.append(k)
        vs.append(cv[rs, hs])
        bs.append(
            jnp.sum(jnp.where(lane == step * PAIR + h, strengths, 0.0), axis=1, keepdims=True)[rs]
        )
        sames.append(segc[rs, :] == segr[:, rs])
    for i in range(len(systems)):
        lows.append(jnp.where(sames[i] & (row > col), mm(ks[i], ks[i], 1, 1), 0.0))
    inverses = unit_lower_inverses([l * b for l, b in zip(lows, bs)], rows_mb)
    us = [mm(a, v * b, 1, 0) for a, v, b in zip(inverses, vs, bs)]
    ps = [
        jnp.where(same & (row >= col), mm(q, k, 1, 1), 0.0)
        for q, k, same in zip(qs, ks, sames)
    ]
    os = [mm(p, u, 1, 0) for p, u in zip(ps, us)]
    for i, (h, b) in enumerate(systems):
        rs = slice(b * rows_mb, (b + 1) * rows_mb)
        hs = slice(h * HEAD_DIM, (h + 1) * HEAD_DIM)
        o = os[i]
        inv = lax.rsqrt(jnp.mean(o * o, axis=-1, keepdims=True) + 1e-05)
        on_ref[rs, hs] = (o * inv * gain[...] * gate[rs, hs]).astype(BF16)
        o_ref[rs, hs] = o
        ainv_ref[h, b] = inverses[i]
        u_ref[h, b] = us[i]
        p_ref[h, b] = ps[i]
        l_ref[h, b] = lows[i]


def mixer_bwd_kernel(
    blocks, rows_mb, pair, step,
    pq, pk, pv, pg, beta, tq, tk, tv, gain, mask, segc, segr,
    don_ref, o_ref, ainv_ref, u_ref, p_ref, l_ref,
    dq_ref, dk_ref, dv_ref, dg_ref, dbeta_ref, dtq, dtk, dtv, dgain_ref,
):
    rows = blocks * rows_mb
    masks = [None] + [mask[:, s : s + 1] for s in range(1, CONV)]
    pres, rolls, cs, sig = [], [], [], []
    for src, taps in ((pq, tq), (pk, tk), (pv, tv)):
        pre, rolled = conv_parts(src[...], taps[...], masks)
        s = sigmoid(pre)
        pres.append(pre)
        rolls.append(rolled)
        sig.append(s)
        cs.append(pre * s)
    cq, ck, cv = cs
    strengths = sigmoid(beta[...])
    lane = iota2(strengths.shape, 1)
    row, col = iota2((rows_mb, rows_mb), 0), iota2((rows_mb, rows_mb), 1)
    gates = pg[...]
    gsig = sigmoid(gates)
    gate = gates * gsig
    dgate = gsig * (1.0 + gates * (1.0 - gsig))
    systems = [(h, b) for h in range(pair) for b in range(blocks)]
    part = []
    dgain = jnp.zeros((1, HEAD_DIM), F32)
    for h, b in systems:
        rs = slice(b * rows_mb, (b + 1) * rows_mb)
        hs = slice(h * HEAD_DIM, (h + 1) * HEAD_DIM)
        k, ik = l2_norm(ck[rs, hs])
        qn, iq = l2_norm(cq[rs, hs])
        v = cv[rs, hs]
        bb = jnp.sum(jnp.where(lane == step * pair + h, strengths, 0.0), axis=1, keepdims=True)[rs]
        same = segc[rs, :] == segr[:, rs]
        o = o_ref[rs, hs]
        don = don_ref[rs, hs]
        inv = lax.rsqrt(jnp.mean(o * o, axis=-1, keepdims=True) + 1e-05)
        no = o * inv
        scaled = don * gain[...]
        dg_ref[rs, hs] = (scaled * no * dgate[rs, hs]).astype(BF16)
        dgain = dgain + jnp.sum(don * no * gate[rs, hs], axis=0, keepdims=True)
        dno = scaled * gate[rs, hs]
        do = inv * (dno - no * jnp.mean(no * dno, axis=-1, keepdims=True))
        part.append([q_ for q_ in (qn, iq, k, ik, v, bb, same, do)])
    dus = [mm(p_ref[h, b], part[i][7], 0, 0) for i, (h, b) in enumerate(systems)]
    dps = [
        jnp.where(part[i][6] & (row >= col), mm(part[i][7], u_ref[h, b], 1, 1), 0.0)
        for i, (h, b) in enumerate(systems)
    ]
    drs = [mm(ainv_ref[h, b], dus[i], 0, 0) for i, (h, b) in enumerate(systems)]
    scale = HEAD_DIM ** (-0.5)
    dqs = [mm(dps[i], part[i][2], 1, 0) * scale for i in range(len(systems))]
    das = [mm(drs[i], u_ref[h, b], 1, 1) for i, (h, b) in enumerate(systems)]
    dks = [mm(dps[i], part[i][0] * scale, 0, 0) for i in range(len(systems))]
    dgs = []
    for i in range(len(systems)):
        g = jnp.where(part[i][6] & (row > col), das[i] * (-part[i][5]), 0.0)
        dgs.append(g + g.T)
    dks = [dks[i] + mm(dgs[i], part[i][2], 1, 0) for i in range(len(systems))]
    dbeta = jnp.zeros(strengths.shape, F32)
    dcs = [[], [], []]
    for i, (h, b) in enumerate(systems):
        qn, iq, k, ik, v, bb, same, do = part[i]
        dv = drs[i] * bb
        db = jnp.sum(drs[i] * v - das[i] * l_ref[h, b], axis=-1, keepdims=True)
        dbp = db * bb * (1.0 - bb)
        pieces = [dbp if b == c else jnp.zeros((rows_mb, 1), F32) for c in range(blocks)]
        column = jnp.concatenate(pieces, axis=0) if blocks > 1 else dbp
        dbeta = dbeta + jnp.where(lane == step * pair + h, column, 0.0)
        dcs[0].append(iq * (dqs[i] - qn * jnp.sum(qn * dqs[i], axis=-1, keepdims=True)))
        dcs[1].append(ik * (dks[i] - k * jnp.sum(k * dks[i], axis=-1, keepdims=True)))
        dcs[2].append(dv)
    for j, (out, dtap, taps) in enumerate(((dq_ref, dtq, tq), (dk_ref, dtk, tk), (dv_ref, dtv, tv))):
        whole = jnp.concatenate(
            [
                jnp.concatenate([dcs[j][h * blocks + b] for b in range(blocks)], axis=0)
                for h in range(pair)
            ],
            axis=1,
        )
        dpre = whole * (sig[j] * (1.0 + pres[j] * (1.0 - sig[j])))
        tap = taps[...]
        grad = dpre * tap[CONV - 1 : CONV, :]
        dtap[CONV - 1 : CONV, :] = jnp.sum(dpre * rolls[j][0], axis=0, keepdims=True)
        for s in range(1, CONV):
            dtap[CONV - 1 - s : CONV - s, :] = jnp.sum(dpre * rolls[j][s], axis=0, keepdims=True)
            grad = grad + pltpu.roll(dpre * masks[s], rows - s, 0) * tap[CONV - 1 - s : CONV - s, :]
        out[...] = grad.astype(BF16)

    @pl.when(step == 0)
    def _():
        dbeta_ref[...] = jnp.zeros_like(dbeta_ref)
        dgain_ref[...] = jnp.zeros_like(dgain_ref)

    dbeta_ref[...] += dbeta
    dgain_ref[...] += dgain


def mixer_specs(rows, blocks, rows_mb):
    width = PAIR * HEAD_DIM
    per = D // width
    col = lambda k: pl.BlockSpec((rows, width), lambda i, k=k: (0, k * per + i))
    tap = lambda k: pl.BlockSpec((CONV, width), lambda i, k=k: (0, k * per + i))
    full = lambda shape: pl.BlockSpec(shape, lambda i: (0,) * len(shape))
    ins = [col(0), col(1), col(2), col(3), full((rows, HEADS)), tap(0), tap(1), tap(2),
           full((1, HEAD_DIM)), full((rows, 8)), full((rows, 1)), full((1, rows))]
    mat = pl.BlockSpec((PAIR, blocks, rows_mb, rows_mb), lambda i: (i, 0, 0, 0))
    one = pl.BlockSpec((rows, width), lambda i: (0, i))
    otap = pl.BlockSpec((CONV, width), lambda i: (0, i))
    return ins, mat, one, otap, full


def lin_index():
    return lax.axis_index("dp") * lax.axis_size("fsdp") + lax.axis_index("fsdp")


def mesh_id(index):
    inner = lax.axis_size("fsdp")
    return (lax.div(index, inner), lax.rem(index, inner))


class Here:
    def __init__(self, shards):
        self.shards, self.me = shards, lin_index()
        self.bits = shards.bit_length() - 1
        own = [lax.rem(lax.div(self.me, 1 << b), 2) for b in range(self.bits)]
        self.core = own[0]
        self.change = [(1 - 2 * o) * (1 << b) for b, o in enumerate(own)]
        self.partner = [mesh_id(self.me + c) for c in self.change]

    def flip(self, bits, number, always=()):
        result = self.me
        for bit in always:
            result = result + self.change[bit]
        for i, bit in enumerate(reversed(bits)):
            if isinstance(number, int):
                if (number >> i) & 1:
                    result = result + self.change[bit]
            else:
                result = result + lax.rem(lax.div(number, 1 << i), 2) * self.change[bit]
        return result


def routes(shards):
    bits = shards.bit_length() - 1
    rest = list(range(4, bits))
    return [[1, 2, 3] + rest, [2, 3, 1] + rest, [3, 1, 2] + rest]


def colours(width, turn):
    tiles = width // 128
    one, three = round(tiles * 0.36), round(tiles * 0.28)
    sizes = (one, tiles - one - three, three)
    return [(sum(sizes[:c]) * 128, sizes[c] * 128) for c in range(3)]


def meet(here, everyone):
    barrier = pltpu.get_barrier_semaphore()
    if everyone:

        def greet(r, _):
            peer = lax.rem(here.me + r, here.shards)
            pl.semaphore_signal(barrier, inc=1, device_id=mesh_id(peer), device_id_type=MESH)
            return 0

        lax.fori_loop(1, here.shards, greet, 0)
        pl.semaphore_wait(barrier, here.shards - 1)
    else:
        for partner in here.partner:
            pl.semaphore_signal(barrier, inc=1, device_id=partner, device_id_type=MESH)
        pl.semaphore_wait(barrier, here.bits)


def spread_order(shards):
    bits = shards.bit_length() - 1
    turned = [sum(((i >> b) & 1) << (bits - 1 - b) for b in range(bits)) for i in range(shards)]
    return turned[1:]


class Exchange:
    def __init__(self, here, sent, got, send, recv, keep, same=False):
        self.here, self.shards, self.me, self.got = here, here.shards, here.me, got
        self.block = (lambda d: sent) if same else (lambda d: sent.at[d])
        self.send, self.recv, self.keep = send, recv, keep

    def own(self):
        return pltpu.make_async_copy(self.block(self.me), self.got.at[self.me], self.keep)

    def start(self):
        self.own().start()

        def one(r, _):
            peer = lax.rem(self.me + r, self.shards)
            pltpu.make_async_remote_copy(
                src_ref=self.block(peer), dst_ref=self.got.at[self.me], send_sem=self.send,
                recv_sem=self.recv, device_id=mesh_id(peer), device_id_type=MESH,
            ).start()
            return 0

        lax.fori_loop(1, self.shards, one, 0)

    def start_part(self, part, parts):
        others = self.shards - 1
        if part == 0:
            self.own().start()
        for r in range(others * part // parts, others * (part + 1) // parts):
            peer = lax.rem(self.me + spread_order(self.shards)[r], self.shards)
            pltpu.make_async_remote_copy(
                src_ref=self.block(peer), dst_ref=self.got.at[self.me], send_sem=self.send,
                recv_sem=self.recv, device_id=mesh_id(peer), device_id_type=MESH,
            ).start()

    def wait(self):
        self.own().wait()
        whole = pl.ds(0, self.shards - 1)
        pltpu.make_async_remote_copy(
            src_ref=self.got.at[whole], dst_ref=self.got.at[whole], send_sem=self.send,
            recv_sem=self.recv, device_id=self.here.partner[0], device_id_type=MESH,
        ).wait()


DEAL_AT = 0
CHUNK = 256
X_STEPS = 5
GT_FROM = 6
SLICE = 256
FF_STEP = FF // 2
MIXER_BUFFERS = 2
DX_PARTS = 6


def pieces_of(widths, split):
    result = []
    for i, width in enumerate(widths):
        tiles, at = width // 128, 0
        for j in range(split[i]):
            size = tiles // split[i] + (1 if j < tiles % split[i] else 0)
            result.append((i, at * 128, size * 128))
            at += size
    return result


class Gather:
    def __init__(self, here, pieces, own, full, sems):
        self.here, self.pieces, self.own, self.full = here, pieces, own, full
        self.send, self.recv, self.pair_send, self.pair_recv, self.keep = sems
        self.stages = here.bits - 1
        self.order = routes(here.shards)
        self.core = here.core
        self.cuts = [
            [(at + a, s) for a, s in colours(size, n)] for n, (_, at, size) in enumerate(pieces)
        ]
        self.last = len(pieces) + self.stages - 1

    @staticmethod
    def semaphores(shards, pieces):
        dma, stages = pltpu.SemaphoreType.DMA, shards.bit_length() - 2
        number = len(pieces)
        return [dma((stages, number, 3)), dma((stages, number, 3)), dma((number,)), dma((number,)),
                dma((number,))]

    def kept(self, i):
        return pltpu.make_async_copy(
            self.own[i], self.full[i].at[lax.div(self.here.me, 2), self.core], self.keep.at[i]
        )

    def begin(self):
        for i in range(len(self.own)):
            self.kept(i).start()

    def partner(self, k, c):
        return self.here.partner[self.order[c][self.stages - 1 - k]]

    def group(self, k, n, c):
        at, size = self.cuts[n][c]
        some = self.full[self.pieces[n][0]].at[pl.ds(0, 1 << k), 0, :, pl.ds(at, size)]
        return pltpu.make_async_remote_copy(
            src_ref=some, dst_ref=some, send_sem=self.send.at[k, n, c],
            recv_sem=self.recv.at[k, n, c], device_id=self.partner(k, c), device_id_type=MESH,
        )

    def half(self, n):
        i, at, size = self.pieces[n]
        some = self.full[i].at[:, self.core, :, pl.ds(at, size)]
        return pltpu.make_async_remote_copy(
            src_ref=some, dst_ref=some, send_sem=self.pair_send.at[n],
            recv_sem=self.pair_recv.at[n], device_id=self.here.partner[0],
            device_id_type=MESH,
        )

    def launch(self, k, n):
        i = self.pieces[n][0]
        for c in range(3):
            at, size = self.cuts[n][c]
            if k > 0:
                self.group(k - 1, n, c).wait_recv()
            have = self.order[c][self.stages - k :]
            for j in range(1 << k):
                d = self.here.flip(have, j)
                there = self.full[i].at[lax.div(d, 2), self.core, :, pl.ds(at, size)]
                pltpu.make_async_remote_copy(
                    src_ref=self.own[i].at[:, pl.ds(at, size)] if j == 0 else there,
                    dst_ref=there, send_sem=self.send.at[k, n, c], recv_sem=self.recv.at[k, n, c],
                    device_id=self.partner(k, c), device_id_type=MESH,
                ).start()

    def finish(self, n):
        for c in range(3):
            self.group(self.stages - 1, n, c).wait_recv()
        if n == 0 or self.pieces[n - 1][0] != self.pieces[n][0]:
            self.kept(self.pieces[n][0]).wait()
        self.half(n).start()

    def slots(self, first, last):
        return sum(
            0 <= t - n <= self.stages for t in range(first, last) for n in range(len(self.pieces))
        )

    def step(self, t, between=None):
        for n in range(len(self.pieces)):
            k = t - n
            if 0 <= k < self.stages:
                self.launch(k, n)
            elif k == self.stages:
                self.finish(n)
            if between is not None and 0 <= k <= self.stages:
                between()

    def end(self, arrived=0):
        for k in range(self.stages):
            for n in range(len(self.pieces)):
                for c in range(3):
                    self.group(k, n, c).wait_send()
        for n in range(len(self.pieces)):
            self.half(n).wait_send()
            if n >= arrived:
                self.half(n).wait_recv()


def first_kernel(shards, pieces, *refs):
    count = 1 + max(i for i, _, _ in pieces)
    own, sent, full, got = refs[:count], refs[count], refs[count + 1 : 2 * count + 1], refs[2 * count + 1]
    sems = refs[2 * count + 2 :]
    here = Here(shards)
    deal = Exchange(here, sent, got, *sems[5:])
    weights = Gather(here, pieces, own, full, sems[:5])
    weights.begin()
    meet(here, True)
    deal.start()
    for t in range(weights.last + 1):
        weights.step(t)
    deal.wait()
    weights.end()


def spread(weight, shards):
    return jax.ShapeDtypeStruct((shards // 2, 2) + weight.shape, weight.dtype)


def first(weights, split, message, shards, collective_id):
    count = len(weights)
    anywhere = pl.BlockSpec(memory_space=pl.ANY)
    pieces = pieces_of([w.shape[1] for w in weights], split)
    dma = pltpu.SemaphoreType.DMA
    *full, got = pl.pallas_call(
        functools.partial(first_kernel, shards, pieces),
        in_specs=[anywhere] * (count + 1),
        out_specs=[anywhere] * (count + 1),
        out_shape=[spread(w, shards) for w in weights]
        + [jax.ShapeDtypeStruct(message.shape, message.dtype)],
        scratch_shapes=Gather.semaphores(shards, pieces) + [dma, dma, dma],
        compiler_params=pltpu.CompilerParams(collective_id=collective_id, has_side_effects=True),
        name="gather_first",
    )(*weights, message)
    return [f.reshape(-1, f.shape[-1]) for f in full], got


def forward_kernel(
    shards, pieces, blocks, rows_mb,
    own_down, own_gu, sent, a1, wq, wk, wv, wg, wout, wbeta, x, gain_two, tq, tk, tv, gain, mask,
    segc, segr,
    full_down, full_gu, got, pq, pk, pv, pg, beta, on, o, ainv, u, p, l, resid, a2,
    *sems,
):
    step = pl.program_id(0)
    steps = HEADS // PAIR
    here = Here(shards)
    weights = Gather(here, pieces, (own_down, own_gu), (full_down, full_gu), sems[:5])
    deal = Exchange(here, sent, got, *sems[5:])

    @pl.when(step == 0)
    def _():
        weights.begin()
        meet(here, True)
        weights.step(0)
        resid[...] = x[...]

    normed = a1[...]
    beta[...] = jnp.dot(normed, wbeta[...], preferred_element_type=F32)
    for out, w in ((pq, wq), (pk, wk), (pv, wv), (pg, wg)):
        out[...] = jnp.dot(normed, w[...], preferred_element_type=F32)
    mixer_fwd_kernel(
        blocks, rows_mb, pq, pk, pv, pg, beta, tq, tk, tv, gain, mask, segc, segr, on, o, ainv, u,
        p, l,
    )
    resid[...] += jnp.dot(on[...], wout[...], preferred_element_type=F32)
    for s in range(steps):

        @pl.when(step == s)
        def _(s=s):
            weights.step(s + 1)
            if s == DEAL_AT:
                deal.start()
            if s == steps - 1:
                r = resid[...]
                a2[...] = (rms(r)[0] * gain_two[...]).astype(BF16)
                for t in range(steps + 1, weights.last + 1):
                    weights.step(t)
                deal.wait()
                weights.end()


def forward(
    w_down, w_gu, message, split, a1, win, wout, wbeta, x, gain_two, taps, gain, mask, segc, segr, blocks,
    shards, collective_id,
):
    rows = x.shape[0]
    rows_mb = rows // blocks
    width = PAIR * HEAD_DIM
    pieces = pieces_of([w_down.shape[1], w_gu.shape[1]], split)
    anywhere = pl.BlockSpec(memory_space=pl.ANY)
    ins, mat, one, _, full = mixer_specs(rows, blocks, rows_mb)
    per = D // width
    wcol = lambda k: pl.BlockSpec((D, width), lambda i, k=k: (0, k * per + i))
    square = jax.ShapeDtypeStruct((HEADS, blocks, rows_mb, rows_mb), F32)
    wide = jax.ShapeDtypeStruct((rows, D), F32)
    dma = pltpu.SemaphoreType.DMA
    full_down, full_gu, got, *rest = pl.pallas_call(
        functools.partial(forward_kernel, shards, pieces, blocks, rows_mb),
        grid=(HEADS // PAIR,),
        in_specs=[
            anywhere, anywhere, anywhere, full((rows, D)), wcol(0), wcol(1), wcol(2), wcol(3),
            pl.BlockSpec((width, D), lambda i: (i, 0)), full((D, HEADS)), full((rows, D)),
            full((1, D)), *ins[5:],
        ],
        out_specs=[anywhere, anywhere, anywhere, one, one, one, one, full((rows, HEADS)), one, one, mat, mat,
                   mat, mat, full((rows, D)), full((rows, D))],
        out_shape=[
            spread(w_down, shards), spread(w_gu, shards),
            jax.ShapeDtypeStruct(message.shape, message.dtype), wide, wide, wide, wide,
            jax.ShapeDtypeStruct((rows, HEADS), F32), jax.ShapeDtypeStruct((rows, D), BF16), wide,
            square, square, square, square, wide, jax.ShapeDtypeStruct((rows, D), BF16),
        ],
        scratch_shapes=Gather.semaphores(shards, pieces) + [dma, dma, dma],
        compiler_params=pltpu.CompilerParams(
            collective_id=collective_id, has_side_effects=True, vmem_limit_bytes=48 << 20
        ),
        name="mixer_forward",
    )(w_down, w_gu, message, a1, win, win, win, win, wout, wbeta, x, gain_two, taps, taps, taps, gain, mask,
      segc, segr)
    return full_down.reshape(FF, D), full_gu.reshape(D, 2 * FF), got, rest


class Scatter:
    def __init__(self, here, pieces, whole, mine, other, coming, sems, kept):
        self.here, self.pieces, self.whole, self.mine = here, pieces, whole, mine
        self.other, self.coming, self.kept_of = other, coming, kept
        self.send, self.recv, self.pair_send, self.pair_recv = sems
        self.stages = here.bits - 1
        self.order = routes(here.shards)
        self.core = here.core
        self.cuts = [
            [(at + a, s) for a, s in colours(size, n)] for n, (_, at, size) in enumerate(pieces)
        ]

    @staticmethod
    def semaphores(shards, number):
        dma, stages = pltpu.SemaphoreType.DMA, shards.bit_length() - 2
        return [dma((stages, number, 3)), dma((stages, number, 3)), dma((number,)), dma((number,))]

    @staticmethod
    def buffers(shards, shapes):
        stages = shards.bit_length() - 2
        return [pltpu.VMEM((shards // 2,) + s, BF16) for s in shapes] + [
            pltpu.VMEM((1 << (stages - 1 - k),) + s, BF16) for s in shapes for k in range(stages)
        ]

    @staticmethod
    def split(shards, count, refs):
        stages = shards.bit_length() - 2
        other, refs = refs[:count], refs[count:]
        return other, [refs[i * stages : (i + 1) * stages] for i in range(count)]

    def pair(self, n):
        i, at, size = self.pieces[n]
        return pltpu.make_async_remote_copy(
            src_ref=self.whole(n, 1 - self.core), dst_ref=self.other[i].at[:, :, pl.ds(at, size)],
            send_sem=self.pair_send.at[n], recv_sem=self.pair_recv.at[n],
            device_id=self.here.partner[0], device_id_type=MESH,
        )

    def hop(self, k, n, c, source, spots):
        i = self.pieces[n][0]
        at, size = self.cuts[n][c]
        cols = pl.ds(at, size)
        return pltpu.make_async_remote_copy(
            src_ref=self.other[i].at[source, :, cols],
            dst_ref=self.coming[i][k].at[spots, :, cols],
            send_sem=self.send.at[k, n, c], recv_sem=self.recv.at[k, n, c],
            device_id=self.here.partner[self.order[c][k]], device_id_type=MESH,
        )

    def group(self, k, n, c):
        all_of = pl.ds(0, 1 << (self.stages - 1 - k))
        return self.hop(k, n, c, all_of, all_of)

    def total(self, k, n, c, shard, spot):
        i = self.pieces[n][0]
        at, size = self.cuts[n][c]
        cols = pl.ds(at, size)
        q = lax.div(shard, 2)
        value = self.mine(i, q, cols).astype(F32) + self.other[i][q, :, cols].astype(F32)
        for p in range(k):
            value = value + self.coming[i][p][spot, :, cols].astype(F32)
        return value

    def launch(self, k, n):
        if k == 0:
            kept = self.kept_of(n)
            if kept is not None:
                kept.wait()
            self.pair(n).wait_recv()
        for c in range(3):
            if k > 0:
                self.group(k - 1, n, c).wait_recv()
            much = 1 << (self.stages - 1 - k)
            at, size = self.cuts[n][c]

            def body(j, _, c=c, at=at, size=size):
                shard = self.here.flip(self.order[c][k + 1 :], j, (self.order[c][k],))
                q = lax.div(shard, 2)
                self.other[self.pieces[n][0]][q, :, pl.ds(at, size)] = self.total(
                    k, n, c, shard, much + j
                ).astype(BF16)
                self.hop(k, n, c, q, j).start()
                return 0

            lax.fori_loop(0, much, body, 0)

    def finish(self, n, write):
        for c in range(3):
            self.group(self.stages - 1, n, c).wait_recv()
            at, size = self.cuts[n][c]
            write(self.pieces[n][0], at, size, self.total(self.stages, n, c, self.here.me, 0))

    def end(self, n, paired=True):
        for k in range(self.stages):
            for c in range(3):
                self.group(k, n, c).wait_send()
        if paired:
            self.pair(n).wait_send()


def front_kernel(shards, blocks, rows_mb, split, *refs):
    (own_in, own_out, own_down, own_gu, small, tokens, cotangent, teacher, deal_row, valid_row, lengths, gain), refs = refs[:12], refs[12:]
    (full_in, full_out, full_down, full_gu, pq, pk, pv, pg, beta, on, o, ainv, u, p, l, resid, a2, x, m, counted, deal, sort_t, gt, taps,
     gain_one, gain_two, wbeta, segc, segr, mask, a1, a1_t, a2_t), refs = refs[:33], refs[33:]
    (sent, got, sent_gt, got_gt, got_small, wbuf, wout, w_sem, out_sem), refs = refs[:9], refs[9:]
    sems, deal_sems, later_sems, small_sems = refs[:5], refs[5:8], refs[8:11], refs[11:14]
    step = pl.program_id(0)
    steps = HEADS // PAIR
    width = PAIR * HEAD_DIM
    rows = blocks * rows_mb
    share = rows // shards
    here = Here(shards)
    pieces = pieces_of([4 * D, D, D, 2 * FF], split)
    weights = Gather(here, pieces, (own_in, own_out, own_down, own_gu), (full_in, full_out, full_down, full_gu), sems)
    first_send = Exchange(here, sent, got, *deal_sems)
    second_send = Exchange(here, sent_gt, got_gt, *later_sems)
    small_send = Exchange(here, small, got_small, *small_sems, same=True)
    of_in = split[0]
    hidden_from = len(pieces) + weights.stages - steps
    deal_to, later_from = X_STEPS, GT_FROM

    def trickle(exchange, first, last):
        parts, done = weights.slots(first, last), [0]

        def at(t):
            if not first <= t < last:
                return None
            done[0] = weights.slots(first, t)

            def one():
                exchange.start_part(done[0], parts)
                done[0] += 1

            return one

        return at

    deal_some = trickle(first_send, 1, deal_to)
    later_some = trickle(second_send, later_from, weights.last + 1)

    def between(t):
        acts = [f for f in (deal_some(t), later_some(t)) if f is not None]
        return (lambda: [f() for f in acts]) if acts else None

    def fetch(s, g):
        return pltpu.make_async_copy(
            full_in.at[:, :, :, pl.ds(g * D + s * width, width)], wbuf.at[s % 2, g], w_sem.at[s % 2, g]
        )

    def fetch_out():
        return pltpu.make_async_copy(full_out, wout, out_sem)

    @pl.when(step == 0)
    def _():
        weights.begin()
        meet(here, True)
        weights.step(0)
        small_send.start()
        row, col = iota2((rows, rows), 0), iota2((rows, rows), 1)
        column = lambda v: jnp.sum(jnp.where(row == col, v, 0.0), axis=1, keepdims=True)
        dealt = deal_row[...].astype(F32)
        target = jnp.floor((dealt + 0.5) * (1.0 / rows))
        valid = valid_row[...].astype(F32)
        target_c = column(target)
        rank = jnp.sum(jnp.where((target == target_c) & (col < row), 1.0, 0.0), axis=1, keepdims=True)
        slot = target_c * share + rank
        sort_t[...] = (slot == col.astype(F32)).astype(BF16)
        lane = iota2((rows, 128), 1)
        notes = jnp.where(
            lane == 0, column(valid),
            jnp.where(lane == 1, column(dealt - target * rows), jnp.where(lane == 2, jnp.sum(valid), 0.0)),
        ).astype(BF16)
        sent[:, :, :D] = tn(sort_t[...], tokens[...]).reshape(shards, share, D).astype(BF16)
        sent[:, :, D:] = tn(sort_t[...], notes).reshape(shards, share, 128).astype(BF16)
        weights.step(1, between(1))
        for at, part in ((0, cotangent), (D, teacher)):
            sent_gt[:, :, at : at + D] = tn(sort_t[...], part[...]).reshape(shards, share, D).astype(BF16)
        weights.step(2, between(2))
        at_row, at_col = iota2((rows, 1), 0), iota2((1, rows), 1)
        seg_c, seg_r = jnp.zeros((rows, 1), F32), jnp.zeros((1, rows), F32)
        lens = lengths[...].astype(F32)
        for b in range(blocks):
            end = jnp.zeros((1, 1), F32) + b * rows_mb
            for i in range(lengths.shape[1]):
                seg_c = seg_c + jnp.where(at_row >= b * rows_mb, 1.0, 0.0) * (i == 0)
                seg_r = seg_r + jnp.where(at_col >= b * rows_mb, 1.0, 0.0) * (i == 0)
                end = end + lens[b : b + 1, i : i + 1]
                if i < lengths.shape[1] - 1:
                    seg_c = seg_c + jnp.where(at_row.astype(F32) >= end, 1.0, 0.0)
                    seg_r = seg_r + jnp.where(at_col.astype(F32) >= end, 1.0, 0.0)
        segc[...] = seg_c.astype(jnp.int32)
        segr[...] = seg_r.astype(jnp.int32)
        lane8 = iota2((rows, 8), 1)
        wide = jnp.broadcast_to(seg_c, (rows, 128))
        marks = jnp.where(lane8 == 0, 1.0, 0.0)
        for s in range(1, CONV):
            before = pltpu.roll(wide, s, 0)[:, :1]
            same = jnp.where((before == seg_c) & (at_row >= s), 1.0, 0.0)
            marks = marks + jnp.where(lane8 == s, same, 0.0)
        mask[...] = marks
        small_send.wait()
        own_taps, own_gain = 3 * D // shards, D // shards
        per = 128 // own_gain
        a, c = iota2((per * 128, per * own_taps), 0), iota2((per * 128, per * own_taps), 1)
        pick_taps = ((a // 128 == c // own_taps) & (a % 128 == c % own_taps)).astype(BF16)
        a, c = iota2((per * 128, 128), 0), iota2((per * 128, 128), 1)
        pick_gain = ((a // 128 == c // own_gain) & (a % 128 == c % own_gain)).astype(BF16)
        for g in range(shards // per):
            left = jnp.concatenate([got_small[g * per + i, :, :128].astype(F32) for i in range(per)], axis=1).astype(BF16)
            right = jnp.concatenate([got_small[g * per + i, :, 128:].astype(F32) for i in range(per)], axis=1).astype(BF16)
            tap = nn(left, pick_taps)
            taps[:, g * per * own_taps : (g + 1) * per * own_taps] = tap[:CONV]
            gains = nn(left, pick_gain)
            gain_one[:, g * 128 : (g + 1) * 128] = gains[4:5]
            gain_two[:, g * 128 : (g + 1) * 128] = gains[5:6]
            wbeta[:, g * 128 : (g + 1) * 128] = nn(right, pick_gain).astype(BF16)
        for t in range(3, hidden_from):
            weights.step(t, between(t))
        first_send.wait()
        flat = got[...].astype(F32).reshape(rows, D + 128)
        notes = flat[:, D:]
        deal[...] = (notes[:, 1:2] == col.astype(F32)).astype(BF16)
        m[...] = tn(deal[...], notes.astype(BF16))[:, :1]
        firsts = jnp.where(lax.rem(iota2((rows, 1), 0), share) == 0, notes[:, 2:3], 0.0)
        counted[...] = jnp.sum(firsts, axis=0, keepdims=True)
        x_now = tn(deal[...], flat[:, :D].astype(BF16))
        x[...] = x_now
        a1[...] = (rms(x_now)[0] * gain_one[...]).astype(BF16)
        beta[...] = nt(a1[...], wbeta[...])
        a1_t[...] = a1[...].T
        for n in range(of_in):
            weights.half(n).wait_recv()
        for g in range(4):
            fetch(0, g).start()

    for s in range(steps):

        @pl.when(step == s)
        def _(s=s):
            for g in range(4):
                fetch(s, g).wait()
            if s + 1 < steps:
                for g in range(4):
                    fetch(s + 1, g).start()

    slot_now = lax.rem(step, 2)
    for g, out in enumerate((pq, pk, pv, pg)):
        out[...] = nn(a1[...], wbuf[slot_now, g].reshape(D, width))
    here_cols = pl.ds(pl.multiple_of(step * width, width), width)
    taps_of = lambda j: taps.at[:, pl.ds(pl.multiple_of(j * D + step * width, width), width)]
    mixer_fwd_kernel(
        blocks, rows_mb, pq, pk, pv, pg, beta, taps_of(0), taps_of(1), taps_of(2), gain, mask, segc, segr,
        on.at[:, here_cols], o, ainv, u, p, l,
    )
    for s in range(steps):

        @pl.when(step == s)
        def _(s=s):
            weights.step(hidden_from + s, between(hidden_from + s))
            if s == steps - 1:
                for n in range(of_in, of_in + split[1]):
                    weights.half(n).wait_recv()
                fetch_out().start()
                second_send.wait()
                gt[...] = tn(deal[...], got_gt[...].astype(F32).reshape(rows, gt.shape[1]).astype(BF16))
                fetch_out().wait()
                r = x[...] + nn(on[...], wout[...].reshape(D, D))
                resid[...] = r
                a2[...] = (rms(r)[0] * gain_two[...]).astype(BF16)
                a2_t[...] = a2[...].T
                weights.end(of_in + split[1])


def front(weights, small, tokens, cotangent, teacher, deal_rows, valid_mask, lengths, gain, shards, collective_id):
    rows, blocks = tokens.shape[0], lengths.shape[0]
    rows_mb, share = rows // blocks, rows // shards
    width = PAIR * HEAD_DIM
    split = (2, 1, 1, 2)
    pieces = pieces_of([w.shape[1] for w in weights], split)
    anywhere = pl.BlockSpec(memory_space=pl.ANY)
    _, mat, one, _, full = mixer_specs(rows, blocks, rows_mb)
    f32 = lambda *shape: jax.ShapeDtypeStruct(shape, F32)
    bf = lambda *shape: jax.ShapeDtypeStruct(shape, BF16)
    square = f32(HEADS, blocks, rows_mb, rows_mb)
    wide = f32(rows, D)
    vm, dma = pltpu.VMEM, pltpu.SemaphoreType.DMA
    outs = [
        (spread(w, shards), anywhere) for w in weights
    ] + [(wide, one)] * 4 + [
        (f32(rows, HEADS), full((rows, HEADS))), (bf(rows, D), full((rows, D))), (wide, one),
        (square, mat), (square, mat), (square, mat), (square, mat), (wide, full((rows, D))),
        (bf(rows, D), full((rows, D))), (wide, full((rows, D))), (f32(rows, 1), full((rows, 1))),
        (f32(1, 1), full((1, 1))), (bf(rows, rows), full((rows, rows))), (bf(rows, rows), full((rows, rows))),
        (f32(rows, 2 * D), full((rows, 2 * D))), (f32(CONV, 3 * D), full((CONV, 3 * D))),
        (f32(1, D), full((1, D))), (f32(1, D), full((1, D))), (bf(8, D), full((8, D))),
        (jax.ShapeDtypeStruct((rows, 1), jnp.int32), full((rows, 1))),
        (jax.ShapeDtypeStruct((1, rows), jnp.int32), full((1, rows))), (f32(rows, 8), full((rows, 8))),
        (bf(rows, D), full((rows, D))), (bf(D, rows), full((D, rows))), (bf(D, rows), full((D, rows))),
    ]
    return pl.pallas_call(
        functools.partial(front_kernel, shards, blocks, rows_mb, split),
        grid=(HEADS // PAIR,),
        in_specs=[anywhere] * 4 + [
            full(small.shape), full((rows, D)), full((rows, D)), full((rows, D)), full((1, rows)), full((1, rows)),
            full(lengths.shape), full((1, HEAD_DIM)),
        ],
        out_specs=[s for _, s in outs],
        out_shape=[s for s, _ in outs],
        scratch_shapes=[
            vm((shards, share, D + 128), BF16), vm((shards, share, D + 128), BF16),
            vm((shards, share, 2 * D), BF16), vm((shards, share, 2 * D), BF16),
            vm((shards,) + small.shape, BF16),
            vm((2, 4, shards // 2, 2, D // shards, width), BF16),
            vm((shards // 2, 2, D // shards, D), BF16), dma((2, 4)), dma,
        ] + Gather.semaphores(shards, pieces) + [dma] * 9,
        compiler_params=pltpu.CompilerParams(
            collective_id=collective_id, has_side_effects=True, vmem_limit_bytes=58 << 20
        ),
        name="front",
    )(*weights, small, tokens, cotangent, teacher, deal_rows[None, :], valid_mask[None, :], lengths, gain)


def backward_kernel(shards, blocks, rows_mb, pieces, *refs):
    (d_down, df, a2, gate, up, wga, wup, wdn, dy, resid, gain_two, wout, wq, wk, wv, wg, a1, on, x,
     gain_one, wbeta, *mixer), refs = refs[:38], refs[38:]
    (g_down, g_gu, dwq, dwk, dwv, dwg, dw_out, d_wbeta, dx, d_two, d_one, dtq, dtk, dtv,
     d_gain), refs = refs[:15], refs[15:]
    (mine_down, d_gu, acc, dresid, dz, don, dpq, dpk, dpv, dpg, dbeta, keep), refs = refs[:12], refs[12:]
    sems, buffers = refs[:4], refs[4:]
    step = pl.program_id(0)
    chunks = FF // CHUNK
    pairs = HEADS // PAIR
    here = Here(shards)
    core = here.core
    other, coming = Scatter.split(shards, 2, buffers)
    r_gu = d_gu.shape[2]

    def whole(n, parity):
        i, at, size = pieces[n]
        if i == 0:
            return d_down.at[:, parity, :, pl.ds(at, size)]
        return d_gu.at[:, parity, :, pl.ds(at, size)]

    def mine(i, q, cols):
        return mine_down[q, :, cols] if i == 0 else d_gu[q, core, :, cols]

    def kept(n):
        if n > 0:
            return None
        return pltpu.make_async_copy(d_down.at[:, core], mine_down, keep)

    net = Scatter(here, pieces, whole, mine, other, coming, sems, kept)

    def write(i, at, size, value):
        if i == 0:
            g_down[:, pl.ds(at, size)] = value
            return
        for tile in range(at // 128, (at + size) // 128):
            chunk, inner = tile * 128 // (2 * CHUNK), tile * 128 % (2 * CHUNK)
            start = chunk * CHUNK + inner if inner < CHUNK else FF + chunk * CHUNK + inner - CHUNK
            g_gu[:, start : start + 128] = value[:, tile * 128 - at : tile * 128 - at + 128]

    @pl.when(step == 0)
    def _():
        kept(0).start()
        meet(here, False)
        net.pair(0).start()
        acc[...] = jnp.zeros_like(acc)

    @pl.when(step < chunks)
    def _():
        dhid = nt(df[...], wdn[...])
        g = gate[...]
        s = sigmoid(g)
        d_gate = (dhid * up[...] * (s * (1.0 + g * (1.0 - s)))).astype(BF16)
        d_up = (dhid * (g * s)).astype(BF16)
        acc[...] += nt(d_gate, wga[...]) + nt(d_up, wup[...])
        for at, part in ((0, d_gate), (CHUNK, d_up)):
            grad = tn(a2[...], part).reshape(shards // 2, 2, r_gu, CHUNK).astype(BF16)
            start = pl.multiple_of(step * (2 * CHUNK) + at, CHUNK)
            d_gu[:, :, :, pl.ds(start, CHUNK)] = grad

    @pl.when(step == chunks - 1)
    def _():
        nr, rr = rms(resid[...])
        da2 = acc[...]
        d_two[...] = jnp.sum(da2 * nr, axis=0, keepdims=True)
        dresid[...] = dy[...] + rms_back(nr, rr, gain_two[...] * da2)
        acc[...] = jnp.zeros_like(acc)
        dz[...] = dresid[...].astype(BF16)

    @pl.when(step >= chunks)
    def _():
        don[...] = nt(dz[...], wout[...])
        mixer_bwd_kernel(
            blocks, rows_mb, PAIR, step - chunks, *mixer[:12], don, *mixer[12:], dpq, dpk, dpv, dpg, dbeta, dtq,
            dtk, dtv, d_gain,
        )
        for dp, w, out in ((dpq, wq, dwq), (dpk, wk, dwk), (dpv, wv, dwv), (dpg, wg, dwg)):
            acc[...] += nt(dp[...], w[...])
            out[...] = tn(a1[...], dp[...]).astype(BF16)
        dw_out[...] = tn(on[...], dz[...]).astype(BF16)

    @pl.when(step == chunks + pairs - 1)
    def _():
        d_beta = dbeta[...].astype(BF16)
        grad = acc[...] + nt(d_beta, wbeta[...])
        d_wbeta[...] = tn(a1[...], d_beta)
        nx, rx = rms(x[...])
        d_one[...] = jnp.sum(grad * nx, axis=0, keepdims=True)
        dx[...] = (dresid[...] + rms_back(nx, rx, gain_one[...] * grad)).astype(BF16)

    ready = {pieces[n][1] // (2 * CHUNK) + pieces[n][2] // (2 * CHUNK) - 1: n for n in (1, 2)}
    plan = {}
    for s, n in ready.items():
        plan.setdefault(s, []).append((net.pair, n))
    tail = range(chunks - 1, chunks + pairs)
    plan.setdefault(3, []).append((net.launch, 0, 0))
    for place, s in enumerate(tail):
        for n in range(3):
            k = place + 1 - n
            if (k, n) != (0, 0) and 0 <= k < net.stages:
                plan.setdefault(s, []).append((net.launch, k, n))
            elif k == net.stages:
                plan.setdefault(s, []).append((net.finish, n, write))
    last = tail[-1]
    for place in range(len(tail), net.stages + 3):
        for n in range(3):
            k = place + 1 - n
            if 0 <= k < net.stages:
                plan[last].append((net.launch, k, n))
            elif k == net.stages:
                plan[last].append((net.finish, n, write))
    for s, actions in plan.items():

        @pl.when(step == s)
        def _(actions=actions, s=s):
            for act, *args in actions:
                result = act(*args)
                if act == net.pair:
                    result.start()
            if s == last:
                for n in range(3):
                    net.end(n)


def backward(
    d_down, df, a2, gu, wgu, wdown, dy, resid, gain_two, wout, win, a1, on, x, gain_one, wbeta, proj,
    beta_pre, taps, gain, mask, segc, segr, saved, blocks, shards, collective_id,
):
    rows = x.shape[0]
    rows_mb = rows // blocks
    width = PAIR * HEAD_DIM
    chunks, pairs = FF // CHUNK, HEADS // PAIR
    anywhere = pl.BlockSpec(memory_space=pl.ANY)
    full = lambda shape: pl.BlockSpec(shape, lambda s: (0,) * len(shape))
    early = lambda s: jnp.minimum(s, chunks - 1)
    late = lambda s: jnp.maximum(s - chunks, 0)
    lane_e = lambda r, w, off=0: pl.BlockSpec((r, w), lambda s: (0, off + early(s)))
    lane_l = lambda r, w, off=0: pl.BlockSpec((r, w), lambda s: (0, off + late(s)))
    wide_l = lambda off=0: pl.BlockSpec(
        (D, width), lambda s: (0, off + late(s)), pipeline_mode=pl.Buffered(1)
    )
    row_l = lambda r, w: pl.BlockSpec((r, w), lambda s: (late(s), 0))
    mat = pl.BlockSpec(
        (PAIR, blocks, rows_mb, rows_mb), lambda s: (late(s), 0, 0, 0), pipeline_mode=pl.Buffered(1)
    )
    part_l = pl.BlockSpec(
        (rows, width), lambda s: (0, late(s)), pipeline_mode=pl.Buffered(1)
    )
    per = D // width
    tap = lambda k: lane_l(CONV, width, k * per)
    r_down, r_gu = FF // shards, D // shards
    a, b = chunks // 2 * 2 * CHUNK, 2 * FF
    pieces = [(0, 0, D), (1, 0, a), (1, a, b - a)]
    f32 = lambda *shape: jax.ShapeDtypeStruct(shape, F32)
    bf = lambda *shape: jax.ShapeDtypeStruct(shape, BF16)
    square = bf(D, D)
    vm = pltpu.VMEM
    return pl.pallas_call(
        functools.partial(backward_kernel, shards, blocks, rows_mb, pieces),
        grid=(chunks + pairs,),
        in_specs=[
            anywhere, full((rows, D)), full((rows, D)), lane_e(rows, CHUNK),
            lane_e(rows, CHUNK, chunks), lane_e(D, CHUNK), lane_e(D, CHUNK, chunks),
            pl.BlockSpec((CHUNK, D), lambda s: (early(s), 0)), full((rows, D)), full((rows, D)),
            full((1, D)), row_l(width, D), wide_l(), wide_l(per), wide_l(2 * per),
            wide_l(3 * per), full((rows, D)),
            lane_l(rows, width), full((rows, D)), full((1, D)), full((D, HEADS)),
            part_l, part_l, part_l, part_l, full((rows, HEADS)), tap(0), tap(1), tap(2), full((1, HEAD_DIM)), full((rows, 8)),
            full((rows, 1)), full((1, rows)), lane_l(rows, width), mat, mat, mat, mat,
        ],
        out_specs=[
            full((r_down, D)), full((r_gu, 2 * FF)), wide_l(), wide_l(), wide_l(), wide_l(),
            row_l(width, D), full((D, HEADS)), full((rows, D)),
            full((1, D)), full((1, D)), lane_l(CONV, width), lane_l(CONV, width),
            lane_l(CONV, width), full((1, HEAD_DIM)),
        ],
        out_shape=[
            f32(r_down, D), f32(r_gu, 2 * FF), square, square, square, square, square,
            f32(D, HEADS), bf(rows, D), f32(1, D), f32(1, D), f32(CONV, D), f32(CONV, D),
            f32(CONV, D), f32(1, HEAD_DIM),
        ],
        scratch_shapes=[
            vm((shards // 2, r_down, D), BF16), vm((shards // 2, 2, r_gu, 2 * FF), BF16),
            vm((rows, D), F32), vm((rows, D), F32), vm((rows, D), BF16), vm((rows, width), F32),
            vm((rows, width), BF16), vm((rows, width), BF16), vm((rows, width), BF16),
            vm((rows, width), BF16), vm((rows, HEADS), F32),
            pltpu.SemaphoreType.DMA,
        ] + Scatter.semaphores(shards, 3) + Scatter.buffers(shards, [(r_down, D), (r_gu, 2 * FF)]),
        compiler_params=pltpu.CompilerParams(
            collective_id=collective_id, has_side_effects=True, vmem_limit_bytes=60 << 20
        ),
        name="backward",
    )(d_down.reshape(shards // 2, 2, r_down, D), df, a2, gu, gu, wgu, wgu, wdown, dy, resid, gain_two,
      wout, win, win, win, win, a1, on, x, gain_one, wbeta, *proj, beta_pre, taps, taps, taps, gain,
      mask, segc, segr, *saved)


def link_plan(half_way, done, last, heads):
    return [
        [4, 9, 11, 12], [half_way + 3, done + 1, done + 2], [done + 1, done + 3], [done + 6], [last], [last],
        [done + 5],
    ]


def rear_kernel(shards, blocks, rows_mb, pieces, *refs):
    (d_down, sent_y, dy, resid, x, a2_t, a1_t, df, gate, up, wga, wup, wdn, gain_two, gain_one, wout, wq, wk, wv, wg,
     on, wbeta, deal, loss, *mixer), refs = refs[:41], refs[41:]
    (g_down, g_gu, g_in, g_out, got_y, got_dx, small_sum), refs = refs[:7], refs[7:]
    (mine_down, mine_gu, mine_in, mine_out, stage_gu, stage_in, stage_out, acc, dresid, held, dz, don, dpq, dpk, dpv,
     dpg, turned, dbeta, dtaps, d_gain, d_two, sent_dx, small, small_got, keep, load, gu_sem, in_sem, out_sem), refs = refs[:29], refs[29:]
    y_sems, dx_sems, small_sems, sems, buffers = refs[:3], refs[3:6], refs[6:9], refs[9:13], refs[13:]
    step = pl.program_id(0)
    chunks, heads = FF // SLICE, HEADS
    rows = blocks * rows_mb
    share, r_gu = rows // shards, D // shards
    here = Here(shards)
    core = here.core
    other, coming = Scatter.split(shards, 4, buffers)
    mines = (mine_down, mine_gu, mine_in, mine_out)
    pair_recv = sems[3]

    def whole(n, parity):
        i, at, size = pieces[n]
        if i == 0:
            return d_down.at[:, parity, :, pl.ds(at, size)]
        return other[i].at[:, :, pl.ds(at, size)]

    def kept(n):
        if n > 0:
            return None
        return pltpu.make_async_copy(d_down.at[:, core], mine_down, keep)

    net = Scatter(
        here, pieces, whole, lambda i, q, cols: mines[i][q, :, cols], other, coming, sems, kept
    )
    give_y = Exchange(here, sent_y, got_y, *y_sems)
    give_dx = Exchange(here, sent_dx, got_dx, *dx_sems)
    give_small = Exchange(here, small, small_got, *small_sems)

    def cross(stage, slot, there, send, n):
        return pltpu.make_async_remote_copy(
            src_ref=stage.at[slot], dst_ref=there, send_sem=send.at[slot], recv_sem=pair_recv.at[n],
            device_id=here.partner[0], device_id_type=MESH,
        )

    def cross_gu(j):
        cols = pl.ds(pl.multiple_of(j * (2 * SLICE), 2 * SLICE), 2 * SLICE)
        return cross(stage_gu, lax.rem(j, 2), other[1].at[:, :, cols], gu_sem, 1 + lax.div(j + chunks % 2, (chunks + 1) // 2))

    def cross_in(s):
        width = 4 * HEAD_DIM
        cols = pl.ds(pl.multiple_of(s * width, width), width)
        return cross(stage_in, lax.rem(s, 2), other[2].at[:, :, cols], in_sem, 3 + lax.div(s, heads // 2) + lax.div(s, 3 * heads // 4))

    def cross_out(s):
        much = shards // 2 // heads
        return cross(stage_out, s % 2, other[3].at[pl.ds(s * much, much)], out_sem, 6)

    def by_core(value):
        first, second = value[:, 0], value[:, 1]
        return (
            jnp.where(core == 0, first, second).astype(BF16), jnp.where(core == 0, second, first).astype(BF16)
        )

    def write(i, at, size, value):
        if i == 0:
            g_down[:, pl.ds(at, size)] = value
        elif i == 3:
            g_out[:, pl.ds(at, size)] = value
        else:
            for tile in range(at // 128, (at + size) // 128):
                if i == 1:
                    chunk, inner = divmod(tile * 128, 2 * SLICE)
                    start = chunk * SLICE + inner + (FF - SLICE if inner >= SLICE else 0)
                else:
                    start = tile % 4 * D + tile // 4 * HEAD_DIM
                target = g_gu if i == 1 else g_in
                target[:, start : start + 128] = value[:, tile * 128 - at : tile * 128 - at + 128]

    load_dy = pltpu.make_async_copy(dy, dresid, load.at[0])
    load_resid = pltpu.make_async_copy(resid, held, load.at[1])
    load_x = pltpu.make_async_copy(x, held, load.at[1])
    load_a2 = pltpu.make_async_copy(a2_t, turned, load.at[2])
    load_a1 = pltpu.make_async_copy(a1_t, turned, load.at[2])

    @pl.when(step == 0)
    def _():
        kept(0).start()
        load_dy.start()
        load_resid.start()
        meet(here, True)
        net.pair(0).start()
        give_y.start()
        acc[...] = jnp.zeros_like(acc)
        load_a2.start()
        load_a2.wait()

    @pl.when(step < chunks)
    def _():
        dhid = nt(df[...], wdn[...])
        g = gate[...]
        s = sigmoid(g)
        d_gate = (dhid * up[...] * (s * (1.0 + g * (1.0 - s)))).astype(BF16)
        d_up = (dhid * (g * s)).astype(BF16)
        acc[...] += nt(d_gate, wga[...]) + nt(d_up, wup[...])

        @pl.when(step >= 2)
        def _():
            cross_gu(step - 2).wait_send()

        slot = lax.rem(step, 2)
        part = jnp.concatenate([d_gate, d_up], axis=1)
        near, far = by_core(nn(turned[...], part).reshape(shards // 2, 2, r_gu, 2 * SLICE))
        mine_gu[:, :, pl.ds(pl.multiple_of(step * (2 * SLICE), 2 * SLICE), 2 * SLICE)] = near
        stage_gu[slot] = far
        cross_gu(step).start()

    @pl.when(step == chunks - 1)
    def _():
        load_dy.wait()
        load_resid.wait()
        nr, rr = rms(held[...])
        da2 = acc[...]
        d_two[...] = jnp.sum(da2 * nr, axis=0, keepdims=True)
        dresid[...] = dresid[...] + rms_back(nr, rr, gain_two[...] * da2)
        dz[...] = dresid[...].astype(BF16)
        acc[...] = jnp.zeros_like(acc)
        load_a1.start()
        load_x.start()
        load_a1.wait()

    @pl.when(step >= chunks)
    def _():
        head = step - chunks
        don[...] = nt(dz[...], wout[...])
        taps_of = lambda j: dtaps.at[:, pl.ds(pl.multiple_of(j * D + head * HEAD_DIM, HEAD_DIM), HEAD_DIM)]
        mixer_bwd_kernel(
            blocks, rows_mb, 1, head, *mixer[:12], don, *mixer[12:], dpq, dpk, dpv, dpg, dbeta, taps_of(0),
            taps_of(1), taps_of(2), d_gain,
        )

        @pl.when(head >= 2)
        def _():
            cross_in(head - 2).wait_send()

        slot = lax.rem(head, 2)
        acc[...] += nt(dpq[...], wq[...]) + nt(dpk[...], wk[...]) + nt(dpv[...], wv[...]) + nt(dpg[...], wg[...])
        width = 4 * HEAD_DIM
        part = jnp.concatenate([dpq[...], dpk[...], dpv[...], dpg[...]], axis=1)
        near, far = by_core(nn(turned[...], part).reshape(shards // 2, 2, r_gu, width))
        mine_in[:, :, pl.ds(pl.multiple_of(head * width, width), width)] = near
        stage_in[slot] = far
        cross_in(head).start()

    @pl.when(step == chunks)
    def _():
        much = shards // 2 // heads
        for s in range(heads):
            if s >= 2:
                cross_out(s - 2).wait_send()
            part = tn(on[:, s * HEAD_DIM : (s + 1) * HEAD_DIM], dz[...])
            near, far = by_core(part.reshape(much, 2, r_gu, D))
            mine_out[s * much : (s + 1) * much] = near
            stage_out[s % 2] = far
            cross_out(s).start()
        for s in (heads - 2, heads - 1):
            cross_out(s).wait_send()

    def last_rows():
        d_beta = dbeta[...].astype(BF16)
        grad = acc[...] + nn(d_beta, wbeta[...])
        d_wbeta = lax.dot_general(
            d_beta, turned[...], (((0,), (1,)), ((), ())), preferred_element_type=F32
        )
        load_x.wait()
        nx, rx = rms(held[...])
        d_one = jnp.sum(grad * nx, axis=0, keepdims=True)
        dx = (dresid[...] + rms_back(nx, rx, gain_one[...] * grad)).astype(BF16)
        sent_dx[...] = nn(deal[...], dx).reshape(shards, share, D).astype(BF16)
        own_taps, own_gain = 3 * D // shards, D // shards
        per = 128 // own_gain
        a, c = iota2((per * own_taps, per * 128), 1), iota2((per * own_taps, per * 128), 0)
        put_taps = ((a // 128 == c // own_taps) & (a % 128 == c % own_taps)).astype(F32)
        a, c = iota2((128, per * 128), 1), iota2((128, per * 128), 0)
        put_gain = ((a // 128 == c // own_gain) & (a % 128 == c % own_gain)).astype(F32)
        lane = iota2((1, 128), 1)
        row8 = iota2((8, 128), 0)
        shared = jnp.where(row8 == 6, d_gain[...], jnp.where((row8 == 7) & (lane == 0), loss[...], 0.0))
        for g in range(shards // per):
            top = jnp.concatenate(
                [dtaps[:, g * per * own_taps : (g + 1) * per * own_taps],
                 jnp.zeros((8 - CONV, per * own_taps), F32)], axis=0
            )
            cols = slice(g * 128, (g + 1) * 128)
            gains = jnp.where(row8 == 4, d_one[:, cols], jnp.where(row8 == 5, d_two[:, cols], 0.0))
            upper = mm(top, put_taps, 1, 0) + mm(gains, put_gain, 1, 0)
            lower = mm(d_wbeta[:, cols], put_gain, 1, 0)
            for i in range(per):
                small[g * per + i, 0:8, :] = upper[:, i * 128 : (i + 1) * 128] + shared
                small[g * per + i, 8:16, :] = lower[:, i * 128 : (i + 1) * 128]

    last = chunks + heads - 1
    half_way, done = chunks // 2 - 1, chunks - 1
    starts = link_plan(half_way, done, last, heads)
    timed = []
    for n in range(len(pieces)):
        for k in range(net.stages + 1):
            at = starts[n][k] if k < len(starts[n]) else starts[n][-1] + 2 * (k - len(starts[n]) + 1)
            timed.append((at, k != net.stages, n, k))
    timed.sort()

    def act(n, k):
        if k < net.stages:
            net.launch(k, n)
        else:
            net.finish(n, write)

    for s in sorted({t[0] for t in timed if t[0] < last}):

        @pl.when(step == s)
        def _(s=s):
            for at, _, n, k in timed:
                if at == s:
                    act(n, k)

    @pl.when(step == last)
    def _():
        for at, _, n, k in timed:
            if at == last:
                act(n, k)
        last_rows()
        give_small.start()
        tail = [(n, k) for at, _, n, k in timed if at > last]
        for i, (n, k) in enumerate(tail):
            act(n, k)
            if i < DX_PARTS:
                give_dx.start_part(i, DX_PARTS)
        give_small.wait()
        small_sum[...] = jnp.sum(small_got[...], axis=0)
        give_y.wait()
        give_dx.wait()
        for j in (chunks - 2, chunks - 1):
            cross_gu(j).wait_send()
        for s in (heads - 2, heads - 1):
            cross_in(s).wait_send()
        for n in range(len(pieces)):
            net.end(n, paired=n == 0)


def rear(
    d_down, sent_y, dy, resid, x, a2_t, a1_t, df, gate, up, wgu, wdown, gain_two, gain_one, wout, win, on, wbeta, deal, loss,
    proj, beta_pre, taps, gain, mask, segc, segr, saved, blocks, shards, collective_id,
):
    rows = x.shape[0]
    rows_mb, share = rows // blocks, rows // shards
    chunks = FF // SLICE
    anywhere = pl.BlockSpec(memory_space=pl.ANY)
    once = pl.Buffered(MIXER_BUFFERS)
    full = lambda shape: pl.BlockSpec(shape, lambda s: (0,) * len(shape))
    early = lambda s: jnp.minimum(s, chunks - 1)
    late = lambda s: jnp.maximum(s - chunks, 0)
    lane_e = lambda r, w, off=0: pl.BlockSpec((r, w), lambda s: (0, off + early(s)))
    lane_l = lambda r, w, off=0: pl.BlockSpec((r, w), lambda s: (0, off + late(s)), pipeline_mode=once)
    mat = pl.BlockSpec((1, blocks, rows_mb, rows_mb), lambda s: (late(s), 0, 0, 0), pipeline_mode=pl.Buffered(1))
    tap = lambda k: pl.BlockSpec((CONV, HEAD_DIM), lambda s: (0, k * HEADS + late(s)))
    r_down, r = FF // shards, D // shards
    a, b = chunks // 2 * 2 * SLICE, 4 * D // 2
    c = b // 2
    pieces = [(0, 0, D), (1, 0, a), (1, a, 2 * FF - a), (2, 0, b), (2, b, c), (2, b + c, c), (3, 0, D)]
    shapes = [(r_down, D), (r, 2 * FF), (r, 4 * D), (r, D)]
    f32 = lambda *shape: jax.ShapeDtypeStruct(shape, F32)
    bf = lambda *shape: jax.ShapeDtypeStruct(shape, BF16)
    vm, dma = pltpu.VMEM, pltpu.SemaphoreType.DMA
    hd = HEAD_DIM
    half = shards // 2
    return pl.pallas_call(
        functools.partial(rear_kernel, shards, blocks, rows_mb, pieces),
        grid=(chunks + HEADS,),
        in_specs=[
            anywhere, anywhere, anywhere, anywhere, anywhere, anywhere, anywhere, full((rows, D)),
            lane_e(rows, SLICE), lane_e(rows, SLICE), lane_e(D, SLICE), lane_e(D, SLICE, chunks),
            pl.BlockSpec((SLICE, D), lambda s: (early(s), 0)), full((1, D)), full((1, D)),
            pl.BlockSpec((hd, D), lambda s: (late(s), 0), pipeline_mode=pl.Buffered(1)), lane_l(D, hd), lane_l(D, hd, HEADS),
            lane_l(D, hd, 2 * HEADS), lane_l(D, hd, 3 * HEADS), full((rows, D)),
            full((HEADS, D)), full((rows, rows)), full((1, 1)),
            lane_l(rows, hd), lane_l(rows, hd), lane_l(rows, hd), lane_l(rows, hd), full((rows, HEADS)), tap(0),
            tap(1), tap(2), full((1, hd)), full((rows, 8)), full((rows, 1)), full((1, rows)), lane_l(rows, hd),
            mat, mat, mat, mat,
        ],
        out_specs=[full(s) for s in shapes] + [anywhere, anywhere, full((16, 128))],
        out_shape=[f32(*s) for s in shapes] + [bf(shards, share, D), bf(shards, share, D), f32(16, 128)],
        scratch_shapes=[vm((half,) + s, BF16) for s in shapes] + [
            vm((2, half, r, 2 * SLICE), BF16), vm((2, half, r, 4 * hd), BF16), vm((2, half // HEADS, r, D), BF16),
            vm((rows, D), F32), vm((rows, D), F32), vm((rows, D), F32), vm((rows, D), BF16), vm((rows, hd), F32),
            vm((rows, hd), BF16), vm((rows, hd), BF16), vm((rows, hd), BF16), vm((rows, hd), BF16),
            vm((D, rows), BF16), vm((rows, HEADS), F32), vm((CONV, 3 * D), F32), vm((1, hd), F32), vm((1, D), F32),
            vm((shards, share, D), BF16), vm((shards, 16, 128), F32), vm((shards, 16, 128), F32),
            dma, dma((3,)), dma((2,)), dma((2,)), dma((2,)),
        ] + [dma] * 9 + Scatter.semaphores(shards, len(pieces)) + Scatter.buffers(shards, shapes),
        compiler_params=pltpu.CompilerParams(
            collective_id=collective_id, has_side_effects=True, vmem_limit_bytes=62 << 20
        ),
        name="rear",
    )(d_down.reshape(half, 2, r_down, D), sent_y, dy, resid, x, a2_t, a1_t, df, gate, up, wgu, wgu, wdown, gain_two, gain_one,
      wout, win, win, win, win, on, wbeta, deal, loss, *proj, beta_pre, taps, taps, taps, gain, mask, segc, segr,
      *saved)


def middle_kernel(
    scale, a2, wga, wup, wdn, resid, later, m, counted, deal,
    gate, up, df, dy, sent_y, loss, d_down,
    hid, acc,
):
    step = pl.program_id(0)
    chunks = FF // FF_STEP

    @pl.when(step == 0)
    def _():
        acc[...] = resid[...]

    @pl.when(step < chunks)
    def _():
        g, u = nn(a2[...], wga[...]), nn(a2[...], wup[...])
        gate[...], up[...] = g, u
        h = (g * sigmoid(g) * u).astype(BF16)
        hid[step] = h
        acc[...] += nn(h, wdn[...])

    @pl.when(step == chunks - 1)
    def _():
        y = acc[...]
        errors = y - later[:, D:]
        masked = m[...] * errors
        loss[...] = jnp.sum(jnp.sum(masked * errors, axis=1, keepdims=True), axis=0, keepdims=True)
        grad = later[:, :D] + (scale / counted[...]) * masked
        dy[...] = grad
        df[...] = grad.astype(BF16)
        sent_y[...] = nn(deal[...], y.astype(BF16)).reshape(sent_y.shape).astype(BF16)

    @pl.when(step >= chunks)
    def _():
        d_down[...] = tn(hid[step - chunks], df[...]).astype(BF16)


def middle(a2, wgu, wdown, resid, later, m, counted, deal, shards):
    rows = a2.shape[0]
    share, chunks = rows // shards, FF // FF_STEP
    full = lambda shape: pl.BlockSpec(shape, lambda s: (0,) * len(shape))
    early = lambda s: jnp.minimum(s, chunks - 1)
    lane = lambda r, off=0: pl.BlockSpec((r, FF_STEP), lambda s: (0, off + early(s)))
    f32 = lambda *shape: jax.ShapeDtypeStruct(shape, F32)
    bf = lambda *shape: jax.ShapeDtypeStruct(shape, BF16)
    return pl.pallas_call(
        functools.partial(middle_kernel, float(rows * shards)),
        grid=(2 * chunks,),
        in_specs=[
            full((rows, D)), lane(D), lane(D, chunks), pl.BlockSpec((FF_STEP, D), lambda s: (early(s), 0)),
            full((rows, D)), full((rows, 2 * D)), full((rows, 1)), full((1, 1)), full((rows, rows)),
        ],
        out_specs=[
            lane(rows), lane(rows), full((rows, D)), full((rows, D)), full((shards, share, D)), full((1, 1)),
            pl.BlockSpec((FF_STEP, D), lambda s: (jnp.maximum(s - chunks, 0), 0)),
        ],
        out_shape=[
            f32(rows, FF), f32(rows, FF), bf(rows, D), f32(rows, D), bf(shards, share, D), f32(1, 1), bf(FF, D),
        ],
        scratch_shapes=[pltpu.VMEM((chunks, rows, FF_STEP), BF16), pltpu.VMEM((rows, D), F32)],
        compiler_params=pltpu.CompilerParams(vmem_limit_bytes=62 << 20),
        name="middle",
    )(a2, wgu, wgu, wdown, resid, later, m, counted, deal)


def settle_kernel(
    got_y, got_dx, sort_t, summed, counted, g_down, g_gu, g_in, g_out,
    output, input_grad, o_in, o_beta, o_taps, o_out, o_one, o_gain, o_two, o_gu, o_down, loss,
):
    shards, share, _ = got_y.shape
    own = o_one.shape[1]
    for got, out in ((got_y, output), (got_dx, input_grad)):
        out[...] = nn(sort_t[...], got[...].astype(F32).reshape(shards * share, D).astype(BF16)).astype(BF16)
    o_in[...], o_out[...], o_gu[...], o_down[...] = g_in[...], g_out[...], g_gu[...], g_down[...]
    total = summed[...]
    o_taps[...] = total[:CONV, : 3 * own]
    o_one[...], o_two[...], o_gain[...] = total[4:5, :own], total[5:6, :own], total[6:7]
    loss[...] = total[7:8, :1] / (D * counted[...])
    o_beta[...] = total[8:, :own]


def settle(got_y, got_dx, sort_t, summed, counted, g_down, g_gu, g_in, g_out):
    rows = sort_t.shape[0]
    own = g_in.shape[0]
    f32 = lambda *shape: jax.ShapeDtypeStruct(shape, F32)
    row = jax.ShapeDtypeStruct((rows, D), BF16)
    return pl.pallas_call(
        settle_kernel,
        out_shape=[row, row, f32(*g_in.shape), f32(HEADS, own), f32(CONV, 3 * own), f32(*g_out.shape), f32(1, own),
                   f32(1, HEAD_DIM), f32(1, own), f32(*g_gu.shape), f32(*g_down.shape), f32(1, 1)],
        name="settle",
    )(got_y, got_dx, sort_t, summed, counted, g_down, g_gu, g_in, g_out)


def scatter_kernel(shards, count, *refs):
    grads, sent, out, got = refs[:count], refs[count], refs[count + 1 : 2 * count + 1], refs[2 * count + 1]
    refs = refs[2 * count + 2 :]
    mine, refs = refs[:count], refs[count:]
    sems, (keep, *back_sems), buffers = refs[:4], refs[4:8], refs[8:]
    here = Here(shards)
    core = here.core
    back = Exchange(here, sent, got, *back_sems)
    other, coming = Scatter.split(shards, count, buffers)
    pieces = [(i, 0, g.shape[-1]) for i, g in enumerate(grads)]

    def kept(n):
        return pltpu.make_async_copy(grads[n].at[:, core], mine[n], keep.at[n])

    net = Scatter(
        here, pieces, lambda n, parity: grads[n].at[:, parity],
        lambda i, q, cols: mine[i][q, :, cols], other, coming, sems, kept,
    )

    def write(i, at, size, value):
        out[i][:, pl.ds(at, size)] = value

    for n in range(count):
        kept(n).start()
    meet(here, True)
    for n in range(count):
        net.pair(n).start()
    back.start()
    for t in range(count + net.stages):
        for n in range(count):
            k = t - n
            if 0 <= k < net.stages:
                net.launch(k, n)
            elif k == net.stages:
                net.finish(n, write)
    back.wait()
    for n in range(count):
        net.end(n)


def scatter(grads, message, shards, collective_id):
    count = len(grads)
    shapes = [(g.shape[0] // shards, g.shape[1]) for g in grads]
    anywhere = pl.BlockSpec(memory_space=pl.ANY)
    dma = pltpu.SemaphoreType.DMA
    *out, got = pl.pallas_call(
        functools.partial(scatter_kernel, shards, count),
        in_specs=[anywhere] * (count + 1),
        out_specs=[pl.BlockSpec(memory_space=pltpu.VMEM)] * count + [anywhere],
        out_shape=[jax.ShapeDtypeStruct(s, F32) for s in shapes]
        + [jax.ShapeDtypeStruct(message.shape, message.dtype)],
        scratch_shapes=[pltpu.VMEM((shards // 2,) + s, BF16) for s in shapes]
        + Scatter.semaphores(shards, count) + [dma((count,)), dma, dma, dma]
        + Scatter.buffers(shards, shapes),
        compiler_params=pltpu.CompilerParams(
            collective_id=collective_id, has_side_effects=True, vmem_limit_bytes=60 << 20
        ),
        name="scatter_last",
    )(*[g.reshape((shards // 2, 2) + s) for g, s in zip(grads, shapes)], message)
    return out, got


def nt(left, right):
    return lax.dot_general(left, right, (((1,), (1,)), ((), ())), preferred_element_type=F32)


def tn(left, right, dtype=F32):
    return lax.dot_general(left, right, (((0,), (0,)), ((), ())), preferred_element_type=dtype)


def nn(left, right):
    return jnp.dot(left, right, preferred_element_type=F32)


def rms(v):
    inv = lax.rsqrt(jnp.mean(v * v, axis=-1, keepdims=True) + 1e-05)
    return v * inv, inv


def rms_back(normed, inv, dn):
    return inv * (dn - normed * jnp.mean(normed * dn, axis=-1, keepdims=True))


def local(
    tokens, cotangent, teacher, valid_mask, deal_rows, lengths, w_in, w_beta, conv_kernel, w_out,
    norm_gain, out_gain, ffn_gain, w_gu, w_down,
):
    shards = lax.axis_size(AXES)
    rows = tokens.shape[0]
    share = rows // shards
    blocks = lengths.shape[0]
    rows_mb = rows // blocks
    a, b, c = CONV * conv_kernel.shape[1], w_beta.shape[0] * HEADS, norm_gain.shape[0]
    small = w_beta.shape[0] * HEADS + CONV * conv_kernel.shape[1] + 2 * norm_gain.shape[0]

    if share % 8 == 0 and (D // shards) % 16 == 0:
        half = jnp.pad(
            jnp.concatenate([conv_kernel, jnp.pad(jnp.stack([norm_gain, ffn_gain]), ((0, 0), (0, conv_kernel.shape[1] - norm_gain.shape[0])))]),
            ((0, 2), (0, 128 - conv_kernel.shape[1])),
        )
        small_block = jnp.concatenate(
            [half, jnp.pad(w_beta.T, ((0, 0), (0, 128 - w_beta.shape[0])))], axis=1
        )
        gain_out = out_gain.astype(F32)[None, :]
        (win, wout, wdown, wgu, *proj, beta_pre, on, o, ainv, u, p, l, resid, a2, x, m, counted, deal_t, sort_t, later,
         taps, gain_one, gain_two, wbeta, segc, segr, mask, a1, a1_t, a2_t) = front(
            [w_in, w_out, w_down, w_gu], small_block, tokens, cotangent, teacher, deal_rows, valid_mask, lengths,
            gain_out, shards, 0,
        )
        win, wout, wdown, wgu = (w.reshape(-1, w.shape[-1]) for w in (win, wout, wdown, wgu))
        saved = (o, ainv, u, p, l)
        gain_one, gain_two = gain_one[0], gain_two[0]
    else:
        target = deal_rows // rows
        spot = deal_rows % rows
        ahead = (target[None, :] == target[:, None]) & (
            jnp.arange(rows)[None, :] < jnp.arange(rows)[:, None]
        )
        slot = target * share + jnp.sum(ahead.astype(jnp.int32), axis=1)
        sort_t = (slot[:, None] == jnp.arange(rows)[None, :]).astype(BF16)
        sort = (slot[None, :] == jnp.arange(rows)[:, None]).astype(BF16)
        count_own = jnp.sum(valid_mask.astype(F32))
        lane = jnp.arange(128)[None, :]
        notes = jnp.where(
            lane == 0,
            valid_mask.astype(F32)[:, None],
            jnp.where(lane == 1, spot.astype(F32)[:, None], jnp.where(lane == 2, count_own, 0.0)),
        ).astype(BF16)
        packed = jnp.concatenate(
            [conv_kernel.reshape(-1), w_beta.reshape(-1), norm_gain, ffn_gain,
             jnp.zeros((share * 128 - small,), BF16)]
        ).reshape(1, share, 128)
        sorted_rows = nn(sort, jnp.concatenate([tokens, notes], axis=1)).astype(BF16)
        message = jnp.concatenate(
            [sorted_rows.reshape(shards, share, -1), jnp.broadcast_to(packed, (shards, share, 128))],
            axis=2,
        )
        later = nn(sort, jnp.concatenate([cotangent, teacher], axis=1)).astype(BF16)
        later = later.reshape(shards, share, 2 * D)
        (win, wout), arrived = first([w_in, w_out], (2, 1), message, shards, 0)

        flat = arrived.reshape(rows, -1)
        info = flat[:, D : D + 128].astype(F32)
        place = info[:, 1].astype(jnp.int32)
        counted = jnp.sum(arrived[:, 0, D + 2].astype(F32))
        extra = arrived[:, :, D + 128 :].reshape(shards, share * 128)
        taps = extra[:, :a].reshape(shards, CONV, -1).swapaxes(0, 1).reshape(CONV, 3 * D).astype(F32)
        wbeta = extra[:, a : a + b].reshape(D, HEADS)
        gain_one = extra[:, a + b : a + b + c].reshape(D).astype(F32)
        gain_two = extra[:, a + b + c : a + b + 2 * c].reshape(D).astype(F32)
        deal = (place[None, :] == jnp.arange(rows)[:, None]).astype(BF16)
        deal_t = (place[:, None] == jnp.arange(rows)[None, :]).astype(BF16)
        dealt = nn(deal, flat[:, : D + 128])
        x = dealt[:, :D]
        m = dealt[:, D : D + 1]

        ends = jnp.cumsum(lengths, axis=1)
        within = jnp.arange(rows_mb, dtype=jnp.int32)
        seg = jnp.sum((within[None, :, None] >= ends[:, None, :]).astype(jnp.int32), axis=2)
        seg = (seg + (lengths.shape[1] + 1) * jnp.arange(blocks, dtype=jnp.int32)[:, None]).reshape(rows)
        position = jnp.arange(rows, dtype=jnp.int32)
        mask = jnp.stack(
            [jnp.ones((rows,), F32)]
            + [((position >= s) & (jnp.roll(seg, s) == seg)).astype(F32) for s in range(1, CONV)]
            + [jnp.zeros((rows,), F32)] * (8 - CONV),
            axis=1,
        )
        segc, segr = seg[:, None], seg[None, :]
        gain_out = out_gain.astype(F32)[None, :]

        nx, rx = rms(x)
        a1 = (nx * gain_one).astype(BF16)
        wdown, wgu, later, (*proj, beta_pre, on, o, ainv, u, p, l, resid, a2) = forward(
            w_down, w_gu, later, (1, 2), a1, win, wout, wbeta, x, gain_two[None, :], taps, gain_out, mask, segc,
            segr, blocks, shards, 2,
        )
        saved = (o, ainv, u, p, l)
        later = nn(deal, later.reshape(rows, 2 * D))
        g, t = later[:, :D], later[:, D:]
    if share % 8 == 0 and (D // shards) % 16 == 0:
        gate, up, df, dy, sent_y, loss_part, d_down = middle(
            a2, wgu, wdown, resid, later, m, counted, deal_t, shards
        )
        g_down, g_gu, g_in, g_out, got_y, got_dx, summed = rear(
            d_down, sent_y, dy, resid, x, a2_t, a1_t, df, gate, up, wgu, wdown, gain_two[None, :], gain_one[None, :],
            wout, win, on, wbeta, deal_t, loss_part, proj, beta_pre, taps, gain_out, mask, segc, segr, saved, blocks,
            shards, 1,
        )
        (output, input_grad, g_in, g_beta, g_taps, g_out, g_gain_one, g_gain_out, g_gain_two, g_gu, g_down,
         loss) = settle(got_y, got_dx, sort_t, summed, counted, g_down, g_gu, g_in, g_out)
        g_gain_one, g_gain_out, g_gain_two = g_gain_one[0], g_gain_out[0], g_gain_two[0]
        loss, g_beta = loss[0, 0], g_beta.T
    else:
        gu = nn(a2, wgu)
        gate, up = gu[:, :FF], gu[:, FF:]
        hid = (gate * sigmoid(gate) * up).astype(BF16)
        y = resid + nn(hid, wdown)
        errors = y - t
        loss_part = jnp.sum(m * errors * errors)
        dy = g + (rows * shards / counted) * m * errors
        df = dy.astype(BF16)
        (g_down, g_gu, dwq, dwk, dwv, dwg, dw_out, d_wbeta, dx, d_gain_two, d_gain_one, dtq, dtk, dtv,
         d_gain_out) = backward(
            tn(hid, df, BF16), df, a2, gu, wgu, wdown, dy, resid, gain_two[None, :], wout, win, a1, on, x,
            gain_one[None, :], wbeta, proj, beta_pre, taps, gain_out, mask, segc, segr, saved, blocks, shards,
            1,
        )
        back = jnp.concatenate([y.astype(BF16), dx], axis=1)
        back = nn(deal_t, back).astype(BF16).reshape(shards, share, 2 * D)
        (g_out, *g_in), back = scatter([dw_out, dwq, dwk, dwv, dwg], back, shards, 3)
        g_in = jnp.concatenate(g_in, axis=1)
        back = nn(sort_t, back.reshape(rows, 2 * D)).astype(BF16)
        output, input_grad = back[:, :D], back[:, D:]

        d_taps = jnp.concatenate([dtq, dtk, dtv], axis=1)
        tail = jnp.concatenate([d_gain_out.reshape(-1), loss_part.reshape(1)])
        extra = jnp.concatenate(
            [
                d_taps.reshape(CONV, shards, -1).swapaxes(0, 1).reshape(shards, a),
                d_wbeta.reshape(shards, b),
                d_gain_one.reshape(shards, c),
                d_gain_two.reshape(shards, c),
                jnp.broadcast_to(tail[None], (shards, tail.shape[0])),
            ],
            axis=1,
        )
        padded = -(-extra.shape[1] // 128) * 128
        extra = jnp.pad(extra, ((0, 0), (0, padded - extra.shape[1])))
        summed = jnp.sum(
            lax.all_to_all(
                extra.reshape(shards, padded // 128, 128), AXES, split_axis=0, concat_axis=0, tiled=True
            ),
            axis=0,
        ).reshape(-1)
        g_taps = summed[:a].reshape(CONV, -1)
        g_beta = summed[a : a + b].reshape(-1, HEADS)
        g_gain_one = summed[a + b : a + b + c]
        g_gain_two = summed[a + b + c : a + b + 2 * c]
        g_gain_out = summed[a + b + 2 * c : a + b + 2 * c + HEAD_DIM]
        loss = summed[a + b + 2 * c + HEAD_DIM] / (D * counted)

    return (
        output, input_grad, g_in, g_beta, g_taps, g_out, g_gain_one, g_gain_out, g_gain_two, g_gu,
        g_down, loss,
    )


def solution(mesh):
    both = P(AXES, None)
    flat = P(AXES)
    in_specs = (both, both, both, flat, flat, both, both, both, P(None, AXES), both, flat, P(), flat,
                both, both)
    out_specs = (both, both, both, both, P(None, AXES), both, flat, P(), flat, both, both, P())
    return jax.shard_map(local, mesh=mesh, in_specs=in_specs, out_specs=out_specs, check_vma=False)
```

```python
import functools

import jax
import jax.numpy as jnp
from jax import lax
from jax.experimental import pallas as pl
from jax.experimental.pallas import tpu as pltpu
from jax.sharding import PartitionSpec as P

D = 1024
HEADS = 8
HEAD_DIM = 128
FF = 2816
CONV = 4
AXES = ("dp", "fsdp")
F32 = jnp.float32
BF16 = jnp.bfloat16
PAIR = 2
MESH = pl.DeviceIdType.MESH


def mm(left, right, lc, rc):
    return lax.dot_general(
        left,
        right,
        (((lc,), (rc,)), ((), ())),
        precision=lax.Precision.HIGHEST,
        preferred_element_type=F32,
    )


def sigmoid(v):
    return 1.0 / (1.0 + jnp.exp(-v))


def iota2(shape, axis):
    return lax.broadcasted_iota(jnp.int32, shape, axis)


def unit_lower_inverses(mats, size):
    row, col = iota2((size, size), 0), iota2((size, size), 1)
    eye = (row == col).astype(F32)
    inverses = None
    width = 1
    while width < size:
        corner = ((row // (2 * width)) == (col // (2 * width))) & (
            (row // width) == (col // width) + 1
        )
        edges = [jnp.where(corner, m, 0.0) for m in mats]
        if inverses is None:
            inverses = [eye - e for e in edges]
        else:
            right = [mm(e, x, 1, 0) for e, x in zip(edges, inverses)]
            inverses = [x - mm(x, r, 1, 0) for x, r in zip(inverses, right)]
        width *= 2
    return inverses


def conv_parts(src, taps, masks):
    rolled = [src]
    total = src * taps[CONV - 1 : CONV, :]
    for s in range(1, CONV):
        moved = pltpu.roll(src, s, 0) * masks[s]
        rolled.append(moved)
        total = total + moved * taps[CONV - 1 - s : CONV - s, :]
    return total, rolled


def l2_norm(c):
    inv = lax.rsqrt(jnp.sum(c * c, axis=-1, keepdims=True) + 1e-06)
    return c * inv, inv


def mixer_fwd_kernel(
    blocks, rows_mb,
    pq, pk, pv, pg, beta, tq, tk, tv, gain, mask, segc, segr,
    on_ref, o_ref, ainv_ref, u_ref, p_ref, l_ref,
):
    step = pl.program_id(0)
    masks = [None] + [mask[:, s : s + 1] for s in range(1, CONV)]
    cs = []
    for src, taps in ((pq, tq), (pk, tk), (pv, tv)):
        pre, _ = conv_parts(src[...], taps[...], masks)
        cs.append(pre * sigmoid(pre))
    cq, ck, cv = cs
    strengths = sigmoid(beta[...])
    lane = iota2(strengths.shape, 1)
    gate = pg[...]
    gate = gate * sigmoid(gate)
    row, col = iota2((rows_mb, rows_mb), 0), iota2((rows_mb, rows_mb), 1)
    systems = [(h, b) for h in range(PAIR) for b in range(blocks)]
    qs, ks, vs, bs, sames, lows = [], [], [], [], [], []
    for h, b in systems:
        rs = slice(b * rows_mb, (b + 1) * rows_mb)
        hs = slice(h * HEAD_DIM, (h + 1) * HEAD_DIM)
        q, _ = l2_norm(cq[rs, hs])
        k, _ = l2_norm(ck[rs, hs])
        qs.append(q * HEAD_DIM ** (-0.5))
        ks.append(k)
        vs.append(cv[rs, hs])
        bs.append(
            jnp.sum(jnp.where(lane == step * PAIR + h, strengths, 0.0), axis=1, keepdims=True)[rs]
        )
        sames.append(segc[rs, :] == segr[:, rs])
    for i in range(len(systems)):
        lows.append(jnp.where(sames[i] & (row > col), mm(ks[i], ks[i], 1, 1), 0.0))
    inverses = unit_lower_inverses([l * b for l, b in zip(lows, bs)], rows_mb)
    us = [mm(a, v * b, 1, 0) for a, v, b in zip(inverses, vs, bs)]
    ps = [
        jnp.where(same & (row >= col), mm(q, k, 1, 1), 0.0)
        for q, k, same in zip(qs, ks, sames)
    ]
    os = [mm(p, u, 1, 0) for p, u in zip(ps, us)]
    for i, (h, b) in enumerate(systems):
        rs = slice(b * rows_mb, (b + 1) * rows_mb)
        hs = slice(h * HEAD_DIM, (h + 1) * HEAD_DIM)
        o = os[i]
        inv = lax.rsqrt(jnp.mean(o * o, axis=-1, keepdims=True) + 1e-05)
        on_ref[rs, hs] = (o * inv * gain[...] * gate[rs, hs]).astype(BF16)
        o_ref[rs, hs] = o
        ainv_ref[h, b] = inverses[i]
        u_ref[h, b] = us[i]
        p_ref[h, b] = ps[i]
        l_ref[h, b] = lows[i]


def mixer_bwd_kernel(
    blocks, rows_mb, pair, step,
    pq, pk, pv, pg, beta, tq, tk, tv, gain, mask, segc, segr,
    don_ref, o_ref, ainv_ref, u_ref, p_ref, l_ref,
    dq_ref, dk_ref, dv_ref, dg_ref, dbeta_ref, dtq, dtk, dtv, dgain_ref,
):
    rows = blocks * rows_mb
    masks = [None] + [mask[:, s : s + 1] for s in range(1, CONV)]
    pres, rolls, cs, sig = [], [], [], []
    for src, taps in ((pq, tq), (pk, tk), (pv, tv)):
        pre, rolled = conv_parts(src[...], taps[...], masks)
        s = sigmoid(pre)
        pres.append(pre)
        rolls.append(rolled)
        sig.append(s)
        cs.append(pre * s)
    cq, ck, cv = cs
    strengths = sigmoid(beta[...])
    lane = iota2(strengths.shape, 1)
    row, col = iota2((rows_mb, rows_mb), 0), iota2((rows_mb, rows_mb), 1)
    gates = pg[...]
    gsig = sigmoid(gates)
    gate = gates * gsig
    dgate = gsig * (1.0 + gates * (1.0 - gsig))
    systems = [(h, b) for h in range(pair) for b in range(blocks)]
    part = []
    dgain = jnp.zeros((1, HEAD_DIM), F32)
    for h, b in systems:
        rs = slice(b * rows_mb, (b + 1) * rows_mb)
        hs = slice(h * HEAD_DIM, (h + 1) * HEAD_DIM)
        k, ik = l2_norm(ck[rs, hs])
        qn, iq = l2_norm(cq[rs, hs])
        v = cv[rs, hs]
        bb = jnp.sum(jnp.where(lane == step * pair + h, strengths, 0.0), axis=1, keepdims=True)[rs]
        same = segc[rs, :] == segr[:, rs]
        o = o_ref[rs, hs]
        don = don_ref[rs, hs]
        inv = lax.rsqrt(jnp.mean(o * o, axis=-1, keepdims=True) + 1e-05)
        no = o * inv
        scaled = don * gain[...]
        dg_ref[rs, hs] = (scaled * no * dgate[rs, hs]).astype(BF16)
        dgain = dgain + jnp.sum(don * no * gate[rs, hs], axis=0, keepdims=True)
        dno = scaled * gate[rs, hs]
        do = inv * (dno - no * jnp.mean(no * dno, axis=-1, keepdims=True))
        part.append([q_ for q_ in (qn, iq, k, ik, v, bb, same, do)])
    dus = [mm(p_ref[h, b], part[i][7], 0, 0) for i, (h, b) in enumerate(systems)]
    dps = [
        jnp.where(part[i][6] & (row >= col), mm(part[i][7], u_ref[h, b], 1, 1), 0.0)
        for i, (h, b) in enumerate(systems)
    ]
    drs = [mm(ainv_ref[h, b], dus[i], 0, 0) for i, (h, b) in enumerate(systems)]
    scale = HEAD_DIM ** (-0.5)
    dqs = [mm(dps[i], part[i][2], 1, 0) * scale for i in range(len(systems))]
    das = [mm(drs[i], u_ref[h, b], 1, 1) for i, (h, b) in enumerate(systems)]
    dks = [mm(dps[i], part[i][0] * scale, 0, 0) for i in range(len(systems))]
    dgs = []
    for i in range(len(systems)):
        g = jnp.where(part[i][6] & (row > col), das[i] * (-part[i][5]), 0.0)
        dgs.append(g + g.T)
    dks = [dks[i] + mm(dgs[i], part[i][2], 1, 0) for i in range(len(systems))]
    dbeta = jnp.zeros(strengths.shape, F32)
    dcs = [[], [], []]
    for i, (h, b) in enumerate(systems):
        qn, iq, k, ik, v, bb, same, do = part[i]
        dv = drs[i] * bb
        db = jnp.sum(drs[i] * v - das[i] * l_ref[h, b], axis=-1, keepdims=True)
        dbp = db * bb * (1.0 - bb)
        pieces = [dbp if b == c else jnp.zeros((rows_mb, 1), F32) for c in range(blocks)]
        column = jnp.concatenate(pieces, axis=0) if blocks > 1 else dbp
        dbeta = dbeta + jnp.where(lane == step * pair + h, column, 0.0)
        dcs[0].append(iq * (dqs[i] - qn * jnp.sum(qn * dqs[i], axis=-1, keepdims=True)))
        dcs[1].append(ik * (dks[i] - k * jnp.sum(k * dks[i], axis=-1, keepdims=True)))
        dcs[2].append(dv)
    for j, (out, dtap, taps) in enumerate(((dq_ref, dtq, tq), (dk_ref, dtk, tk), (dv_ref, dtv, tv))):
        whole = jnp.concatenate(
            [
                jnp.concatenate([dcs[j][h * blocks + b] for b in range(blocks)], axis=0)
                for h in range(pair)
            ],
            axis=1,
        )
        dpre = whole * (sig[j] * (1.0 + pres[j] * (1.0 - sig[j])))
        tap = taps[...]
        grad = dpre * tap[CONV - 1 : CONV, :]
        dtap[CONV - 1 : CONV, :] = jnp.sum(dpre * rolls[j][0], axis=0, keepdims=True)
        for s in range(1, CONV):
            dtap[CONV - 1 - s : CONV - s, :] = jnp.sum(dpre * rolls[j][s], axis=0, keepdims=True)
            grad = grad + pltpu.roll(dpre * masks[s], rows - s, 0) * tap[CONV - 1 - s : CONV - s, :]
        out[...] = grad.astype(BF16)

    @pl.when(step == 0)
    def _():
        dbeta_ref[...] = jnp.zeros_like(dbeta_ref)
        dgain_ref[...] = jnp.zeros_like(dgain_ref)

    dbeta_ref[...] += dbeta
    dgain_ref[...] += dgain


def mixer_specs(rows, blocks, rows_mb):
    width = PAIR * HEAD_DIM
    per = D // width
    col = lambda k: pl.BlockSpec((rows, width), lambda i, k=k: (0, k * per + i))
    tap = lambda k: pl.BlockSpec((CONV, width), lambda i, k=k: (0, k * per + i))
    full = lambda shape: pl.BlockSpec(shape, lambda i: (0,) * len(shape))
    ins = [col(0), col(1), col(2), col(3), full((rows, HEADS)), tap(0), tap(1), tap(2),
           full((1, HEAD_DIM)), full((rows, 8)), full((rows, 1)), full((1, rows))]
    mat = pl.BlockSpec((PAIR, blocks, rows_mb, rows_mb), lambda i: (i, 0, 0, 0))
    one = pl.BlockSpec((rows, width), lambda i: (0, i))
    otap = pl.BlockSpec((CONV, width), lambda i: (0, i))
    return ins, mat, one, otap, full


def lin_index():
    return lax.axis_index("dp") * lax.axis_size("fsdp") + lax.axis_index("fsdp")


def mesh_id(index):
    inner = lax.axis_size("fsdp")
    return (lax.div(index, inner), lax.rem(index, inner))


class Here:
    def __init__(self, shards):
        self.shards, self.me = shards, lin_index()
        self.bits = shards.bit_length() - 1
        own = [lax.rem(lax.div(self.me, 1 << b), 2) for b in range(self.bits)]
        self.core = own[0]
        self.change = [(1 - 2 * o) * (1 << b) for b, o in enumerate(own)]
        self.partner = [mesh_id(self.me + c) for c in self.change]

    def flip(self, bits, number, always=()):
        result = self.me
        for bit in always:
            result = result + self.change[bit]
        for i, bit in enumerate(reversed(bits)):
            if isinstance(number, int):
                if (number >> i) & 1:
                    result = result + self.change[bit]
            else:
                result = result + lax.rem(lax.div(number, 1 << i), 2) * self.change[bit]
        return result


def routes(shards):
    bits = shards.bit_length() - 1
    rest = list(range(4, bits))
    return [[1, 2, 3] + rest, [2, 3, 1] + rest, [3, 1, 2] + rest]


def colours(width, turn):
    tiles = width // 128
    one, three = round(tiles * 0.36), round(tiles * 0.28)
    sizes = (one, tiles - one - three, three)
    return [(sum(sizes[:c]) * 128, sizes[c] * 128) for c in range(3)]


def meet(here, everyone):
    barrier = pltpu.get_barrier_semaphore()
    if everyone:

        def greet(r, _):
            peer = lax.rem(here.me + r, here.shards)
            pl.semaphore_signal(barrier, inc=1, device_id=mesh_id(peer), device_id_type=MESH)
            return 0

        lax.fori_loop(1, here.shards, greet, 0)
        pl.semaphore_wait(barrier, here.shards - 1)
    else:
        for partner in here.partner:
            pl.semaphore_signal(barrier, inc=1, device_id=partner, device_id_type=MESH)
        pl.semaphore_wait(barrier, here.bits)


def spread_order(shards):
    bits = shards.bit_length() - 1
    turned = [sum(((i >> b) & 1) << (bits - 1 - b) for b in range(bits)) for i in range(shards)]
    return turned[1:]


class Exchange:
    def __init__(self, here, sent, got, send, recv, keep, same=False):
        self.here, self.shards, self.me, self.got = here, here.shards, here.me, got
        self.block = (lambda d: sent) if same else (lambda d: sent.at[d])
        self.send, self.recv, self.keep = send, recv, keep

    def own(self):
        return pltpu.make_async_copy(self.block(self.me), self.got.at[self.me], self.keep)

    def start(self):
        self.own().start()

        def one(r, _):
            peer = lax.rem(self.me + r, self.shards)
            pltpu.make_async_remote_copy(
                src_ref=self.block(peer), dst_ref=self.got.at[self.me], send_sem=self.send,
                recv_sem=self.recv, device_id=mesh_id(peer), device_id_type=MESH,
            ).start()
            return 0

        lax.fori_loop(1, self.shards, one, 0)

    def start_part(self, part, parts):
        others = self.shards - 1
        if part == 0:
            self.own().start()
        for r in range(others * part // parts, others * (part + 1) // parts):
            peer = lax.rem(self.me + spread_order(self.shards)[r], self.shards)
            pltpu.make_async_remote_copy(
                src_ref=self.block(peer), dst_ref=self.got.at[self.me], send_sem=self.send,
                recv_sem=self.recv, device_id=mesh_id(peer), device_id_type=MESH,
            ).start()

    def wait(self):
        self.own().wait()
        whole = pl.ds(0, self.shards - 1)
        pltpu.make_async_remote_copy(
            src_ref=self.got.at[whole], dst_ref=self.got.at[whole], send_sem=self.send,
            recv_sem=self.recv, device_id=self.here.partner[0], device_id_type=MESH,
        ).wait()


DEAL_AT = 0
CHUNK = 256
X_STEPS = 5
GT_FROM = 6
SLICE = 256
FF_STEP = FF // 2
MIXER_BUFFERS = 2
DX_PARTS = 6


def pieces_of(widths, split):
    result = []
    for i, width in enumerate(widths):
        tiles, at = width // 128, 0
        for j in range(split[i]):
            size = tiles // split[i] + (1 if j < tiles % split[i] else 0)
            result.append((i, at * 128, size * 128))
            at += size
    return result


class Gather:
    def __init__(self, here, pieces, own, full, sems):
        self.here, self.pieces, self.own, self.full = here, pieces, own, full
        self.send, self.recv, self.pair_send, self.pair_recv, self.keep = sems
        self.stages = here.bits - 1
        self.order = routes(here.shards)
        self.core = here.core
        self.cuts = [
            [(at + a, s) for a, s in colours(size, n)] for n, (_, at, size) in enumerate(pieces)
        ]
        self.last = len(pieces) + self.stages - 1

    @staticmethod
    def semaphores(shards, pieces):
        dma, stages = pltpu.SemaphoreType.DMA, shards.bit_length() - 2
        number = len(pieces)
        return [dma((stages, number, 3)), dma((stages, number, 3)), dma((number,)), dma((number,)),
                dma((number,))]

    def kept(self, i):
        return pltpu.make_async_copy(
            self.own[i], self.full[i].at[lax.div(self.here.me, 2), self.core], self.keep.at[i]
        )

    def begin(self):
        for i in range(len(self.own)):
            self.kept(i).start()

    def partner(self, k, c):
        return self.here.partner[self.order[c][self.stages - 1 - k]]

    def group(self, k, n, c):
        at, size = self.cuts[n][c]
        some = self.full[self.pieces[n][0]].at[pl.ds(0, 1 << k), 0, :, pl.ds(at, size)]
        return pltpu.make_async_remote_copy(
            src_ref=some, dst_ref=some, send_sem=self.send.at[k, n, c],
            recv_sem=self.recv.at[k, n, c], device_id=self.partner(k, c), device_id_type=MESH,
        )

    def half(self, n):
        i, at, size = self.pieces[n]
        some = self.full[i].at[:, self.core, :, pl.ds(at, size)]
        return pltpu.make_async_remote_copy(
            src_ref=some, dst_ref=some, send_sem=self.pair_send.at[n],
            recv_sem=self.pair_recv.at[n], device_id=self.here.partner[0],
            device_id_type=MESH,
        )

    def launch(self, k, n):
        i = self.pieces[n][0]
        for c in range(3):
            at, size = self.cuts[n][c]
            if k > 0:
                self.group(k - 1, n, c).wait_recv()
            have = self.order[c][self.stages - k :]
            for j in range(1 << k):
                d = self.here.flip(have, j)
                there = self.full[i].at[lax.div(d, 2), self.core, :, pl.ds(at, size)]
                pltpu.make_async_remote_copy(
                    src_ref=self.own[i].at[:, pl.ds(at, size)] if j == 0 else there,
                    dst_ref=there, send_sem=self.send.at[k, n, c], recv_sem=self.recv.at[k, n, c],
                    device_id=self.partner(k, c), device_id_type=MESH,
                ).start()

    def finish(self, n):
        for c in range(3):
            self.group(self.stages - 1, n, c).wait_recv()
        if n == 0 or self.pieces[n - 1][0] != self.pieces[n][0]:
            self.kept(self.pieces[n][0]).wait()
        self.half(n).start()

    def slots(self, first, last):
        return sum(
            0 <= t - n <= self.stages for t in range(first, last) for n in range(len(self.pieces))
        )

    def step(self, t, between=None):
        for n in range(len(self.pieces)):
            k = t - n
            if 0 <= k < self.stages:
                self.launch(k, n)
            elif k == self.stages:
                self.finish(n)
            if between is not None and 0 <= k <= self.stages:
                between()

    def end(self, arrived=0):
        for k in range(self.stages):
            for n in range(len(self.pieces)):
                for c in range(3):
                    self.group(k, n, c).wait_send()
        for n in range(len(self.pieces)):
            self.half(n).wait_send()
            if n >= arrived:
                self.half(n).wait_recv()


def first_kernel(shards, pieces, *refs):
    count = 1 + max(i for i, _, _ in pieces)
    own, sent, full, got = refs[:count], refs[count], refs[count + 1 : 2 * count + 1], refs[2 * count + 1]
    sems = refs[2 * count + 2 :]
    here = Here(shards)
    deal = Exchange(here, sent, got, *sems[5:])
    weights = Gather(here, pieces, own, full, sems[:5])
    weights.begin()
    meet(here, True)
    deal.start()
    for t in range(weights.last + 1):
        weights.step(t)
    deal.wait()
    weights.end()


def spread(weight, shards):
    return jax.ShapeDtypeStruct((shards // 2, 2) + weight.shape, weight.dtype)


def first(weights, split, message, shards, collective_id):
    count = len(weights)
    anywhere = pl.BlockSpec(memory_space=pl.ANY)
    pieces = pieces_of([w.shape[1] for w in weights], split)
    dma = pltpu.SemaphoreType.DMA
    *full, got = pl.pallas_call(
        functools.partial(first_kernel, shards, pieces),
        in_specs=[anywhere] * (count + 1),
        out_specs=[anywhere] * (count + 1),
        out_shape=[spread(w, shards) for w in weights]
        + [jax.ShapeDtypeStruct(message.shape, message.dtype)],
        scratch_shapes=Gather.semaphores(shards, pieces) + [dma, dma, dma],
        compiler_params=pltpu.CompilerParams(collective_id=collective_id, has_side_effects=True),
        name="gather_first",
    )(*weights, message)
    return [f.reshape(-1, f.shape[-1]) for f in full], got


def forward_kernel(
    shards, pieces, blocks, rows_mb,
    own_down, own_gu, sent, a1, wq, wk, wv, wg, wout, wbeta, x, gain_two, tq, tk, tv, gain, mask,
    segc, segr,
    full_down, full_gu, got, pq, pk, pv, pg, beta, on, o, ainv, u, p, l, resid, a2,
    *sems,
):
    step = pl.program_id(0)
    steps = HEADS // PAIR
    here = Here(shards)
    weights = Gather(here, pieces, (own_down, own_gu), (full_down, full_gu), sems[:5])
    deal = Exchange(here, sent, got, *sems[5:])

    @pl.when(step == 0)
    def _():
        weights.begin()
        meet(here, True)
        weights.step(0)
        resid[...] = x[...]

    normed = a1[...]
    beta[...] = jnp.dot(normed, wbeta[...], preferred_element_type=F32)
    for out, w in ((pq, wq), (pk, wk), (pv, wv), (pg, wg)):
        out[...] = jnp.dot(normed, w[...], preferred_element_type=F32)
    mixer_fwd_kernel(
        blocks, rows_mb, pq, pk, pv, pg, beta, tq, tk, tv, gain, mask, segc, segr, on, o, ainv, u,
        p, l,
    )
    resid[...] += jnp.dot(on[...], wout[...], preferred_element_type=F32)
    for s in range(steps):

        @pl.when(step == s)
        def _(s=s):
            weights.step(s + 1)
            if s == DEAL_AT:
                deal.start()
            if s == steps - 1:
                r = resid[...]
                a2[...] = (rms(r)[0] * gain_two[...]).astype(BF16)
                for t in range(steps + 1, weights.last + 1):
                    weights.step(t)
                deal.wait()
                weights.end()


def forward(
    w_down, w_gu, message, split, a1, win, wout, wbeta, x, gain_two, taps, gain, mask, segc, segr, blocks,
    shards, collective_id,
):
    rows = x.shape[0]
    rows_mb = rows // blocks
    width = PAIR * HEAD_DIM
    pieces = pieces_of([w_down.shape[1], w_gu.shape[1]], split)
    anywhere = pl.BlockSpec(memory_space=pl.ANY)
    ins, mat, one, _, full = mixer_specs(rows, blocks, rows_mb)
    per = D // width
    wcol = lambda k: pl.BlockSpec((D, width), lambda i, k=k: (0, k * per + i))
    square = jax.ShapeDtypeStruct((HEADS, blocks, rows_mb, rows_mb), F32)
    wide = jax.ShapeDtypeStruct((rows, D), F32)
    dma = pltpu.SemaphoreType.DMA
    full_down, full_gu, got, *rest = pl.pallas_call(
        functools.partial(forward_kernel, shards, pieces, blocks, rows_mb),
        grid=(HEADS // PAIR,),
        in_specs=[
            anywhere, anywhere, anywhere, full((rows, D)), wcol(0), wcol(1), wcol(2), wcol(3),
            pl.BlockSpec((width, D), lambda i: (i, 0)), full((D, HEADS)), full((rows, D)),
            full((1, D)), *ins[5:],
        ],
        out_specs=[anywhere, anywhere, anywhere, one, one, one, one, full((rows, HEADS)), one, one, mat, mat,
                   mat, mat, full((rows, D)), full((rows, D))],
        out_shape=[
            spread(w_down, shards), spread(w_gu, shards),
            jax.ShapeDtypeStruct(message.shape, message.dtype), wide, wide, wide, wide,
            jax.ShapeDtypeStruct((rows, HEADS), F32), jax.ShapeDtypeStruct((rows, D), BF16), wide,
            square, square, square, square, wide, jax.ShapeDtypeStruct((rows, D), BF16),
        ],
        scratch_shapes=Gather.semaphores(shards, pieces) + [dma, dma, dma],
        compiler_params=pltpu.CompilerParams(
            collective_id=collective_id, has_side_effects=True, vmem_limit_bytes=48 << 20
        ),
        name="mixer_forward",
    )(w_down, w_gu, message, a1, win, win, win, win, wout, wbeta, x, gain_two, taps, taps, taps, gain, mask,
      segc, segr)
    return full_down.reshape(FF, D), full_gu.reshape(D, 2 * FF), got, rest


class Scatter:
    def __init__(self, here, pieces, whole, mine, other, coming, sems, kept):
        self.here, self.pieces, self.whole, self.mine = here, pieces, whole, mine
        self.other, self.coming, self.kept_of = other, coming, kept
        self.send, self.recv, self.pair_send, self.pair_recv = sems
        self.stages = here.bits - 1
        self.order = routes(here.shards)
        self.core = here.core
        self.cuts = [
            [(at + a, s) for a, s in colours(size, n)] for n, (_, at, size) in enumerate(pieces)
        ]

    @staticmethod
    def semaphores(shards, number):
        dma, stages = pltpu.SemaphoreType.DMA, shards.bit_length() - 2
        return [dma((stages, number, 3)), dma((stages, number, 3)), dma((number,)), dma((number,))]

    @staticmethod
    def buffers(shards, shapes):
        stages = shards.bit_length() - 2
        return [pltpu.VMEM((shards // 2,) + s, BF16) for s in shapes] + [
            pltpu.VMEM((1 << (stages - 1 - k),) + s, BF16) for s in shapes for k in range(stages)
        ]

    @staticmethod
    def split(shards, count, refs):
        stages = shards.bit_length() - 2
        other, refs = refs[:count], refs[count:]
        return other, [refs[i * stages : (i + 1) * stages] for i in range(count)]

    def pair(self, n):
        i, at, size = self.pieces[n]
        return pltpu.make_async_remote_copy(
            src_ref=self.whole(n, 1 - self.core), dst_ref=self.other[i].at[:, :, pl.ds(at, size)],
            send_sem=self.pair_send.at[n], recv_sem=self.pair_recv.at[n],
            device_id=self.here.partner[0], device_id_type=MESH,
        )

    def hop(self, k, n, c, source, spots):
        i = self.pieces[n][0]
        at, size = self.cuts[n][c]
        cols = pl.ds(at, size)
        return pltpu.make_async_remote_copy(
            src_ref=self.other[i].at[source, :, cols],
            dst_ref=self.coming[i][k].at[spots, :, cols],
            send_sem=self.send.at[k, n, c], recv_sem=self.recv.at[k, n, c],
            device_id=self.here.partner[self.order[c][k]], device_id_type=MESH,
        )

    def group(self, k, n, c):
        all_of = pl.ds(0, 1 << (self.stages - 1 - k))
        return self.hop(k, n, c, all_of, all_of)

    def total(self, k, n, c, shard, spot):
        i = self.pieces[n][0]
        at, size = self.cuts[n][c]
        cols = pl.ds(at, size)
        q = lax.div(shard, 2)
        value = self.mine(i, q, cols).astype(F32) + self.other[i][q, :, cols].astype(F32)
        for p in range(k):
            value = value + self.coming[i][p][spot, :, cols].astype(F32)
        return value

    def launch(self, k, n):
        if k == 0:
            kept = self.kept_of(n)
            if kept is not None:
                kept.wait()
            self.pair(n).wait_recv()
        for c in range(3):
            if k > 0:
                self.group(k - 1, n, c).wait_recv()
            much = 1 << (self.stages - 1 - k)
            at, size = self.cuts[n][c]

            def body(j, _, c=c, at=at, size=size):
                shard = self.here.flip(self.order[c][k + 1 :], j, (self.order[c][k],))
                q = lax.div(shard, 2)
                self.other[self.pieces[n][0]][q, :, pl.ds(at, size)] = self.total(
                    k, n, c, shard, much + j
                ).astype(BF16)
                self.hop(k, n, c, q, j).start()
                return 0

            lax.fori_loop(0, much, body, 0)

    def finish(self, n, write):
        for c in range(3):
            self.group(self.stages - 1, n, c).wait_recv()
            at, size = self.cuts[n][c]
            write(self.pieces[n][0], at, size, self.total(self.stages, n, c, self.here.me, 0))

    def end(self, n, paired=True):
        for k in range(self.stages):
            for c in range(3):
                self.group(k, n, c).wait_send()
        if paired:
            self.pair(n).wait_send()


def front_kernel(shards, blocks, rows_mb, split, *refs):
    (own_in, own_out, own_down, own_gu, small, tokens, cotangent, teacher, deal_row, valid_row, lengths), refs = refs[:11], refs[11:]
    (full_in, full_out, full_down, full_gu, pq, pk, pv, pg, beta, on, o, ainv, u, p, l, resid, a2, x, m, counted, deal, sort_t, gt, taps,
     gain_one, gain_two, wbeta, segc, segr, mask, a1, a1_t, a2_t, gain), refs = refs[:34], refs[34:]
    (sent, got, sent_gt, got_gt, got_small, wbuf, wout, w_sem, out_sem), refs = refs[:9], refs[9:]
    sems, deal_sems, later_sems, small_sems = refs[:5], refs[5:8], refs[8:11], refs[11:14]
    step = pl.program_id(0)
    steps = HEADS // PAIR
    width = PAIR * HEAD_DIM
    rows = blocks * rows_mb
    share = rows // shards
    here = Here(shards)
    pieces = pieces_of([4 * D, D, D, 2 * FF], split)
    weights = Gather(here, pieces, (own_in, own_out, own_down, own_gu), (full_in, full_out, full_down, full_gu), sems)
    first_send = Exchange(here, sent, got, *deal_sems)
    second_send = Exchange(here, sent_gt, got_gt, *later_sems)
    small_send = Exchange(here, small, got_small, *small_sems, same=True)
    of_in = split[0]
    hidden_from = len(pieces) + weights.stages - steps
    deal_to, later_from = X_STEPS, GT_FROM

    def trickle(exchange, first, last):
        parts, done = weights.slots(first, last), [0]

        def at(t):
            if not first <= t < last:
                return None
            done[0] = weights.slots(first, t)

            def one():
                exchange.start_part(done[0], parts)
                done[0] += 1

            return one

        return at

    deal_some = trickle(first_send, 1, deal_to)
    later_some = trickle(second_send, later_from, weights.last + 1)

    def between(t):
        acts = [f for f in (deal_some(t), later_some(t)) if f is not None]
        return (lambda: [f() for f in acts]) if acts else None

    def fetch(s, g):
        return pltpu.make_async_copy(
            full_in.at[:, :, :, pl.ds(g * D + s * width, width)], wbuf.at[s % 2, g], w_sem.at[s % 2, g]
        )

    def fetch_out():
        return pltpu.make_async_copy(full_out, wout, out_sem)

    @pl.when(step == 0)
    def _():
        weights.begin()
        meet(here, True)
        weights.step(0)
        small_send.start()
        gain[...] = small[...].astype(F32)[6:7, :HEAD_DIM]
        row, col = iota2((rows, rows), 0), iota2((rows, rows), 1)
        column = lambda v: jnp.sum(jnp.where(row == col, v, 0.0), axis=1, keepdims=True)
        dealt = deal_row[...].astype(F32)
        target = jnp.floor((dealt + 0.5) * (1.0 / rows))
        valid = valid_row[...].astype(F32)
        target_c = column(target)
        rank = jnp.sum(jnp.where((target == target_c) & (col < row), 1.0, 0.0), axis=1, keepdims=True)
        slot = target_c * share + rank
        sort_t[...] = (slot == col.astype(F32)).astype(BF16)
        lane = iota2((rows, 128), 1)
        notes = jnp.where(
            lane == 0, column(valid),
            jnp.where(lane == 1, column(dealt - target * rows), jnp.where(lane == 2, jnp.sum(valid), 0.0)),
        ).astype(BF16)
        sent[:, :, :D] = tn(sort_t[...], tokens[...]).reshape(shards, share, D).astype(BF16)
        sent[:, :, D:] = tn(sort_t[...], notes).reshape(shards, share, 128).astype(BF16)
        weights.step(1, between(1))
        for at, part in ((0, cotangent), (D, teacher)):
            sent_gt[:, :, at : at + D] = tn(sort_t[...], part[...]).reshape(shards, share, D).astype(BF16)
        weights.step(2, between(2))
        at_row, at_col = iota2((rows, 1), 0), iota2((1, rows), 1)
        seg_c, seg_r = jnp.zeros((rows, 1), F32), jnp.zeros((1, rows), F32)
        lens = lengths[...].astype(F32)
        for b in range(blocks):
            end = jnp.zeros((1, 1), F32) + b * rows_mb
            for i in range(lengths.shape[1]):
                seg_c = seg_c + jnp.where(at_row >= b * rows_mb, 1.0, 0.0) * (i == 0)
                seg_r = seg_r + jnp.where(at_col >= b * rows_mb, 1.0, 0.0) * (i == 0)
                end = end + lens[b : b + 1, i : i + 1]
                if i < lengths.shape[1] - 1:
                    seg_c = seg_c + jnp.where(at_row.astype(F32) >= end, 1.0, 0.0)
                    seg_r = seg_r + jnp.where(at_col.astype(F32) >= end, 1.0, 0.0)
        segc[...] = seg_c.astype(jnp.int32)
        segr[...] = seg_r.astype(jnp.int32)
        lane8 = iota2((rows, 8), 1)
        wide = jnp.broadcast_to(seg_c, (rows, 128))
        marks = jnp.where(lane8 == 0, 1.0, 0.0)
        for s in range(1, CONV):
            before = pltpu.roll(wide, s, 0)[:, :1]
            same = jnp.where((before == seg_c) & (at_row >= s), 1.0, 0.0)
            marks = marks + jnp.where(lane8 == s, same, 0.0)
        mask[...] = marks
        small_send.wait()
        own_taps, own_gain = 3 * D // shards, D // shards
        per = 128 // own_gain
        a, c = iota2((per * 128, per * own_taps), 0), iota2((per * 128, per * own_taps), 1)
        pick_taps = ((a // 128 == c // own_taps) & (a % 128 == c % own_taps)).astype(BF16)
        a, c = iota2((per * 128, 128), 0), iota2((per * 128, 128), 1)
        pick_gain = ((a // 128 == c // own_gain) & (a % 128 == c % own_gain)).astype(BF16)
        for g in range(shards // per):
            left = jnp.concatenate([got_small[g * per + i, :, :128].astype(F32) for i in range(per)], axis=1).astype(BF16)
            right = jnp.concatenate([got_small[g * per + i, :, 128:].astype(F32) for i in range(per)], axis=1).astype(BF16)
            tap = nn(left, pick_taps)
            taps[:, g * per * own_taps : (g + 1) * per * own_taps] = tap[:CONV]
            gains = nn(left, pick_gain)
            gain_one[:, g * 128 : (g + 1) * 128] = gains[4:5]
            gain_two[:, g * 128 : (g + 1) * 128] = gains[5:6]
            wbeta[:, g * 128 : (g + 1) * 128] = nn(right, pick_gain).astype(BF16)
        for t in range(3, hidden_from):
            weights.step(t, between(t))
        first_send.wait()
        flat = got[...].astype(F32).reshape(rows, D + 128)
        notes = flat[:, D:]
        deal[...] = (notes[:, 1:2] == col.astype(F32)).astype(BF16)
        m[...] = tn(deal[...], notes.astype(BF16))[:, :1]
        firsts = jnp.where(lax.rem(iota2((rows, 1), 0), share) == 0, notes[:, 2:3], 0.0)
        counted[...] = jnp.sum(firsts, axis=0, keepdims=True)
        x_now = tn(deal[...], flat[:, :D].astype(BF16))
        x[...] = x_now
        a1[...] = (rms(x_now)[0] * gain_one[...]).astype(BF16)
        beta[...] = nt(a1[...], wbeta[...])
        a1_t[...] = a1[...].T
        for n in range(of_in):
            weights.half(n).wait_recv()
        for g in range(4):
            fetch(0, g).start()

    for s in range(steps):

        @pl.when(step == s)
        def _(s=s):
            for g in range(4):
                fetch(s, g).wait()
            if s + 1 < steps:
                for g in range(4):
                    fetch(s + 1, g).start()

    slot_now = lax.rem(step, 2)
    for g, out in enumerate((pq, pk, pv, pg)):
        out[...] = nn(a1[...], wbuf[slot_now, g].reshape(D, width))
    here_cols = pl.ds(pl.multiple_of(step * width, width), width)
    taps_of = lambda j: taps.at[:, pl.ds(pl.multiple_of(j * D + step * width, width), width)]
    mixer_fwd_kernel(
        blocks, rows_mb, pq, pk, pv, pg, beta, taps_of(0), taps_of(1), taps_of(2), gain, mask, segc, segr,
        on.at[:, here_cols], o, ainv, u, p, l,
    )
    for s in range(steps):

        @pl.when(step == s)
        def _(s=s):
            weights.step(hidden_from + s, between(hidden_from + s))
            if s == steps - 1:
                for n in range(of_in, of_in + split[1]):
                    weights.half(n).wait_recv()
                fetch_out().start()
                second_send.wait()
                gt[...] = tn(deal[...], got_gt[...].astype(F32).reshape(rows, gt.shape[1]).astype(BF16))
                fetch_out().wait()
                r = x[...] + nn(on[...], wout[...].reshape(D, D))
                resid[...] = r
                a2[...] = (rms(r)[0] * gain_two[...]).astype(BF16)
                a2_t[...] = a2[...].T
                weights.end(of_in + split[1])


def front(weights, small, tokens, cotangent, teacher, deal_rows, valid_mask, lengths, shards, collective_id):
    rows, blocks = tokens.shape[0], lengths.shape[0]
    rows_mb, share = rows // blocks, rows // shards
    width = PAIR * HEAD_DIM
    split = (2, 1, 1, 2)
    pieces = pieces_of([w.shape[1] for w in weights], split)
    anywhere = pl.BlockSpec(memory_space=pl.ANY)
    _, mat, one, _, full = mixer_specs(rows, blocks, rows_mb)
    f32 = lambda *shape: jax.ShapeDtypeStruct(shape, F32)
    bf = lambda *shape: jax.ShapeDtypeStruct(shape, BF16)
    square = f32(HEADS, blocks, rows_mb, rows_mb)
    wide = f32(rows, D)
    vm, dma = pltpu.VMEM, pltpu.SemaphoreType.DMA
    outs = [
        (spread(w, shards), anywhere) for w in weights
    ] + [(wide, one)] * 4 + [
        (f32(rows, HEADS), full((rows, HEADS))), (bf(rows, D), full((rows, D))), (wide, one),
        (square, mat), (square, mat), (square, mat), (square, mat), (wide, full((rows, D))),
        (bf(rows, D), full((rows, D))), (wide, full((rows, D))), (f32(rows, 1), full((rows, 1))),
        (f32(1, 1), full((1, 1))), (bf(rows, rows), full((rows, rows))), (bf(rows, rows), full((rows, rows))),
        (f32(rows, 2 * D), full((rows, 2 * D))), (f32(CONV, 3 * D), full((CONV, 3 * D))),
        (f32(1, D), full((1, D))), (f32(1, D), full((1, D))), (bf(8, D), full((8, D))),
        (jax.ShapeDtypeStruct((rows, 1), jnp.int32), full((rows, 1))),
        (jax.ShapeDtypeStruct((1, rows), jnp.int32), full((1, rows))), (f32(rows, 8), full((rows, 8))),
        (bf(rows, D), full((rows, D))), (bf(D, rows), full((D, rows))), (bf(D, rows), full((D, rows))),
        (f32(1, HEAD_DIM), full((1, HEAD_DIM))),
    ]
    return pl.pallas_call(
        functools.partial(front_kernel, shards, blocks, rows_mb, split),
        grid=(HEADS // PAIR,),
        in_specs=[anywhere] * 4 + [
            full(small.shape), full((rows, D)), full((rows, D)), full((rows, D)), full((1, rows)), full((1, rows)),
            full(lengths.shape),
        ],
        out_specs=[s for _, s in outs],
        out_shape=[s for s, _ in outs],
        scratch_shapes=[
            vm((shards, share, D + 128), BF16), vm((shards, share, D + 128), BF16),
            vm((shards, share, 2 * D), BF16), vm((shards, share, 2 * D), BF16),
            vm((shards,) + small.shape, BF16),
            vm((2, 4, shards // 2, 2, D // shards, width), BF16),
            vm((shards // 2, 2, D // shards, D), BF16), dma((2, 4)), dma,
        ] + Gather.semaphores(shards, pieces) + [dma] * 9,
        compiler_params=pltpu.CompilerParams(
            collective_id=collective_id, has_side_effects=True, vmem_limit_bytes=58 << 20
        ),
        name="front",
    )(*weights, small, tokens, cotangent, teacher, deal_rows[None, :], valid_mask[None, :], lengths)


def backward_kernel(shards, blocks, rows_mb, pieces, *refs):
    (d_down, df, a2, gate, up, wga, wup, wdn, dy, resid, gain_two, wout, wq, wk, wv, wg, a1, on, x,
     gain_one, wbeta, *mixer), refs = refs[:38], refs[38:]
    (g_down, g_gu, dwq, dwk, dwv, dwg, dw_out, d_wbeta, dx, d_two, d_one, dtq, dtk, dtv,
     d_gain), refs = refs[:15], refs[15:]
    (mine_down, d_gu, acc, dresid, dz, don, dpq, dpk, dpv, dpg, dbeta, keep), refs = refs[:12], refs[12:]
    sems, buffers = refs[:4], refs[4:]
    step = pl.program_id(0)
    chunks = FF // CHUNK
    pairs = HEADS // PAIR
    here = Here(shards)
    core = here.core
    other, coming = Scatter.split(shards, 2, buffers)
    r_gu = d_gu.shape[2]

    def whole(n, parity):
        i, at, size = pieces[n]
        if i == 0:
            return d_down.at[:, parity, :, pl.ds(at, size)]
        return d_gu.at[:, parity, :, pl.ds(at, size)]

    def mine(i, q, cols):
        return mine_down[q, :, cols] if i == 0 else d_gu[q, core, :, cols]

    def kept(n):
        if n > 0:
            return None
        return pltpu.make_async_copy(d_down.at[:, core], mine_down, keep)

    net = Scatter(here, pieces, whole, mine, other, coming, sems, kept)

    def write(i, at, size, value):
        if i == 0:
            g_down[:, pl.ds(at, size)] = value
            return
        for tile in range(at // 128, (at + size) // 128):
            chunk, inner = tile * 128 // (2 * CHUNK), tile * 128 % (2 * CHUNK)
            start = chunk * CHUNK + inner if inner < CHUNK else FF + chunk * CHUNK + inner - CHUNK
            g_gu[:, start : start + 128] = value[:, tile * 128 - at : tile * 128 - at + 128]

    @pl.when(step == 0)
    def _():
        kept(0).start()
        meet(here, False)
        net.pair(0).start()
        acc[...] = jnp.zeros_like(acc)

    @pl.when(step < chunks)
    def _():
        dhid = nt(df[...], wdn[...])
        g = gate[...]
        s = sigmoid(g)
        d_gate = (dhid * up[...] * (s * (1.0 + g * (1.0 - s)))).astype(BF16)
        d_up = (dhid * (g * s)).astype(BF16)
        acc[...] += nt(d_gate, wga[...]) + nt(d_up, wup[...])
        for at, part in ((0, d_gate), (CHUNK, d_up)):
            grad = tn(a2[...], part).reshape(shards // 2, 2, r_gu, CHUNK).astype(BF16)
            start = pl.multiple_of(step * (2 * CHUNK) + at, CHUNK)
            d_gu[:, :, :, pl.ds(start, CHUNK)] = grad

    @pl.when(step == chunks - 1)
    def _():
        nr, rr = rms(resid[...])
        da2 = acc[...]
        d_two[...] = jnp.sum(da2 * nr, axis=0, keepdims=True)
        dresid[...] = dy[...] + rms_back(nr, rr, gain_two[...] * da2)
        acc[...] = jnp.zeros_like(acc)
        dz[...] = dresid[...].astype(BF16)

    @pl.when(step >= chunks)
    def _():
        don[...] = nt(dz[...], wout[...])
        mixer_bwd_kernel(
            blocks, rows_mb, PAIR, step - chunks, *mixer[:12], don, *mixer[12:], dpq, dpk, dpv, dpg, dbeta, dtq,
            dtk, dtv, d_gain,
        )
        for dp, w, out in ((dpq, wq, dwq), (dpk, wk, dwk), (dpv, wv, dwv), (dpg, wg, dwg)):
            acc[...] += nt(dp[...], w[...])
            out[...] = tn(a1[...], dp[...]).astype(BF16)
        dw_out[...] = tn(on[...], dz[...]).astype(BF16)

    @pl.when(step == chunks + pairs - 1)
    def _():
        d_beta = dbeta[...].astype(BF16)
        grad = acc[...] + nt(d_beta, wbeta[...])
        d_wbeta[...] = tn(a1[...], d_beta)
        nx, rx = rms(x[...])
        d_one[...] = jnp.sum(grad * nx, axis=0, keepdims=True)
        dx[...] = (dresid[...] + rms_back(nx, rx, gain_one[...] * grad)).astype(BF16)

    ready = {pieces[n][1] // (2 * CHUNK) + pieces[n][2] // (2 * CHUNK) - 1: n for n in (1, 2)}
    plan = {}
    for s, n in ready.items():
        plan.setdefault(s, []).append((net.pair, n))
    tail = range(chunks - 1, chunks + pairs)
    plan.setdefault(3, []).append((net.launch, 0, 0))
    for place, s in enumerate(tail):
        for n in range(3):
            k = place + 1 - n
            if (k, n) != (0, 0) and 0 <= k < net.stages:
                plan.setdefault(s, []).append((net.launch, k, n))
            elif k == net.stages:
                plan.setdefault(s, []).append((net.finish, n, write))
    last = tail[-1]
    for place in range(len(tail), net.stages + 3):
        for n in range(3):
            k = place + 1 - n
            if 0 <= k < net.stages:
                plan[last].append((net.launch, k, n))
            elif k == net.stages:
                plan[last].append((net.finish, n, write))
    for s, actions in plan.items():

        @pl.when(step == s)
        def _(actions=actions, s=s):
            for act, *args in actions:
                result = act(*args)
                if act == net.pair:
                    result.start()
            if s == last:
                for n in range(3):
                    net.end(n)


def backward(
    d_down, df, a2, gu, wgu, wdown, dy, resid, gain_two, wout, win, a1, on, x, gain_one, wbeta, proj,
    beta_pre, taps, gain, mask, segc, segr, saved, blocks, shards, collective_id,
):
    rows = x.shape[0]
    rows_mb = rows // blocks
    width = PAIR * HEAD_DIM
    chunks, pairs = FF // CHUNK, HEADS // PAIR
    anywhere = pl.BlockSpec(memory_space=pl.ANY)
    full = lambda shape: pl.BlockSpec(shape, lambda s: (0,) * len(shape))
    early = lambda s: jnp.minimum(s, chunks - 1)
    late = lambda s: jnp.maximum(s - chunks, 0)
    lane_e = lambda r, w, off=0: pl.BlockSpec((r, w), lambda s: (0, off + early(s)))
    lane_l = lambda r, w, off=0: pl.BlockSpec((r, w), lambda s: (0, off + late(s)))
    wide_l = lambda off=0: pl.BlockSpec(
        (D, width), lambda s: (0, off + late(s)), pipeline_mode=pl.Buffered(1)
    )
    row_l = lambda r, w: pl.BlockSpec((r, w), lambda s: (late(s), 0))
    mat = pl.BlockSpec(
        (PAIR, blocks, rows_mb, rows_mb), lambda s: (late(s), 0, 0, 0), pipeline_mode=pl.Buffered(1)
    )
    part_l = pl.BlockSpec(
        (rows, width), lambda s: (0, late(s)), pipeline_mode=pl.Buffered(1)
    )
    per = D // width
    tap = lambda k: lane_l(CONV, width, k * per)
    r_down, r_gu = FF // shards, D // shards
    a, b = chunks // 2 * 2 * CHUNK, 2 * FF
    pieces = [(0, 0, D), (1, 0, a), (1, a, b - a)]
    f32 = lambda *shape: jax.ShapeDtypeStruct(shape, F32)
    bf = lambda *shape: jax.ShapeDtypeStruct(shape, BF16)
    square = bf(D, D)
    vm = pltpu.VMEM
    return pl.pallas_call(
        functools.partial(backward_kernel, shards, blocks, rows_mb, pieces),
        grid=(chunks + pairs,),
        in_specs=[
            anywhere, full((rows, D)), full((rows, D)), lane_e(rows, CHUNK),
            lane_e(rows, CHUNK, chunks), lane_e(D, CHUNK), lane_e(D, CHUNK, chunks),
            pl.BlockSpec((CHUNK, D), lambda s: (early(s), 0)), full((rows, D)), full((rows, D)),
            full((1, D)), row_l(width, D), wide_l(), wide_l(per), wide_l(2 * per),
            wide_l(3 * per), full((rows, D)),
            lane_l(rows, width), full((rows, D)), full((1, D)), full((D, HEADS)),
            part_l, part_l, part_l, part_l, full((rows, HEADS)), tap(0), tap(1), tap(2), full((1, HEAD_DIM)), full((rows, 8)),
            full((rows, 1)), full((1, rows)), lane_l(rows, width), mat, mat, mat, mat,
        ],
        out_specs=[
            full((r_down, D)), full((r_gu, 2 * FF)), wide_l(), wide_l(), wide_l(), wide_l(),
            row_l(width, D), full((D, HEADS)), full((rows, D)),
            full((1, D)), full((1, D)), lane_l(CONV, width), lane_l(CONV, width),
            lane_l(CONV, width), full((1, HEAD_DIM)),
        ],
        out_shape=[
            f32(r_down, D), f32(r_gu, 2 * FF), square, square, square, square, square,
            f32(D, HEADS), bf(rows, D), f32(1, D), f32(1, D), f32(CONV, D), f32(CONV, D),
            f32(CONV, D), f32(1, HEAD_DIM),
        ],
        scratch_shapes=[
            vm((shards // 2, r_down, D), BF16), vm((shards // 2, 2, r_gu, 2 * FF), BF16),
            vm((rows, D), F32), vm((rows, D), F32), vm((rows, D), BF16), vm((rows, width), F32),
            vm((rows, width), BF16), vm((rows, width), BF16), vm((rows, width), BF16),
            vm((rows, width), BF16), vm((rows, HEADS), F32),
            pltpu.SemaphoreType.DMA,
        ] + Scatter.semaphores(shards, 3) + Scatter.buffers(shards, [(r_down, D), (r_gu, 2 * FF)]),
        compiler_params=pltpu.CompilerParams(
            collective_id=collective_id, has_side_effects=True, vmem_limit_bytes=60 << 20
        ),
        name="backward",
    )(d_down.reshape(shards // 2, 2, r_down, D), df, a2, gu, gu, wgu, wgu, wdown, dy, resid, gain_two,
      wout, win, win, win, win, a1, on, x, gain_one, wbeta, *proj, beta_pre, taps, taps, taps, gain,
      mask, segc, segr, *saved)


def link_plan(half_way, done, last, heads):
    return [
        [4, 9, 11, 12], [half_way + 3, done + 1, done + 2], [done + 1, done + 3], [done + 6], [last], [last],
        [done + 5],
    ]


def rear_kernel(shards, blocks, rows_mb, pieces, *refs):
    (d_down, sent_y, dy, resid, x, a2_t, a1_t, df, gate, up, wga, wup, wdn, gain_two, gain_one, wout, wq, wk, wv, wg,
     on, wbeta, deal, loss, *mixer), refs = refs[:41], refs[41:]
    (g_down, g_gu, g_in, g_out, got_y, got_dx, small_sum), refs = refs[:7], refs[7:]
    (mine_down, mine_gu, mine_in, mine_out, stage_gu, stage_in, stage_out, acc, dresid, held, dz, don, dpq, dpk, dpv,
     dpg, turned, dbeta, dtaps, d_gain, d_two, sent_dx, small, small_got, keep, load, gu_sem, in_sem, out_sem), refs = refs[:29], refs[29:]
    y_sems, dx_sems, small_sems, sems, buffers = refs[:3], refs[3:6], refs[6:9], refs[9:13], refs[13:]
    step = pl.program_id(0)
    chunks, heads = FF // SLICE, HEADS
    rows = blocks * rows_mb
    share, r_gu = rows // shards, D // shards
    here = Here(shards)
    core = here.core
    other, coming = Scatter.split(shards, 4, buffers)
    mines = (mine_down, mine_gu, mine_in, mine_out)
    pair_recv = sems[3]

    def whole(n, parity):
        i, at, size = pieces[n]
        if i == 0:
            return d_down.at[:, parity, :, pl.ds(at, size)]
        return other[i].at[:, :, pl.ds(at, size)]

    def kept(n):
        if n > 0:
            return None
        return pltpu.make_async_copy(d_down.at[:, core], mine_down, keep)

    net = Scatter(
        here, pieces, whole, lambda i, q, cols: mines[i][q, :, cols], other, coming, sems, kept
    )
    give_y = Exchange(here, sent_y, got_y, *y_sems)
    give_dx = Exchange(here, sent_dx, got_dx, *dx_sems)
    give_small = Exchange(here, small, small_got, *small_sems)

    def cross(stage, slot, there, send, n):
        return pltpu.make_async_remote_copy(
            src_ref=stage.at[slot], dst_ref=there, send_sem=send.at[slot], recv_sem=pair_recv.at[n],
            device_id=here.partner[0], device_id_type=MESH,
        )

    def cross_gu(j):
        cols = pl.ds(pl.multiple_of(j * (2 * SLICE), 2 * SLICE), 2 * SLICE)
        return cross(stage_gu, lax.rem(j, 2), other[1].at[:, :, cols], gu_sem, 1 + lax.div(j + chunks % 2, (chunks + 1) // 2))

    def cross_in(s):
        width = 4 * HEAD_DIM
        cols = pl.ds(pl.multiple_of(s * width, width), width)
        return cross(stage_in, lax.rem(s, 2), other[2].at[:, :, cols], in_sem, 3 + lax.div(s, heads // 2) + lax.div(s, 3 * heads // 4))

    def cross_out(s):
        much = shards // 2 // heads
        return cross(stage_out, s % 2, other[3].at[pl.ds(s * much, much)], out_sem, 6)

    def by_core(value):
        first, second = value[:, 0], value[:, 1]
        return (
            jnp.where(core == 0, first, second).astype(BF16), jnp.where(core == 0, second, first).astype(BF16)
        )

    def write(i, at, size, value):
        if i == 0:
            g_down[:, pl.ds(at, size)] = value
        elif i == 3:
            g_out[:, pl.ds(at, size)] = value
        else:
            for tile in range(at // 128, (at + size) // 128):
                if i == 1:
                    chunk, inner = divmod(tile * 128, 2 * SLICE)
                    start = chunk * SLICE + inner + (FF - SLICE if inner >= SLICE else 0)
                else:
                    start = tile % 4 * D + tile // 4 * HEAD_DIM
                target = g_gu if i == 1 else g_in
                target[:, start : start + 128] = value[:, tile * 128 - at : tile * 128 - at + 128]

    load_dy = pltpu.make_async_copy(dy, dresid, load.at[0])
    load_resid = pltpu.make_async_copy(resid, held, load.at[1])
    load_x = pltpu.make_async_copy(x, held, load.at[1])
    load_a2 = pltpu.make_async_copy(a2_t, turned, load.at[2])
    load_a1 = pltpu.make_async_copy(a1_t, turned, load.at[2])

    @pl.when(step == 0)
    def _():
        kept(0).start()
        load_dy.start()
        load_resid.start()
        meet(here, True)
        net.pair(0).start()
        give_y.start()
        acc[...] = jnp.zeros_like(acc)
        load_a2.start()
        load_a2.wait()

    @pl.when(step < chunks)
    def _():
        dhid = nt(df[...], wdn[...])
        g = gate[...]
        s = sigmoid(g)
        d_gate = (dhid * up[...] * (s * (1.0 + g * (1.0 - s)))).astype(BF16)
        d_up = (dhid * (g * s)).astype(BF16)
        acc[...] += nt(d_gate, wga[...]) + nt(d_up, wup[...])

        @pl.when(step >= 2)
        def _():
            cross_gu(step - 2).wait_send()

        slot = lax.rem(step, 2)
        part = jnp.concatenate([d_gate, d_up], axis=1)
        near, far = by_core(nn(turned[...], part).reshape(shards // 2, 2, r_gu, 2 * SLICE))
        mine_gu[:, :, pl.ds(pl.multiple_of(step * (2 * SLICE), 2 * SLICE), 2 * SLICE)] = near
        stage_gu[slot] = far
        cross_gu(step).start()

    @pl.when(step == chunks - 1)
    def _():
        load_dy.wait()
        load_resid.wait()
        nr, rr = rms(held[...])
        da2 = acc[...]
        d_two[...] = jnp.sum(da2 * nr, axis=0, keepdims=True)
        dresid[...] = dresid[...] + rms_back(nr, rr, gain_two[...] * da2)
        dz[...] = dresid[...].astype(BF16)
        acc[...] = jnp.zeros_like(acc)
        load_a1.start()
        load_x.start()
        load_a1.wait()

    @pl.when(step >= chunks)
    def _():
        head = step - chunks
        don[...] = nt(dz[...], wout[...])
        taps_of = lambda j: dtaps.at[:, pl.ds(pl.multiple_of(j * D + head * HEAD_DIM, HEAD_DIM), HEAD_DIM)]
        mixer_bwd_kernel(
            blocks, rows_mb, 1, head, *mixer[:12], don, *mixer[12:], dpq, dpk, dpv, dpg, dbeta, taps_of(0),
            taps_of(1), taps_of(2), d_gain,
        )

        @pl.when(head >= 2)
        def _():
            cross_in(head - 2).wait_send()

        slot = lax.rem(head, 2)
        acc[...] += nt(dpq[...], wq[...]) + nt(dpk[...], wk[...]) + nt(dpv[...], wv[...]) + nt(dpg[...], wg[...])
        width = 4 * HEAD_DIM
        part = jnp.concatenate([dpq[...], dpk[...], dpv[...], dpg[...]], axis=1)
        near, far = by_core(nn(turned[...], part).reshape(shards // 2, 2, r_gu, width))
        mine_in[:, :, pl.ds(pl.multiple_of(head * width, width), width)] = near
        stage_in[slot] = far
        cross_in(head).start()

    @pl.when(step == chunks)
    def _():
        much = shards // 2 // heads
        for s in range(heads):
            if s >= 2:
                cross_out(s - 2).wait_send()
            part = tn(on[:, s * HEAD_DIM : (s + 1) * HEAD_DIM], dz[...])
            near, far = by_core(part.reshape(much, 2, r_gu, D))
            mine_out[s * much : (s + 1) * much] = near
            stage_out[s % 2] = far
            cross_out(s).start()
        for s in (heads - 2, heads - 1):
            cross_out(s).wait_send()

    def last_rows():
        d_beta = dbeta[...].astype(BF16)
        grad = acc[...] + nn(d_beta, wbeta[...])
        d_wbeta = lax.dot_general(
            d_beta, turned[...], (((0,), (1,)), ((), ())), preferred_element_type=F32
        )
        load_x.wait()
        nx, rx = rms(held[...])
        d_one = jnp.sum(grad * nx, axis=0, keepdims=True)
        dx = (dresid[...] + rms_back(nx, rx, gain_one[...] * grad)).astype(BF16)
        sent_dx[...] = nn(deal[...], dx).reshape(shards, share, D).astype(BF16)
        own_taps, own_gain = 3 * D // shards, D // shards
        per = 128 // own_gain
        a, c = iota2((per * own_taps, per * 128), 1), iota2((per * own_taps, per * 128), 0)
        put_taps = ((a // 128 == c // own_taps) & (a % 128 == c % own_taps)).astype(F32)
        a, c = iota2((128, per * 128), 1), iota2((128, per * 128), 0)
        put_gain = ((a // 128 == c // own_gain) & (a % 128 == c % own_gain)).astype(F32)
        lane = iota2((1, 128), 1)
        row8 = iota2((8, 128), 0)
        shared = jnp.where(row8 == 6, d_gain[...], jnp.where((row8 == 7) & (lane == 0), loss[...], 0.0))
        for g in range(shards // per):
            top = jnp.concatenate(
                [dtaps[:, g * per * own_taps : (g + 1) * per * own_taps],
                 jnp.zeros((8 - CONV, per * own_taps), F32)], axis=0
            )
            cols = slice(g * 128, (g + 1) * 128)
            gains = jnp.where(row8 == 4, d_one[:, cols], jnp.where(row8 == 5, d_two[:, cols], 0.0))
            upper = mm(top, put_taps, 1, 0) + mm(gains, put_gain, 1, 0)
            lower = mm(d_wbeta[:, cols], put_gain, 1, 0)
            for i in range(per):
                small[g * per + i, 0:8, :] = upper[:, i * 128 : (i + 1) * 128] + shared
                small[g * per + i, 8:16, :] = lower[:, i * 128 : (i + 1) * 128]

    last = chunks + heads - 1
    half_way, done = chunks // 2 - 1, chunks - 1
    starts = link_plan(half_way, done, last, heads)
    timed = []
    for n in range(len(pieces)):
        for k in range(net.stages + 1):
            at = starts[n][k] if k < len(starts[n]) else starts[n][-1] + 2 * (k - len(starts[n]) + 1)
            timed.append((at, k != net.stages, n, k))
    timed.sort()

    def act(n, k):
        if k < net.stages:
            net.launch(k, n)
        else:
            net.finish(n, write)

    for s in sorted({t[0] for t in timed if t[0] < last}):

        @pl.when(step == s)
        def _(s=s):
            for at, _, n, k in timed:
                if at == s:
                    act(n, k)

    @pl.when(step == last)
    def _():
        for at, _, n, k in timed:
            if at == last:
                act(n, k)
        last_rows()
        give_small.start()
        tail = [(n, k) for at, _, n, k in timed if at > last]
        for i, (n, k) in enumerate(tail):
            act(n, k)
            if i < DX_PARTS:
                give_dx.start_part(i, DX_PARTS)
        give_small.wait()
        small_sum[...] = jnp.sum(small_got[...], axis=0)
        give_y.wait()
        give_dx.wait()
        for j in (chunks - 2, chunks - 1):
            cross_gu(j).wait_send()
        for s in (heads - 2, heads - 1):
            cross_in(s).wait_send()
        for n in range(len(pieces)):
            net.end(n, paired=n == 0)


def rear(
    d_down, sent_y, dy, resid, x, a2_t, a1_t, df, gate, up, wgu, wdown, gain_two, gain_one, wout, win, on, wbeta, deal, loss,
    proj, beta_pre, taps, gain, mask, segc, segr, saved, blocks, shards, collective_id,
):
    rows = x.shape[0]
    rows_mb, share = rows // blocks, rows // shards
    chunks = FF // SLICE
    anywhere = pl.BlockSpec(memory_space=pl.ANY)
    once = pl.Buffered(MIXER_BUFFERS)
    full = lambda shape: pl.BlockSpec(shape, lambda s: (0,) * len(shape))
    early = lambda s: jnp.minimum(s, chunks - 1)
    late = lambda s: jnp.maximum(s - chunks, 0)
    lane_e = lambda r, w, off=0: pl.BlockSpec((r, w), lambda s: (0, off + early(s)))
    lane_l = lambda r, w, off=0: pl.BlockSpec((r, w), lambda s: (0, off + late(s)), pipeline_mode=once)
    mat = pl.BlockSpec((1, blocks, rows_mb, rows_mb), lambda s: (late(s), 0, 0, 0), pipeline_mode=pl.Buffered(1))
    tap = lambda k: pl.BlockSpec((CONV, HEAD_DIM), lambda s: (0, k * HEADS + late(s)))
    r_down, r = FF // shards, D // shards
    a, b = chunks // 2 * 2 * SLICE, 4 * D // 2
    c = b // 2
    pieces = [(0, 0, D), (1, 0, a), (1, a, 2 * FF - a), (2, 0, b), (2, b, c), (2, b + c, c), (3, 0, D)]
    shapes = [(r_down, D), (r, 2 * FF), (r, 4 * D), (r, D)]
    f32 = lambda *shape: jax.ShapeDtypeStruct(shape, F32)
    bf = lambda *shape: jax.ShapeDtypeStruct(shape, BF16)
    vm, dma = pltpu.VMEM, pltpu.SemaphoreType.DMA
    hd = HEAD_DIM
    half = shards // 2
    return pl.pallas_call(
        functools.partial(rear_kernel, shards, blocks, rows_mb, pieces),
        grid=(chunks + HEADS,),
        in_specs=[
            anywhere, anywhere, anywhere, anywhere, anywhere, anywhere, anywhere, full((rows, D)),
            lane_e(rows, SLICE), lane_e(rows, SLICE), lane_e(D, SLICE), lane_e(D, SLICE, chunks),
            pl.BlockSpec((SLICE, D), lambda s: (early(s), 0)), full((1, D)), full((1, D)),
            pl.BlockSpec((hd, D), lambda s: (late(s), 0), pipeline_mode=pl.Buffered(1)), lane_l(D, hd), lane_l(D, hd, HEADS),
            lane_l(D, hd, 2 * HEADS), lane_l(D, hd, 3 * HEADS), full((rows, D)),
            full((HEADS, D)), full((rows, rows)), full((1, 1)),
            lane_l(rows, hd), lane_l(rows, hd), lane_l(rows, hd), lane_l(rows, hd), full((rows, HEADS)), tap(0),
            tap(1), tap(2), full((1, hd)), full((rows, 8)), full((rows, 1)), full((1, rows)), lane_l(rows, hd),
            mat, mat, mat, mat,
        ],
        out_specs=[full(s) for s in shapes] + [anywhere, anywhere, full((16, 128))],
        out_shape=[f32(*s) for s in shapes] + [bf(shards, share, D), bf(shards, share, D), f32(16, 128)],
        scratch_shapes=[vm((half,) + s, BF16) for s in shapes] + [
            vm((2, half, r, 2 * SLICE), BF16), vm((2, half, r, 4 * hd), BF16), vm((2, half // HEADS, r, D), BF16),
            vm((rows, D), F32), vm((rows, D), F32), vm((rows, D), F32), vm((rows, D), BF16), vm((rows, hd), F32),
            vm((rows, hd), BF16), vm((rows, hd), BF16), vm((rows, hd), BF16), vm((rows, hd), BF16),
            vm((D, rows), BF16), vm((rows, HEADS), F32), vm((CONV, 3 * D), F32), vm((1, hd), F32), vm((1, D), F32),
            vm((shards, share, D), BF16), vm((shards, 16, 128), F32), vm((shards, 16, 128), F32),
            dma, dma((3,)), dma((2,)), dma((2,)), dma((2,)),
        ] + [dma] * 9 + Scatter.semaphores(shards, len(pieces)) + Scatter.buffers(shards, shapes),
        compiler_params=pltpu.CompilerParams(
            collective_id=collective_id, has_side_effects=True, vmem_limit_bytes=62 << 20
        ),
        name="rear",
    )(d_down.reshape(half, 2, r_down, D), sent_y, dy, resid, x, a2_t, a1_t, df, gate, up, wgu, wgu, wdown, gain_two, gain_one,
      wout, win, win, win, win, on, wbeta, deal, loss, *proj, beta_pre, taps, taps, taps, gain, mask, segc, segr,
      *saved)


def middle_kernel(
    scale, a2, wga, wup, wdn, resid, later, m, counted, deal,
    gate, up, df, dy, sent_y, loss, d_down,
    hid, acc,
):
    step = pl.program_id(0)
    chunks = FF // FF_STEP

    @pl.when(step == 0)
    def _():
        acc[...] = resid[...]

    @pl.when(step < chunks)
    def _():
        g, u = nn(a2[...], wga[...]), nn(a2[...], wup[...])
        gate[...], up[...] = g, u
        h = (g * sigmoid(g) * u).astype(BF16)
        hid[step] = h
        acc[...] += nn(h, wdn[...])

    @pl.when(step == chunks - 1)
    def _():
        y = acc[...]
        errors = y - later[:, D:]
        masked = m[...] * errors
        loss[...] = jnp.sum(jnp.sum(masked * errors, axis=1, keepdims=True), axis=0, keepdims=True)
        grad = later[:, :D] + (scale / counted[...]) * masked
        dy[...] = grad
        df[...] = grad.astype(BF16)
        sent_y[...] = nn(deal[...], y.astype(BF16)).reshape(sent_y.shape).astype(BF16)

    @pl.when(step >= chunks)
    def _():
        d_down[...] = tn(hid[step - chunks], df[...]).astype(BF16)


def middle(a2, wgu, wdown, resid, later, m, counted, deal, shards):
    rows = a2.shape[0]
    share, chunks = rows // shards, FF // FF_STEP
    full = lambda shape: pl.BlockSpec(shape, lambda s: (0,) * len(shape))
    early = lambda s: jnp.minimum(s, chunks - 1)
    lane = lambda r, off=0: pl.BlockSpec((r, FF_STEP), lambda s: (0, off + early(s)))
    f32 = lambda *shape: jax.ShapeDtypeStruct(shape, F32)
    bf = lambda *shape: jax.ShapeDtypeStruct(shape, BF16)
    return pl.pallas_call(
        functools.partial(middle_kernel, float(rows * shards)),
        grid=(2 * chunks,),
        in_specs=[
            full((rows, D)), lane(D), lane(D, chunks), pl.BlockSpec((FF_STEP, D), lambda s: (early(s), 0)),
            full((rows, D)), full((rows, 2 * D)), full((rows, 1)), full((1, 1)), full((rows, rows)),
        ],
        out_specs=[
            lane(rows), lane(rows), full((rows, D)), full((rows, D)), full((shards, share, D)), full((1, 1)),
            pl.BlockSpec((FF_STEP, D), lambda s: (jnp.maximum(s - chunks, 0), 0)),
        ],
        out_shape=[
            f32(rows, FF), f32(rows, FF), bf(rows, D), f32(rows, D), bf(shards, share, D), f32(1, 1), bf(FF, D),
        ],
        scratch_shapes=[pltpu.VMEM((chunks, rows, FF_STEP), BF16), pltpu.VMEM((rows, D), F32)],
        compiler_params=pltpu.CompilerParams(vmem_limit_bytes=62 << 20),
        name="middle",
    )(a2, wgu, wgu, wdown, resid, later, m, counted, deal)


def settle_kernel(
    got_y, got_dx, sort_t, summed, counted, g_down, g_gu, g_in, g_out,
    output, input_grad, o_in, o_beta, o_taps, o_out, o_one, o_gain, o_two, o_gu, o_down, loss,
):
    shards, share, _ = got_y.shape
    own = o_one.shape[1]
    for got, out in ((got_y, output), (got_dx, input_grad)):
        out[...] = nn(sort_t[...], got[...].astype(F32).reshape(shards * share, D).astype(BF16)).astype(BF16)
    o_in[...], o_out[...], o_gu[...], o_down[...] = g_in[...], g_out[...], g_gu[...], g_down[...]
    total = summed[...]
    o_taps[...] = total[:CONV, : 3 * own]
    o_one[...], o_two[...], o_gain[...] = total[4:5, :own], total[5:6, :own], total[6:7]
    loss[...] = total[7:8, :1] / (D * counted[...])
    o_beta[...] = total[8:, :own]


def settle(got_y, got_dx, sort_t, summed, counted, g_down, g_gu, g_in, g_out):
    rows = sort_t.shape[0]
    own = g_in.shape[0]
    f32 = lambda *shape: jax.ShapeDtypeStruct(shape, F32)
    row = jax.ShapeDtypeStruct((rows, D), BF16)
    return pl.pallas_call(
        settle_kernel,
        out_shape=[row, row, f32(*g_in.shape), f32(HEADS, own), f32(CONV, 3 * own), f32(*g_out.shape), f32(1, own),
                   f32(1, HEAD_DIM), f32(1, own), f32(*g_gu.shape), f32(*g_down.shape), f32(1, 1)],
        name="settle",
    )(got_y, got_dx, sort_t, summed, counted, g_down, g_gu, g_in, g_out)


def scatter_kernel(shards, count, *refs):
    grads, sent, out, got = refs[:count], refs[count], refs[count + 1 : 2 * count + 1], refs[2 * count + 1]
    refs = refs[2 * count + 2 :]
    mine, refs = refs[:count], refs[count:]
    sems, (keep, *back_sems), buffers = refs[:4], refs[4:8], refs[8:]
    here = Here(shards)
    core = here.core
    back = Exchange(here, sent, got, *back_sems)
    other, coming = Scatter.split(shards, count, buffers)
    pieces = [(i, 0, g.shape[-1]) for i, g in enumerate(grads)]

    def kept(n):
        return pltpu.make_async_copy(grads[n].at[:, core], mine[n], keep.at[n])

    net = Scatter(
        here, pieces, lambda n, parity: grads[n].at[:, parity],
        lambda i, q, cols: mine[i][q, :, cols], other, coming, sems, kept,
    )

    def write(i, at, size, value):
        out[i][:, pl.ds(at, size)] = value

    for n in range(count):
        kept(n).start()
    meet(here, True)
    for n in range(count):
        net.pair(n).start()
    back.start()
    for t in range(count + net.stages):
        for n in range(count):
            k = t - n
            if 0 <= k < net.stages:
                net.launch(k, n)
            elif k == net.stages:
                net.finish(n, write)
    back.wait()
    for n in range(count):
        net.end(n)


def scatter(grads, message, shards, collective_id):
    count = len(grads)
    shapes = [(g.shape[0] // shards, g.shape[1]) for g in grads]
    anywhere = pl.BlockSpec(memory_space=pl.ANY)
    dma = pltpu.SemaphoreType.DMA
    *out, got = pl.pallas_call(
        functools.partial(scatter_kernel, shards, count),
        in_specs=[anywhere] * (count + 1),
        out_specs=[pl.BlockSpec(memory_space=pltpu.VMEM)] * count + [anywhere],
        out_shape=[jax.ShapeDtypeStruct(s, F32) for s in shapes]
        + [jax.ShapeDtypeStruct(message.shape, message.dtype)],
        scratch_shapes=[pltpu.VMEM((shards // 2,) + s, BF16) for s in shapes]
        + Scatter.semaphores(shards, count) + [dma((count,)), dma, dma, dma]
        + Scatter.buffers(shards, shapes),
        compiler_params=pltpu.CompilerParams(
            collective_id=collective_id, has_side_effects=True, vmem_limit_bytes=60 << 20
        ),
        name="scatter_last",
    )(*[g.reshape((shards // 2, 2) + s) for g, s in zip(grads, shapes)], message)
    return out, got


def nt(left, right):
    return lax.dot_general(left, right, (((1,), (1,)), ((), ())), preferred_element_type=F32)


def tn(left, right, dtype=F32):
    return lax.dot_general(left, right, (((0,), (0,)), ((), ())), preferred_element_type=dtype)


def nn(left, right):
    return jnp.dot(left, right, preferred_element_type=F32)


def rms(v):
    inv = lax.rsqrt(jnp.mean(v * v, axis=-1, keepdims=True) + 1e-05)
    return v * inv, inv


def rms_back(normed, inv, dn):
    return inv * (dn - normed * jnp.mean(normed * dn, axis=-1, keepdims=True))


def local(
    tokens, cotangent, teacher, valid_mask, deal_rows, lengths, w_in, w_beta, conv_kernel, w_out,
    norm_gain, out_gain, ffn_gain, w_gu, w_down,
):
    shards = lax.axis_size(AXES)
    rows = tokens.shape[0]
    share = rows // shards
    blocks = lengths.shape[0]
    rows_mb = rows // blocks
    a, b, c = CONV * conv_kernel.shape[1], w_beta.shape[0] * HEADS, norm_gain.shape[0]
    small = w_beta.shape[0] * HEADS + CONV * conv_kernel.shape[1] + 2 * norm_gain.shape[0]

    if share % 8 == 0 and (D // shards) % 16 == 0:
        wide = lambda v: jnp.pad(v, ((0, 0), (0, 128 - v.shape[1])))
        half = jnp.concatenate(
            [wide(conv_kernel), wide(norm_gain[None, :]), wide(ffn_gain[None, :]), wide(out_gain[None, :]),
             jnp.zeros((1, 128), BF16)]
        )
        small_block = jnp.concatenate(
            [half, jnp.pad(w_beta.T, ((0, 0), (0, 128 - w_beta.shape[0])))], axis=1
        )
        (win, wout, wdown, wgu, *proj, beta_pre, on, o, ainv, u, p, l, resid, a2, x, m, counted, deal_t, sort_t, later,
         taps, gain_one, gain_two, wbeta, segc, segr, mask, a1, a1_t, a2_t, gain_out) = front(
            [w_in, w_out, w_down, w_gu], small_block, tokens, cotangent, teacher, deal_rows, valid_mask, lengths,
            shards, 0,
        )
        win, wout, wdown, wgu = (w.reshape(-1, w.shape[-1]) for w in (win, wout, wdown, wgu))
        saved = (o, ainv, u, p, l)
        gain_one, gain_two = gain_one[0], gain_two[0]
    else:
        target = deal_rows // rows
        spot = deal_rows % rows
        ahead = (target[None, :] == target[:, None]) & (
            jnp.arange(rows)[None, :] < jnp.arange(rows)[:, None]
        )
        slot = target * share + jnp.sum(ahead.astype(jnp.int32), axis=1)
        sort_t = (slot[:, None] == jnp.arange(rows)[None, :]).astype(BF16)
        sort = (slot[None, :] == jnp.arange(rows)[:, None]).astype(BF16)
        count_own = jnp.sum(valid_mask.astype(F32))
        lane = jnp.arange(128)[None, :]
        notes = jnp.where(
            lane == 0,
            valid_mask.astype(F32)[:, None],
            jnp.where(lane == 1, spot.astype(F32)[:, None], jnp.where(lane == 2, count_own, 0.0)),
        ).astype(BF16)
        packed = jnp.concatenate(
            [conv_kernel.reshape(-1), w_beta.reshape(-1), norm_gain, ffn_gain,
             jnp.zeros((share * 128 - small,), BF16)]
        ).reshape(1, share, 128)
        sorted_rows = nn(sort, jnp.concatenate([tokens, notes], axis=1)).astype(BF16)
        message = jnp.concatenate(
            [sorted_rows.reshape(shards, share, -1), jnp.broadcast_to(packed, (shards, share, 128))],
            axis=2,
        )
        later = nn(sort, jnp.concatenate([cotangent, teacher], axis=1)).astype(BF16)
        later = later.reshape(shards, share, 2 * D)
        (win, wout), arrived = first([w_in, w_out], (2, 1), message, shards, 0)

        flat = arrived.reshape(rows, -1)
        info = flat[:, D : D + 128].astype(F32)
        place = info[:, 1].astype(jnp.int32)
        counted = jnp.sum(arrived[:, 0, D + 2].astype(F32))
        extra = arrived[:, :, D + 128 :].reshape(shards, share * 128)
        taps = extra[:, :a].reshape(shards, CONV, -1).swapaxes(0, 1).reshape(CONV, 3 * D).astype(F32)
        wbeta = extra[:, a : a + b].reshape(D, HEADS)
        gain_one = extra[:, a + b : a + b + c].reshape(D).astype(F32)
        gain_two = extra[:, a + b + c : a + b + 2 * c].reshape(D).astype(F32)
        deal = (place[None, :] == jnp.arange(rows)[:, None]).astype(BF16)
        deal_t = (place[:, None] == jnp.arange(rows)[None, :]).astype(BF16)
        dealt = nn(deal, flat[:, : D + 128])
        x = dealt[:, :D]
        m = dealt[:, D : D + 1]

        ends = jnp.cumsum(lengths, axis=1)
        within = jnp.arange(rows_mb, dtype=jnp.int32)
        seg = jnp.sum((within[None, :, None] >= ends[:, None, :]).astype(jnp.int32), axis=2)
        seg = (seg + (lengths.shape[1] + 1) * jnp.arange(blocks, dtype=jnp.int32)[:, None]).reshape(rows)
        position = jnp.arange(rows, dtype=jnp.int32)
        mask = jnp.stack(
            [jnp.ones((rows,), F32)]
            + [((position >= s) & (jnp.roll(seg, s) == seg)).astype(F32) for s in range(1, CONV)]
            + [jnp.zeros((rows,), F32)] * (8 - CONV),
            axis=1,
        )
        segc, segr = seg[:, None], seg[None, :]
        gain_out = out_gain.astype(F32)[None, :]

        nx, rx = rms(x)
        a1 = (nx * gain_one).astype(BF16)
        wdown, wgu, later, (*proj, beta_pre, on, o, ainv, u, p, l, resid, a2) = forward(
            w_down, w_gu, later, (1, 2), a1, win, wout, wbeta, x, gain_two[None, :], taps, gain_out, mask, segc,
            segr, blocks, shards, 2,
        )
        saved = (o, ainv, u, p, l)
        later = nn(deal, later.reshape(rows, 2 * D))
        g, t = later[:, :D], later[:, D:]
    if share % 8 == 0 and (D // shards) % 16 == 0:
        gate, up, df, dy, sent_y, loss_part, d_down = middle(
            a2, wgu, wdown, resid, later, m, counted, deal_t, shards
        )
        g_down, g_gu, g_in, g_out, got_y, got_dx, summed = rear(
            d_down, sent_y, dy, resid, x, a2_t, a1_t, df, gate, up, wgu, wdown, gain_two[None, :], gain_one[None, :],
            wout, win, on, wbeta, deal_t, loss_part, proj, beta_pre, taps, gain_out, mask, segc, segr, saved, blocks,
            shards, 1,
        )
        (output, input_grad, g_in, g_beta, g_taps, g_out, g_gain_one, g_gain_out, g_gain_two, g_gu, g_down,
         loss) = settle(got_y, got_dx, sort_t, summed, counted, g_down, g_gu, g_in, g_out)
        g_gain_one, g_gain_out, g_gain_two = g_gain_one[0], g_gain_out[0], g_gain_two[0]
        loss, g_beta = loss[0, 0], g_beta.T
    else:
        gu = nn(a2, wgu)
        gate, up = gu[:, :FF], gu[:, FF:]
        hid = (gate * sigmoid(gate) * up).astype(BF16)
        y = resid + nn(hid, wdown)
        errors = y - t
        loss_part = jnp.sum(m * errors * errors)
        dy = g + (rows * shards / counted) * m * errors
        df = dy.astype(BF16)
        (g_down, g_gu, dwq, dwk, dwv, dwg, dw_out, d_wbeta, dx, d_gain_two, d_gain_one, dtq, dtk, dtv,
         d_gain_out) = backward(
            tn(hid, df, BF16), df, a2, gu, wgu, wdown, dy, resid, gain_two[None, :], wout, win, a1, on, x,
            gain_one[None, :], wbeta, proj, beta_pre, taps, gain_out, mask, segc, segr, saved, blocks, shards,
            1,
        )
        back = jnp.concatenate([y.astype(BF16), dx], axis=1)
        back = nn(deal_t, back).astype(BF16).reshape(shards, share, 2 * D)
        (g_out, *g_in), back = scatter([dw_out, dwq, dwk, dwv, dwg], back, shards, 3)
        g_in = jnp.concatenate(g_in, axis=1)
        back = nn(sort_t, back.reshape(rows, 2 * D)).astype(BF16)
        output, input_grad = back[:, :D], back[:, D:]

        d_taps = jnp.concatenate([dtq, dtk, dtv], axis=1)
        tail = jnp.concatenate([d_gain_out.reshape(-1), loss_part.reshape(1)])
        extra = jnp.concatenate(
            [
                d_taps.reshape(CONV, shards, -1).swapaxes(0, 1).reshape(shards, a),
                d_wbeta.reshape(shards, b),
                d_gain_one.reshape(shards, c),
                d_gain_two.reshape(shards, c),
                jnp.broadcast_to(tail[None], (shards, tail.shape[0])),
            ],
            axis=1,
        )
        padded = -(-extra.shape[1] // 128) * 128
        extra = jnp.pad(extra, ((0, 0), (0, padded - extra.shape[1])))
        summed = jnp.sum(
            lax.all_to_all(
                extra.reshape(shards, padded // 128, 128), AXES, split_axis=0, concat_axis=0, tiled=True
            ),
            axis=0,
        ).reshape(-1)
        g_taps = summed[:a].reshape(CONV, -1)
        g_beta = summed[a : a + b].reshape(-1, HEADS)
        g_gain_one = summed[a + b : a + b + c]
        g_gain_two = summed[a + b + c : a + b + 2 * c]
        g_gain_out = summed[a + b + 2 * c : a + b + 2 * c + HEAD_DIM]
        loss = summed[a + b + 2 * c + HEAD_DIM] / (D * counted)

    return (
        output, input_grad, g_in, g_beta, g_taps, g_out, g_gain_one, g_gain_out, g_gain_two, g_gu,
        g_down, loss,
    )


def solution(mesh):
    both = P(AXES, None)
    flat = P(AXES)
    in_specs = (both, both, both, flat, flat, both, both, both, P(None, AXES), both, flat, P(), flat,
                both, both)
    out_specs = (both, both, both, both, P(None, AXES), both, flat, P(), flat, both, both, P())
    return jax.shard_map(local, mesh=mesh, in_specs=in_specs, out_specs=out_specs, check_vma=False)
```
